32 devices in a mesh: ctx: 2 (over core), shard: 16 (over z, y, x).
Axes of the slice: x: 2, y: 2, z: 4, core: 2. Of those that a mesh axis runs over, the one named last changes fastest.
Arguments:
- tokens: bfloat16 [2, 16, 1024, 768], P(None, 'shard', 'ctx'), may hold values from -6 to 6
- cotangent: bfloat16 [2, 16, 1024, 768], P(None, 'shard', 'ctx'), may hold values from -6 to 6
- segment_ids: int32 [2, 16, 1024], P(None, 'shard', 'ctx'), may hold values from 0 to 1, never falling along the last dimension, each value on 1 to 896 neighbouring positions
- padding: int32 [2, 16, 1024], P(None, 'shard', 'ctx'), may hold values 0 or 1
- routes: int32 [2, 16, 1024, 1], P(None, 'shard', 'ctx'), may hold values from 0 to 15; in each aligned block of 512 rows (0 to 511, 512 to 1023, ..., all dimensions but the last counted through in order) at most 64 rows name the same one
- norm_one_gain: bfloat16 [768], replicated, may hold values from 0.5 to 1.5
- qkv_weight: bfloat16 [768, 2304], P('shard'), may hold values from -0.21875 to 0.21875
- out_weight: bfloat16 [768, 768], P('shard'), may hold values from -1.75 to 1.75
- norm_two_gain: bfloat16 [768], replicated, may hold values from 0.5 to 1.5
- centroids: bfloat16 [768, 16], replicated, may hold values from -0.15625 to 0.15625
- expert_in: bfloat16 [16, 768, 3072], P('shard'), may hold values from -0.21875 to 0.21875
- expert_out: bfloat16 [16, 3072, 768], P('shard'), may hold values from -0.21875 to 0.21875
Outputs:
- block_out: bfloat16 [2, 16, 1024, 768], P(None, 'shard', 'ctx')
- grad_tokens: float32 [2, 16, 1024, 768], P(None, 'shard', 'ctx')
- grad_norm_one: float32 [768], P(('ctx', 'shard'))
- grad_qkv: float32 [768, 2304], P(('ctx', 'shard'))
- grad_out_proj: float32 [768, 768], P(('ctx', 'shard'))
- grad_norm_two: float32 [768], P(('ctx', 'shard'))
- grad_centroids: float32 [768, 16], P(('ctx', 'shard'))
- grad_expert_in: float32 [16, 768, 3072], P('shard', None, 'ctx')
- grad_expert_out: float32 [16, 3072, 768], P('shard', 'ctx')
The draws below stay inside these ranges and needn't reach their ends.
Inputs may be any that keep to these rules, and one draw needn't show every extreme that they name: `segment_ids`: segment ids never fall along a sequence; each sequence holds two documents, each of at least 128 and at most 896 positions; where the split falls varies from sequence to sequence. `routes`: within each aligned block of 512 positions of a sequence, no expert is named more than 64 times; some block names some expert exactly 64 times.
All inputs are finite; a program needn't handle non-finite values. No bound on the sum of `padding` on one device may be relied on, other than what follows from the above.
Results may differ from the reference program's by a relative error of at most 0.013.
Values may be sent and summed in bfloat16 or wider, within the bound.
A program may use at most 384 MiB of HBM per device.

```python
import math
import jax
import jax.numpy as jnp
import numpy as np
from jax import lax

D = 768
HEADS = 12
HEAD_DIM = 64
FF = 3072
SEQ_LEN = 1024
MICRO = 2
EXPERTS = 16
SEQS = 16
LOCAL_LEN = 512
CAP = 64
N_CTX = 2


def with_ends(array, key, low, top_value):
    dims = array.shape
    place = [jax.random.randint(jax.random.fold_in(key, axis), (), 0, dims[axis]) for axis in range(len(dims))]
    array = array.at[tuple(place)].set(low)
    longest = dims.index(max(dims))
    place[longest] = (place[longest] + 1) % dims[longest]
    return array.at[tuple(place)].set(top_value)


def level_of(rng, dims, cuts, least, high):
    level, own = 1.0, jax.random.fold_in(rng, 6)
    for dim, shards_of in cuts:
        draws = jnp.exp(jax.random.uniform(jax.random.fold_in(own, dim), (shards_of,), jnp.float32, least / len(cuts), high / len(cuts)))
        level = level * jnp.repeat(draws, dims[dim] // shards_of).reshape([-1 if axis == dim else 1 for axis in range(len(dims))])
    return level


def length_profile(number_of, total, bound, skew):
    weights = [(1 << 20) // math.isqrt(standing ** skew) + 1 for standing in range(2, number_of + 1)]
    spare, given = total - bound - (number_of - 1), [1] * (number_of - 1)
    while spare > 0:
        free = [i for i in range(number_of - 1) if given[i] < bound]
        whole, remaining = sum([weights[i] for i in free]), spare
        for i in free:
            addition = min(bound - given[i], max(1, remaining * weights[i] // whole), spare)
            given[i] = given[i] + addition
            spare = spare - addition
    return np.array([bound] + given)


def ragged(own_key, count, total, reach, lean):
    if count == 2:
        one = jax.random.randint(own_key, (), max(1, total - reach), min(reach, total - 1) + 1)
        return jnp.stack([one, total - one])
    sizes = jnp.asarray(length_profile(count, total, reach, lean), jnp.int32)
    couples = (count - 1) // 2
    donor, taker = sizes[1:1 + 2 * couples:2], sizes[2:2 + 2 * couples:2]
    margin = jnp.minimum(donor - 1, reach - taker)
    passed = jax.random.randint(jax.random.fold_in(own_key, 1), (couples,), 0, 1 << 20) % (margin + 1)
    sizes = sizes.at[1:1 + 2 * couples:2].set(donor - passed).at[2:2 + 2 * couples:2].set(taker + passed)
    return sizes[jax.random.permutation(jax.random.fold_in(own_key, 2), count)]


def assign_block(rng, own, number, rows, number_of, top, reach, skew):
    ranking = jax.random.permutation(rng, number_of)
    crowded, ordinary = load_shares(number_of, rows * top, reach, skew, True), load_shares(number_of, rows * top, reach, skew, False)
    places = jnp.arange(number_of)

    def named(sizes, offset_by):
        used = int((sizes > 0).sum())
        fixed = max(1, used // 4)
        passed = fixed + (places - fixed + offset_by * (used - fixed)) % max(1, number_of - fixed)
        return jnp.zeros((number_of,), jnp.int32).at[ranking[jnp.where(places < fixed, places, passed)]].set(jnp.asarray(sizes, jnp.int32))

    sizes = jnp.where(number % 4 == 0, named(crowded, number // 4), named(ordinary, number - number // 4 - 1))
    mixed = jax.random.permutation(jax.random.fold_in(own, 3), number_of)
    donor, receiver = mixed[0:number_of // 2 * 2:2], mixed[1:number_of // 2 * 2:2]
    margin = jnp.minimum(sizes[donor] - 1, reach - sizes[receiver]) // 2
    margin = jnp.where((donor == ranking[0]) | (receiver == ranking[0]) | (sizes[receiver] == 0), 0, jnp.maximum(margin, 0))
    passed = jax.random.randint(jax.random.fold_in(own, 4), (number_of // 2,), 0, 1 << 20) % (margin + 1)
    sizes = sizes.at[donor].add(-passed).at[receiver].add(passed)
    items = jnp.searchsorted(jnp.cumsum(sizes), jnp.arange(rows * top), side="right").astype(jnp.int32)
    grid = items.reshape(top, rows).T
    grid = grid[jax.random.permutation(jax.random.fold_in(own, 1), rows)]
    offset_by = jax.random.randint(jax.random.fold_in(own, 2), (rows, 1), 0, top)
    return jnp.take_along_axis(grid, (jnp.arange(top)[None, :] + offset_by) % top, axis=1)


def load_shares(count, total, bound, slope, full):
    portions = [(1 << 20) // math.isqrt(standing ** slope) + 1 for standing in range(1, count + 1)]
    largest = bound if full else min(bound, max(-(-total // count), total * portions[0] // sum(portions)))
    least = 1 if total - largest >= count - 1 else 0
    given, surplus = [largest] + [least] * (count - 1), total - largest - least * (count - 1)
    while surplus > 0:
        free = [i for i in range(1, count) if given[i] < largest] or [i for i in range(1, count) if given[i] < bound]
        whole, budget = sum([portions[i] for i in free]), surplus
        for i in free:
            addition = min(bound - given[i], max(1, budget * portions[i] // whole), surplus)
            given[i] = given[i] + addition
            surplus = surplus - addition
    return np.array(given)


def gaussian(stream_key, shape, deviation, reach, cuts=(), kind=jnp.bfloat16):
    gain = level_of(stream_key, shape, cuts, -0.22, 0.18) if cuts else 1.0
    values = jax.random.normal(stream_key, shape, jnp.float32) * deviation * gain
    return jnp.minimum(jnp.maximum(values, -reach), reach).astype(kind)


def setup_inputs(seed: int = 0) -> dict:
    keys = jax.random.split(jax.random.key(seed), 13)
    tokens = gaussian(keys[0], (MICRO, SEQS, SEQ_LEN, D), 1.0, 6.0, ((1, 16), (2, 2)))
    cotangent = gaussian(keys[1], (MICRO, SEQS, SEQ_LEN, D), 1.0, 6.0, ((1, 16), (2, 2)))
    segment_ids = jax.vmap(lambda own: jnp.searchsorted(jnp.cumsum(ragged(own, 2, SEQ_LEN, SEQ_LEN - SEQ_LEN // 8, 0)), jnp.arange(SEQ_LEN), side="right"))(jax.random.split(keys[2], MICRO * SEQS)).reshape((MICRO, SEQS, SEQ_LEN)).astype(jnp.int32)
    padding = with_ends((jax.random.randint(keys[3], (MICRO, SEQS, SEQ_LEN), 0, 8) < 7).astype(jnp.int32), jax.random.fold_in(keys[3], 1), 0, 1)
    routes_keys = jax.random.split(jax.random.fold_in(keys[4], 1), MICRO * SEQS * SEQ_LEN // LOCAL_LEN)
    routes_turns = jax.random.permutation(jax.random.fold_in(keys[4], 3), MICRO * SEQS * SEQ_LEN // LOCAL_LEN)
    routes = jax.vmap(lambda own, number: assign_block(jax.random.fold_in(keys[4], 2), own, number, LOCAL_LEN, EXPERTS, 1, CAP, 2))(routes_keys, routes_turns).reshape((MICRO, SEQS, SEQ_LEN, 1))
    norm_one_gain = jnp.clip(1.0 + 0.1 * jax.random.normal(keys[5], (D,), jnp.float32), 0.5, 1.5).astype(jnp.bfloat16)
    qkv_weight = gaussian(keys[6], (D, 3 * D), D ** -0.5, 0.21875, ((0, 16),))
    out_weight = gaussian(keys[7], (D, D), (D // 64) ** -0.5, 1.75, ((0, 16),))
    norm_two_gain = jnp.clip(1.0 + 0.1 * jax.random.normal(keys[8], (D,), jnp.float32), 0.5, 1.5).astype(jnp.bfloat16)
    centroids = gaussian(keys[9], (D, EXPERTS), (2 * D) ** -0.5, 0.15625)
    expert_in = gaussian(keys[10], (EXPERTS, D, FF), D ** -0.5, 0.21875, ((0, 16),))
    expert_out = gaussian(keys[11], (EXPERTS, FF, D), (FF // 4) ** -0.5, 0.21875, ((0, 16),))
    return dict(tokens=tokens, cotangent=cotangent, segment_ids=segment_ids, padding=padding, routes=routes, norm_one_gain=norm_one_gain, qkv_weight=qkv_weight, out_weight=out_weight, norm_two_gain=norm_two_gain, centroids=centroids, expert_in=expert_in, expert_out=expert_out)


@jax.custom_vjp
def low(v):
    return lax.optimization_barrier(v.astype(jnp.bfloat16)).astype(jnp.float32)

@jax.custom_vjp
def low_back(v):
    return v

def low_keep(v):
    return (low(v), None)

def low_pass(kept, grad):
    return (grad,)

def back_keep(v):
    return (v, None)

def back_low(kept, grad):
    return (low(grad),)
low.defvjp(low_keep, low_pass)
low_back.defvjp(back_keep, back_low)
EPSILON = 1e-05
NEGATIVE = -1e+30
HIGH = lax.Precision.HIGHEST

def layer_norm(values, gain_vec):
    centre = values - lax.optimization_barrier(jnp.mean(values, axis=1, keepdims=True))
    spread = lax.optimization_barrier(jnp.mean(centre * centre, axis=1, keepdims=True))
    return centre * lax.rsqrt(spread + EPSILON) * gain_vec

def slot_table(route_ids):
    expert_ids = jnp.arange(EXPERTS, dtype=jnp.int32)
    choose_mask = (route_ids[:, None] == expert_ids[None, :]).astype(jnp.int32)
    counts = jnp.cumsum(choose_mask.reshape(N_CTX, LOCAL_LEN, EXPERTS), axis=1).reshape(SEQ_LEN, EXPERTS)
    slot_rank = lax.optimization_barrier(jnp.sum(counts * choose_mask, axis=1)) - 1
    positions = jnp.arange(SEQ_LEN, dtype=jnp.int32)
    slot_index = positions // LOCAL_LEN * CAP + slot_rank
    table = jnp.full((EXPERTS, N_CTX * CAP), SEQ_LEN, dtype=jnp.int32)
    return table.at[route_ids, slot_index.astype(jnp.int32)].set(positions)

def forward(params, inputs, doc_ids, pad_mask, route_ids, table):
    gain_one, qkv_full, out_full, gain_two, centre_w, up_all, down_all = params
    normed_one = low(layer_norm(inputs, gain_one))
    qkv = jnp.dot(normed_one, qkv_full, precision=HIGH)
    queries = low_back(low(qkv[:, :D])).reshape(SEQ_LEN, HEADS, HEAD_DIM)
    key_rows = low_back(low(qkv[:, D:2 * D])).reshape(SEQ_LEN, HEADS, HEAD_DIM)
    value_rows = low_back(low(qkv[:, 2 * D:])).reshape(SEQ_LEN, HEADS, HEAD_DIM)
    positions = jnp.arange(SEQ_LEN, dtype=jnp.int32)
    block_rows = min(512, SEQ_LEN)
    blocks = SEQ_LEN // block_rows

    def attend(pieces):
        query_block, query_pos, query_doc = pieces
        scores = jnp.einsum('qhd,khd->hqk', query_block, key_rows, precision=HIGH) * HEAD_DIM ** (-0.5)
        scores = low_back(scores)
        allowed = (query_doc[:, None] == doc_ids[None, :]) & (positions[None, :] <= query_pos[:, None])
        allowed = allowed & ((pad_mask[None, :] == 1) | (positions[None, :] == query_pos[:, None]))
        scores = jnp.where(allowed[None], scores, NEGATIVE)
        probs_now = low(jax.nn.softmax(scores, axis=2))
        return jnp.einsum('hqk,khd->qhd', probs_now, value_rows, precision=HIGH)
    attended = lax.map(jax.checkpoint(attend), (queries.reshape(blocks, block_rows, HEADS, HEAD_DIM), positions.reshape(blocks, block_rows), doc_ids.reshape(blocks, block_rows)))
    attended = low_back(low(attended.reshape(SEQ_LEN, D)))
    residual = inputs + low_back(jnp.dot(attended, out_full, precision=HIGH))
    normed_two = low(layer_norm(residual, gain_two))
    choose_f = (route_ids[:, None] == jnp.arange(EXPERTS, dtype=jnp.int32)[None, :]).astype(jnp.float32)
    logit = lax.optimization_barrier(jnp.sum(jnp.dot(normed_two, centre_w, precision=HIGH) * choose_f, axis=1))
    gate_value = jax.nn.sigmoid(logit)
    extended = jnp.concatenate([normed_two, jnp.zeros((1, D), jnp.float32)], axis=0)
    slot_rows = low_back(extended[table])
    upward = low_back(jnp.einsum('esd,edf->esf', slot_rows, up_all, precision=HIGH))
    hidden = low(jax.nn.gelu(upward, approximate=True))
    result = jnp.einsum('esf,efd->esd', hidden, down_all, precision=HIGH)
    expert_rows = jnp.zeros((SEQ_LEN + 1, D), jnp.float32).at[table.reshape(-1)].add(result.reshape(-1, D))[:SEQ_LEN]
    expert_rows = low_back(low(expert_rows))
    return residual + gate_value[:, None] * expert_rows

def reference(tokens, cotangent, segment_ids, padding, routes, norm_one_gain, qkv_weight, out_weight, norm_two_gain, centroids, expert_in, expert_out):
    params = (norm_one_gain.astype(jnp.float32), qkv_weight.astype(jnp.float32), out_weight.astype(jnp.float32), norm_two_gain.astype(jnp.float32), centroids.astype(jnp.float32), expert_in.astype(jnp.float32), expert_out.astype(jnp.float32))
    sequences = MICRO * SEQS
    flat_tokens = tokens.astype(jnp.float32).reshape(sequences, SEQ_LEN, D)
    flat_grads = cotangent.astype(jnp.float32).reshape(sequences, SEQ_LEN, D)
    flat_docs = segment_ids.reshape(sequences, SEQ_LEN)
    flat_pads = padding.reshape(sequences, SEQ_LEN)
    flat_routes = routes.reshape(sequences, SEQ_LEN)
    tables = jax.vmap(slot_table)(flat_routes)
    zero_grads = jax.tree.map(jnp.zeros_like, params)

    def one_sequence(running, pieces):
        inputs, grad_out, doc_ids, pad_mask, route_ids, table = pieces

        def seq_forward(params_in, inputs_in):
            return forward(params_in, inputs_in, doc_ids, pad_mask, route_ids, table)
        block_value, pullback = jax.vjp(seq_forward, params, inputs)
        grad_params, grad_inputs = pullback(grad_out)
        running = jax.tree.map(jnp.add, running, grad_params)
        return (running, (block_value.astype(jnp.bfloat16), grad_inputs))
    grad_sums, (block_outs, input_grads) = lax.scan(one_sequence, zero_grads, (flat_tokens, flat_grads, flat_docs, flat_pads, flat_routes, tables))
    out_shape = (MICRO, SEQS, SEQ_LEN, D)
    return (block_outs.reshape(out_shape), input_grads.reshape(out_shape), grad_sums[0], grad_sums[1], grad_sums[2], grad_sums[3], grad_sums[4], grad_sums[5], grad_sums[6])
```

```python
import functools

import jax
import jax.numpy as jnp
from jax import lax
from jax.experimental import pallas as pl
from jax.experimental.pallas import tpu as pltpu
from jax.sharding import PartitionSpec as P

D = 768
HEADS = 12
HEAD_DIM = 64
FF = 3072
MICRO = 2


EPSILON = 1e-05
NEGATIVE = -1e30
HIGH = lax.Precision.HIGHEST


def layer_norm(values, gain_vec):
    centre = values - jnp.mean(values, axis=1, keepdims=True)
    spread = jnp.mean(centre * centre, axis=1, keepdims=True)
    return centre * lax.rsqrt(spread + EPSILON) * gain_vec


def gelu_tanh(values):
    return jax.nn.gelu(values, approximate=True)


def masked_scores(queries, key_heads, query_pos, key_pos, query_doc, key_doc, key_pad):
    scores = jnp.einsum(
        "qhd,khd->hqk", queries, key_heads, preferred_element_type=jnp.float32
    ) * HEAD_DIM ** (-0.5)
    allowed = (query_doc[:, None] == key_doc[None, :]) & (key_pos[None, :] <= query_pos[:, None])
    allowed = allowed & ((key_pad[None, :] == 1) | (key_pos[None, :] == query_pos[:, None]))
    return jnp.where(allowed[None], scores, NEGATIVE)


def rows_first(left, right):
    return lax.dot_general(
        left, right, (((0,), (0,)), ((), ())), preferred_element_type=jnp.float32
    )


def rows_last(left, right):
    return lax.dot_general(
        left, right, (((1,), (1,)), ((), ())), preferred_element_type=jnp.float32
    )


def body(
    tokens,
    cotangent,
    segment_ids,
    padding,
    routes,
    norm_one_gain,
    qkv_weight,
    out_weight,
    norm_two_gain,
    centroids,
    expert_in,
    expert_out,
):
    local_len = tokens.shape[2]
    experts = centroids.shape[1]
    capacity = max(2, 2 * local_len // experts)
    seq_len = local_len * lax.axis_size("ctx")
    qkv_full, out_full = (
        lax.all_gather(qkv_weight, "shard", axis=0, tiled=True),
        lax.all_gather(out_weight, "shard", axis=0, tiled=True),
    )
    gain_one = norm_one_gain.astype(jnp.float32)
    gain_two = norm_two_gain.astype(jnp.float32)
    centre_f = centroids.astype(jnp.float32)
    up_local = expert_in[0]
    down_local = expert_out[0]
    query_pos = lax.axis_index("ctx") * local_len + jnp.arange(local_len, dtype=jnp.int32)
    all_pos = jnp.arange(seq_len, dtype=jnp.int32)
    slot_ids = jnp.arange(experts * capacity, dtype=jnp.int32)
    expert_ids = jnp.arange(experts, dtype=jnp.int32)
    score_scale = HEAD_DIM ** (-0.5)
    grad_qkv_sum = jnp.zeros((D, 3 * D), jnp.float32)
    grad_out_sum = jnp.zeros((D, D), jnp.float32)
    grad_one_sum = jnp.zeros((D,), jnp.float32)
    grad_two_sum = jnp.zeros((D,), jnp.float32)
    grad_centre = jnp.zeros((D, experts), jnp.float32)
    grad_up_sum = jnp.zeros((D, FF), jnp.float32)
    grad_down_sum = jnp.zeros((D, FF), jnp.float32)
    block_list = []
    input_list = []
    for micro_index in range(MICRO):
        inputs = tokens[micro_index, 0].astype(jnp.float32)
        doc_ids = segment_ids[micro_index, 0]
        pad_mask = padding[micro_index, 0]
        route_ids = routes[micro_index, 0, :, 0]
        normed_one, norm_one_back = jax.vjp(layer_norm, inputs, gain_one)
        first_bf = normed_one.astype(jnp.bfloat16)
        qkv = jnp.dot(first_bf, qkv_full, preferred_element_type=jnp.float32)
        queries = qkv[:, :D].astype(jnp.bfloat16)
        key_rows = qkv[:, D : 2 * D].astype(jnp.bfloat16)
        value_rows = qkv[:, 2 * D :].astype(jnp.bfloat16)
        key_all, value_all, doc_all, pad_all = (
            lax.all_gather(key_rows, "ctx", axis=0, tiled=True),
            lax.all_gather(value_rows, "ctx", axis=0, tiled=True),
            lax.all_gather(doc_ids, "ctx", axis=0, tiled=True),
            lax.all_gather(pad_mask, "ctx", axis=0, tiled=True),
        )
        query_heads = queries.reshape(local_len, HEADS, HEAD_DIM)
        key_heads = key_all.reshape(seq_len, HEADS, HEAD_DIM)
        value_heads = value_all.reshape(seq_len, HEADS, HEAD_DIM)
        scores = masked_scores(
            query_heads, key_heads, query_pos, all_pos, doc_ids, doc_all, pad_all
        )
        row_max = jnp.max(scores, axis=2, keepdims=True)
        weights = jnp.exp(scores - row_max)
        row_total = jnp.sum(weights, axis=2, keepdims=True)
        probs_now = weights / row_total
        log_total = row_max + jnp.log(row_total)
        attended = jnp.einsum(
            "hqk,khd->qhd",
            probs_now.astype(jnp.bfloat16),
            value_heads,
            preferred_element_type=jnp.float32,
        )
        attended = attended.reshape(local_len, D).astype(jnp.bfloat16)
        residual = inputs + jnp.dot(attended, out_full, preferred_element_type=jnp.float32)
        normed_two, norm_two_back = jax.vjp(layer_norm, residual, gain_two)
        second_bf = normed_two.astype(jnp.bfloat16)
        choose_mask = route_ids[:, None] == expert_ids[None, :]
        choose_f = choose_mask.astype(jnp.float32)
        logit = jnp.sum(
            jnp.dot(second_bf, centroids, preferred_element_type=jnp.float32) * choose_f, axis=1
        )
        gate_value = jax.nn.sigmoid(logit)
        choose_int = choose_mask.astype(jnp.int32)
        counts = jnp.cumsum(choose_int, axis=0)
        slot_rank = jnp.sum(counts * choose_int, axis=1) - 1
        target = route_ids * capacity + slot_rank
        dispatch = (slot_ids[:, None] == target[None, :]).astype(jnp.bfloat16)
        outbound = jnp.dot(dispatch, second_bf, preferred_element_type=jnp.float32).astype(
            jnp.bfloat16
        )
        outbound = outbound.reshape(experts, capacity, D)
        received = lax.all_to_all(outbound, "shard", split_axis=0, concat_axis=0, tiled=True)
        slot_rows = received.reshape(-1, D)
        upward = jnp.dot(slot_rows, up_local, preferred_element_type=jnp.float32)
        hidden = gelu_tanh(upward).astype(jnp.bfloat16)
        result = jnp.dot(hidden, down_local, preferred_element_type=jnp.float32).astype(
            jnp.bfloat16
        )
        returned = lax.all_to_all(
            result.reshape(received.shape), "shard", split_axis=0, concat_axis=0, tiled=True
        )
        returned, received, upward = (
            returned,
            received,
            upward.reshape(received.shape[0], received.shape[1], FF),
        )
        expert_rows = rows_first(dispatch, returned.reshape(experts * capacity, D))
        block_list.append((residual + gate_value[:, None] * expert_rows).astype(jnp.bfloat16))
        grad_out = cotangent[micro_index, 0].astype(jnp.float32)
        grad_gate = jnp.sum(grad_out * expert_rows, axis=1)
        grad_logit = grad_gate * gate_value * (1.0 - gate_value)
        grad_rows = (gate_value[:, None] * grad_out).astype(jnp.bfloat16)
        grad_outbound = jnp.dot(dispatch, grad_rows, preferred_element_type=jnp.float32).astype(
            jnp.bfloat16
        )
        grad_received = lax.all_to_all(
            grad_outbound.reshape(experts, capacity, D),
            "shard",
            split_axis=0,
            concat_axis=0,
            tiled=True,
        )
        grad_result = grad_received.reshape(-1, D)
        hidden_again, gelu_back = jax.vjp(gelu_tanh, upward.reshape(-1, FF))
        grad_down_sum = grad_down_sum + rows_first(grad_result, hidden_again.astype(jnp.bfloat16))
        grad_hidden = rows_last(grad_result, down_local)
        grad_upward = gelu_back(grad_hidden)[0].astype(jnp.bfloat16)
        grad_up_sum = grad_up_sum + rows_first(received.reshape(-1, D), grad_upward)
        grad_send = (
            rows_last(grad_upward, up_local).astype(jnp.bfloat16).reshape(grad_received.shape)
        )
        grad_back = lax.all_to_all(grad_send, "shard", split_axis=0, concat_axis=0, tiled=True)
        grad_second = rows_first(dispatch, grad_back.reshape(experts * capacity, D))
        grad_second = grad_second + grad_logit[:, None] * jnp.dot(
            choose_f, centre_f.T, precision=HIGH
        )
        grad_centre = grad_centre + jnp.dot(
            second_bf.astype(jnp.float32).T, choose_f * grad_logit[:, None], precision=HIGH
        )
        grad_resid_norm, grad_two_term = norm_two_back(grad_second)
        grad_residual = grad_out + grad_resid_norm
        grad_two_sum = grad_two_sum + grad_two_term
        grad_branch = grad_residual.astype(jnp.bfloat16)
        grad_out_sum = grad_out_sum + rows_first(attended, grad_branch)
        grad_attend = (
            rows_last(grad_branch, out_full)
            .astype(jnp.bfloat16)
            .reshape(local_len, HEADS, HEAD_DIM)
        )
        probs_again = jnp.exp(
            masked_scores(query_heads, key_heads, query_pos, all_pos, doc_ids, doc_all, pad_all)
            - log_total
        )
        grad_probs = jnp.einsum(
            "qhd,khd->hqk", grad_attend, value_heads, preferred_element_type=jnp.float32
        )
        row_terms = jnp.sum(probs_again * grad_probs, axis=2, keepdims=True)
        grad_scores = (probs_again * (grad_probs - row_terms)).astype(jnp.bfloat16)
        grad_query = (
            jnp.einsum("hqk,khd->qhd", grad_scores, key_heads, preferred_element_type=jnp.float32)
            * score_scale
        )
        grad_key_all = (
            jnp.einsum("hqk,qhd->khd", grad_scores, query_heads, preferred_element_type=jnp.float32)
            * score_scale
        )
        grad_value_all = jnp.einsum(
            "hqk,qhd->khd",
            probs_again.astype(jnp.bfloat16),
            grad_attend,
            preferred_element_type=jnp.float32,
        )
        grad_key, grad_value = (
            lax.psum_scatter(
                grad_key_all.reshape(seq_len, D).astype(jnp.bfloat16),
                "ctx",
                scatter_dimension=0,
                tiled=True,
            ).astype(jnp.float32),
            lax.psum_scatter(
                grad_value_all.reshape(seq_len, D).astype(jnp.bfloat16),
                "ctx",
                scatter_dimension=0,
                tiled=True,
            ).astype(jnp.float32),
        )
        grad_qkv_rows = jnp.concatenate(
            [grad_query.reshape(local_len, D), grad_key, grad_value], axis=1
        ).astype(jnp.bfloat16)
        grad_qkv_sum = grad_qkv_sum + rows_first(first_bf, grad_qkv_rows)
        grad_first = rows_last(grad_qkv_rows, qkv_full)
        grad_in_norm, grad_one_term = norm_one_back(grad_first)
        grad_one_sum = grad_one_sum + grad_one_term
        input_list.append(grad_residual + grad_in_norm)
    dense_sums = (
        lax.psum_scatter(grad_one_sum, ("ctx", "shard"), scatter_dimension=0, tiled=True),
        lax.psum_scatter(grad_qkv_sum, ("ctx", "shard"), scatter_dimension=0, tiled=True),
        lax.psum_scatter(grad_out_sum, ("ctx", "shard"), scatter_dimension=0, tiled=True),
        lax.psum_scatter(grad_two_sum, ("ctx", "shard"), scatter_dimension=0, tiled=True),
        lax.psum_scatter(grad_centre, ("ctx", "shard"), scatter_dimension=0, tiled=True),
    )
    expert_sums = (
        lax.psum_scatter(
            grad_up_sum.astype(jnp.bfloat16), "ctx", scatter_dimension=1, tiled=True
        ).astype(jnp.float32),
        lax.psum_scatter(
            grad_down_sum.astype(jnp.bfloat16), "ctx", scatter_dimension=1, tiled=True
        ).astype(jnp.float32),
    )
    block_out = jnp.stack(block_list)[:, None]
    grad_tokens = jnp.stack(input_list)[:, None]
    return (
        block_out,
        grad_tokens,
        dense_sums[0],
        dense_sums[1],
        dense_sums[2],
        dense_sums[3],
        dense_sums[4],
        expert_sums[0][None],
        expert_sums[1].T[None],
    )


BF = jnp.bfloat16
F32 = jnp.float32
QB = 256
GELU_K = 0.7978845608028654
VMEM_WHOLE = pl.BlockSpec(memory_space=pltpu.VMEM)


def nn(left, right):
    return lax.dot_general(left, right, (((1,), (0,)), ((), ())), preferred_element_type=F32)


def nt(left, right):
    return lax.dot_general(left, right, (((1,), (1,)), ((), ())), preferred_element_type=F32)


def tn(left, right):
    return lax.dot_general(left, right, (((0,), (0,)), ((), ())), preferred_element_type=F32)


def lanes_of(shape, half):
    lane = lax.broadcasted_iota(jnp.int32, shape, 1)
    return (lane < HEAD_DIM) if half == 0 else (lane >= HEAD_DIM)


def attend_kernel(h_ref, w_ref, doc_col_ref, code_row_ref, qkv_ref, o_ref, lse_ref):
    seq, width = h_ref.shape[0], o_ref.shape[1]
    scale = HEAD_DIM ** (-0.5)

    def project(block, carry):
        rows = pl.ds(block * QB, QB)
        qkv_ref[rows, :] = nn(h_ref[rows, :], w_ref[:, 0 : 3 * width]).astype(BF)
        return carry

    lax.fori_loop(0, seq // QB, project, 0)
    for block in range(seq // QB):
        low, kend = block * QB, (block + 1) * QB
        rows = slice(low, kend)
        qpos = lax.broadcasted_iota(jnp.int32, (QB, kend), 0) + low
        kpos = lax.broadcasted_iota(jnp.int32, (QB, kend), 1)
        same = doc_col_ref[rows, :] == code_row_ref[:, 0:kend]
        allowed = (same & (kpos < qpos)) | (kpos == qpos)
        bias = jnp.where(allowed, 0.0, NEGATIVE).astype(F32)
        lane = lax.broadcasted_iota(jnp.int32, (QB, 128), 1)

        def pair(index, stats):
            at = pl.multiple_of(index * 128, 128)
            q = qkv_ref[rows, pl.ds(at, 128)] * jnp.asarray(scale, BF)
            k = qkv_ref[0:kend, pl.ds(width + at, 128)]
            v = qkv_ref[0:kend, pl.ds(2 * width + at, 128)]
            outs = []
            for half in range(2):
                qm = jnp.where(lanes_of(q.shape, half), q, jnp.zeros_like(q))
                s = nt(qm, k) + bias
                top = jnp.max(s, axis=1, keepdims=True)
                e = jnp.exp(s - top)
                total = jnp.sum(e, axis=1, keepdims=True)
                outs.append(nn(e.astype(BF), v) * (1.0 / total))
                stats = jnp.where(lane == 2 * index + half, top + jnp.log(total), stats)
            o_ref[rows, pl.ds(at, 128)] = jnp.where(
                lanes_of(outs[0].shape, 0), outs[0], outs[1]
            ).astype(BF)
            return stats

        stats = lax.fori_loop(0, width // 128, pair, jnp.zeros((QB, 128), F32))
        lse_ref[:, rows] = jnp.transpose(stats)[0 : lse_ref.shape[0], :]


def attend(h_all, w_own, doc_col, code_row):
    seq, width = h_all.shape[0], D // 2
    flops = 2 * seq * D * 3 * width + 4 * seq * seq * width
    return pl.pallas_call(
        attend_kernel,
        out_shape=(
            jax.ShapeDtypeStruct((seq, 3 * width), BF),
            jax.ShapeDtypeStruct((seq, width), BF),
            jax.ShapeDtypeStruct((8, seq), F32),
        ),
        in_specs=[VMEM_WHOLE] * 4,
        out_specs=(VMEM_WHOLE,) * 3,
        compiler_params=pltpu.CompilerParams(vmem_limit_bytes=48 << 20),
        cost_estimate=pl.CostEstimate(
            flops=4 * flops, bytes_accessed=8 << 20, transcendentals=seq * seq * width // 128
        ),
        name="attend",
    )(h_all, w_own, doc_col, code_row)


def attend_back_kernel(has_prev, *refs):
    if has_prev:
        (h_ref, w_ref, qkv_ref, do_ref, lse_ref, doc_row_ref, code_col_ref, prev_ref,
         gw_ref, dh_ref, dqkv_ref, dk_ref, dv_ref, kt_ref) = refs
    else:
        (h_ref, w_ref, qkv_ref, do_ref, lse_ref, doc_row_ref, code_col_ref,
         gw_ref, dh_ref, dqkv_ref, dk_ref, dv_ref, kt_ref) = refs
    seq, width = do_ref.shape
    scale = HEAD_DIM ** (-0.5)
    dk_ref[...] = jnp.zeros_like(dk_ref)
    dv_ref[...] = jnp.zeros_like(dv_ref)
    kt_ref[...] = jnp.transpose(qkv_ref[:, width : 2 * width])
    for block in range(seq // QB):
        low, kend = block * QB, (block + 1) * QB
        rows = slice(low, kend)
        qpos = lax.broadcasted_iota(jnp.int32, (kend, QB), 1) + low
        kpos = lax.broadcasted_iota(jnp.int32, (kend, QB), 0)
        same = doc_row_ref[:, rows] == code_col_ref[0:kend, :]
        allowed = (same & (kpos < qpos)) | (kpos == qpos)
        bias = jnp.where(allowed, 0.0, NEGATIVE).astype(F32)

        def pair(index, carry):
            at = pl.multiple_of(index * 128, 128)
            q = qkv_ref[rows, pl.ds(at, 128)] * jnp.asarray(scale, BF)
            k = qkv_ref[0:kend, pl.ds(width + at, 128)]
            v = qkv_ref[0:kend, pl.ds(2 * width + at, 128)]
            do = do_ref[rows, pl.ds(at, 128)]
            dqt = jnp.zeros((128, QB), F32)
            dv = dk = None
            for half in range(2):
                keep = lanes_of(q.shape, half)
                qm = jnp.where(keep, q, jnp.zeros_like(q))
                dom = jnp.where(keep, do, jnp.zeros_like(do))
                p = jnp.exp(nt(k, qm) + bias - lse_ref[pl.ds(2 * index + half, 1), rows])
                dp = nt(v, dom)
                delta = jnp.sum(p * dp, axis=0, keepdims=True)
                ds = (p * (dp - delta)).astype(BF)
                dv_half = nn(p.astype(BF), dom)
                dk_half = nn(ds, qm)
                dv = dv_half if dv is None else dv + dv_half
                dk = dk_half if dk is None else dk + dk_half
                kt = kt_ref[pl.ds(pl.multiple_of(at + half * HEAD_DIM, HEAD_DIM), HEAD_DIM), 0:kend]
                dqt = nn(kt, ds) if half == 0 else jnp.concatenate([dqt, nn(kt, ds)], axis=0)
            dv_ref[0:kend, pl.ds(at, 128)] += dv
            dk_ref[0:kend, pl.ds(at, 128)] += dk
            dqkv_ref[rows, pl.ds(at, 128)] = (jnp.transpose(dqt) * scale).astype(BF)
            return carry

        lax.fori_loop(0, width // 128, pair, 0)
    dqkv_ref[:, width : 2 * width] = dk_ref[...].astype(BF)
    dqkv_ref[:, 2 * width :] = dv_ref[...].astype(BF)

    def spread(block, carry):
        rows = pl.ds(block * QB, QB)
        dh_ref[rows, :] = nt(dqkv_ref[rows, :], w_ref[:, 0 : 3 * width])
        return carry

    lax.fori_loop(0, seq // QB, spread, 0)

    def weigh(block, carry):
        cols = pl.ds(pl.multiple_of(block * 128, 128), 128)
        grad = tn(h_ref[...], dqkv_ref[:, cols])
        if has_prev:
            grad = grad + prev_ref[:, cols]
        gw_ref[:, cols] = grad.astype(gw_ref.dtype)
        return carry

    lax.fori_loop(0, 3 * width // 128, weigh, 0)


def attend_back(h_all, w_own, qkv, do_all, lse, doc_row, code_col, prev):
    seq, width = do_all.shape
    flops = 2 * seq * D * 3 * width * 2 + 10 * seq * seq * width
    args = [h_all, w_own, qkv, do_all, lse, doc_row, code_col]
    if prev is not None:
        args.append(prev)
    return pl.pallas_call(
        functools.partial(attend_back_kernel, prev is not None),
        out_shape=(
            jax.ShapeDtypeStruct((D, 3 * width), F32),
            jax.ShapeDtypeStruct((seq, D), F32),
        ),
        in_specs=[VMEM_WHOLE] * len(args),
        out_specs=(VMEM_WHOLE,) * 2,
        scratch_shapes=[
            pltpu.VMEM((seq, 3 * width), BF),
            pltpu.VMEM((seq, width), F32),
            pltpu.VMEM((seq, width), F32),
            pltpu.VMEM((width, seq), BF),
        ],
        compiler_params=pltpu.CompilerParams(vmem_limit_bytes=56 << 20),
        cost_estimate=pl.CostEstimate(
            flops=4 * flops, bytes_accessed=16 << 20, transcendentals=seq * seq * width // 128
        ),
        name="attend_back",
    )(*args)


FB = 512


def expert_kernel(has_prev, side_ref, h_ref, g_ref, c_ref, up_ref, down_ref, *refs):
    if has_prev:
        (prev_up_ref, prev_down_ref, y_ref, dh_ref, gc_ref, gup_ref, gdown_ref,
         dz_ref, gate_ref, z_ref, acc_ref, a_ref, du_ref) = refs
    else:
        (y_ref, dh_ref, gc_ref, gup_ref, gdown_ref,
         dz_ref, gate_ref, z_ref, acc_ref, a_ref, du_ref) = refs
    step, steps = pl.program_id(0), pl.num_programs(0)
    rows_all = h_ref.shape[0]
    blocks = rows_all // QB

    @pl.when(step == 0)
    def _():
        def start(block, carry):
            rows = pl.ds(block * QB, QB)
            logit = jnp.sum(h_ref[rows, :].astype(F32) * c_ref[...], axis=1, keepdims=True)
            gate = 1.0 / (1.0 + jnp.exp(-logit))
            gate_ref[rows, :] = gate
            dz_ref[rows, :] = (gate * g_ref[rows, :].astype(F32)).astype(BF)
            z_ref[rows, :] = jnp.zeros((QB, D), F32)
            acc_ref[rows, :] = jnp.zeros((QB, D), F32)
            return carry

        lax.fori_loop(0, blocks, start, 0)

    def forward(block, carry):
        rows = pl.ds(block * QB, QB)
        u = nn(h_ref[rows, :], up_ref[...])
        square = u * u
        t = jnp.tanh(GELU_K * u * (1.0 + 0.044715 * square))
        a = (0.5 * u * (1.0 + t)).astype(BF)
        slope = 0.5 * (1.0 + t) + 0.5 * u * (1.0 - t * t) * (
            GELU_K * (1.0 + 3 * 0.044715 * square)
        )
        a_ref[rows, :] = a
        z_ref[rows, :] += nn(a, down_ref[...])
        du = (nt(dz_ref[rows, :], down_ref[...]) * slope).astype(BF)
        du_ref[rows, :] = du
        acc_ref[rows, :] += nt(du, up_ref[...])
        return carry

    lax.fori_loop(0, blocks, forward, 0)
    gup = tn(h_ref[...], du_ref[...])
    gdown = tn(a_ref[...], dz_ref[...])
    if has_prev:
        gup = gup + prev_up_ref[...]
        gdown = gdown + prev_down_ref[...]
    gup_ref[...] = gup
    gdown_ref[...] = gdown

    @pl.when(step == steps - 1)
    def _():
        def finish(block, total):
            rows = pl.ds(block * QB, QB)
            z = z_ref[rows, :].astype(BF).astype(F32)
            gate = gate_ref[rows, :]
            dgate = jnp.sum(g_ref[rows, :].astype(F32) * z, axis=1, keepdims=True)
            dlogit = dgate * gate * (1.0 - gate)
            y_ref[rows, :] = (gate * z).astype(BF)
            dh_ref[rows, :] = (acc_ref[rows, :] + dlogit * c_ref[...]).astype(BF)
            return total + jnp.sum(
                dlogit * h_ref[rows, :].astype(F32), axis=0, keepdims=True
            )

        gc_ref[...] = lax.fori_loop(0, blocks, finish, jnp.zeros((1, D), F32))


def expert(side, h_slots, g_slots, g_block, centre, up, down, prev):
    rows = h_slots.shape[0]
    ff = up.shape[1]
    steps = ff // FB
    half = steps // 2
    whole = lambda step, side: (0, 0)
    turn = lambda step, side: (step + half * (1 - side[0])) % steps
    up_map = lambda step, side: (0, turn(step, side))
    down_map = lambda step, side: (turn(step, side), 0)
    in_specs = [
        pl.BlockSpec((rows, D), whole, pipeline_mode=pl.Buffered(1)),
        pl.BlockSpec((rows, D), lambda step, side: (g_block, 0), pipeline_mode=pl.Buffered(1)),
        pl.BlockSpec((1, D), whole),
        pl.BlockSpec((D, FB), up_map),
        pl.BlockSpec((FB, D), down_map),
    ]
    up_at = lambda step, side: (0, step)
    down_at = lambda step, side: (step, 0)
    args = [h_slots, g_slots, centre, up, down]
    if prev is not None:
        in_specs += [pl.BlockSpec((D, FB), up_at), pl.BlockSpec((FB, D), down_at)]
        args += list(prev)
    flops = 12 * rows * D * ff
    return pl.pallas_call(
        functools.partial(expert_kernel, prev is not None),
        out_shape=(
            jax.ShapeDtypeStruct((rows, D), BF),
            jax.ShapeDtypeStruct((rows, D), BF),
            jax.ShapeDtypeStruct((1, D), F32),
            jax.ShapeDtypeStruct((D, ff), F32),
            jax.ShapeDtypeStruct((ff, D), F32),
        ),
        grid_spec=pltpu.PrefetchScalarGridSpec(
            num_scalar_prefetch=1,
            grid=(steps,),
            in_specs=in_specs,
            out_specs=(
                pl.BlockSpec((rows, D), whole),
                pl.BlockSpec((rows, D), whole),
                pl.BlockSpec((1, D), whole),
                pl.BlockSpec((D, FB), up_at),
                pl.BlockSpec((FB, D), down_at),
            ),
            scratch_shapes=[
                pltpu.VMEM((rows, D), BF),
                pltpu.VMEM((rows, 1), F32),
                pltpu.VMEM((rows, D), F32),
                pltpu.VMEM((rows, D), F32),
                pltpu.VMEM((rows, FB), BF),
                pltpu.VMEM((rows, FB), BF),
            ],
        ),
        compiler_params=pltpu.CompilerParams(vmem_limit_bytes=56 << 20),
        cost_estimate=pl.CostEstimate(
            flops=flops, bytes_accessed=40 << 20, transcendentals=rows * ff
        ),
        name="expert",
    )(side, *args)


def swap(array):
    return lax.ppermute(array, "ctx", [(0, 1), (1, 0)])


def half_of(array, index, axis):
    size = array.shape[axis] // 2
    return lax.dynamic_slice_in_dim(array, index * size, size, axis)


def greet(peers):
    barrier = pltpu.get_barrier_semaphore()
    for peer in peers:
        pl.semaphore_signal(
            barrier, inc=1, device_id=peer, device_id_type=pl.DeviceIdType.MESH
        )
    pl.semaphore_wait(barrier, len(peers))


def send(src, dst, send_sem, recv_sem, peer):
    return pltpu.make_async_remote_copy(
        src_ref=src,
        dst_ref=dst,
        send_sem=send_sem,
        recv_sem=recv_sem,
        device_id=peer,
        device_id_type=pl.DeviceIdType.MESH,
    )


def places():
    me, core = lax.axis_index("shard"), lax.axis_index("ctx")
    z, y, x = me // 4, (me // 2) % 2, me % 2
    along_y, along_x = me + 2 - 4 * y, me + 1 - 2 * x
    first = along_y * (1 - core) + along_x * core
    second = along_x * (1 - core) + along_y * core
    far = 4 * z + 3 - me % 4
    line = [z, z + 1 - 2 * (z % 2), (z + 2) % 4, 3 - z]
    return me, first, second, far, line


def gather_kernel(w_ref, out_ref, send_sem, recv_sem):
    size = w_ref.shape[0]
    me, first, second, far, line = places()
    lines = [4 * z for z in line]

    def rows(block):
        return out_ref.at[pl.ds(pl.multiple_of(block * size, 16), size), :]

    peers = [{"shard": lines[j] + me % 4} for j in (1, 2, 3)]
    one, two = {"shard": first}, {"shard": second}
    greet(peers + [one, two])
    copies = []

    def push(block, role, peer, src=None):
        copy = send(
            rows(block) if src is None else src,
            rows(block),
            send_sem.at[len(copies)],
            recv_sem.at[role],
            peer,
        )
        copy.start()
        copies.append(copy)

    def arrive(block, role):
        send(rows(block), rows(block), send_sem.at[0], recv_sem.at[role], one).wait_recv()

    push(me, 3, one, w_ref)
    push(me, 7, two, w_ref)
    for j in (1, 2, 3):
        push(me, j - 1, peers[j - 1], w_ref)
    out_ref[pl.ds(pl.multiple_of(me * size, 16), size), :] = w_ref[...]
    arrive(lines[0] + first % 4, 3)
    push(lines[0] + first % 4, 11, two)
    for j in (1, 2, 3):
        block = lines[j] + me % 4
        arrive(block, j - 1)
        push(block, 3 + j, one)
        push(block, 7 + j, two)
        if j > 1:
            block = lines[j - 1] + first % 4
            arrive(block, 3 + j - 1)
            push(block, 11 + j - 1, two)
    block = lines[3] + first % 4
    arrive(block, 6)
    push(block, 14, two)
    for j in range(4):
        arrive(lines[j] + second % 4, 7 + j)
        arrive(lines[j] + far % 4, 11 + j)
    for copy in copies:
        copy.wait_send()


def gather_weights(w_mine):
    size, columns = w_mine.shape
    return pl.pallas_call(
        gather_kernel,
        out_shape=jax.ShapeDtypeStruct((16 * size, columns), BF),
        in_specs=[VMEM_WHOLE],
        out_specs=VMEM_WHOLE,
        scratch_shapes=[pltpu.SemaphoreType.DMA((15,)), pltpu.SemaphoreType.DMA((15,))],
        compiler_params=pltpu.CompilerParams(
            collective_id=0, has_side_effects=True, vmem_limit_bytes=16 << 20
        ),
        name="gather_weights",
    )(w_mine)


def scatter_kernel(
    gw_ref, go_ref, rows_ref, total_ref, theirs_ref,
    packed_ref, rx1_ref, rx2_ref, rx3_ref, tx1_ref, tx2_ref, sum_ref, small_ref,
    send_sem, recv_sem,
):
    me, first, second, far, line = places()
    core = lax.axis_index("ctx")
    lines = [4 * z for z in line]
    part = sum_ref.shape[0] // 2
    wide, half = gw_ref.shape[1], go_ref.shape[1]
    peers = [{"shard": lines[j] + me % 4} for j in (1, 2, 3)]
    one, two, twin = {"shard": first}, {"shard": second}, {"ctx": 1 - core}
    greet(peers + [one, two, twin])
    small_ref[...] = jnp.transpose(rows_ref[...])

    def pack(chunk, carry):
        top = pl.ds(pl.multiple_of(chunk * part, 8), part)
        low = pl.ds(pl.multiple_of(D // 2 + chunk * part, 8), part)
        for ref, at, size in ((gw_ref, 0, wide), (go_ref, wide, half), (small_ref, wide + half, 128)):
            both = jnp.concatenate([ref[top, :], ref[low, :]], axis=0)
            packed_ref[chunk, :, at : at + size] = both.astype(BF)
        return carry

    lax.fori_loop(0, 16, pack, 0)
    copies = []

    def push(src, dst, role, peer):
        copy = send(src, dst, send_sem.at[role], recv_sem.at[role], peer)
        copy.start()
        copies.append(copy)

    def arrive(dst, role):
        send(dst, dst, send_sem.at[role], recv_sem.at[role], one).wait_recv()

    order = (3, 2, 1, 0)
    for j in order:
        push(packed_ref.at[lines[j] + far % 4], rx1_ref.at[j], j, two)
    for j in order:
        push(packed_ref.at[lines[j] + second % 4], rx1_ref.at[4 + j], 4 + j, two)
    for j in order:
        arrive(rx1_ref.at[j], j)
        total = packed_ref[lines[j] + first % 4].astype(F32) + rx1_ref[j].astype(F32)
        tx1_ref[j] = total.astype(BF)
        push(tx1_ref.at[j], rx2_ref.at[j], 8 + j, one)
    own = None
    for j in order:
        arrive(rx1_ref.at[4 + j], 4 + j)
        total = packed_ref[lines[j] + me % 4].astype(F32) + rx1_ref[4 + j].astype(F32)
        arrive(rx2_ref.at[j], 8 + j)
        total = total + rx2_ref[j].astype(F32)
        if j:
            tx2_ref[j - 1] = total.astype(BF)
            push(tx2_ref.at[j - 1], rx3_ref.at[j - 1], 11 + j, peers[j - 1])
        else:
            own = total
    for j in (1, 2, 3):
        arrive(rx3_ref.at[j - 1], 11 + j)
        own = own + rx3_ref[j - 1].astype(F32)
    sum_ref[...] = own
    push(
        sum_ref.at[pl.ds(pl.multiple_of((1 - core) * part, 8), part), :], theirs_ref, 15, twin
    )
    total_ref[...] = sum_ref[pl.ds(pl.multiple_of(core * part, 8), part), :]
    arrive(theirs_ref, 15)
    for copy in copies:
        copy.wait_send()


def scatter_grads(grad_w, grad_out, rows):
    columns = grad_w.shape[1] + grad_out.shape[1] + 128
    part = D // 32
    chunk = (2 * part, columns)
    return pl.pallas_call(
        scatter_kernel,
        out_shape=(
            jax.ShapeDtypeStruct((part, columns), F32),
            jax.ShapeDtypeStruct((part, columns), F32),
        ),
        in_specs=[VMEM_WHOLE] * 3,
        out_specs=(VMEM_WHOLE,) * 2,
        scratch_shapes=[
            pltpu.VMEM((16,) + chunk, BF),
            pltpu.VMEM((8,) + chunk, BF),
            pltpu.VMEM((4,) + chunk, BF),
            pltpu.VMEM((3,) + chunk, BF),
            pltpu.VMEM((4,) + chunk, BF),
            pltpu.VMEM((3,) + chunk, BF),
            pltpu.VMEM(chunk, F32),
            pltpu.VMEM((D, 128), F32),
            pltpu.SemaphoreType.DMA((16,)),
            pltpu.SemaphoreType.DMA((16,)),
        ],
        compiler_params=pltpu.CompilerParams(
            collective_id=1, has_side_effects=True, vmem_limit_bytes=40 << 20
        ),
        name="scatter_grads",
    )(grad_w, grad_out, rows)


def normal(values):
    centre = values - jnp.mean(values, axis=1, keepdims=True)
    spread = jnp.mean(centre * centre, axis=1, keepdims=True)
    scale = lax.rsqrt(spread + EPSILON)
    return centre * scale, scale


def normal_back(unit, scale, gain, grad):
    pull = grad * gain
    return scale * (
        pull
        - jnp.mean(pull, axis=1, keepdims=True)
        - unit * jnp.mean(pull * unit, axis=1, keepdims=True)
    )


RB = 128


def post_kernel(
    x_ref, o_ref, wo_ref, gain_ref, target_ref, slots_ref, x1_ref, full_ref, h_ref, send_sem, recv_sem
):
    core = lax.axis_index("ctx")
    rows, width = x_ref.shape[0], o_ref.shape[1]
    twin = {"ctx": 1 - core}
    mine = pl.ds(pl.multiple_of(core * width, 128), width)
    greet([twin])
    copy = send(
        o_ref.at[pl.ds(pl.multiple_of((1 - core) * rows, 128), rows), :],
        full_ref.at[:, mine],
        send_sem,
        recv_sem,
        twin,
    )
    copy.start()
    full_ref[:, mine] = o_ref[pl.ds(pl.multiple_of(core * rows, 128), rows), :]
    copy.wait()

    def norm(block, carry):
        at = pl.ds(pl.multiple_of(block * RB, RB), RB)
        value = x_ref[at, :].astype(F32) + nn(full_ref[at, :], wo_ref[...])
        x1_ref[at, :] = value
        h_ref[at, :] = (normal(value)[0] * gain_ref[...]).astype(BF)
        return carry

    lax.fori_loop(0, rows // RB, norm, 0)

    def place(block, carry):
        at = pl.multiple_of(block * QB, QB)
        slot = lax.broadcasted_iota(jnp.int32, (QB, rows), 0) + at
        pick = (slot == target_ref[...]).astype(F32).astype(BF)
        slots_ref[pl.ds(at, QB), :] = nn(pick, h_ref[...]).astype(BF)
        return carry

    lax.fori_loop(0, slots_ref.shape[0] // QB, place, 0)


def post(x, o_own, wo, gain, target, slots):
    rows = x.shape[0]
    return pl.pallas_call(
        post_kernel,
        out_shape=(
            jax.ShapeDtypeStruct((slots, D), BF),
            jax.ShapeDtypeStruct((rows, D), F32),
            jax.ShapeDtypeStruct((rows, D), BF),
        ),
        in_specs=[VMEM_WHOLE] * 5,
        out_specs=(VMEM_WHOLE,) * 3,
        scratch_shapes=[
            pltpu.VMEM((rows, D), BF),
            pltpu.SemaphoreType.DMA,
            pltpu.SemaphoreType.DMA,
        ],
        compiler_params=pltpu.CompilerParams(
            collective_id=2, has_side_effects=True, vmem_limit_bytes=32 << 20
        ),
        cost_estimate=pl.CostEstimate(
            flops=8 * rows * D * (D + slots), bytes_accessed=8 << 20, transcendentals=0
        ),
        name="post",
    )(x, o_own, wo, gain, target)


def fore_kernel(
    dh_ref, target_ref, g_ref, x1_ref, gain_ref, wo_ref, full_ref, prev_out_ref, prev_two_ref,
    do_ref, dx_ref, gout_ref, gtwo_ref, dy_ref, all_ref, send_sem, recv_sem,
):
    core = lax.axis_index("ctx")
    rows, width = g_ref.shape[0], do_ref.shape[1]
    slots = dh_ref.shape[0]
    twin = {"ctx": 1 - core}
    greet([twin])

    def norm(block, total):
        at = pl.ds(pl.multiple_of(block * RB, RB), RB)
        slot = lax.broadcasted_iota(jnp.int32, (RB, slots), 1)
        pick = (slot == target_ref[at, :]).astype(F32).astype(BF)
        grad = nn(pick, dh_ref[...])
        unit, scale = normal(x1_ref[at, :])
        dx = g_ref[at, :].astype(F32) + normal_back(unit, scale, gain_ref[...], grad)
        dx_ref[at, :] = dx
        dy = dx.astype(BF)
        dy_ref[at, :] = dy
        all_ref[at, :] = nt(dy, wo_ref[...]).astype(BF)
        return total + jnp.sum(grad * unit, axis=0, keepdims=True)

    gtwo_ref[...] = prev_two_ref[...] + lax.fori_loop(
        0, rows // RB, norm, jnp.zeros((1, D), F32)
    )
    mine = pl.ds(pl.multiple_of(core * rows, 128), rows)
    copy = send(
        all_ref.at[:, pl.ds(pl.multiple_of((1 - core) * width, 128), width)],
        do_ref.at[mine, :],
        send_sem,
        recv_sem,
        twin,
    )
    copy.start()
    do_ref[mine, :] = all_ref[:, pl.ds(pl.multiple_of(core * width, 128), width)]
    gout_ref[...] = prev_out_ref[...] + tn(full_ref[...], dy_ref[...])
    copy.wait()


def fore(dh, target, g, x1, gain, wo, full, prev_out, prev_two):
    rows, slots = g.shape[0], dh.shape[0]
    return pl.pallas_call(
        fore_kernel,
        out_shape=(
            jax.ShapeDtypeStruct((2 * rows, D // 2), BF),
            jax.ShapeDtypeStruct((rows, D), F32),
            jax.ShapeDtypeStruct((D, D), F32),
            jax.ShapeDtypeStruct((1, D), F32),
        ),
        in_specs=[VMEM_WHOLE] * 9,
        out_specs=(VMEM_WHOLE,) * 4,
        scratch_shapes=[
            pltpu.VMEM((rows, D), BF),
            pltpu.VMEM((rows, D), BF),
            pltpu.SemaphoreType.DMA,
            pltpu.SemaphoreType.DMA,
        ],
        compiler_params=pltpu.CompilerParams(
            collective_id=3, has_side_effects=True, vmem_limit_bytes=40 << 20
        ),
        cost_estimate=pl.CostEstimate(
            flops=8 * rows * D * (2 * D + slots), bytes_accessed=8 << 20, transcendentals=0
        ),
        name="fore",
    )(dh, target, g, x1, gain, wo, full, prev_out, prev_two)


def tail_kernel(
    dh_ref, x_ref, dx_ref, gain_ref, prev_ref, grad_ref, gone_ref, tx_ref, rx_ref, send_sem, recv_sem
):
    core = lax.axis_index("ctx")
    rows = x_ref.shape[0]
    twin = {"ctx": 1 - core}
    greet([twin])
    tx_ref[...] = dh_ref[pl.ds(pl.multiple_of((1 - core) * rows, 128), rows), :].astype(BF)
    copy = send(tx_ref, rx_ref, send_sem, recv_sem, twin)
    copy.start()
    copy.wait()

    def norm(block, total):
        off = pl.multiple_of(block * RB, RB)
        at = pl.ds(off, RB)
        grad = dh_ref[pl.ds(core * rows + off, RB), :] + rx_ref[at, :].astype(F32)
        unit, scale = normal(x_ref[at, :].astype(F32))
        grad_ref[at, :] = dx_ref[at, :] + normal_back(unit, scale, gain_ref[...], grad)
        return total + jnp.sum(grad * unit, axis=0, keepdims=True)

    gone_ref[...] = prev_ref[...] + lax.fori_loop(0, rows // RB, norm, jnp.zeros((1, D), F32))


def tail(dh, x, dx, gain, prev):
    rows = x.shape[0]
    return pl.pallas_call(
        tail_kernel,
        out_shape=(
            jax.ShapeDtypeStruct((rows, D), F32),
            jax.ShapeDtypeStruct((1, D), F32),
        ),
        in_specs=[VMEM_WHOLE] * 5,
        out_specs=(VMEM_WHOLE,) * 2,
        scratch_shapes=[
            pltpu.VMEM((rows, D), BF),
            pltpu.VMEM((rows, D), BF),
            pltpu.SemaphoreType.DMA,
            pltpu.SemaphoreType.DMA,
        ],
        compiler_params=pltpu.CompilerParams(
            collective_id=4, has_side_effects=True, vmem_limit_bytes=32 << 20
        ),
        cost_estimate=pl.CostEstimate(
            flops=40 * rows * D, bytes_accessed=8 << 20, transcendentals=0
        ),
        name="tail",
    )(dh, x, dx, gain, prev)


def body_pair(
    tokens,
    cotangent,
    segment_ids,
    padding,
    routes,
    norm_one_gain,
    qkv_weight,
    out_weight,
    norm_two_gain,
    centroids,
    expert_in,
    expert_out,
):
    local_len = tokens.shape[2]
    experts = centroids.shape[1]
    capacity = max(2, 2 * local_len // experts)
    slots = experts * capacity
    width = D // 2
    me = lax.axis_index("ctx")
    other = 1 - me
    gain_one = norm_one_gain.astype(F32)[None, :]
    gain_two = norm_two_gain.astype(F32)[None, :]
    slot_ids = jnp.arange(slots, dtype=jnp.int32)
    expert_ids = jnp.arange(experts, dtype=jnp.int32)

    rows_of = qkv_weight.shape[0]
    w_mine = lax.dynamic_index_in_dim(
        qkv_weight.reshape(rows_of, 3, 2, width), me, 2, keepdims=False
    ).reshape(rows_of, 3 * width)
    w_all = gather_weights(jnp.concatenate([w_mine, half_of(out_weight, me, 1)], axis=1))
    out_full = lax.all_gather(w_all[:, 3 * width :], "ctx", axis=1, tiled=True)

    targets = []
    for micro in range(MICRO):
        route = routes[micro, 0, :, 0]
        choose = (route[:, None] == expert_ids[None, :]).astype(jnp.int32)
        rank = jnp.sum(jnp.cumsum(choose, axis=0) * choose, axis=1) - 1
        targets.append(route * capacity + rank)
    g_out = jnp.concatenate(
        [
            jnp.dot(
                (slot_ids[:, None] == targets[m][None, :]).astype(BF),
                cotangent[m, 0],
                preferred_element_type=F32,
            )
            .astype(BF)
            .reshape(experts, capacity, D)
            for m in range(MICRO)
        ],
        axis=1,
    )
    g_in = lax.all_to_all(g_out, "shard", split_axis=0, concat_axis=0, tiled=True)
    g_in = g_in.reshape(-1, MICRO, capacity, D)
    g_in = [g_in[:, m].reshape(-1, D) for m in range(MICRO)]

    centre = lax.dynamic_slice_in_dim(centroids.astype(F32).T, lax.axis_index("shard"), 1, 0)
    side = me.astype(jnp.int32).reshape(1)
    shape = (experts, capacity, D)

    kept = []
    for m in range(MICRO):
        normed = layer_norm(tokens[m, 0].astype(F32), gain_one)
        h_all = lax.all_gather(normed.astype(BF), "ctx", axis=0, tiled=True)
        doc_all = lax.all_gather(segment_ids[m, 0], "ctx", axis=0, tiled=True)
        pad_all = lax.all_gather(padding[m, 0], "ctx", axis=0, tiled=True)
        code = jnp.where(pad_all == 1, doc_all, -1)
        qkv, o_own, lse = attend(h_all, w_all, doc_all[:, None], code[None, :])
        outbound, x1, o_full = post(
            tokens[m, 0], o_own, out_full, gain_two, targets[m][None, :], slots
        )
        received = lax.all_to_all(
            outbound.reshape(shape), "shard", split_axis=0, concat_axis=0, tiled=True
        )
        kept.append((h_all, doc_all, code, qkv, o_full, lse, x1, received))

    prev = None
    back = []
    grad_centre = jnp.zeros((1, D), F32)
    for m in range(MICRO):
        y, dh2, gc, gup, gdown = expert(
            side, kept[m][-1].reshape(-1, D), g_in[m], 0, centre, expert_in[0], expert_out[0], prev
        )
        prev = (gup, gdown)
        grad_centre = grad_centre + gc
        dh2 = lax.all_to_all(dh2.reshape(shape), "shard", split_axis=0, concat_axis=0, tiled=True)
        y = lax.all_to_all(y.reshape(shape), "shard", split_axis=0, concat_axis=0, tiled=True)
        back.append((y.reshape(slots, D), dh2.reshape(slots, D)))
    gup, gdown = prev
    ff_half = gup.shape[1] // 2
    grad_up = gup[:, ff_half:] + swap(gup[:, :ff_half].astype(BF)).astype(F32)
    grad_down = gdown[ff_half:] + swap(gdown[:ff_half].astype(BF)).astype(F32)

    block_list, input_list = [], []
    grad_one = jnp.zeros((1, D), F32)
    grad_two = jnp.zeros((1, D), F32)
    grad_out = jnp.zeros((D, D), F32)
    grad_w = None
    for m in range(MICRO):
        h_all, doc_all, code, qkv, o_full, lse, x1, _ = kept[m]
        y, dh2 = back[m]
        do_all, dx1, grad_out, grad_two = fore(
            dh2, targets[m][:, None], cotangent[m, 0], x1, gain_two, out_full, o_full,
            grad_out, grad_two,
        )
        grad_w, dh_part = attend_back(
            h_all, w_all, qkv, do_all, lse, doc_all[None, :], code[:, None], grad_w
        )
        grad_in, grad_one = tail(dh_part, tokens[m, 0], dx1, gain_one, grad_one)
        input_list.append(grad_in)
        combine = (slot_ids[:, None] == targets[m][None, :]).astype(BF)
        block_list.append((x1 + rows_first(combine, y)).astype(BF))

    grad_out = half_of(grad_out, me, 1) + swap(half_of(grad_out, other, 1).astype(BF)).astype(F32)
    column = (jnp.arange(128) == 2 + lax.axis_index("shard")).astype(F32)[:, None]
    rows = jnp.concatenate(
        [grad_one, grad_two, jnp.zeros((126, D), F32)], axis=0
    ) + column * grad_centre
    mine, theirs = scatter_grads(grad_w, grad_out, rows)
    low = jnp.where(me == 0, mine, theirs)
    high = jnp.where(me == 0, theirs, mine)
    part = mine.shape[0]
    grad_qkv = jnp.stack(
        [
            low[:, : 3 * width].reshape(part, 3, width),
            high[:, : 3 * width].reshape(part, 3, width),
        ],
        axis=2,
    ).reshape(part, 3 * D)
    grad_out = jnp.concatenate(
        [low[:, 3 * width : 4 * width], high[:, 3 * width : 4 * width]], axis=1
    )
    small = mine[:, 4 * width :] + theirs[:, 4 * width :]

    return (
        jnp.stack(block_list)[:, None],
        jnp.stack(input_list)[:, None],
        small[:, 0],
        grad_qkv,
        grad_out,
        small[:, 1],
        small[:, 2 : 2 + experts],
        grad_up[None],
        grad_down[None],
    )


def solution(mesh):
    plan = body_pair if (mesh.shape["ctx"], mesh.shape["shard"]) == (2, 16) else body
    in_specs = (
        P(None, "shard", "ctx", None),
        P(None, "shard", "ctx", None),
        P(None, "shard", "ctx"),
        P(None, "shard", "ctx"),
        P(None, "shard", "ctx", None),
        P(),
        P("shard", None),
        P("shard", None),
        P(),
        P(),
        P("shard", None, None),
        P("shard", None, None),
    )
    out_specs = (
        P(None, "shard", "ctx", None),
        P(None, "shard", "ctx", None),
        P(("ctx", "shard")),
        P(("ctx", "shard"), None),
        P(("ctx", "shard"), None),
        P(("ctx", "shard")),
        P(("ctx", "shard"), None),
        P("shard", None, "ctx"),
        P("shard", "ctx", None),
    )
    return jax.shard_map(plan, mesh=mesh, in_specs=in_specs, out_specs=out_specs, check_vma=False)
```

```python
import functools

import jax
import jax.numpy as jnp
from jax import lax
from jax.experimental import pallas as pl
from jax.experimental.pallas import tpu as pltpu
from jax.sharding import PartitionSpec as P

D = 768
HEADS = 12
HEAD_DIM = 64
FF = 3072
MICRO = 2


EPSILON = 1e-05
NEGATIVE = -1e30
HIGH = lax.Precision.HIGHEST


def layer_norm(values, gain_vec):
    centre = values - jnp.mean(values, axis=1, keepdims=True)
    spread = jnp.mean(centre * centre, axis=1, keepdims=True)
    return centre * lax.rsqrt(spread + EPSILON) * gain_vec


def gelu_tanh(values):
    return jax.nn.gelu(values, approximate=True)


def masked_scores(queries, key_heads, query_pos, key_pos, query_doc, key_doc, key_pad):
    scores = jnp.einsum(
        "qhd,khd->hqk", queries, key_heads, preferred_element_type=jnp.float32
    ) * HEAD_DIM ** (-0.5)
    allowed = (query_doc[:, None] == key_doc[None, :]) & (key_pos[None, :] <= query_pos[:, None])
    allowed = allowed & ((key_pad[None, :] == 1) | (key_pos[None, :] == query_pos[:, None]))
    return jnp.where(allowed[None], scores, NEGATIVE)


def rows_first(left, right):
    return lax.dot_general(
        left, right, (((0,), (0,)), ((), ())), preferred_element_type=jnp.float32
    )


def rows_last(left, right):
    return lax.dot_general(
        left, right, (((1,), (1,)), ((), ())), preferred_element_type=jnp.float32
    )


def body(
    tokens,
    cotangent,
    segment_ids,
    padding,
    routes,
    norm_one_gain,
    qkv_weight,
    out_weight,
    norm_two_gain,
    centroids,
    expert_in,
    expert_out,
):
    local_len = tokens.shape[2]
    experts = centroids.shape[1]
    capacity = max(2, 2 * local_len // experts)
    seq_len = local_len * lax.axis_size("ctx")
    qkv_full, out_full = (
        lax.all_gather(qkv_weight, "shard", axis=0, tiled=True),
        lax.all_gather(out_weight, "shard", axis=0, tiled=True),
    )
    gain_one = norm_one_gain.astype(jnp.float32)
    gain_two = norm_two_gain.astype(jnp.float32)
    centre_f = centroids.astype(jnp.float32)
    up_local = expert_in[0]
    down_local = expert_out[0]
    query_pos = lax.axis_index("ctx") * local_len + jnp.arange(local_len, dtype=jnp.int32)
    all_pos = jnp.arange(seq_len, dtype=jnp.int32)
    slot_ids = jnp.arange(experts * capacity, dtype=jnp.int32)
    expert_ids = jnp.arange(experts, dtype=jnp.int32)
    score_scale = HEAD_DIM ** (-0.5)
    grad_qkv_sum = jnp.zeros((D, 3 * D), jnp.float32)
    grad_out_sum = jnp.zeros((D, D), jnp.float32)
    grad_one_sum = jnp.zeros((D,), jnp.float32)
    grad_two_sum = jnp.zeros((D,), jnp.float32)
    grad_centre = jnp.zeros((D, experts), jnp.float32)
    grad_up_sum = jnp.zeros((D, FF), jnp.float32)
    grad_down_sum = jnp.zeros((D, FF), jnp.float32)
    block_list = []
    input_list = []
    for micro_index in range(MICRO):
        inputs = tokens[micro_index, 0].astype(jnp.float32)
        doc_ids = segment_ids[micro_index, 0]
        pad_mask = padding[micro_index, 0]
        route_ids = routes[micro_index, 0, :, 0]
        normed_one, norm_one_back = jax.vjp(layer_norm, inputs, gain_one)
        first_bf = normed_one.astype(jnp.bfloat16)
        qkv = jnp.dot(first_bf, qkv_full, preferred_element_type=jnp.float32)
        queries = qkv[:, :D].astype(jnp.bfloat16)
        key_rows = qkv[:, D : 2 * D].astype(jnp.bfloat16)
        value_rows = qkv[:, 2 * D :].astype(jnp.bfloat16)
        key_all, value_all, doc_all, pad_all = (
            lax.all_gather(key_rows, "ctx", axis=0, tiled=True),
            lax.all_gather(value_rows, "ctx", axis=0, tiled=True),
            lax.all_gather(doc_ids, "ctx", axis=0, tiled=True),
            lax.all_gather(pad_mask, "ctx", axis=0, tiled=True),
        )
        query_heads = queries.reshape(local_len, HEADS, HEAD_DIM)
        key_heads = key_all.reshape(seq_len, HEADS, HEAD_DIM)
        value_heads = value_all.reshape(seq_len, HEADS, HEAD_DIM)
        scores = masked_scores(
            query_heads, key_heads, query_pos, all_pos, doc_ids, doc_all, pad_all
        )
        row_max = jnp.max(scores, axis=2, keepdims=True)
        weights = jnp.exp(scores - row_max)
        row_total = jnp.sum(weights, axis=2, keepdims=True)
        probs_now = weights / row_total
        log_total = row_max + jnp.log(row_total)
        attended = jnp.einsum(
            "hqk,khd->qhd",
            probs_now.astype(jnp.bfloat16),
            value_heads,
            preferred_element_type=jnp.float32,
        )
        attended = attended.reshape(local_len, D).astype(jnp.bfloat16)
        residual = inputs + jnp.dot(attended, out_full, preferred_element_type=jnp.float32)
        normed_two, norm_two_back = jax.vjp(layer_norm, residual, gain_two)
        second_bf = normed_two.astype(jnp.bfloat16)
        choose_mask = route_ids[:, None] == expert_ids[None, :]
        choose_f = choose_mask.astype(jnp.float32)
        logit = jnp.sum(
            jnp.dot(second_bf, centroids, preferred_element_type=jnp.float32) * choose_f, axis=1
        )
        gate_value = jax.nn.sigmoid(logit)
        choose_int = choose_mask.astype(jnp.int32)
        counts = jnp.cumsum(choose_int, axis=0)
        slot_rank = jnp.sum(counts * choose_int, axis=1) - 1
        target = route_ids * capacity + slot_rank
        dispatch = (slot_ids[:, None] == target[None, :]).astype(jnp.bfloat16)
        outbound = jnp.dot(dispatch, second_bf, preferred_element_type=jnp.float32).astype(
            jnp.bfloat16
        )
        outbound = outbound.reshape(experts, capacity, D)
        received = lax.all_to_all(outbound, "shard", split_axis=0, concat_axis=0, tiled=True)
        slot_rows = received.reshape(-1, D)
        upward = jnp.dot(slot_rows, up_local, preferred_element_type=jnp.float32)
        hidden = gelu_tanh(upward).astype(jnp.bfloat16)
        result = jnp.dot(hidden, down_local, preferred_element_type=jnp.float32).astype(
            jnp.bfloat16
        )
        returned = lax.all_to_all(
            result.reshape(received.shape), "shard", split_axis=0, concat_axis=0, tiled=True
        )
        returned, received, upward = (
            returned,
            received,
            upward.reshape(received.shape[0], received.shape[1], FF),
        )
        expert_rows = rows_first(dispatch, returned.reshape(experts * capacity, D))
        block_list.append((residual + gate_value[:, None] * expert_rows).astype(jnp.bfloat16))
        grad_out = cotangent[micro_index, 0].astype(jnp.float32)
        grad_gate = jnp.sum(grad_out * expert_rows, axis=1)
        grad_logit = grad_gate * gate_value * (1.0 - gate_value)
        grad_rows = (gate_value[:, None] * grad_out).astype(jnp.bfloat16)
        grad_outbound = jnp.dot(dispatch, grad_rows, preferred_element_type=jnp.float32).astype(
            jnp.bfloat16
        )
        grad_received = lax.all_to_all(
            grad_outbound.reshape(experts, capacity, D),
            "shard",
            split_axis=0,
            concat_axis=0,
            tiled=True,
        )
        grad_result = grad_received.reshape(-1, D)
        hidden_again, gelu_back = jax.vjp(gelu_tanh, upward.reshape(-1, FF))
        grad_down_sum = grad_down_sum + rows_first(grad_result, hidden_again.astype(jnp.bfloat16))
        grad_hidden = rows_last(grad_result, down_local)
        grad_upward = gelu_back(grad_hidden)[0].astype(jnp.bfloat16)
        grad_up_sum = grad_up_sum + rows_first(received.reshape(-1, D), grad_upward)
        grad_send = (
            rows_last(grad_upward, up_local).astype(jnp.bfloat16).reshape(grad_received.shape)
        )
        grad_back = lax.all_to_all(grad_send, "shard", split_axis=0, concat_axis=0, tiled=True)
        grad_second = rows_first(dispatch, grad_back.reshape(experts * capacity, D))
        grad_second = grad_second + grad_logit[:, None] * jnp.dot(
            choose_f, centre_f.T, precision=HIGH
        )
        grad_centre = grad_centre + jnp.dot(
            second_bf.astype(jnp.float32).T, choose_f * grad_logit[:, None], precision=HIGH
        )
        grad_resid_norm, grad_two_term = norm_two_back(grad_second)
        grad_residual = grad_out + grad_resid_norm
        grad_two_sum = grad_two_sum + grad_two_term
        grad_branch = grad_residual.astype(jnp.bfloat16)
        grad_out_sum = grad_out_sum + rows_first(attended, grad_branch)
        grad_attend = (
            rows_last(grad_branch, out_full)
            .astype(jnp.bfloat16)
            .reshape(local_len, HEADS, HEAD_DIM)
        )
        probs_again = jnp.exp(
            masked_scores(query_heads, key_heads, query_pos, all_pos, doc_ids, doc_all, pad_all)
            - log_total
        )
        grad_probs = jnp.einsum(
            "qhd,khd->hqk", grad_attend, value_heads, preferred_element_type=jnp.float32
        )
        row_terms = jnp.sum(probs_again * grad_probs, axis=2, keepdims=True)
        grad_scores = (probs_again * (grad_probs - row_terms)).astype(jnp.bfloat16)
        grad_query = (
            jnp.einsum("hqk,khd->qhd", grad_scores, key_heads, preferred_element_type=jnp.float32)
            * score_scale
        )
        grad_key_all = (
            jnp.einsum("hqk,qhd->khd", grad_scores, query_heads, preferred_element_type=jnp.float32)
            * score_scale
        )
        grad_value_all = jnp.einsum(
            "hqk,qhd->khd",
            probs_again.astype(jnp.bfloat16),
            grad_attend,
            preferred_element_type=jnp.float32,
        )
        grad_key, grad_value = (
            lax.psum_scatter(
                grad_key_all.reshape(seq_len, D).astype(jnp.bfloat16),
                "ctx",
                scatter_dimension=0,
                tiled=True,
            ).astype(jnp.float32),
            lax.psum_scatter(
                grad_value_all.reshape(seq_len, D).astype(jnp.bfloat16),
                "ctx",
                scatter_dimension=0,
                tiled=True,
            ).astype(jnp.float32),
        )
        grad_qkv_rows = jnp.concatenate(
            [grad_query.reshape(local_len, D), grad_key, grad_value], axis=1
        ).astype(jnp.bfloat16)
        grad_qkv_sum = grad_qkv_sum + rows_first(first_bf, grad_qkv_rows)
        grad_first = rows_last(grad_qkv_rows, qkv_full)
        grad_in_norm, grad_one_term = norm_one_back(grad_first)
        grad_one_sum = grad_one_sum + grad_one_term
        input_list.append(grad_residual + grad_in_norm)
    dense_sums = (
        lax.psum_scatter(grad_one_sum, ("ctx", "shard"), scatter_dimension=0, tiled=True),
        lax.psum_scatter(grad_qkv_sum, ("ctx", "shard"), scatter_dimension=0, tiled=True),
        lax.psum_scatter(grad_out_sum, ("ctx", "shard"), scatter_dimension=0, tiled=True),
        lax.psum_scatter(grad_two_sum, ("ctx", "shard"), scatter_dimension=0, tiled=True),
        lax.psum_scatter(grad_centre, ("ctx", "shard"), scatter_dimension=0, tiled=True),
    )
    expert_sums = (
        lax.psum_scatter(
            grad_up_sum.astype(jnp.bfloat16), "ctx", scatter_dimension=1, tiled=True
        ).astype(jnp.float32),
        lax.psum_scatter(
            grad_down_sum.astype(jnp.bfloat16), "ctx", scatter_dimension=1, tiled=True
        ).astype(jnp.float32),
    )
    block_out = jnp.stack(block_list)[:, None]
    grad_tokens = jnp.stack(input_list)[:, None]
    return (
        block_out,
        grad_tokens,
        dense_sums[0],
        dense_sums[1],
        dense_sums[2],
        dense_sums[3],
        dense_sums[4],
        expert_sums[0][None],
        expert_sums[1].T[None],
    )


BF = jnp.bfloat16
F32 = jnp.float32
QB = 256
AB = 512
GELU_K = 0.7978845608028654
VMEM_WHOLE = pl.BlockSpec(memory_space=pltpu.VMEM)
HBM_WHOLE = pl.BlockSpec(memory_space=pltpu.HBM)


def nn(left, right):
    return lax.dot_general(left, right, (((1,), (0,)), ((), ())), preferred_element_type=F32)


def nt(left, right):
    return lax.dot_general(left, right, (((1,), (1,)), ((), ())), preferred_element_type=F32)


def tn(left, right):
    return lax.dot_general(left, right, (((0,), (0,)), ((), ())), preferred_element_type=F32)


def lanes_of(shape, half):
    lane = lax.broadcasted_iota(jnp.int32, shape, 1)
    return (lane < HEAD_DIM) if half == 0 else (lane >= HEAD_DIM)


def masks_of(label_ref, micro):
    doc = label_ref[micro : micro + 1, :].astype(F32)
    real = label_ref[MICRO + micro : MICRO + micro + 1, :] == 1
    return doc, jnp.where(real, doc, -1.0)


def as_column(row):
    return jnp.transpose(jnp.broadcast_to(row, (128, row.shape[1])))[:, 0:1]


def attend_kernel(
    micro, h_ref, w_ref, label_ref, saved_ref, o_ref, lse_ref, col_ref, qkv_ref, sems
):
    seq, width = h_ref.shape[0], o_ref.shape[1]
    scale = HEAD_DIM ** (-0.5)
    doc_row, code_row = masks_of(label_ref, micro)
    col_ref[...] = as_column(doc_row)

    def project(block, carry):
        rows = pl.ds(block * AB, AB)
        qkv_ref[rows, :] = nn(h_ref[rows, :], w_ref[:, 0 : 3 * width]).astype(BF)
        return carry

    lax.fori_loop(0, seq // AB, project, 0)
    save = pltpu.make_async_copy(qkv_ref, saved_ref, sems.at[0])
    save.start()
    for block in range(seq // AB):
        low, kend = block * AB, (block + 1) * AB
        rows = slice(low, kend)
        qpos = lax.broadcasted_iota(jnp.int32, (AB, kend), 0) + low
        kpos = lax.broadcasted_iota(jnp.int32, (AB, kend), 1)
        same = col_ref[rows, :] == code_row[:, 0:kend]
        allowed = (same & (kpos < qpos)) | (kpos == qpos)
        bias = jnp.where(allowed, 0.0, NEGATIVE).astype(F32)
        lane = lax.broadcasted_iota(jnp.int32, (AB, 128), 1)

        def pair(index, stats):
            at = pl.multiple_of(index * 128, 128)
            q = qkv_ref[rows, pl.ds(at, 128)] * jnp.asarray(scale, BF)
            k = qkv_ref[0:kend, pl.ds(width + at, 128)]
            v = qkv_ref[0:kend, pl.ds(2 * width + at, 128)]
            outs = []
            for half in range(2):
                qm = jnp.where(lanes_of(q.shape, half), q, jnp.zeros_like(q))
                s = nt(qm, k) + bias
                top = jnp.max(s, axis=1, keepdims=True)
                e = jnp.exp(s - top)
                total = jnp.sum(e, axis=1, keepdims=True)
                outs.append(nn(e.astype(BF), v) * (1.0 / total))
                stats = jnp.where(lane == 2 * index + half, top + jnp.log(total), stats)
            o_ref[rows, pl.ds(at, 128)] = jnp.where(
                lanes_of(outs[0].shape, 0), outs[0], outs[1]
            ).astype(BF)
            return stats

        stats = lax.fori_loop(0, width // 128, pair, jnp.zeros((AB, 128), F32), unroll=True)
        lse_ref[:, rows] = jnp.transpose(stats)[0 : lse_ref.shape[0], :]
    save.wait()


def attend(micro, h_all, w_own, labels):
    seq, width = h_all.shape[0], D // 2
    flops = 2 * seq * D * 3 * width + 4 * seq * seq * width
    return pl.pallas_call(
        functools.partial(attend_kernel, micro),
        out_shape=(
            pltpu.HBM((seq, 3 * width), BF),
            jax.ShapeDtypeStruct((seq, width), BF),
            jax.ShapeDtypeStruct((8, seq), F32),
        ),
        in_specs=[VMEM_WHOLE] * 3,
        out_specs=(HBM_WHOLE, VMEM_WHOLE, VMEM_WHOLE),
        scratch_shapes=[
            pltpu.VMEM((seq, 1), F32),
            pltpu.VMEM((seq, 3 * width), BF),
            pltpu.SemaphoreType.DMA((1,)),
        ],
        compiler_params=pltpu.CompilerParams(vmem_limit_bytes=24 << 20),
        cost_estimate=pl.CostEstimate(
            flops=4 * flops, bytes_accessed=8 << 20, transcendentals=seq * seq * width // 128
        ),
        name="attend",
    )(h_all, w_own, labels)


def attend_back_kernel(micro, has_prev, *refs):
    if has_prev:
        (h_ref, w_ref, qkv_ref, do_ref, lse_ref, label_ref, prev_ref,
         gw_ref, dh_ref, dqkv_ref, dk_ref, dv_ref, kt_ref, col_ref) = refs
    else:
        (h_ref, w_ref, qkv_ref, do_ref, lse_ref, label_ref,
         gw_ref, dh_ref, dqkv_ref, dk_ref, dv_ref, kt_ref, col_ref) = refs
    seq, width = do_ref.shape
    doc_row, code_row = masks_of(label_ref, micro)
    col_ref[...] = as_column(code_row)
    scale = HEAD_DIM ** (-0.5)
    dk_ref[...] = jnp.zeros_like(dk_ref)
    dv_ref[...] = jnp.zeros_like(dv_ref)
    kt_ref[...] = jnp.transpose(qkv_ref[:, width : 2 * width])
    for block in range(seq // AB):
        low, kend = block * AB, (block + 1) * AB
        rows = slice(low, kend)
        qpos = lax.broadcasted_iota(jnp.int32, (kend, AB), 1) + low
        kpos = lax.broadcasted_iota(jnp.int32, (kend, AB), 0)
        same = doc_row[:, rows] == col_ref[0:kend, :]
        allowed = (same & (kpos < qpos)) | (kpos == qpos)
        bias = jnp.where(allowed, 0.0, NEGATIVE).astype(F32)

        def pair(index, carry):
            at = pl.multiple_of(index * 128, 128)
            q = qkv_ref[rows, pl.ds(at, 128)] * jnp.asarray(scale, BF)
            k = qkv_ref[0:kend, pl.ds(width + at, 128)]
            v = qkv_ref[0:kend, pl.ds(2 * width + at, 128)]
            do = do_ref[rows, pl.ds(at, 128)]
            dqt = jnp.zeros((128, AB), F32)
            dv = dk = None
            for half in range(2):
                keep = lanes_of(q.shape, half)
                qm = jnp.where(keep, q, jnp.zeros_like(q))
                dom = jnp.where(keep, do, jnp.zeros_like(do))
                p = jnp.exp(nt(k, qm) + bias - lse_ref[pl.ds(2 * index + half, 1), rows])
                dp = nt(v, dom)
                delta = jnp.sum(p * dp, axis=0, keepdims=True)
                ds = (p * (dp - delta)).astype(BF)
                dv_half = nn(p.astype(BF), dom)
                dk_half = nn(ds, qm)
                dv = dv_half if dv is None else dv + dv_half
                dk = dk_half if dk is None else dk + dk_half
                kt = kt_ref[pl.ds(pl.multiple_of(at + half * HEAD_DIM, HEAD_DIM), HEAD_DIM), 0:kend]
                dqt = nn(kt, ds) if half == 0 else jnp.concatenate([dqt, nn(kt, ds)], axis=0)
            dv_ref[0:kend, pl.ds(at, 128)] += dv
            dk_ref[0:kend, pl.ds(at, 128)] += dk
            dqkv_ref[rows, pl.ds(at, 128)] = (jnp.transpose(dqt) * scale).astype(BF)
            return carry

        lax.fori_loop(0, width // 128, pair, 0, unroll=True)
    dqkv_ref[:, width : 2 * width] = dk_ref[...].astype(BF)
    dqkv_ref[:, 2 * width :] = dv_ref[...].astype(BF)

    def spread(block, carry):
        rows = pl.ds(block * AB, AB)
        dh_ref[rows, :] = nt(dqkv_ref[rows, :], w_ref[:, 0 : 3 * width])
        return carry

    lax.fori_loop(0, seq // AB, spread, 0)

    def weigh(block, carry):
        cols = pl.ds(pl.multiple_of(block * 384, 384), 384)
        grad = tn(h_ref[...], dqkv_ref[:, cols])
        if has_prev:
            grad = grad + prev_ref[:, cols]
        gw_ref[:, cols] = grad.astype(gw_ref.dtype)
        return carry

    lax.fori_loop(0, 3 * width // 384, weigh, 0)


def attend_back(micro, h_all, w_own, qkv, do_all, lse, labels, prev):
    seq, width = do_all.shape
    flops = 2 * seq * D * 3 * width * 2 + 10 * seq * seq * width
    args = [h_all, w_own, qkv, do_all, lse, labels]
    if prev is not None:
        args.append(prev)
    return pl.pallas_call(
        functools.partial(attend_back_kernel, micro, prev is not None),
        out_shape=(
            jax.ShapeDtypeStruct((D, 3 * width), F32),
            jax.ShapeDtypeStruct((seq, D), F32),
        ),
        in_specs=[VMEM_WHOLE] * len(args),
        out_specs=(VMEM_WHOLE,) * 2,
        scratch_shapes=[
            pltpu.VMEM((seq, 3 * width), BF),
            pltpu.VMEM((seq, width), F32),
            pltpu.VMEM((seq, width), F32),
            pltpu.VMEM((width, seq), BF),
            pltpu.VMEM((seq, 1), F32),
        ],
        compiler_params=pltpu.CompilerParams(vmem_limit_bytes=30 << 20),
        cost_estimate=pl.CostEstimate(
            flops=4 * flops, bytes_accessed=16 << 20, transcendentals=seq * seq * width // 128
        ),
        name="attend_back",
    )(*args)


def expert_kernel(has_prev, half, h_ref, g_ref, c_ref, up_ref, down_ref, *refs):
    if has_prev:
        (prev_up_ref, prev_down_ref, _, y_out_ref, dh_out_ref, gc_ref, gup_ref, gdown_ref,
         sup_ref, sdown_ref,
         dz_ref, gate_ref, z_ref, acc_ref, a_ref, du_ref, y_ref, dh_ref, sems) = refs
    else:
        (y_out_ref, dh_out_ref, gc_ref, gup_ref, gdown_ref,
         dz_ref, gate_ref, z_ref, acc_ref, a_ref, du_ref, y_ref, dh_ref, sems) = refs
    step, steps = pl.program_id(0), pl.num_programs(0)
    micro = 1 if has_prev else 0
    capacity = h_ref.shape[1]
    rows_all = h_ref.shape[0] * capacity
    blocks = rows_all // QB
    each = QB // capacity

    def take(ref, block):
        return ref[pl.ds(pl.multiple_of(block * each, each), each)].reshape(QB, D)

    @pl.when(step == 0)
    def _():
        def start(block, carry):
            rows = pl.ds(pl.multiple_of(block * QB, QB), QB)
            logit = jnp.sum(take(h_ref, block).astype(F32) * c_ref[...], axis=1, keepdims=True)
            gate = 1.0 / (1.0 + jnp.exp(-logit))
            gate_ref[rows, :] = gate
            dz_ref[rows, :] = (gate * take(g_ref, block).astype(F32)).astype(BF)
            z_ref[rows, :] = jnp.zeros((QB, D), F32)
            acc_ref[rows, :] = jnp.zeros((QB, D), F32)
            return carry

        lax.fori_loop(0, blocks, start, 0)

    def forward(block, carry):
        rows = pl.ds(pl.multiple_of(block * QB, QB), QB)
        u = nn(take(h_ref, block), up_ref[...])
        square = u * u
        t = jnp.tanh(GELU_K * u * (1.0 + 0.044715 * square))
        a = (0.5 * u * (1.0 + t)).astype(BF)
        slope = 0.5 * (1.0 + t) + 0.5 * u * (1.0 - t * t) * (
            GELU_K * (1.0 + 3 * 0.044715 * square)
        )
        a_ref[rows, :] = a
        z_ref[rows, :] += nn(a, down_ref[...])
        du = (nt(dz_ref[rows, :], down_ref[...]) * slope).astype(BF)
        du_ref[rows, :] = du
        acc_ref[rows, :] += nt(du, up_ref[...])
        return carry

    lax.fori_loop(0, blocks, forward, 0, unroll=True)
    gup = tn(h_ref[...].reshape(rows_all, D), du_ref[...])
    gdown = tn(a_ref[...], dz_ref[...])
    if has_prev:
        gup = gup + prev_up_ref[...]
        gdown = gdown + prev_down_ref[...]

        @pl.when(step < half)
        def _():
            sup_ref[...] = gup.astype(BF)
            sdown_ref[...] = gdown.astype(BF)

        @pl.when(step >= half)
        def _():
            gup_ref[...] = gup
            gdown_ref[...] = gdown
    else:
        gup_ref[...] = gup
        gdown_ref[...] = gdown

    @pl.when(step == steps - 1)
    def _():
        saves = []
        total = jnp.zeros((1, D), F32)
        for block in range(blocks):
            rows = slice(block * QB, (block + 1) * QB)
            group = slice(block * each, (block + 1) * each)
            z = z_ref[rows, :].astype(BF).astype(F32)
            gate = gate_ref[rows, :]
            dgate = jnp.sum(take(g_ref, block).astype(F32) * z, axis=1, keepdims=True)
            dlogit = dgate * gate * (1.0 - gate)
            y_ref[group] = (gate * z).astype(BF).reshape(each, capacity, D)
            dh_ref[rows, :] = (acc_ref[rows, :] + dlogit * c_ref[...]).astype(BF)
            total = total + jnp.sum(dlogit * take(h_ref, block).astype(F32), axis=0, keepdims=True)
            saves += [
                pltpu.make_async_copy(
                    dh_ref.at[rows, :], dh_out_ref.at[rows, :], sems.at[2 * block]
                ),
                pltpu.make_async_copy(
                    y_ref.at[group], y_out_ref.at[group, micro], sems.at[2 * block + 1]
                ),
            ]
            for save in saves[-2:]:
                save.start()
        gc_ref[...] = total
        for save in saves:
            save.wait()


def expert(h_slots, h_plane, g_slots, g_plane, centre, up, down, prev):
    groups, _, capacity, _ = h_slots.shape
    rows = groups * capacity
    ff = up.shape[1]
    wide = ff // 3 if prev is None else ff // 4
    steps = ff // wide
    half = steps // 2
    whole = lambda step: (0, 0)
    plane = lambda index: (lambda step: (0, index, 0, 0))
    slot_block = (groups, None, capacity, D)

    turn = lambda step: (step * wide + (ff // 2) * (1 - lax.axis_index("ctx"))) % ff // wide
    early = lambda step: (step // half) * (half - 1) + (1 - step // half) * step
    late = lambda step: (step // half) * (step - half)
    if prev is None:
        turn = lambda step: step
    in_specs = [
        pl.BlockSpec(slot_block, plane(h_plane), pipeline_mode=pl.Buffered(1)),
        pl.BlockSpec(slot_block, plane(g_plane), pipeline_mode=pl.Buffered(1)),
        pl.BlockSpec((1, D), whole),
        pl.BlockSpec((D, wide), lambda step: (0, turn(step))),
        pl.BlockSpec((wide, D), lambda step: (turn(step), 0)),
    ]
    args = [h_slots, g_slots, centre, up, down]
    out_shape = [
        pltpu.HBM((groups, MICRO, capacity, D), BF),
        pltpu.HBM((rows, D), BF),
        jax.ShapeDtypeStruct((1, D), F32),
    ]
    out_specs = [HBM_WHOLE, HBM_WHOLE, pl.BlockSpec((1, D), whole)]
    if prev is None:
        out_shape += [pltpu.HBM((D, ff), F32), pltpu.HBM((ff, D), F32)]
        out_specs += [
            pl.BlockSpec((D, wide), lambda step: (0, step)),
            pl.BlockSpec((wide, D), lambda step: (step, 0)),
        ]
    else:
        in_specs += [
            pl.BlockSpec((D, wide), lambda step: (0, turn(step))),
            pl.BlockSpec((wide, D), lambda step: (turn(step), 0)),
            HBM_WHOLE,
        ]
        args += list(prev)
        for kind, at in ((F32, late), (BF, early)):
            out_shape += [pltpu.HBM((D, ff // 2), kind), pltpu.HBM((ff // 2, D), kind)]
            out_specs += [
                pl.BlockSpec((D, wide), lambda step, at=at: (0, at(step))),
                pl.BlockSpec((wide, D), lambda step, at=at: (at(step), 0)),
            ]
    return pl.pallas_call(
        functools.partial(expert_kernel, prev is not None, half),
        out_shape=tuple(out_shape),
        grid=(steps,),
        in_specs=in_specs,
        out_specs=tuple(out_specs),
        scratch_shapes=[
            pltpu.VMEM((rows, D), BF),
            pltpu.VMEM((rows, 1), F32),
            pltpu.VMEM((rows, D), F32),
            pltpu.VMEM((rows, D), F32),
            pltpu.VMEM((rows, wide), BF),
            pltpu.VMEM((rows, wide), BF),
            pltpu.VMEM((groups, capacity, D), BF),
            pltpu.VMEM((rows, D), BF),
            pltpu.SemaphoreType.DMA((2 * rows // QB,)),
        ],
        input_output_aliases={} if prev is None else {7: 0},
        compiler_params=pltpu.CompilerParams(vmem_limit_bytes=56 << 20),
        cost_estimate=pl.CostEstimate(
            flops=12 * rows * D * ff, bytes_accessed=40 << 20, transcendentals=rows * ff
        ),
        name="expert",
    )(*args)


def emit_kernel(x0_ref, x1_ref, y_ref, target_ref, out_ref):
    rows = x0_ref.shape[0]
    groups, _, capacity, _ = y_ref.shape
    slots = groups * capacity
    for micro, x_ref in enumerate((x0_ref, x1_ref)):
        value = y_ref[:, micro].reshape(slots, D)

        def combine(block, carry):
            off = pl.multiple_of(block * AB, AB)
            at = pl.ds(off, AB)
            slot = lax.broadcasted_iota(jnp.int32, (AB, slots), 1)
            pick = (slot == target_ref[at, micro : micro + 1]).astype(F32).astype(BF)
            out_ref[pl.ds(micro * rows + off, AB), :] = (x_ref[at, :] + nn(pick, value)).astype(BF)
            return carry

        lax.fori_loop(0, rows // AB, combine, 0)


def emit(x0, x1, y, target):
    rows = x0.shape[0]
    return pl.pallas_call(
        emit_kernel,
        out_shape=jax.ShapeDtypeStruct((MICRO * rows, D), BF),
        in_specs=[VMEM_WHOLE] * 4,
        out_specs=VMEM_WHOLE,
        compiler_params=pltpu.CompilerParams(vmem_limit_bytes=10 << 20),
        cost_estimate=pl.CostEstimate(
            flops=4 * rows * D * y.shape[0] * y.shape[2], bytes_accessed=8 << 20, transcendentals=0
        ),
        name="emit",
    )(x0, x1, y, target)


def swap(array):
    return lax.ppermute(array, "ctx", [(0, 1), (1, 0)])


def half_of(array, index, axis):
    size = array.shape[axis] // 2
    return lax.dynamic_slice_in_dim(array, index * size, size, axis)


def greet(peers):
    barrier = pltpu.get_barrier_semaphore()
    for peer in peers:
        pl.semaphore_signal(
            barrier, inc=1, device_id=peer, device_id_type=pl.DeviceIdType.MESH
        )
    pl.semaphore_wait(barrier, len(peers))


def send(src, dst, send_sem, recv_sem, peer):
    return pltpu.make_async_remote_copy(
        src_ref=src,
        dst_ref=dst,
        send_sem=send_sem,
        recv_sem=recv_sem,
        device_id=peer,
        device_id_type=pl.DeviceIdType.MESH,
    )


def places():
    me, core = lax.axis_index("shard"), lax.axis_index("ctx")
    z, y, x = me // 4, (me // 2) % 2, me % 2
    along_y, along_x = me + 2 - 4 * y, me + 1 - 2 * x
    first = along_y * (1 - core) + along_x * core
    second = along_x * (1 - core) + along_y * core
    far = 4 * z + 3 - me % 4
    line = [z, z + 1 - 2 * (z % 2), (z + 2) % 4, 3 - z]
    return me, first, second, far, line


def head_kernel(
    experts, capacity, qkv_ref, proj_ref, seg_ref, pad_ref, route_ref, x_ref, g_ref, gain_ref,
    out_ref, full_ref, h0_ref, h1_ref, all_ref, target_ref, sent_ref,
    w_ref, label_ref, slots_ref, send_sem, recv_sem, sems,
):
    size = w_ref.shape[0]
    half = full_ref.shape[1] // 2
    wide = w_ref.shape[1] - half
    count = label_ref.shape[1]
    me, first, second, far, line = places()
    core = lax.axis_index("ctx")
    own = pl.multiple_of(core * half, 128)
    for at in range(3):
        w_ref[:, at * half : (at + 1) * half] = qkv_ref[:, pl.ds(2 * at * half + own, half)]
    w_ref[:, wide:] = proj_ref[:, pl.ds(own, half)]
    label_ref[...] = jnp.zeros_like(label_ref)
    for at, ref in enumerate((seg_ref, pad_ref, route_ref)):
        for micro in range(MICRO):
            row = MICRO * at + micro
            label_ref[row : row + 1, :] = ref[micro]
    twin = {"ctx": 1 - core}
    lines = [4 * z for z in line]

    def rows(block):
        return out_ref.at[pl.ds(pl.multiple_of(block * size, 16), size), :]

    peers = [{"shard": lines[j] + me % 4} for j in (1, 2, 3)]
    one, two = {"shard": first}, {"shard": second}
    greet(peers + [one, two, twin])
    copies = []

    def push(block, role, peer, src=None):
        copy = send(
            rows(block) if src is None else src, rows(block), send_sem.at[role], recv_sem.at[role], peer
        )
        copy.start()
        copies.append(copy)

    def arrive(block, role):
        send(rows(block), rows(block), send_sem.at[0], recv_sem.at[role], one).wait_recv()

    push(me, 3, one, w_ref)
    push(me, 7, two, w_ref)
    for j in (1, 2, 3):
        push(me, j - 1, peers[j - 1], w_ref)
    out_ref[pl.ds(pl.multiple_of(me * size, 16), size), :] = w_ref[...]
    mine = pl.ds(pl.multiple_of(core * count, 128), count)
    share = [send(label_ref, all_ref.at[:, mine], send_sem.at[15], recv_sem.at[15], twin)]
    share[0].start()
    all_ref[:, mine] = label_ref[...]

    def normed(micro, h_ref):
        def norm(block, carry):
            off = pl.multiple_of(block * RB, RB)
            unit = normal(x_ref[pl.ds(micro * count + off, RB), :].astype(F32))[0]
            at = pl.ds(pl.multiple_of(core * count + off, RB), RB)
            h_ref[at, :] = (unit * gain_ref[...]).astype(BF)
            return carry

        lax.fori_loop(0, count // RB, norm, 0)
        copy = send(
            h_ref.at[mine, :], h_ref.at[mine, :], send_sem.at[16 + micro], recv_sem.at[16 + micro], twin
        )
        copy.start()
        share.append(copy)

    normed(0, h0_ref)
    arrive(lines[0] + first % 4, 3)
    push(lines[0] + first % 4, 11, two)
    block = lines[1] + me % 4
    arrive(block, 0)
    push(block, 4, one)
    push(block, 8, two)
    normed(1, h1_ref)

    before = lax.broadcasted_iota(jnp.int32, (count, count), 0)
    after = lax.broadcasted_iota(jnp.int32, (count, count), 1)
    upto = (before <= after).astype(F32).astype(BF)
    ids = lax.broadcasted_iota(jnp.int32, (experts, count), 0)
    target_ref[...] = jnp.zeros_like(target_ref)
    for micro in range(MICRO):
        route = label_ref[2 * MICRO + micro : 2 * MICRO + micro + 1, :]
        chosen = (ids == route).astype(F32)
        rank = jnp.sum(nn(chosen.astype(BF), upto) * chosen, axis=0, keepdims=True)
        target_ref[micro : micro + 1, :] = route * capacity + rank.astype(jnp.int32) - 1

    for j in (2, 3):
        block = lines[j] + me % 4
        arrive(block, j - 1)
        push(block, 3 + j, one)
        push(block, 7 + j, two)
        block = lines[j - 1] + first % 4
        arrive(block, 3 + j - 1)
        push(block, 11 + j - 1, two)

    def place(block, carry):
        at = pl.multiple_of(block * QB, QB)
        slot = lax.broadcasted_iota(jnp.int32, (QB, count), 0) + at
        pick = (slot == target_ref[0:1, :]).astype(F32).astype(BF)
        slots_ref[pl.ds(at, QB), :] = nn(pick, g_ref[0:count, :]).astype(BF)
        return carry

    lax.fori_loop(0, slots_ref.shape[0] // QB, place, 0)
    save = pltpu.make_async_copy(slots_ref, sent_ref, sems.at[0])
    save.start()
    block = lines[3] + first % 4
    arrive(block, 6)
    push(block, 14, two)
    for j in range(4):
        arrive(lines[j] + second % 4, 7 + j)
        arrive(lines[j] + far % 4, 11 + j)
    side = pl.ds(pl.multiple_of(core * half, 128), half)
    copy = send(
        out_ref.at[:, wide : wide + half], full_ref.at[:, side], send_sem.at[18], recv_sem.at[18], twin
    )
    copy.start()
    full_ref[:, side] = out_ref[:, wide : wide + half]
    copy.wait()
    for copy in share:
        copy.wait()
    for copy in copies:
        copy.wait_send()
    save.wait()


def head(experts, capacity, qkv_weight, out_weight, seg, pad, route, x, g, gain):
    size, columns = qkv_weight.shape[0], 2 * D
    count = seg.shape[2]
    return pl.pallas_call(
        functools.partial(head_kernel, experts, capacity),
        out_shape=(
            jax.ShapeDtypeStruct((16 * size, columns), BF),
            jax.ShapeDtypeStruct((16 * size, D), BF),
            jax.ShapeDtypeStruct((2 * count, D), BF),
            jax.ShapeDtypeStruct((2 * count, D), BF),
            jax.ShapeDtypeStruct((8, 2 * count), jnp.int32),
            jax.ShapeDtypeStruct((8, count), jnp.int32),
            pltpu.HBM((experts * capacity, D), BF),
        ),
        in_specs=[VMEM_WHOLE] * 8,
        out_specs=(VMEM_WHOLE,) * 6 + (HBM_WHOLE,),
        scratch_shapes=[
            pltpu.VMEM((size, columns), BF),
            pltpu.VMEM((8, count), jnp.int32),
            pltpu.VMEM((experts * capacity, D), BF),
            pltpu.SemaphoreType.DMA((19,)),
            pltpu.SemaphoreType.DMA((19,)),
            pltpu.SemaphoreType.DMA((1,)),
        ],
        compiler_params=pltpu.CompilerParams(
            collective_id=0, has_side_effects=True, vmem_limit_bytes=12 << 20
        ),
        cost_estimate=pl.CostEstimate(flops=0, bytes_accessed=100 << 20, transcendentals=0),
        name="head",
    )(qkv_weight, out_weight, seg, pad, route, x, g, gain)


def scatter_kernel(
    gw_ref, go_ref, rows_ref, gqkv_ref, gout_ref, gsmall_ref,
    theirs_ref, packed_ref, rx1_ref, rx2_ref, rx3_ref, tx1_ref, tx2_ref, sum_ref, small_ref,
    send_sem, recv_sem,
):
    me, first, second, far, line = places()
    core = lax.axis_index("ctx")
    lines = [4 * z for z in line]
    part = sum_ref.shape[0] // 2
    wide, half = gw_ref.shape[1], go_ref.shape[1]
    peers = [{"shard": lines[j] + me % 4} for j in (1, 2, 3)]
    one, two, twin = {"shard": first}, {"shard": second}, {"ctx": 1 - core}
    greet(peers + [one, two, twin])
    small_ref[...] = jnp.transpose(rows_ref[...])

    def pack(chunk, carry):
        top = pl.ds(pl.multiple_of(chunk * part, 8), part)
        low = pl.ds(pl.multiple_of(D // 2 + chunk * part, 8), part)
        for ref, at, size in ((gw_ref, 0, wide), (go_ref, wide, half), (small_ref, wide + half, 128)):
            both = jnp.concatenate([ref[top, :], ref[low, :]], axis=0)
            packed_ref[chunk, :, at : at + size] = both.astype(BF)
        return carry

    lax.fori_loop(0, 16, pack, 0)
    copies = []

    def push(src, dst, role, peer):
        copy = send(src, dst, send_sem.at[role], recv_sem.at[role], peer)
        copy.start()
        copies.append(copy)

    def arrive(dst, role):
        send(dst, dst, send_sem.at[role], recv_sem.at[role], one).wait_recv()

    order = (3, 2, 1, 0)
    for j in order:
        push(packed_ref.at[lines[j] + far % 4], rx1_ref.at[j], j, two)
    for j in order:
        push(packed_ref.at[lines[j] + second % 4], rx1_ref.at[4 + j], 4 + j, two)
    for j in order:
        arrive(rx1_ref.at[j], j)
        total = packed_ref[lines[j] + first % 4].astype(F32) + rx1_ref[j].astype(F32)
        tx1_ref[j] = total.astype(BF)
        push(tx1_ref.at[j], rx2_ref.at[j], 8 + j, one)
    own = None
    for j in order:
        arrive(rx1_ref.at[4 + j], 4 + j)
        total = packed_ref[lines[j] + me % 4].astype(F32) + rx1_ref[4 + j].astype(F32)
        arrive(rx2_ref.at[j], 8 + j)
        total = total + rx2_ref[j].astype(F32)
        if j:
            tx2_ref[j - 1] = total.astype(BF)
            push(tx2_ref.at[j - 1], rx3_ref.at[j - 1], 11 + j, peers[j - 1])
        else:
            own = total
    for j in (1, 2, 3):
        arrive(rx3_ref.at[j - 1], 11 + j)
        own = own + rx3_ref[j - 1].astype(F32)
    sum_ref[...] = own
    push(
        sum_ref.at[pl.ds(pl.multiple_of((1 - core) * part, 8), part), :], theirs_ref, 15, twin
    )
    arrive(theirs_ref, 15)
    mine, theirs = sum_ref[pl.ds(pl.multiple_of(core * part, 8), part), :], theirs_ref[...]
    low = jnp.where(core == 0, mine, theirs)
    high = jnp.where(core == 0, theirs, mine)
    for at in range(3):
        gqkv_ref[:, 2 * at * half : (2 * at + 1) * half] = low[:, at * half : (at + 1) * half]
        gqkv_ref[:, (2 * at + 1) * half : (2 * at + 2) * half] = high[:, at * half : (at + 1) * half]
    gout_ref[:, 0:half] = low[:, wide : wide + half]
    gout_ref[:, half:] = high[:, wide : wide + half]
    gsmall_ref[...] = mine[:, wide + half :] + theirs[:, wide + half :]
    for copy in copies:
        copy.wait_send()


def scatter_grads(grad_w, grad_out, rows):
    columns = grad_w.shape[1] + grad_out.shape[1] + 128
    part = D // 32
    chunk = (2 * part, columns)
    return pl.pallas_call(
        scatter_kernel,
        out_shape=(
            jax.ShapeDtypeStruct((part, 3 * D), F32),
            jax.ShapeDtypeStruct((part, D), F32),
            jax.ShapeDtypeStruct((part, 128), F32),
        ),
        in_specs=[VMEM_WHOLE] * 3,
        out_specs=(VMEM_WHOLE,) * 3,
        scratch_shapes=[
            pltpu.VMEM((part, columns), F32),
            pltpu.VMEM((16,) + chunk, BF),
            pltpu.VMEM((8,) + chunk, BF),
            pltpu.VMEM((4,) + chunk, BF),
            pltpu.VMEM((3,) + chunk, BF),
            pltpu.VMEM((4,) + chunk, BF),
            pltpu.VMEM((3,) + chunk, BF),
            pltpu.VMEM(chunk, F32),
            pltpu.VMEM((D, 128), F32),
            pltpu.SemaphoreType.DMA((16,)),
            pltpu.SemaphoreType.DMA((16,)),
        ],
        compiler_params=pltpu.CompilerParams(
            collective_id=1, has_side_effects=True, vmem_limit_bytes=16 << 20
        ),
        cost_estimate=pl.CostEstimate(flops=0, bytes_accessed=100 << 20, transcendentals=0),
        name="scatter_grads",
    )(grad_w, grad_out, rows)


def normal(values):
    centre = values - jnp.mean(values, axis=1, keepdims=True)
    spread = jnp.mean(centre * centre, axis=1, keepdims=True)
    scale = lax.rsqrt(spread + EPSILON)
    return centre * scale, scale


def normal_back(unit, scale, gain, grad):
    pull = grad * gain
    return scale * (
        pull
        - jnp.mean(pull, axis=1, keepdims=True)
        - unit * jnp.mean(pull * unit, axis=1, keepdims=True)
    )


RB = 256


def post_kernel(micro, two, capacity, *refs):
    if two:
        (x_ref, o_ref, wo_ref, gain_ref, target_ref, g_ref, sent_ref, x1_out_ref, full_out_ref,
         slots_ref, x1_ref, full_ref, h_ref, sems, send_sem, recv_sem) = refs
    else:
        (x_ref, o_ref, wo_ref, gain_ref, target_ref, sent_ref, x1_out_ref, full_out_ref,
         slots_ref, x1_ref, full_ref, h_ref, sems, send_sem, recv_sem) = refs
    core = lax.axis_index("ctx")
    rows, width = x1_ref.shape[0], o_ref.shape[1]
    twin = {"ctx": 1 - core}
    mine = pl.ds(pl.multiple_of(core * width, 128), width)
    greet([twin])
    copy = send(
        o_ref.at[pl.ds(pl.multiple_of((1 - core) * rows, 128), rows), :],
        full_ref.at[:, mine],
        send_sem,
        recv_sem,
        twin,
    )
    copy.start()
    full_ref[:, mine] = o_ref[pl.ds(pl.multiple_of(core * rows, 128), rows), :]
    copy.wait()

    def norm(block, carry):
        at = pl.ds(pl.multiple_of(block * RB, RB), RB)
        value = x_ref[pl.ds(micro * rows + pl.multiple_of(block * RB, RB), RB), :].astype(F32)
        value = value + nn(full_ref[at, :], wo_ref[...])
        x1_ref[at, :] = value
        h_ref[at, :] = (normal(value)[0] * gain_ref[...]).astype(BF)
        return carry

    lax.fori_loop(0, rows // RB, norm, 0)
    saves = [
        pltpu.make_async_copy(full_ref, full_out_ref, sems.at[0]),
        pltpu.make_async_copy(x1_ref, x1_out_ref, sems.at[1]),
    ]
    for save in saves:
        save.start()

    def place(block):
        slot = lax.broadcasted_iota(jnp.int32, (QB, rows), 0) + block * QB
        pick = (slot == target_ref[micro : micro + 1, :]).astype(F32).astype(BF)
        group = slice(block * each, (block + 1) * each)
        slots_ref[group, 0] = nn(pick, h_ref[...]).astype(BF).reshape(each, capacity, D)
        if two:
            given = g_ref[micro * rows : (micro + 1) * rows, :]
            slots_ref[group, 1] = nn(pick, given).astype(BF).reshape(each, capacity, D)
        save = pltpu.make_async_copy(slots_ref.at[group], sent_ref.at[group], sems.at[2 + block])
        save.start()
        saves.append(save)

    each = QB // capacity
    for block in range(slots_ref.shape[0] // each):
        place(block)
    for save in saves:
        save.wait()


def post(micro, x, o_own, wo, gain, target, g, experts, capacity):
    rows = x.shape[0] // MICRO
    slots = experts * capacity
    args = [x, o_own, wo, gain, target] + ([] if g is None else [g])
    planes = 1 if g is None else 2
    return pl.pallas_call(
        functools.partial(post_kernel, micro, g is not None, capacity),
        out_shape=(
            pltpu.HBM((experts, planes, capacity, D), BF),
            pltpu.HBM((rows, D), F32),
            pltpu.HBM((rows, D), BF),
        ),
        in_specs=[VMEM_WHOLE] * len(args),
        out_specs=(HBM_WHOLE,) * 3,
        scratch_shapes=[
            pltpu.VMEM((experts, planes, capacity, D), BF),
            pltpu.VMEM((rows, D), F32),
            pltpu.VMEM((rows, D), BF),
            pltpu.VMEM((rows, D), BF),
            pltpu.SemaphoreType.DMA((2 + slots // QB,)),
            pltpu.SemaphoreType.DMA,
            pltpu.SemaphoreType.DMA,
        ],
        compiler_params=pltpu.CompilerParams(
            collective_id=2 + micro, has_side_effects=True, vmem_limit_bytes=18 << 20
        ),
        cost_estimate=pl.CostEstimate(
            flops=8 * rows * D * (D + slots), bytes_accessed=8 << 20, transcendentals=0
        ),
        name="post",
    )(*args)


def fore_kernel(
    micro, dh_ref, target_ref, g_ref, x1_ref, gain_ref, wo_ref, full_ref, prev_out_ref, prev_two_ref,
    do_ref, dx_ref, gout_ref, gtwo_ref, dy_ref, all_ref, send_sem, recv_sem,
):
    core = lax.axis_index("ctx")
    rows, width = x1_ref.shape[0], do_ref.shape[1]
    slots = dh_ref.shape[0]
    twin = {"ctx": 1 - core}
    greet([twin])

    def norm(block, total):
        at = pl.ds(pl.multiple_of(block * RB, RB), RB)
        slot = lax.broadcasted_iota(jnp.int32, (RB, slots), 1)
        pick = (slot == target_ref[at, micro : micro + 1]).astype(F32).astype(BF)
        grad = nn(pick, dh_ref[...])
        unit, scale = normal(x1_ref[at, :])
        given = g_ref[pl.ds(micro * rows + pl.multiple_of(block * RB, RB), RB), :].astype(F32)
        dx = given + normal_back(unit, scale, gain_ref[...], grad)
        dx_ref[at, :] = dx
        dy = dx.astype(BF)
        dy_ref[at, :] = dy
        all_ref[at, :] = nt(dy, wo_ref[...]).astype(BF)
        return total + jnp.sum(grad * unit, axis=0, keepdims=True)

    gtwo_ref[...] = prev_two_ref[...] + lax.fori_loop(
        0, rows // RB, norm, jnp.zeros((1, D), F32)
    )
    mine = pl.ds(pl.multiple_of(core * rows, 128), rows)
    copy = send(
        all_ref.at[:, pl.ds(pl.multiple_of((1 - core) * width, 128), width)],
        do_ref.at[mine, :],
        send_sem,
        recv_sem,
        twin,
    )
    copy.start()
    do_ref[mine, :] = all_ref[:, pl.ds(pl.multiple_of(core * width, 128), width)]
    gout_ref[...] = prev_out_ref[...] + tn(full_ref[...], dy_ref[...])
    copy.wait()


def fore(micro, dh, target, g, x1, gain, wo, full, prev_out, prev_two):
    rows, slots = x1.shape[0], dh.shape[0]
    return pl.pallas_call(
        functools.partial(fore_kernel, micro),
        out_shape=(
            jax.ShapeDtypeStruct((2 * rows, D // 2), BF),
            jax.ShapeDtypeStruct((rows, D), F32),
            jax.ShapeDtypeStruct((D, D), F32),
            jax.ShapeDtypeStruct((1, D), F32),
        ),
        in_specs=[VMEM_WHOLE] * 9,
        out_specs=(VMEM_WHOLE,) * 4,
        scratch_shapes=[
            pltpu.VMEM((rows, D), BF),
            pltpu.VMEM((rows, D), BF),
            pltpu.SemaphoreType.DMA,
            pltpu.SemaphoreType.DMA,
        ],
        compiler_params=pltpu.CompilerParams(
            collective_id=4 + micro, has_side_effects=True, vmem_limit_bytes=12 << 20
        ),
        cost_estimate=pl.CostEstimate(
            flops=8 * rows * D * (2 * D + slots), bytes_accessed=8 << 20, transcendentals=0
        ),
        name="fore",
    )(dh, target, g, x1, gain, wo, full, prev_out, prev_two)


def tail_kernel(
    micro, dh_ref, x_ref, dx_ref, gain_ref, prev_ref, grad_out_ref, gone_ref,
    grad_ref, tx_ref, rx_ref, sems, send_sem, recv_sem,
):
    core = lax.axis_index("ctx")
    rows = dx_ref.shape[0]
    twin = {"ctx": 1 - core}
    greet([twin])
    tx_ref[...] = dh_ref[pl.ds(pl.multiple_of((1 - core) * rows, 128), rows), :].astype(BF)
    copy = send(tx_ref, rx_ref, send_sem, recv_sem, twin)
    copy.start()
    copy.wait()

    saves = []
    total = jnp.zeros((1, D), F32)
    for off in range(0, rows, RB):
        at = slice(off, off + RB)
        mine = pl.ds(pl.multiple_of(core * rows + off, RB), RB)
        grad = dh_ref[mine, :] + rx_ref[at, :].astype(F32)
        unit, scale = normal(x_ref[pl.ds(micro * rows + off, RB), :].astype(F32))
        grad_ref[at, :] = dx_ref[at, :] + normal_back(unit, scale, gain_ref[...], grad)
        save = pltpu.make_async_copy(grad_ref.at[at, :], grad_out_ref.at[at, :], sems.at[off // RB])
        save.start()
        saves.append(save)
        total = total + jnp.sum(grad * unit, axis=0, keepdims=True)
    gone_ref[...] = prev_ref[...] + total
    for save in saves:
        save.wait()


def tail(micro, dh, x, dx, gain, prev):
    rows = dx.shape[0]
    return pl.pallas_call(
        functools.partial(tail_kernel, micro),
        out_shape=(
            pltpu.HBM((rows, D), F32),
            jax.ShapeDtypeStruct((1, D), F32),
        ),
        in_specs=[VMEM_WHOLE] * 5,
        out_specs=(HBM_WHOLE, VMEM_WHOLE),
        scratch_shapes=[
            pltpu.VMEM((rows, D), F32),
            pltpu.VMEM((rows, D), BF),
            pltpu.VMEM((rows, D), BF),
            pltpu.SemaphoreType.DMA((rows // RB,)),
            pltpu.SemaphoreType.DMA,
            pltpu.SemaphoreType.DMA,
        ],
        compiler_params=pltpu.CompilerParams(
            collective_id=6 + micro, has_side_effects=True, vmem_limit_bytes=10 << 20
        ),
        cost_estimate=pl.CostEstimate(
            flops=40 * rows * D, bytes_accessed=8 << 20, transcendentals=0
        ),
        name="tail",
    )(dh, x, dx, gain, prev)


def body_pair(
    tokens,
    cotangent,
    segment_ids,
    padding,
    routes,
    norm_one_gain,
    qkv_weight,
    out_weight,
    norm_two_gain,
    centroids,
    expert_in,
    expert_out,
):
    local_len = tokens.shape[2]
    experts = centroids.shape[1]
    capacity = max(2, 2 * local_len // experts)
    slots = experts * capacity
    width = D // 2
    me = lax.axis_index("ctx")
    other = 1 - me
    gain_one = norm_one_gain.astype(F32)[None, :]
    gain_two = norm_two_gain.astype(F32)[None, :]

    x_all = tokens.reshape(MICRO * local_len, D)
    g_all = cotangent.reshape(MICRO * local_len, D)
    w_all, out_full, h0, h1, labels, target, g_out = head(
        experts, capacity, qkv_weight, out_weight, segment_ids, padding,
        routes.reshape(MICRO, 1, local_len), x_all, g_all, gain_one
    )
    columns = target.T
    centre = lax.dynamic_slice_in_dim(centroids.astype(F32).T, lax.axis_index("shard"), 1, 0)

    def exchange(rows):
        planes = rows.size // (slots * D)
        return lax.all_to_all(
            rows.reshape(experts, planes * capacity, D),
            "shard",
            split_axis=0,
            concat_axis=0,
            tiled=True,
        ).reshape(experts, planes, capacity, D)

    g0_in = exchange(g_out)
    qkv0, o_own, lse0 = attend(0, h0, w_all, labels)
    sent0, x10, full0 = post(
        0, x_all, o_own, out_full, gain_two, target, None, experts, capacity
    )
    h1, sent0, g0_in = lax.optimization_barrier((h1, sent0, g0_in))
    h0_in = exchange(sent0)
    qkv1, o_own, lse1 = attend(1, h1, w_all, labels)
    sent1, x11, full1 = post(
        1, x_all, o_own, out_full, gain_two, target, g_all, experts, capacity
    )
    h0_in, sent1 = lax.optimization_barrier((h0_in, sent1))
    both_in = exchange(sent1)
    kept = [(h0, qkv0, full0, lse0, x10), (h1, qkv1, full1, lse1, x11)]

    y, dh0, gc0, gup, gdown = expert(
        h0_in, 0, g0_in, 0, centre, expert_in[0], expert_out[0], None
    )
    dh0 = exchange(dh0)
    y, dh1, gc1, gup, gdown, sup, sdown = expert(
        both_in, 0, both_in, 1, centre, expert_in[0], expert_out[0], (gup, gdown, y)
    )
    dh0, dh1, y = lax.optimization_barrier((dh0, dh1, y))
    dh1 = exchange(dh1)
    grad_centre = gc0 + gc1
    grad_up = gup + swap(sup).astype(F32)
    grad_down = gdown + swap(sdown).astype(F32)

    def backward(m, dh2, grad_out, grad_two, grad_w, grad_one):
        h_all, qkv, o_full, lse, x1 = kept[m]
        do_all, dx1, grad_out, grad_two = fore(
            m, dh2.reshape(slots, D), columns, g_all, x1, gain_two, out_full, o_full,
            grad_out, grad_two,
        )
        grad_w, dh_part = attend_back(m, h_all, w_all, qkv, do_all, lse, labels, grad_w)
        grad_in, grad_one = tail(m, dh_part, x_all, dx1, gain_one, grad_one)
        return grad_in, grad_out, grad_two, grad_w, grad_one

    zero_row = jnp.zeros((1, D), F32)
    in0, grad_out, grad_two, grad_w, grad_one = backward(
        0, dh0, jnp.zeros((D, D), F32), zero_row, None, zero_row
    )
    dh1, grad_one, y = lax.optimization_barrier((dh1, grad_one, y))
    y = exchange(y)
    in1, grad_out, grad_two, grad_w, grad_one = backward(
        1, dh1, grad_out, grad_two, grad_w, grad_one
    )

    grad_out = half_of(grad_out, me, 1) + swap(half_of(grad_out, other, 1).astype(BF)).astype(F32)
    column = (jnp.arange(128) == 2 + lax.axis_index("shard")).astype(F32)[:, None]
    rows = jnp.concatenate(
        [grad_one, grad_two, jnp.zeros((126, D), F32)], axis=0
    ) + column * grad_centre
    grad_qkv, grad_out, small = scatter_grads(grad_w, grad_out, rows)
    y, small = lax.optimization_barrier((y, small))
    block_out = emit(x10, x11, y, columns)

    return (
        block_out.reshape(MICRO, 1, local_len, D),
        jnp.stack([in0, in1])[:, None],
        small[:, 0],
        grad_qkv,
        grad_out,
        small[:, 1],
        small[:, 2 : 2 + experts],
        grad_up[None],
        grad_down[None],
    )


def solution(mesh):
    plan = body_pair if (mesh.shape["ctx"], mesh.shape["shard"]) == (2, 16) else body
    in_specs = (
        P(None, "shard", "ctx", None),
        P(None, "shard", "ctx", None),
        P(None, "shard", "ctx"),
        P(None, "shard", "ctx"),
        P(None, "shard", "ctx", None),
        P(),
        P("shard", None),
        P("shard", None),
        P(),
        P(),
        P("shard", None, None),
        P("shard", None, None),
    )
    out_specs = (
        P(None, "shard", "ctx", None),
        P(None, "shard", "ctx", None),
        P(("ctx", "shard")),
        P(("ctx", "shard"), None),
        P(("ctx", "shard"), None),
        P(("ctx", "shard")),
        P(("ctx", "shard"), None),
        P("shard", None, "ctx"),
        P("shard", "ctx", None),
    )
    return jax.shard_map(plan, mesh=mesh, in_specs=in_specs, out_specs=out_specs, check_vma=False)
```

```python
import functools

import jax
import jax.numpy as jnp
from jax import lax
from jax.experimental import pallas as pl
from jax.experimental.pallas import tpu as pltpu
from jax.sharding import PartitionSpec as P

D = 768
HEADS = 12
HEAD_DIM = 64
FF = 3072
MICRO = 2


EPSILON = 1e-05
NEGATIVE = -1e30
HIGH = lax.Precision.HIGHEST


def layer_norm(values, gain_vec):
    centre = values - jnp.mean(values, axis=1, keepdims=True)
    spread = jnp.mean(centre * centre, axis=1, keepdims=True)
    return centre * lax.rsqrt(spread + EPSILON) * gain_vec


def gelu_tanh(values):
    return jax.nn.gelu(values, approximate=True)


def masked_scores(queries, key_heads, query_pos, key_pos, query_doc, key_doc, key_pad):
    scores = jnp.einsum(
        "qhd,khd->hqk", queries, key_heads, preferred_element_type=jnp.float32
    ) * HEAD_DIM ** (-0.5)
    allowed = (query_doc[:, None] == key_doc[None, :]) & (key_pos[None, :] <= query_pos[:, None])
    allowed = allowed & ((key_pad[None, :] == 1) | (key_pos[None, :] == query_pos[:, None]))
    return jnp.where(allowed[None], scores, NEGATIVE)


def rows_first(left, right):
    return lax.dot_general(
        left, right, (((0,), (0,)), ((), ())), preferred_element_type=jnp.float32
    )


def rows_last(left, right):
    return lax.dot_general(
        left, right, (((1,), (1,)), ((), ())), preferred_element_type=jnp.float32
    )


def body(
    tokens,
    cotangent,
    segment_ids,
    padding,
    routes,
    norm_one_gain,
    qkv_weight,
    out_weight,
    norm_two_gain,
    centroids,
    expert_in,
    expert_out,
):
    local_len = tokens.shape[2]
    experts = centroids.shape[1]
    capacity = max(2, 2 * local_len // experts)
    seq_len = local_len * lax.axis_size("ctx")
    qkv_full, out_full = (
        lax.all_gather(qkv_weight, "shard", axis=0, tiled=True),
        lax.all_gather(out_weight, "shard", axis=0, tiled=True),
    )
    gain_one = norm_one_gain.astype(jnp.float32)
    gain_two = norm_two_gain.astype(jnp.float32)
    centre_f = centroids.astype(jnp.float32)
    up_local = expert_in[0]
    down_local = expert_out[0]
    query_pos = lax.axis_index("ctx") * local_len + jnp.arange(local_len, dtype=jnp.int32)
    all_pos = jnp.arange(seq_len, dtype=jnp.int32)
    slot_ids = jnp.arange(experts * capacity, dtype=jnp.int32)
    expert_ids = jnp.arange(experts, dtype=jnp.int32)
    score_scale = HEAD_DIM ** (-0.5)
    grad_qkv_sum = jnp.zeros((D, 3 * D), jnp.float32)
    grad_out_sum = jnp.zeros((D, D), jnp.float32)
    grad_one_sum = jnp.zeros((D,), jnp.float32)
    grad_two_sum = jnp.zeros((D,), jnp.float32)
    grad_centre = jnp.zeros((D, experts), jnp.float32)
    grad_up_sum = jnp.zeros((D, FF), jnp.float32)
    grad_down_sum = jnp.zeros((D, FF), jnp.float32)
    block_list = []
    input_list = []
    for micro_index in range(MICRO):
        inputs = tokens[micro_index, 0].astype(jnp.float32)
        doc_ids = segment_ids[micro_index, 0]
        pad_mask = padding[micro_index, 0]
        route_ids = routes[micro_index, 0, :, 0]
        normed_one, norm_one_back = jax.vjp(layer_norm, inputs, gain_one)
        first_bf = normed_one.astype(jnp.bfloat16)
        qkv = jnp.dot(first_bf, qkv_full, preferred_element_type=jnp.float32)
        queries = qkv[:, :D].astype(jnp.bfloat16)
        key_rows = qkv[:, D : 2 * D].astype(jnp.bfloat16)
        value_rows = qkv[:, 2 * D :].astype(jnp.bfloat16)
        key_all, value_all, doc_all, pad_all = (
            lax.all_gather(key_rows, "ctx", axis=0, tiled=True),
            lax.all_gather(value_rows, "ctx", axis=0, tiled=True),
            lax.all_gather(doc_ids, "ctx", axis=0, tiled=True),
            lax.all_gather(pad_mask, "ctx", axis=0, tiled=True),
        )
        query_heads = queries.reshape(local_len, HEADS, HEAD_DIM)
        key_heads = key_all.reshape(seq_len, HEADS, HEAD_DIM)
        value_heads = value_all.reshape(seq_len, HEADS, HEAD_DIM)
        scores = masked_scores(
            query_heads, key_heads, query_pos, all_pos, doc_ids, doc_all, pad_all
        )
        row_max = jnp.max(scores, axis=2, keepdims=True)
        weights = jnp.exp(scores - row_max)
        row_total = jnp.sum(weights, axis=2, keepdims=True)
        probs_now = weights / row_total
        log_total = row_max + jnp.log(row_total)
        attended = jnp.einsum(
            "hqk,khd->qhd",
            probs_now.astype(jnp.bfloat16),
            value_heads,
            preferred_element_type=jnp.float32,
        )
        attended = attended.reshape(local_len, D).astype(jnp.bfloat16)
        residual = inputs + jnp.dot(attended, out_full, preferred_element_type=jnp.float32)
        normed_two, norm_two_back = jax.vjp(layer_norm, residual, gain_two)
        second_bf = normed_two.astype(jnp.bfloat16)
        choose_mask = route_ids[:, None] == expert_ids[None, :]
        choose_f = choose_mask.astype(jnp.float32)
        logit = jnp.sum(
            jnp.dot(second_bf, centroids, preferred_element_type=jnp.float32) * choose_f, axis=1
        )
        gate_value = jax.nn.sigmoid(logit)
        choose_int = choose_mask.astype(jnp.int32)
        counts = jnp.cumsum(choose_int, axis=0)
        slot_rank = jnp.sum(counts * choose_int, axis=1) - 1
        target = route_ids * capacity + slot_rank
        dispatch = (slot_ids[:, None] == target[None, :]).astype(jnp.bfloat16)
        outbound = jnp.dot(dispatch, second_bf, preferred_element_type=jnp.float32).astype(
            jnp.bfloat16
        )
        outbound = outbound.reshape(experts, capacity, D)
        received = lax.all_to_all(outbound, "shard", split_axis=0, concat_axis=0, tiled=True)
        slot_rows = received.reshape(-1, D)
        upward = jnp.dot(slot_rows, up_local, preferred_element_type=jnp.float32)
        hidden = gelu_tanh(upward).astype(jnp.bfloat16)
        result = jnp.dot(hidden, down_local, preferred_element_type=jnp.float32).astype(
            jnp.bfloat16
        )
        returned = lax.all_to_all(
            result.reshape(received.shape), "shard", split_axis=0, concat_axis=0, tiled=True
        )
        returned, received, upward = (
            returned,
            received,
            upward.reshape(received.shape[0], received.shape[1], FF),
        )
        expert_rows = rows_first(dispatch, returned.reshape(experts * capacity, D))
        block_list.append((residual + gate_value[:, None] * expert_rows).astype(jnp.bfloat16))
        grad_out = cotangent[micro_index, 0].astype(jnp.float32)
        grad_gate = jnp.sum(grad_out * expert_rows, axis=1)
        grad_logit = grad_gate * gate_value * (1.0 - gate_value)
        grad_rows = (gate_value[:, None] * grad_out).astype(jnp.bfloat16)
        grad_outbound = jnp.dot(dispatch, grad_rows, preferred_element_type=jnp.float32).astype(
            jnp.bfloat16
        )
        grad_received = lax.all_to_all(
            grad_outbound.reshape(experts, capacity, D),
            "shard",
            split_axis=0,
            concat_axis=0,
            tiled=True,
        )
        grad_result = grad_received.reshape(-1, D)
        hidden_again, gelu_back = jax.vjp(gelu_tanh, upward.reshape(-1, FF))
        grad_down_sum = grad_down_sum + rows_first(grad_result, hidden_again.astype(jnp.bfloat16))
        grad_hidden = rows_last(grad_result, down_local)
        grad_upward = gelu_back(grad_hidden)[0].astype(jnp.bfloat16)
        grad_up_sum = grad_up_sum + rows_first(received.reshape(-1, D), grad_upward)
        grad_send = (
            rows_last(grad_upward, up_local).astype(jnp.bfloat16).reshape(grad_received.shape)
        )
        grad_back = lax.all_to_all(grad_send, "shard", split_axis=0, concat_axis=0, tiled=True)
        grad_second = rows_first(dispatch, grad_back.reshape(experts * capacity, D))
        grad_second = grad_second + grad_logit[:, None] * jnp.dot(
            choose_f, centre_f.T, precision=HIGH
        )
        grad_centre = grad_centre + jnp.dot(
            second_bf.astype(jnp.float32).T, choose_f * grad_logit[:, None], precision=HIGH
        )
        grad_resid_norm, grad_two_term = norm_two_back(grad_second)
        grad_residual = grad_out + grad_resid_norm
        grad_two_sum = grad_two_sum + grad_two_term
        grad_branch = grad_residual.astype(jnp.bfloat16)
        grad_out_sum = grad_out_sum + rows_first(attended, grad_branch)
        grad_attend = (
            rows_last(grad_branch, out_full)
            .astype(jnp.bfloat16)
            .reshape(local_len, HEADS, HEAD_DIM)
        )
        probs_again = jnp.exp(
            masked_scores(query_heads, key_heads, query_pos, all_pos, doc_ids, doc_all, pad_all)
            - log_total
        )
        grad_probs = jnp.einsum(
            "qhd,khd->hqk", grad_attend, value_heads, preferred_element_type=jnp.float32
        )
        row_terms = jnp.sum(probs_again * grad_probs, axis=2, keepdims=True)
        grad_scores = (probs_again * (grad_probs - row_terms)).astype(jnp.bfloat16)
        grad_query = (
            jnp.einsum("hqk,khd->qhd", grad_scores, key_heads, preferred_element_type=jnp.float32)
            * score_scale
        )
        grad_key_all = (
            jnp.einsum("hqk,qhd->khd", grad_scores, query_heads, preferred_element_type=jnp.float32)
            * score_scale
        )
        grad_value_all = jnp.einsum(
            "hqk,qhd->khd",
            probs_again.astype(jnp.bfloat16),
            grad_attend,
            preferred_element_type=jnp.float32,
        )
        grad_key, grad_value = (
            lax.psum_scatter(
                grad_key_all.reshape(seq_len, D).astype(jnp.bfloat16),
                "ctx",
                scatter_dimension=0,
                tiled=True,
            ).astype(jnp.float32),
            lax.psum_scatter(
                grad_value_all.reshape(seq_len, D).astype(jnp.bfloat16),
                "ctx",
                scatter_dimension=0,
                tiled=True,
            ).astype(jnp.float32),
        )
        grad_qkv_rows = jnp.concatenate(
            [grad_query.reshape(local_len, D), grad_key, grad_value], axis=1
        ).astype(jnp.bfloat16)
        grad_qkv_sum = grad_qkv_sum + rows_first(first_bf, grad_qkv_rows)
        grad_first = rows_last(grad_qkv_rows, qkv_full)
        grad_in_norm, grad_one_term = norm_one_back(grad_first)
        grad_one_sum = grad_one_sum + grad_one_term
        input_list.append(grad_residual + grad_in_norm)
    dense_sums = (
        lax.psum_scatter(grad_one_sum, ("ctx", "shard"), scatter_dimension=0, tiled=True),
        lax.psum_scatter(grad_qkv_sum, ("ctx", "shard"), scatter_dimension=0, tiled=True),
        lax.psum_scatter(grad_out_sum, ("ctx", "shard"), scatter_dimension=0, tiled=True),
        lax.psum_scatter(grad_two_sum, ("ctx", "shard"), scatter_dimension=0, tiled=True),
        lax.psum_scatter(grad_centre, ("ctx", "shard"), scatter_dimension=0, tiled=True),
    )
    expert_sums = (
        lax.psum_scatter(
            grad_up_sum.astype(jnp.bfloat16), "ctx", scatter_dimension=1, tiled=True
        ).astype(jnp.float32),
        lax.psum_scatter(
            grad_down_sum.astype(jnp.bfloat16), "ctx", scatter_dimension=1, tiled=True
        ).astype(jnp.float32),
    )
    block_out = jnp.stack(block_list)[:, None]
    grad_tokens = jnp.stack(input_list)[:, None]
    return (
        block_out,
        grad_tokens,
        dense_sums[0],
        dense_sums[1],
        dense_sums[2],
        dense_sums[3],
        dense_sums[4],
        expert_sums[0][None],
        expert_sums[1].T[None],
    )


BF = jnp.bfloat16
F32 = jnp.float32
QB = 256
AB = 512
GELU_K = 0.7978845608028654
VMEM_WHOLE = pl.BlockSpec(memory_space=pltpu.VMEM)
HBM_WHOLE = pl.BlockSpec(memory_space=pltpu.HBM)


def nn(left, right):
    return lax.dot_general(left, right, (((1,), (0,)), ((), ())), preferred_element_type=F32)


def nt(left, right):
    return lax.dot_general(left, right, (((1,), (1,)), ((), ())), preferred_element_type=F32)


def tn(left, right):
    return lax.dot_general(left, right, (((0,), (0,)), ((), ())), preferred_element_type=F32)


def lanes_of(shape, half):
    lane = lax.broadcasted_iota(jnp.int32, shape, 1)
    return (lane < HEAD_DIM) if half == 0 else (lane >= HEAD_DIM)


def masks_of(label_ref, micro):
    doc = label_ref[micro : micro + 1, :].astype(F32)
    real = label_ref[MICRO + micro : MICRO + micro + 1, :] == 1
    return doc, jnp.where(real, doc, -1.0)


def as_column(row):
    return jnp.transpose(jnp.broadcast_to(row, (128, row.shape[1])))[:, 0:1]


def attend_kernel(
    micro, h_ref, w_ref, label_ref, saved_ref, o_ref, lse_ref, col_ref, qkv_ref, sem
):
    seq, width = h_ref.shape[0], o_ref.shape[1]
    scale = HEAD_DIM ** (-0.5)
    doc_row, code_row = masks_of(label_ref, micro)
    col_ref[...] = as_column(doc_row)

    def project(block, carry):
        rows = pl.ds(block * AB, AB)
        qkv_ref[rows, :] = nn(h_ref[rows, :], w_ref[:, 0 : 3 * width]).astype(BF)
        return carry

    lax.fori_loop(0, seq // AB, project, 0)
    save = pltpu.make_async_copy(qkv_ref, saved_ref, sem)
    save.start()
    for block in range(seq // AB):
        low, kend = block * AB, (block + 1) * AB
        rows = slice(low, kend)
        qpos = lax.broadcasted_iota(jnp.int32, (AB, kend), 0) + low
        kpos = lax.broadcasted_iota(jnp.int32, (AB, kend), 1)
        same = col_ref[rows, :] == code_row[:, 0:kend]
        allowed = (same & (kpos < qpos)) | (kpos == qpos)
        bias = jnp.where(allowed, 0.0, NEGATIVE).astype(F32)
        lane = lax.broadcasted_iota(jnp.int32, (AB, 128), 1)

        def pair(index, stats):
            at = pl.multiple_of(index * 128, 128)
            q = qkv_ref[rows, pl.ds(at, 128)] * jnp.asarray(scale, BF)
            k = qkv_ref[0:kend, pl.ds(width + at, 128)]
            v = qkv_ref[0:kend, pl.ds(2 * width + at, 128)]
            outs = []
            for half in range(2):
                qm = jnp.where(lanes_of(q.shape, half), q, jnp.zeros_like(q))
                s = nt(qm, k) + bias
                top = jnp.max(s, axis=1, keepdims=True)
                e = jnp.exp(s - top)
                total = jnp.sum(e, axis=1, keepdims=True)
                outs.append(nn(e.astype(BF), v) * (1.0 / total))
                stats = jnp.where(lane == 2 * index + half, top + jnp.log(total), stats)
            o_ref[rows, pl.ds(at, 128)] = jnp.where(
                lanes_of(outs[0].shape, 0), outs[0], outs[1]
            ).astype(BF)
            return stats

        stats = lax.fori_loop(0, width // 128, pair, jnp.zeros((AB, 128), F32), unroll=True)
        lse_ref[:, rows] = jnp.transpose(stats)[0 : lse_ref.shape[0], :]
    save.wait()


def attend(micro, h_all, w_own, labels):
    seq, width = h_all.shape[0], D // 2
    flops = 2 * seq * D * 3 * width + 4 * seq * seq * width
    return pl.pallas_call(
        functools.partial(attend_kernel, micro),
        out_shape=(
            pltpu.HBM((seq, 3 * width), BF),
            jax.ShapeDtypeStruct((seq, width), BF),
            jax.ShapeDtypeStruct((8, seq), F32),
        ),
        in_specs=[VMEM_WHOLE] * 3,
        out_specs=(HBM_WHOLE, VMEM_WHOLE, VMEM_WHOLE),
        scratch_shapes=[
            pltpu.VMEM((seq, 1), F32),
            pltpu.VMEM((seq, 3 * width), BF),
            pltpu.SemaphoreType.DMA,
        ],
        compiler_params=pltpu.CompilerParams(vmem_limit_bytes=24 << 20),
        cost_estimate=pl.CostEstimate(
            flops=4 * flops, bytes_accessed=8 << 20, transcendentals=seq * seq * width // 128
        ),
        name="attend",
    )(h_all, w_own, labels)


def attend_back_kernel(micro, has_prev, *refs):
    if has_prev:
        (h_ref, w_ref, qkv_ref, do_ref, lse_ref, label_ref, prev_ref,
         gw_ref, dh_ref, dqkv_ref, dk_ref, dv_ref, kt_ref, col_ref) = refs
    else:
        (h_ref, w_ref, qkv_ref, do_ref, lse_ref, label_ref,
         gw_ref, dh_ref, dqkv_ref, dk_ref, dv_ref, kt_ref, col_ref) = refs
    seq, width = do_ref.shape
    doc_row, code_row = masks_of(label_ref, micro)
    col_ref[...] = as_column(code_row)
    scale = HEAD_DIM ** (-0.5)
    dk_ref[...] = jnp.zeros_like(dk_ref)
    dv_ref[...] = jnp.zeros_like(dv_ref)
    kt_ref[...] = jnp.transpose(qkv_ref[:, width : 2 * width])
    for block in range(seq // AB):
        low, kend = block * AB, (block + 1) * AB
        rows = slice(low, kend)
        qpos = lax.broadcasted_iota(jnp.int32, (kend, AB), 1) + low
        kpos = lax.broadcasted_iota(jnp.int32, (kend, AB), 0)
        same = doc_row[:, rows] == col_ref[0:kend, :]
        allowed = (same & (kpos < qpos)) | (kpos == qpos)
        bias = jnp.where(allowed, 0.0, NEGATIVE).astype(F32)

        def pair(index, carry):
            at = pl.multiple_of(index * 128, 128)
            q = qkv_ref[rows, pl.ds(at, 128)] * jnp.asarray(scale, BF)
            k = qkv_ref[0:kend, pl.ds(width + at, 128)]
            v = qkv_ref[0:kend, pl.ds(2 * width + at, 128)]
            do = do_ref[rows, pl.ds(at, 128)]
            dqt = jnp.zeros((128, AB), F32)
            dv = dk = None
            for half in range(2):
                keep = lanes_of(q.shape, half)
                qm = jnp.where(keep, q, jnp.zeros_like(q))
                dom = jnp.where(keep, do, jnp.zeros_like(do))
                p = jnp.exp(nt(k, qm) + bias - lse_ref[pl.ds(2 * index + half, 1), rows])
                dp = nt(v, dom)
                delta = jnp.sum(p * dp, axis=0, keepdims=True)
                ds = (p * (dp - delta)).astype(BF)
                dv_half = nn(p.astype(BF), dom)
                dk_half = nn(ds, qm)
                dv = dv_half if dv is None else dv + dv_half
                dk = dk_half if dk is None else dk + dk_half
                kt = kt_ref[pl.ds(pl.multiple_of(at + half * HEAD_DIM, HEAD_DIM), HEAD_DIM), 0:kend]
                dqt = nn(kt, ds) if half == 0 else jnp.concatenate([dqt, nn(kt, ds)], axis=0)
            dv_ref[0:kend, pl.ds(at, 128)] += dv
            dk_ref[0:kend, pl.ds(at, 128)] += dk
            dqkv_ref[rows, pl.ds(at, 128)] = (jnp.transpose(dqt) * scale).astype(BF)
            return carry

        lax.fori_loop(0, width // 128, pair, 0, unroll=True)
    dqkv_ref[:, width : 2 * width] = dk_ref[...].astype(BF)
    dqkv_ref[:, 2 * width :] = dv_ref[...].astype(BF)

    def spread(block, carry):
        rows = pl.ds(block * AB, AB)
        dh_ref[rows, :] = nt(dqkv_ref[rows, :], w_ref[:, 0 : 3 * width])
        return carry

    lax.fori_loop(0, seq // AB, spread, 0)

    def weigh(block, carry):
        cols = pl.ds(pl.multiple_of(block * 384, 384), 384)
        grad = tn(h_ref[...], dqkv_ref[:, cols])
        if has_prev:
            grad = grad + prev_ref[:, cols]
        gw_ref[:, cols] = grad.astype(gw_ref.dtype)
        return carry

    lax.fori_loop(0, 3 * width // 384, weigh, 0)


def attend_back(micro, h_all, w_own, qkv, do_all, lse, labels, prev):
    seq, width = do_all.shape
    flops = 2 * seq * D * 3 * width * 2 + 10 * seq * seq * width
    args = [h_all, w_own, qkv, do_all, lse, labels]
    if prev is not None:
        args.append(prev)
    return pl.pallas_call(
        functools.partial(attend_back_kernel, micro, prev is not None),
        out_shape=(
            jax.ShapeDtypeStruct((D, 3 * width), F32),
            jax.ShapeDtypeStruct((seq, D), F32),
        ),
        in_specs=[VMEM_WHOLE] * len(args),
        out_specs=(VMEM_WHOLE,) * 2,
        scratch_shapes=[
            pltpu.VMEM((seq, 3 * width), BF),
            pltpu.VMEM((seq, width), F32),
            pltpu.VMEM((seq, width), F32),
            pltpu.VMEM((width, seq), BF),
            pltpu.VMEM((seq, 1), F32),
        ],
        compiler_params=pltpu.CompilerParams(vmem_limit_bytes=30 << 20),
        cost_estimate=pl.CostEstimate(
            flops=4 * flops, bytes_accessed=16 << 20, transcendentals=seq * seq * width // 128
        ),
        name="attend_back",
    )(*args)


def expert_kernel(has_prev, half, h_ref, g_ref, c_ref, up_ref, down_ref, *refs):
    if has_prev:
        (prev_up_ref, prev_down_ref, _, y_out_ref, dh_out_ref, gc_ref, gup_ref, gdown_ref,
         sup_ref, sdown_ref,
         dz_ref, gate_ref, z_ref, acc_ref, a_ref, du_ref, y_ref, dh_ref, sems) = refs
    else:
        (y_out_ref, dh_out_ref, gc_ref, gup_ref, gdown_ref,
         dz_ref, gate_ref, z_ref, acc_ref, a_ref, du_ref, y_ref, dh_ref, sems) = refs
    step, steps = pl.program_id(0), pl.num_programs(0)
    micro = 1 if has_prev else 0
    capacity = h_ref.shape[1]
    rows_all = h_ref.shape[0] * capacity
    blocks = rows_all // QB
    each = QB // capacity

    def take(ref, block):
        return ref[pl.ds(pl.multiple_of(block * each, each), each)].reshape(QB, D)

    @pl.when(step == 0)
    def _():
        def start(block, carry):
            rows = pl.ds(pl.multiple_of(block * QB, QB), QB)
            logit = jnp.sum(take(h_ref, block).astype(F32) * c_ref[...], axis=1, keepdims=True)
            gate = 1.0 / (1.0 + jnp.exp(-logit))
            gate_ref[rows, :] = gate
            dz_ref[rows, :] = (gate * take(g_ref, block).astype(F32)).astype(BF)
            z_ref[rows, :] = jnp.zeros((QB, D), F32)
            acc_ref[rows, :] = jnp.zeros((QB, D), F32)
            return carry

        lax.fori_loop(0, blocks, start, 0)

    def forward(block, carry):
        rows = pl.ds(pl.multiple_of(block * QB, QB), QB)
        u = nn(take(h_ref, block), up_ref[...])
        square = u * u
        t = jnp.tanh(GELU_K * u * (1.0 + 0.044715 * square))
        a = (0.5 * u * (1.0 + t)).astype(BF)
        slope = 0.5 * (1.0 + t) + 0.5 * u * (1.0 - t * t) * (
            GELU_K * (1.0 + 3 * 0.044715 * square)
        )
        a_ref[rows, :] = a
        z_ref[rows, :] += nn(a, down_ref[...])
        du = (nt(dz_ref[rows, :], down_ref[...]) * slope).astype(BF)
        du_ref[rows, :] = du
        acc_ref[rows, :] += nt(du, up_ref[...])
        return carry

    lax.fori_loop(0, blocks, forward, 0, unroll=True)
    gup = tn(h_ref[...].reshape(rows_all, D), du_ref[...])
    gdown = tn(a_ref[...], dz_ref[...])
    if has_prev:
        gup = gup + prev_up_ref[...]
        gdown = gdown + prev_down_ref[...]

        @pl.when(step < half)
        def _():
            sup_ref[...] = gup.astype(BF)
            sdown_ref[...] = gdown.astype(BF)

        @pl.when(step >= half)
        def _():
            gup_ref[...] = gup
            gdown_ref[...] = gdown
    else:
        gup_ref[...] = gup
        gdown_ref[...] = gdown

    @pl.when(step == steps - 1)
    def _():
        saves = []
        total = jnp.zeros((1, D), F32)
        for block in range(blocks):
            rows = slice(block * QB, (block + 1) * QB)
            group = slice(block * each, (block + 1) * each)
            z = z_ref[rows, :].astype(BF).astype(F32)
            gate = gate_ref[rows, :]
            dgate = jnp.sum(take(g_ref, block).astype(F32) * z, axis=1, keepdims=True)
            dlogit = dgate * gate * (1.0 - gate)
            y_ref[group] = (gate * z).astype(BF).reshape(each, capacity, D)
            dh_ref[rows, :] = (acc_ref[rows, :] + dlogit * c_ref[...]).astype(BF)
            total = total + jnp.sum(dlogit * take(h_ref, block).astype(F32), axis=0, keepdims=True)
            saves += [
                pltpu.make_async_copy(
                    dh_ref.at[rows, :], dh_out_ref.at[rows, :], sems.at[2 * block]
                ),
                pltpu.make_async_copy(
                    y_ref.at[group], y_out_ref.at[group, micro], sems.at[2 * block + 1]
                ),
            ]
            for save in saves[-2:]:
                save.start()
        gc_ref[...] = total
        for save in saves:
            save.wait()


def expert(h_slots, h_plane, g_slots, g_plane, centre, up, down, prev):
    groups, _, capacity, _ = h_slots.shape
    rows = groups * capacity
    ff = up.shape[1]
    wide = ff // 3 if prev is None else ff // 4
    steps = ff // wide
    half = steps // 2
    whole = lambda step: (0, 0)
    plane = lambda index: (lambda step: (0, index, 0, 0))
    slot_block = (groups, None, capacity, D)

    turn = lambda step: (step * wide + (ff // 2) * (1 - lax.axis_index("ctx"))) % ff // wide
    early = lambda step: (step // half) * (half - 1) + (1 - step // half) * step
    late = lambda step: (step // half) * (step - half)
    if prev is None:
        turn = lambda step: step
    in_specs = [
        pl.BlockSpec(slot_block, plane(h_plane), pipeline_mode=pl.Buffered(1)),
        pl.BlockSpec(slot_block, plane(g_plane), pipeline_mode=pl.Buffered(1)),
        pl.BlockSpec((1, D), whole),
        pl.BlockSpec((D, wide), lambda step: (0, turn(step))),
        pl.BlockSpec((wide, D), lambda step: (turn(step), 0)),
    ]
    args = [h_slots, g_slots, centre, up, down]
    out_shape = [
        pltpu.HBM((groups, MICRO, capacity, D), BF),
        pltpu.HBM((rows, D), BF),
        jax.ShapeDtypeStruct((1, D), F32),
    ]
    out_specs = [HBM_WHOLE, HBM_WHOLE, pl.BlockSpec((1, D), whole)]
    if prev is None:
        out_shape += [pltpu.HBM((D, ff), F32), pltpu.HBM((ff, D), F32)]
        out_specs += [
            pl.BlockSpec((D, wide), lambda step: (0, step)),
            pl.BlockSpec((wide, D), lambda step: (step, 0)),
        ]
    else:
        in_specs += [
            pl.BlockSpec((D, wide), lambda step: (0, turn(step))),
            pl.BlockSpec((wide, D), lambda step: (turn(step), 0)),
            HBM_WHOLE,
        ]
        args += list(prev)
        for kind, at in ((F32, late), (BF, early)):
            out_shape += [pltpu.HBM((D, ff // 2), kind), pltpu.HBM((ff // 2, D), kind)]
            out_specs += [
                pl.BlockSpec((D, wide), lambda step, at=at: (0, at(step))),
                pl.BlockSpec((wide, D), lambda step, at=at: (at(step), 0)),
            ]
    return pl.pallas_call(
        functools.partial(expert_kernel, prev is not None, half),
        out_shape=tuple(out_shape),
        grid=(steps,),
        in_specs=in_specs,
        out_specs=tuple(out_specs),
        scratch_shapes=[
            pltpu.VMEM((rows, D), BF),
            pltpu.VMEM((rows, 1), F32),
            pltpu.VMEM((rows, D), F32),
            pltpu.VMEM((rows, D), F32),
            pltpu.VMEM((rows, wide), BF),
            pltpu.VMEM((rows, wide), BF),
            pltpu.VMEM((groups, capacity, D), BF),
            pltpu.VMEM((rows, D), BF),
            pltpu.SemaphoreType.DMA((2 * rows // QB,)),
        ],
        input_output_aliases={} if prev is None else {7: 0},
        compiler_params=pltpu.CompilerParams(vmem_limit_bytes=56 << 20),
        cost_estimate=pl.CostEstimate(
            flops=12 * rows * D * ff, bytes_accessed=40 << 20, transcendentals=rows * ff
        ),
        name="expert",
    )(*args)


def emit_kernel(x0_ref, x1_ref, y_ref, target_ref, out_ref):
    rows = x0_ref.shape[0]
    groups, _, capacity, _ = y_ref.shape
    slots = groups * capacity
    for micro, x_ref in enumerate((x0_ref, x1_ref)):
        value = y_ref[:, micro].reshape(slots, D)

        def combine(block, carry):
            off = pl.multiple_of(block * AB, AB)
            at = pl.ds(off, AB)
            slot = lax.broadcasted_iota(jnp.int32, (AB, slots), 1)
            pick = (slot == target_ref[at, micro : micro + 1]).astype(F32).astype(BF)
            out_ref[pl.ds(micro * rows + off, AB), :] = (x_ref[at, :] + nn(pick, value)).astype(BF)
            return carry

        lax.fori_loop(0, rows // AB, combine, 0)


def emit(x0, x1, y, target):
    rows = x0.shape[0]
    return pl.pallas_call(
        emit_kernel,
        out_shape=jax.ShapeDtypeStruct((MICRO * rows, D), BF),
        in_specs=[VMEM_WHOLE] * 4,
        out_specs=VMEM_WHOLE,
        compiler_params=pltpu.CompilerParams(vmem_limit_bytes=10 << 20),
        cost_estimate=pl.CostEstimate(
            flops=4 * rows * D * y.shape[0] * y.shape[2], bytes_accessed=8 << 20, transcendentals=0
        ),
        name="emit",
    )(x0, x1, y, target)


def swap(array):
    return lax.ppermute(array, "ctx", [(0, 1), (1, 0)])


def half_of(array, index, axis):
    size = array.shape[axis] // 2
    return lax.dynamic_slice_in_dim(array, index * size, size, axis)


def greet(peers):
    barrier = pltpu.get_barrier_semaphore()
    for peer in peers:
        pl.semaphore_signal(
            barrier, inc=1, device_id=peer, device_id_type=pl.DeviceIdType.MESH
        )
    pl.semaphore_wait(barrier, len(peers))


def send(src, dst, send_sem, recv_sem, peer):
    return pltpu.make_async_remote_copy(
        src_ref=src,
        dst_ref=dst,
        send_sem=send_sem,
        recv_sem=recv_sem,
        device_id=peer,
        device_id_type=pl.DeviceIdType.MESH,
    )


def places():
    me, core = lax.axis_index("shard"), lax.axis_index("ctx")
    z, y, x = me // 4, (me // 2) % 2, me % 2
    along_y, along_x = me + 2 - 4 * y, me + 1 - 2 * x
    first = along_y * (1 - core) + along_x * core
    second = along_x * (1 - core) + along_y * core
    far = 4 * z + 3 - me % 4
    line = [z, z + 1 - 2 * (z % 2), (z + 2) % 4, 3 - z]
    return me, first, second, far, line


def head_kernel(
    experts, capacity, qkv_ref, proj_ref, seg_ref, pad_ref, route_ref, tok_ref, cot_ref,
    gain_ref, gain_two_ref,
    out_save_ref, full_save_ref, h0_save_ref, h1_save_ref, all_ref, target_ref, in0_ref, in1_ref,
    saved_ref, lse_ref, sent_ref, x1_out_ref, attended_ref,
    w_ref, x_ref, g_ref, label_ref, slots_ref, out_ref, full_ref, h0_ref, h1_ref,
    col_ref, heads_ref, o_ref, first_ref, x1_ref, joined_ref, h2_ref,
    send_sem, recv_sem, swap_send, swap_recv, sems, post_sems,
):
    size = w_ref.shape[0]
    half = full_ref.shape[1] // 2
    wide = w_ref.shape[1] - half
    count = label_ref.shape[1]
    me, first, second, far, line = places()
    core = lax.axis_index("ctx")
    own = pl.multiple_of(core * half, 128)
    loads = [
        pltpu.make_async_copy(
            qkv_ref.at[:, pl.ds(2 * at * half + own, half)],
            w_ref.at[:, at * half : (at + 1) * half],
            sems.at[at],
        )
        for at in range(3)
    ]
    loads += [
        pltpu.make_async_copy(proj_ref.at[:, pl.ds(own, half)], w_ref.at[:, wide:], sems.at[3]),
        pltpu.make_async_copy(cot_ref, g_ref, sems.at[4]),
        pltpu.make_async_copy(tok_ref, x_ref, sems.at[5]),
    ]
    for load in loads:
        load.start()
    label_ref[...] = jnp.zeros_like(label_ref)
    for at, ref in enumerate((seg_ref, pad_ref, route_ref)):
        for micro in range(MICRO):
            row = MICRO * at + micro
            label_ref[row : row + 1, :] = ref[micro]
    twin = {"ctx": 1 - core}
    lines = [4 * z for z in line]
    y, x = (me // 2) % 2, me % 2
    turns = [me % 4, me % 4 + 1 - 2 * x, me % 4 + 2 - 4 * y, 3 - me % 4]

    def rows(block):
        return out_ref.at[pl.ds(pl.multiple_of(block * size, 16), size), :]

    chips = [lines[j] + turns[i] for j in range(4) for i in range(4)]
    peers = [{"shard": chips[4 * j]} for j in (1, 2, 3)]
    one, two = {"shard": first}, {"shard": second}
    greet([{"shard": chip} for chip in chips[1:]] + [twin])
    copies, share = [], []

    def push(block, role, peer, src=None):
        copy = send(
            rows(block) if src is None else src, rows(block), send_sem.at[role], recv_sem.at[role], peer
        )
        copy.start()
        copies.append(copy)

    def arrive(block, role):
        send(rows(block), rows(block), send_sem.at[0], recv_sem.at[role], one).wait_recv()

    for load in loads[:4]:
        load.wait()
    push(me, 3, one, w_ref)
    push(me, 7, two, w_ref)
    for j in (1, 2, 3):
        push(me, j - 1, peers[j - 1], w_ref)
    out_ref[pl.ds(pl.multiple_of(me * size, 16), size), :] = w_ref[...]
    mine = pl.ds(pl.multiple_of(core * count, 128), count)
    share.append(send(label_ref, all_ref.at[:, mine], send_sem.at[15], recv_sem.at[15], twin))
    share[0].start()
    all_ref[:, mine] = label_ref[...]

    before = lax.broadcasted_iota(jnp.int32, (count, count), 0)
    after = lax.broadcasted_iota(jnp.int32, (count, count), 1)
    upto = (before <= after).astype(F32).astype(BF)
    ids = lax.broadcasted_iota(jnp.int32, (experts, count), 0)
    target_ref[...] = jnp.zeros_like(target_ref)
    for micro in range(MICRO):
        route = label_ref[2 * MICRO + micro : 2 * MICRO + micro + 1, :]
        chosen = (ids == route).astype(F32)
        rank = jnp.sum(nn(chosen.astype(BF), upto) * chosen, axis=0, keepdims=True)
        target_ref[micro : micro + 1, :] = route * capacity + rank.astype(jnp.int32) - 1

    def place(micro, group):
        slot = lax.broadcasted_iota(jnp.int32, (4 * capacity, count), 0) + group * capacity
        pick = (slot == target_ref[micro : micro + 1, :]).astype(F32).astype(BF)
        value = nn(pick, g_ref[micro * count : (micro + 1) * count, :]).astype(BF)
        slots_ref[micro, pl.ds(pl.multiple_of(group, 4), 4)] = value.reshape(4, capacity, D)

    swaps = []

    def pass_on(micro, j):
        for i in range(4):
            role = 4 * j + i
            if role:
                copy = send(
                    slots_ref.at[micro, chips[role]],
                    (in1_ref if micro else in0_ref).at[me],
                    swap_send.at[16 * micro + role],
                    swap_recv.at[16 * micro + role],
                    {"shard": chips[role]},
                )
                copy.start()
                swaps.append(copy)

    loads[4].wait()
    place(0, lines[2])
    pass_on(0, 2)

    def normed(micro, h_ref):
        def norm(block, carry):
            off = pl.multiple_of(block * RB, RB)
            unit = normal(x_ref[pl.ds(micro * count + off, RB), :].astype(F32))[0]
            at = pl.ds(pl.multiple_of(core * count + off, RB), RB)
            h_ref[at, :] = (unit * gain_ref[...]).astype(BF)
            return carry

        lax.fori_loop(0, count // RB, norm, 0)
        copy = send(
            h_ref.at[mine, :], h_ref.at[mine, :], send_sem.at[16 + micro], recv_sem.at[16 + micro], twin
        )
        copy.start()
        share.append(copy)

    arrive(lines[0] + first % 4, 3)
    push(lines[0] + first % 4, 11, two)
    block = lines[1] + me % 4
    arrive(block, 0)
    push(block, 4, one)
    push(block, 8, two)
    place(0, lines[3])
    pass_on(0, 3)
    loads[5].wait()
    normed(0, h0_ref)
    for j in (2, 3):
        block = lines[j] + me % 4
        arrive(block, j - 1)
        push(block, 3 + j, one)
        push(block, 7 + j, two)
        block = lines[j - 1] + first % 4
        arrive(block, 3 + j - 1)
        push(block, 11 + j - 1, two)
        if j == 2:
            place(0, lines[1])
            pass_on(0, 1)
    block = lines[3] + first % 4
    arrive(block, 6)
    push(block, 14, two)
    place(0, lines[0])
    pass_on(0, 0)
    normed(1, h1_ref)
    for group in range(0, experts, 4):
        place(1, group)
    saves = [
        pltpu.make_async_copy(slots_ref.at[0, me], in0_ref.at[me], sems.at[6]),
        pltpu.make_async_copy(slots_ref.at[1, me], in1_ref.at[me], sems.at[7]),
    ]
    for j in range(4):
        arrive(lines[j] + second % 4, 7 + j)
        arrive(lines[j] + far % 4, 11 + j)
    for j in (2, 3, 1, 0):
        pass_on(1, j)
    side = pl.ds(pl.multiple_of(core * half, 128), half)
    joint = send(
        out_ref.at[:, wide : wide + half], full_ref.at[:, side], send_sem.at[18], recv_sem.at[18], twin
    )
    joint.start()
    full_ref[:, side] = out_ref[:, wide : wide + half]
    for copy in share:
        copy.wait()
    saves += [
        pltpu.make_async_copy(out_ref, out_save_ref, sems.at[8]),
        pltpu.make_async_copy(h0_ref, h0_save_ref, sems.at[9]),
        pltpu.make_async_copy(h1_ref, h1_save_ref, sems.at[10]),
        pltpu.make_async_copy(full_ref, full_save_ref, sems.at[11]),
    ]
    for save in saves[:-1]:
        save.start()
    attend_kernel(
        0, h0_ref, out_ref, all_ref, saved_ref, o_ref, lse_ref, col_ref, heads_ref, sems.at[12]
    )
    joint.wait()
    saves[-1].start()
    post_stage(
        0, capacity, x_ref, o_ref, full_ref, gain_two_ref, target_ref, sent_ref, x1_out_ref,
        attended_ref, first_ref, x1_ref, joined_ref, h2_ref, post_sems, send_sem.at[19], recv_sem.at[19],
    )
    for copy in copies:
        copy.wait_send()
    for save in saves:
        save.wait()
    for copy in swaps:
        copy.wait()


def head(experts, capacity, qkv_weight, out_weight, seg, pad, route, x, g, gain, gain_two):
    size, columns = qkv_weight.shape[0], 2 * D
    count = seg.shape[2]
    half = D // 2
    slots = experts * capacity
    in_hbm = lambda array: pltpu.with_memory_space_constraint(array, pltpu.HBM)
    return pl.pallas_call(
        functools.partial(head_kernel, experts, capacity),
        out_shape=(
            pltpu.HBM((16 * size, columns), BF),
            pltpu.HBM((16 * size, D), BF),
            pltpu.HBM((2 * count, D), BF),
            pltpu.HBM((2 * count, D), BF),
            jax.ShapeDtypeStruct((8, 2 * count), jnp.int32),
            jax.ShapeDtypeStruct((8, count), jnp.int32),
            pltpu.HBM((experts, capacity, D), BF),
            pltpu.HBM((experts, capacity, D), BF),
            pltpu.HBM((2 * count, 3 * half), BF),
            jax.ShapeDtypeStruct((8, 2 * count), F32),
            pltpu.HBM((experts, capacity, D), BF),
            pltpu.HBM((count, D), F32),
            pltpu.HBM((count, D), BF),
        ),
        in_specs=[HBM_WHOLE] * 2 + [VMEM_WHOLE] * 3 + [HBM_WHOLE] * 2 + [VMEM_WHOLE] * 2,
        out_specs=(HBM_WHOLE,) * 4
        + (VMEM_WHOLE,) * 2
        + (HBM_WHOLE,) * 3
        + (VMEM_WHOLE,)
        + (HBM_WHOLE,) * 3,
        scratch_shapes=[
            pltpu.VMEM((size, columns), BF),
            pltpu.VMEM((MICRO * count, D), BF),
            pltpu.VMEM((MICRO * count, D), BF),
            pltpu.VMEM((8, count), jnp.int32),
            pltpu.VMEM((MICRO, experts, capacity, D), BF),
            pltpu.VMEM((16 * size, columns), BF),
            pltpu.VMEM((16 * size, D), BF),
            pltpu.VMEM((2 * count, D), BF),
            pltpu.VMEM((2 * count, D), BF),
            pltpu.VMEM((2 * count, 1), F32),
            pltpu.VMEM((2 * count, 3 * half), BF),
            pltpu.VMEM((2 * count, half), BF),
            pltpu.VMEM((experts, capacity, D), BF),
            pltpu.VMEM((count, D), F32),
            pltpu.VMEM((count, D), BF),
            pltpu.VMEM((count, D), BF),
            pltpu.SemaphoreType.DMA((20,)),
            pltpu.SemaphoreType.DMA((20,)),
            pltpu.SemaphoreType.DMA((32,)),
            pltpu.SemaphoreType.DMA((32,)),
            pltpu.SemaphoreType.DMA((13,)),
            pltpu.SemaphoreType.DMA((2 + slots // QB,)),
        ],
        compiler_params=pltpu.CompilerParams(
            collective_id=0, has_side_effects=True, vmem_limit_bytes=52 << 20
        ),
        cost_estimate=pl.CostEstimate(flops=0, bytes_accessed=100 << 20, transcendentals=0),
        name="head",
    )(
        in_hbm(qkv_weight), in_hbm(out_weight), seg, pad, route, in_hbm(x), in_hbm(g), gain, gain_two
    )


def scatter_kernel(
    gw_ref, go_ref, rows_ref, gqkv_ref, gout_ref, gsmall_ref,
    theirs_ref, packed_ref, rx1_ref, rx2_ref, rx3_ref, tx1_ref, tx2_ref, sum_ref, small_ref,
    send_sem, recv_sem,
):
    me, first, second, far, line = places()
    core = lax.axis_index("ctx")
    lines = [4 * z for z in line]
    part = sum_ref.shape[0] // 2
    wide, half = gw_ref.shape[1], go_ref.shape[1]
    peers = [{"shard": lines[j] + me % 4} for j in (1, 2, 3)]
    one, two, twin = {"shard": first}, {"shard": second}, {"ctx": 1 - core}
    greet(peers + [one, two, twin])
    small_ref[...] = jnp.transpose(rows_ref[...])

    def pack(chunk, carry):
        top = pl.ds(pl.multiple_of(chunk * part, 8), part)
        low = pl.ds(pl.multiple_of(D // 2 + chunk * part, 8), part)
        for ref, at, size in ((gw_ref, 0, wide), (go_ref, wide, half), (small_ref, wide + half, 128)):
            both = jnp.concatenate([ref[top, :], ref[low, :]], axis=0)
            packed_ref[chunk, :, at : at + size] = both.astype(BF)
        return carry

    lax.fori_loop(0, 16, pack, 0)
    copies = []

    def push(src, dst, role, peer):
        copy = send(src, dst, send_sem.at[role], recv_sem.at[role], peer)
        copy.start()
        copies.append(copy)

    def arrive(dst, role):
        send(dst, dst, send_sem.at[role], recv_sem.at[role], one).wait_recv()

    order = (3, 2, 1, 0)
    for j in order:
        push(packed_ref.at[lines[j] + far % 4], rx1_ref.at[j], j, two)
    for j in order:
        push(packed_ref.at[lines[j] + second % 4], rx1_ref.at[4 + j], 4 + j, two)
    for j in order:
        arrive(rx1_ref.at[j], j)
        total = packed_ref[lines[j] + first % 4].astype(F32) + rx1_ref[j].astype(F32)
        tx1_ref[j] = total.astype(BF)
        push(tx1_ref.at[j], rx2_ref.at[j], 8 + j, one)
    own = None
    for j in order:
        arrive(rx1_ref.at[4 + j], 4 + j)
        total = packed_ref[lines[j] + me % 4].astype(F32) + rx1_ref[4 + j].astype(F32)
        arrive(rx2_ref.at[j], 8 + j)
        total = total + rx2_ref[j].astype(F32)
        if j:
            tx2_ref[j - 1] = total.astype(BF)
            push(tx2_ref.at[j - 1], rx3_ref.at[j - 1], 11 + j, peers[j - 1])
        else:
            own = total
    for j in (1, 2, 3):
        arrive(rx3_ref.at[j - 1], 11 + j)
        own = own + rx3_ref[j - 1].astype(F32)
    sum_ref[...] = own
    push(
        sum_ref.at[pl.ds(pl.multiple_of((1 - core) * part, 8), part), :], theirs_ref, 15, twin
    )
    arrive(theirs_ref, 15)
    mine, theirs = sum_ref[pl.ds(pl.multiple_of(core * part, 8), part), :], theirs_ref[...]
    low = jnp.where(core == 0, mine, theirs)
    high = jnp.where(core == 0, theirs, mine)
    for at in range(3):
        gqkv_ref[:, 2 * at * half : (2 * at + 1) * half] = low[:, at * half : (at + 1) * half]
        gqkv_ref[:, (2 * at + 1) * half : (2 * at + 2) * half] = high[:, at * half : (at + 1) * half]
    gout_ref[:, 0:half] = low[:, wide : wide + half]
    gout_ref[:, half:] = high[:, wide : wide + half]
    gsmall_ref[...] = mine[:, wide + half :] + theirs[:, wide + half :]
    for copy in copies:
        copy.wait_send()


def scatter_grads(grad_w, grad_out, rows):
    columns = grad_w.shape[1] + grad_out.shape[1] + 128
    part = D // 32
    chunk = (2 * part, columns)
    return pl.pallas_call(
        scatter_kernel,
        out_shape=(
            jax.ShapeDtypeStruct((part, 3 * D), F32),
            jax.ShapeDtypeStruct((part, D), F32),
            jax.ShapeDtypeStruct((part, 128), F32),
        ),
        in_specs=[VMEM_WHOLE] * 3,
        out_specs=(VMEM_WHOLE,) * 3,
        scratch_shapes=[
            pltpu.VMEM((part, columns), F32),
            pltpu.VMEM((16,) + chunk, BF),
            pltpu.VMEM((8,) + chunk, BF),
            pltpu.VMEM((4,) + chunk, BF),
            pltpu.VMEM((3,) + chunk, BF),
            pltpu.VMEM((4,) + chunk, BF),
            pltpu.VMEM((3,) + chunk, BF),
            pltpu.VMEM(chunk, F32),
            pltpu.VMEM((D, 128), F32),
            pltpu.SemaphoreType.DMA((16,)),
            pltpu.SemaphoreType.DMA((16,)),
        ],
        compiler_params=pltpu.CompilerParams(
            collective_id=1, has_side_effects=True, vmem_limit_bytes=16 << 20
        ),
        cost_estimate=pl.CostEstimate(flops=0, bytes_accessed=100 << 20, transcendentals=0),
        name="scatter_grads",
    )(grad_w, grad_out, rows)


def normal(values):
    centre = values - jnp.mean(values, axis=1, keepdims=True)
    spread = jnp.mean(centre * centre, axis=1, keepdims=True)
    scale = lax.rsqrt(spread + EPSILON)
    return centre * scale, scale


def normal_back(unit, scale, gain, grad):
    pull = grad * gain
    return scale * (
        pull
        - jnp.mean(pull, axis=1, keepdims=True)
        - unit * jnp.mean(pull * unit, axis=1, keepdims=True)
    )


RB = 256


def post_kernel(micro, capacity, *refs):
    greet([{"ctx": 1 - lax.axis_index("ctx")}])
    post_stage(micro, capacity, *refs)


def post_stage(
    micro, capacity, x_ref, o_ref, wo_ref, gain_ref, target_ref, sent_ref, x1_out_ref, full_out_ref,
    slots_ref, x1_ref, full_ref, h_ref, sems, send_sem, recv_sem,
):
    core = lax.axis_index("ctx")
    rows, width = x1_ref.shape[0], o_ref.shape[1]
    twin = {"ctx": 1 - core}
    mine = pl.ds(pl.multiple_of(core * width, 128), width)
    copy = send(
        o_ref.at[pl.ds(pl.multiple_of((1 - core) * rows, 128), rows), :],
        full_ref.at[:, mine],
        send_sem,
        recv_sem,
        twin,
    )
    copy.start()
    full_ref[:, mine] = o_ref[pl.ds(pl.multiple_of(core * rows, 128), rows), :]
    copy.wait()

    def norm(block, carry):
        at = pl.ds(pl.multiple_of(block * RB, RB), RB)
        value = x_ref[pl.ds(micro * rows + pl.multiple_of(block * RB, RB), RB), :].astype(F32)
        value = value + nn(full_ref[at, :], wo_ref[...])
        x1_ref[at, :] = value
        h_ref[at, :] = (normal(value)[0] * gain_ref[...]).astype(BF)
        return carry

    lax.fori_loop(0, rows // RB, norm, 0)
    saves = [
        pltpu.make_async_copy(full_ref, full_out_ref, sems.at[0]),
        pltpu.make_async_copy(x1_ref, x1_out_ref, sems.at[1]),
    ]
    for save in saves:
        save.start()
    each = QB // capacity
    for block in range(slots_ref.shape[0] // each):
        slot = lax.broadcasted_iota(jnp.int32, (QB, rows), 0) + block * QB
        pick = (slot == target_ref[micro : micro + 1, :]).astype(F32).astype(BF)
        group = slice(block * each, (block + 1) * each)
        slots_ref[group] = nn(pick, h_ref[...]).astype(BF).reshape(each, capacity, D)
        save = pltpu.make_async_copy(slots_ref.at[group], sent_ref.at[group], sems.at[2 + block])
        save.start()
        saves.append(save)
    for save in saves:
        save.wait()


def post(micro, x, o_own, wo, gain, target, experts, capacity):
    rows = x.shape[0] // MICRO
    slots = experts * capacity
    return pl.pallas_call(
        functools.partial(post_kernel, micro, capacity),
        out_shape=(
            pltpu.HBM((experts, capacity, D), BF),
            pltpu.HBM((rows, D), F32),
            pltpu.HBM((rows, D), BF),
        ),
        in_specs=[VMEM_WHOLE] * 5,
        out_specs=(HBM_WHOLE,) * 3,
        scratch_shapes=[
            pltpu.VMEM((experts, capacity, D), BF),
            pltpu.VMEM((rows, D), F32),
            pltpu.VMEM((rows, D), BF),
            pltpu.VMEM((rows, D), BF),
            pltpu.SemaphoreType.DMA((2 + slots // QB,)),
            pltpu.SemaphoreType.DMA,
            pltpu.SemaphoreType.DMA,
        ],
        compiler_params=pltpu.CompilerParams(
            collective_id=2 + micro, has_side_effects=True, vmem_limit_bytes=18 << 20
        ),
        cost_estimate=pl.CostEstimate(
            flops=8 * rows * D * (D + slots), bytes_accessed=8 << 20, transcendentals=0
        ),
        name="post",
    )(x, o_own, wo, gain, target)


def fore_kernel(
    micro, dh_ref, target_ref, g_ref, x1_ref, gain_ref, wo_ref, full_ref, prev_out_ref, prev_two_ref,
    do_ref, dx_ref, gout_ref, gtwo_ref, dy_ref, all_ref, send_sem, recv_sem,
):
    core = lax.axis_index("ctx")
    rows, width = x1_ref.shape[0], do_ref.shape[1]
    slots = dh_ref.shape[0]
    twin = {"ctx": 1 - core}
    greet([twin])

    def norm(block, total):
        at = pl.ds(pl.multiple_of(block * RB, RB), RB)
        slot = lax.broadcasted_iota(jnp.int32, (RB, slots), 1)
        pick = (slot == target_ref[at, micro : micro + 1]).astype(F32).astype(BF)
        grad = nn(pick, dh_ref[...])
        unit, scale = normal(x1_ref[at, :])
        given = g_ref[pl.ds(micro * rows + pl.multiple_of(block * RB, RB), RB), :].astype(F32)
        dx = given + normal_back(unit, scale, gain_ref[...], grad)
        dx_ref[at, :] = dx
        dy = dx.astype(BF)
        dy_ref[at, :] = dy
        all_ref[at, :] = nt(dy, wo_ref[...]).astype(BF)
        return total + jnp.sum(grad * unit, axis=0, keepdims=True)

    gtwo_ref[...] = prev_two_ref[...] + lax.fori_loop(
        0, rows // RB, norm, jnp.zeros((1, D), F32)
    )
    mine = pl.ds(pl.multiple_of(core * rows, 128), rows)
    copy = send(
        all_ref.at[:, pl.ds(pl.multiple_of((1 - core) * width, 128), width)],
        do_ref.at[mine, :],
        send_sem,
        recv_sem,
        twin,
    )
    copy.start()
    do_ref[mine, :] = all_ref[:, pl.ds(pl.multiple_of(core * width, 128), width)]
    gout_ref[...] = prev_out_ref[...] + tn(full_ref[...], dy_ref[...])
    copy.wait()


def fore(micro, dh, target, g, x1, gain, wo, full, prev_out, prev_two):
    rows, slots = x1.shape[0], dh.shape[0]
    return pl.pallas_call(
        functools.partial(fore_kernel, micro),
        out_shape=(
            jax.ShapeDtypeStruct((2 * rows, D // 2), BF),
            jax.ShapeDtypeStruct((rows, D), F32),
            jax.ShapeDtypeStruct((D, D), F32),
            jax.ShapeDtypeStruct((1, D), F32),
        ),
        in_specs=[VMEM_WHOLE] * 9,
        out_specs=(VMEM_WHOLE,) * 4,
        scratch_shapes=[
            pltpu.VMEM((rows, D), BF),
            pltpu.VMEM((rows, D), BF),
            pltpu.SemaphoreType.DMA,
            pltpu.SemaphoreType.DMA,
        ],
        compiler_params=pltpu.CompilerParams(
            collective_id=4 + micro, has_side_effects=True, vmem_limit_bytes=12 << 20
        ),
        cost_estimate=pl.CostEstimate(
            flops=8 * rows * D * (2 * D + slots), bytes_accessed=8 << 20, transcendentals=0
        ),
        name="fore",
    )(dh, target, g, x1, gain, wo, full, prev_out, prev_two)


def tail_kernel(
    micro, dh_ref, x_ref, dx_ref, gain_ref, prev_ref, grad_out_ref, gone_ref,
    grad_ref, tx_ref, rx_ref, sems, send_sem, recv_sem,
):
    core = lax.axis_index("ctx")
    rows = dx_ref.shape[0]
    twin = {"ctx": 1 - core}
    greet([twin])
    tx_ref[...] = dh_ref[pl.ds(pl.multiple_of((1 - core) * rows, 128), rows), :].astype(BF)
    copy = send(tx_ref, rx_ref, send_sem, recv_sem, twin)
    copy.start()
    copy.wait()

    saves = []
    total = jnp.zeros((1, D), F32)
    for off in range(0, rows, RB):
        at = slice(off, off + RB)
        mine = pl.ds(pl.multiple_of(core * rows + off, RB), RB)
        grad = dh_ref[mine, :] + rx_ref[at, :].astype(F32)
        unit, scale = normal(x_ref[pl.ds(micro * rows + off, RB), :].astype(F32))
        grad_ref[at, :] = dx_ref[at, :] + normal_back(unit, scale, gain_ref[...], grad)
        save = pltpu.make_async_copy(grad_ref.at[at, :], grad_out_ref.at[at, :], sems.at[off // RB])
        save.start()
        saves.append(save)
        total = total + jnp.sum(grad * unit, axis=0, keepdims=True)
    gone_ref[...] = prev_ref[...] + total
    for save in saves:
        save.wait()


def tail(micro, dh, x, dx, gain, prev):
    rows = dx.shape[0]
    return pl.pallas_call(
        functools.partial(tail_kernel, micro),
        out_shape=(
            pltpu.HBM((rows, D), F32),
            jax.ShapeDtypeStruct((1, D), F32),
        ),
        in_specs=[VMEM_WHOLE] * 5,
        out_specs=(HBM_WHOLE, VMEM_WHOLE),
        scratch_shapes=[
            pltpu.VMEM((rows, D), F32),
            pltpu.VMEM((rows, D), BF),
            pltpu.VMEM((rows, D), BF),
            pltpu.SemaphoreType.DMA((rows // RB,)),
            pltpu.SemaphoreType.DMA,
            pltpu.SemaphoreType.DMA,
        ],
        compiler_params=pltpu.CompilerParams(
            collective_id=6 + micro, has_side_effects=True, vmem_limit_bytes=10 << 20
        ),
        cost_estimate=pl.CostEstimate(
            flops=40 * rows * D, bytes_accessed=8 << 20, transcendentals=0
        ),
        name="tail",
    )(dh, x, dx, gain, prev)


def body_pair(
    tokens,
    cotangent,
    segment_ids,
    padding,
    routes,
    norm_one_gain,
    qkv_weight,
    out_weight,
    norm_two_gain,
    centroids,
    expert_in,
    expert_out,
):
    local_len = tokens.shape[2]
    experts = centroids.shape[1]
    capacity = max(2, 2 * local_len // experts)
    slots = experts * capacity
    width = D // 2
    me = lax.axis_index("ctx")
    other = 1 - me
    gain_one = norm_one_gain.astype(F32)[None, :]
    gain_two = norm_two_gain.astype(F32)[None, :]

    x_all = tokens.reshape(MICRO * local_len, D)
    g_all = cotangent.reshape(MICRO * local_len, D)
    (w_all, out_full, h0, h1, labels, target, g0_in, g1_in, qkv0, lse0, sent0, x10, full0) = head(
        experts, capacity, qkv_weight, out_weight, segment_ids, padding,
        routes.reshape(MICRO, 1, local_len), x_all, g_all, gain_one, gain_two
    )
    columns = target.T
    centre = lax.dynamic_slice_in_dim(centroids.astype(F32).T, lax.axis_index("shard"), 1, 0)

    def exchange(rows):
        planes = rows.size // (slots * D)
        return lax.all_to_all(
            rows.reshape(experts, planes * capacity, D),
            "shard",
            split_axis=0,
            concat_axis=0,
            tiled=True,
        ).reshape(experts, planes, capacity, D)

    h0_in = exchange(sent0)
    qkv1, o_own, lse1 = attend(1, h1, w_all, labels)
    sent1, x11, full1 = post(1, x_all, o_own, out_full, gain_two, target, experts, capacity)
    h0_in, sent1 = lax.optimization_barrier((h0_in, sent1))
    h1_in = exchange(sent1)
    kept = [(h0, qkv0, full0, lse0, x10), (h1, qkv1, full1, lse1, x11)]

    y, dh0, gc0, gup, gdown = expert(
        h0_in, 0, g0_in[:, None], 0, centre, expert_in[0], expert_out[0], None
    )
    dh0 = exchange(dh0)
    y, dh1, gc1, gup, gdown, sup, sdown = expert(
        h1_in, 0, g1_in[:, None], 0, centre, expert_in[0], expert_out[0], (gup, gdown, y)
    )
    dh0, dh1, y = lax.optimization_barrier((dh0, dh1, y))
    dh1 = exchange(dh1)
    grad_centre = gc0 + gc1
    grad_up = gup + swap(sup).astype(F32)
    grad_down = gdown + swap(sdown).astype(F32)

    def backward(m, dh2, grad_out, grad_two, grad_w, grad_one):
        h_all, qkv, o_full, lse, x1 = kept[m]
        do_all, dx1, grad_out, grad_two = fore(
            m, dh2.reshape(slots, D), columns, g_all, x1, gain_two, out_full, o_full,
            grad_out, grad_two,
        )
        grad_w, dh_part = attend_back(m, h_all, w_all, qkv, do_all, lse, labels, grad_w)
        grad_in, grad_one = tail(m, dh_part, x_all, dx1, gain_one, grad_one)
        return grad_in, grad_out, grad_two, grad_w, grad_one

    zero_row = jnp.zeros((1, D), F32)
    in0, grad_out, grad_two, grad_w, grad_one = backward(
        0, dh0, jnp.zeros((D, D), F32), zero_row, None, zero_row
    )
    dh1, grad_one, y = lax.optimization_barrier((dh1, grad_one, y))
    y = exchange(y)
    in1, grad_out, grad_two, grad_w, grad_one = backward(
        1, dh1, grad_out, grad_two, grad_w, grad_one
    )

    grad_out = half_of(grad_out, me, 1) + swap(half_of(grad_out, other, 1).astype(BF)).astype(F32)
    column = (jnp.arange(128) == 2 + lax.axis_index("shard")).astype(F32)[:, None]
    rows = jnp.concatenate(
        [grad_one, grad_two, jnp.zeros((126, D), F32)], axis=0
    ) + column * grad_centre
    grad_qkv, grad_out, small = scatter_grads(grad_w, grad_out, rows)
    y, small = lax.optimization_barrier((y, small))
    block_out = emit(x10, x11, y, columns)

    return (
        block_out.reshape(MICRO, 1, local_len, D),
        jnp.stack([in0, in1])[:, None],
        small[:, 0],
        grad_qkv,
        grad_out,
        small[:, 1],
        small[:, 2 : 2 + experts],
        grad_up[None],
        grad_down[None],
    )


def solution(mesh):
    plan = body_pair if (mesh.shape["ctx"], mesh.shape["shard"]) == (2, 16) else body
    in_specs = (
        P(None, "shard", "ctx", None),
        P(None, "shard", "ctx", None),
        P(None, "shard", "ctx"),
        P(None, "shard", "ctx"),
        P(None, "shard", "ctx", None),
        P(),
        P("shard", None),
        P("shard", None),
        P(),
        P(),
        P("shard", None, None),
        P("shard", None, None),
    )
    out_specs = (
        P(None, "shard", "ctx", None),
        P(None, "shard", "ctx", None),
        P(("ctx", "shard")),
        P(("ctx", "shard"), None),
        P(("ctx", "shard"), None),
        P(("ctx", "shard")),
        P(("ctx", "shard"), None),
        P("shard", None, "ctx"),
        P("shard", "ctx", None),
    )
    return jax.shard_map(plan, mesh=mesh, in_specs=in_specs, out_specs=out_specs, check_vma=False)
```

```python
import functools

import jax
import jax.numpy as jnp
from jax import lax
from jax.experimental import pallas as pl
from jax.experimental.pallas import tpu as pltpu
from jax.sharding import PartitionSpec as P

D = 768
HEADS = 12
HEAD_DIM = 64
FF = 3072
MICRO = 2


EPSILON = 1e-05
NEGATIVE = -1e30
HIGH = lax.Precision.HIGHEST


def layer_norm(values, gain_vec):
    centre = values - jnp.mean(values, axis=1, keepdims=True)
    spread = jnp.mean(centre * centre, axis=1, keepdims=True)
    return centre * lax.rsqrt(spread + EPSILON) * gain_vec


def gelu_tanh(values):
    return jax.nn.gelu(values, approximate=True)


def masked_scores(queries, key_heads, query_pos, key_pos, query_doc, key_doc, key_pad):
    scores = jnp.einsum(
        "qhd,khd->hqk", queries, key_heads, preferred_element_type=jnp.float32
    ) * HEAD_DIM ** (-0.5)
    allowed = (query_doc[:, None] == key_doc[None, :]) & (key_pos[None, :] <= query_pos[:, None])
    allowed = allowed & ((key_pad[None, :] == 1) | (key_pos[None, :] == query_pos[:, None]))
    return jnp.where(allowed[None], scores, NEGATIVE)


def rows_first(left, right):
    return lax.dot_general(
        left, right, (((0,), (0,)), ((), ())), preferred_element_type=jnp.float32
    )


def rows_last(left, right):
    return lax.dot_general(
        left, right, (((1,), (1,)), ((), ())), preferred_element_type=jnp.float32
    )


def body(
    tokens,
    cotangent,
    segment_ids,
    padding,
    routes,
    norm_one_gain,
    qkv_weight,
    out_weight,
    norm_two_gain,
    centroids,
    expert_in,
    expert_out,
):
    local_len = tokens.shape[2]
    experts = centroids.shape[1]
    capacity = max(2, 2 * local_len // experts)
    seq_len = local_len * lax.axis_size("ctx")
    qkv_full, out_full = (
        lax.all_gather(qkv_weight, "shard", axis=0, tiled=True),
        lax.all_gather(out_weight, "shard", axis=0, tiled=True),
    )
    gain_one = norm_one_gain.astype(jnp.float32)
    gain_two = norm_two_gain.astype(jnp.float32)
    centre_f = centroids.astype(jnp.float32)
    up_local = expert_in[0]
    down_local = expert_out[0]
    query_pos = lax.axis_index("ctx") * local_len + jnp.arange(local_len, dtype=jnp.int32)
    all_pos = jnp.arange(seq_len, dtype=jnp.int32)
    slot_ids = jnp.arange(experts * capacity, dtype=jnp.int32)
    expert_ids = jnp.arange(experts, dtype=jnp.int32)
    score_scale = HEAD_DIM ** (-0.5)
    grad_qkv_sum = jnp.zeros((D, 3 * D), jnp.float32)
    grad_out_sum = jnp.zeros((D, D), jnp.float32)
    grad_one_sum = jnp.zeros((D,), jnp.float32)
    grad_two_sum = jnp.zeros((D,), jnp.float32)
    grad_centre = jnp.zeros((D, experts), jnp.float32)
    grad_up_sum = jnp.zeros((D, FF), jnp.float32)
    grad_down_sum = jnp.zeros((D, FF), jnp.float32)
    block_list = []
    input_list = []
    for micro_index in range(MICRO):
        inputs = tokens[micro_index, 0].astype(jnp.float32)
        doc_ids = segment_ids[micro_index, 0]
        pad_mask = padding[micro_index, 0]
        route_ids = routes[micro_index, 0, :, 0]
        normed_one, norm_one_back = jax.vjp(layer_norm, inputs, gain_one)
        first_bf = normed_one.astype(jnp.bfloat16)
        qkv = jnp.dot(first_bf, qkv_full, preferred_element_type=jnp.float32)
        queries = qkv[:, :D].astype(jnp.bfloat16)
        key_rows = qkv[:, D : 2 * D].astype(jnp.bfloat16)
        value_rows = qkv[:, 2 * D :].astype(jnp.bfloat16)
        key_all, value_all, doc_all, pad_all = (
            lax.all_gather(key_rows, "ctx", axis=0, tiled=True),
            lax.all_gather(value_rows, "ctx", axis=0, tiled=True),
            lax.all_gather(doc_ids, "ctx", axis=0, tiled=True),
            lax.all_gather(pad_mask, "ctx", axis=0, tiled=True),
        )
        query_heads = queries.reshape(local_len, HEADS, HEAD_DIM)
        key_heads = key_all.reshape(seq_len, HEADS, HEAD_DIM)
        value_heads = value_all.reshape(seq_len, HEADS, HEAD_DIM)
        scores = masked_scores(
            query_heads, key_heads, query_pos, all_pos, doc_ids, doc_all, pad_all
        )
        row_max = jnp.max(scores, axis=2, keepdims=True)
        weights = jnp.exp(scores - row_max)
        row_total = jnp.sum(weights, axis=2, keepdims=True)
        probs_now = weights / row_total
        log_total = row_max + jnp.log(row_total)
        attended = jnp.einsum(
            "hqk,khd->qhd",
            probs_now.astype(jnp.bfloat16),
            value_heads,
            preferred_element_type=jnp.float32,
        )
        attended = attended.reshape(local_len, D).astype(jnp.bfloat16)
        residual = inputs + jnp.dot(attended, out_full, preferred_element_type=jnp.float32)
        normed_two, norm_two_back = jax.vjp(layer_norm, residual, gain_two)
        second_bf = normed_two.astype(jnp.bfloat16)
        choose_mask = route_ids[:, None] == expert_ids[None, :]
        choose_f = choose_mask.astype(jnp.float32)
        logit = jnp.sum(
            jnp.dot(second_bf, centroids, preferred_element_type=jnp.float32) * choose_f, axis=1
        )
        gate_value = jax.nn.sigmoid(logit)
        choose_int = choose_mask.astype(jnp.int32)
        counts = jnp.cumsum(choose_int, axis=0)
        slot_rank = jnp.sum(counts * choose_int, axis=1) - 1
        target = route_ids * capacity + slot_rank
        dispatch = (slot_ids[:, None] == target[None, :]).astype(jnp.bfloat16)
        outbound = jnp.dot(dispatch, second_bf, preferred_element_type=jnp.float32).astype(
            jnp.bfloat16
        )
        outbound = outbound.reshape(experts, capacity, D)
        received = lax.all_to_all(outbound, "shard", split_axis=0, concat_axis=0, tiled=True)
        slot_rows = received.reshape(-1, D)
        upward = jnp.dot(slot_rows, up_local, preferred_element_type=jnp.float32)
        hidden = gelu_tanh(upward).astype(jnp.bfloat16)
        result = jnp.dot(hidden, down_local, preferred_element_type=jnp.float32).astype(
            jnp.bfloat16
        )
        returned = lax.all_to_all(
            result.reshape(received.shape), "shard", split_axis=0, concat_axis=0, tiled=True
        )
        returned, received, upward = (
            returned,
            received,
            upward.reshape(received.shape[0], received.shape[1], FF),
        )
        expert_rows = rows_first(dispatch, returned.reshape(experts * capacity, D))
        block_list.append((residual + gate_value[:, None] * expert_rows).astype(jnp.bfloat16))
        grad_out = cotangent[micro_index, 0].astype(jnp.float32)
        grad_gate = jnp.sum(grad_out * expert_rows, axis=1)
        grad_logit = grad_gate * gate_value * (1.0 - gate_value)
        grad_rows = (gate_value[:, None] * grad_out).astype(jnp.bfloat16)
        grad_outbound = jnp.dot(dispatch, grad_rows, preferred_element_type=jnp.float32).astype(
            jnp.bfloat16
        )
        grad_received = lax.all_to_all(
            grad_outbound.reshape(experts, capacity, D),
            "shard",
            split_axis=0,
            concat_axis=0,
            tiled=True,
        )
        grad_result = grad_received.reshape(-1, D)
        hidden_again, gelu_back = jax.vjp(gelu_tanh, upward.reshape(-1, FF))
        grad_down_sum = grad_down_sum + rows_first(grad_result, hidden_again.astype(jnp.bfloat16))
        grad_hidden = rows_last(grad_result, down_local)
        grad_upward = gelu_back(grad_hidden)[0].astype(jnp.bfloat16)
        grad_up_sum = grad_up_sum + rows_first(received.reshape(-1, D), grad_upward)
        grad_send = (
            rows_last(grad_upward, up_local).astype(jnp.bfloat16).reshape(grad_received.shape)
        )
        grad_back = lax.all_to_all(grad_send, "shard", split_axis=0, concat_axis=0, tiled=True)
        grad_second = rows_first(dispatch, grad_back.reshape(experts * capacity, D))
        grad_second = grad_second + grad_logit[:, None] * jnp.dot(
            choose_f, centre_f.T, precision=HIGH
        )
        grad_centre = grad_centre + jnp.dot(
            second_bf.astype(jnp.float32).T, choose_f * grad_logit[:, None], precision=HIGH
        )
        grad_resid_norm, grad_two_term = norm_two_back(grad_second)
        grad_residual = grad_out + grad_resid_norm
        grad_two_sum = grad_two_sum + grad_two_term
        grad_branch = grad_residual.astype(jnp.bfloat16)
        grad_out_sum = grad_out_sum + rows_first(attended, grad_branch)
        grad_attend = (
            rows_last(grad_branch, out_full)
            .astype(jnp.bfloat16)
            .reshape(local_len, HEADS, HEAD_DIM)
        )
        probs_again = jnp.exp(
            masked_scores(query_heads, key_heads, query_pos, all_pos, doc_ids, doc_all, pad_all)
            - log_total
        )
        grad_probs = jnp.einsum(
            "qhd,khd->hqk", grad_attend, value_heads, preferred_element_type=jnp.float32
        )
        row_terms = jnp.sum(probs_again * grad_probs, axis=2, keepdims=True)
        grad_scores = (probs_again * (grad_probs - row_terms)).astype(jnp.bfloat16)
        grad_query = (
            jnp.einsum("hqk,khd->qhd", grad_scores, key_heads, preferred_element_type=jnp.float32)
            * score_scale
        )
        grad_key_all = (
            jnp.einsum("hqk,qhd->khd", grad_scores, query_heads, preferred_element_type=jnp.float32)
            * score_scale
        )
        grad_value_all = jnp.einsum(
            "hqk,qhd->khd",
            probs_again.astype(jnp.bfloat16),
            grad_attend,
            preferred_element_type=jnp.float32,
        )
        grad_key, grad_value = (
            lax.psum_scatter(
                grad_key_all.reshape(seq_len, D).astype(jnp.bfloat16),
                "ctx",
                scatter_dimension=0,
                tiled=True,
            ).astype(jnp.float32),
            lax.psum_scatter(
                grad_value_all.reshape(seq_len, D).astype(jnp.bfloat16),
                "ctx",
                scatter_dimension=0,
                tiled=True,
            ).astype(jnp.float32),
        )
        grad_qkv_rows = jnp.concatenate(
            [grad_query.reshape(local_len, D), grad_key, grad_value], axis=1
        ).astype(jnp.bfloat16)
        grad_qkv_sum = grad_qkv_sum + rows_first(first_bf, grad_qkv_rows)
        grad_first = rows_last(grad_qkv_rows, qkv_full)
        grad_in_norm, grad_one_term = norm_one_back(grad_first)
        grad_one_sum = grad_one_sum + grad_one_term
        input_list.append(grad_residual + grad_in_norm)
    dense_sums = (
        lax.psum_scatter(grad_one_sum, ("ctx", "shard"), scatter_dimension=0, tiled=True),
        lax.psum_scatter(grad_qkv_sum, ("ctx", "shard"), scatter_dimension=0, tiled=True),
        lax.psum_scatter(grad_out_sum, ("ctx", "shard"), scatter_dimension=0, tiled=True),
        lax.psum_scatter(grad_two_sum, ("ctx", "shard"), scatter_dimension=0, tiled=True),
        lax.psum_scatter(grad_centre, ("ctx", "shard"), scatter_dimension=0, tiled=True),
    )
    expert_sums = (
        lax.psum_scatter(
            grad_up_sum.astype(jnp.bfloat16), "ctx", scatter_dimension=1, tiled=True
        ).astype(jnp.float32),
        lax.psum_scatter(
            grad_down_sum.astype(jnp.bfloat16), "ctx", scatter_dimension=1, tiled=True
        ).astype(jnp.float32),
    )
    block_out = jnp.stack(block_list)[:, None]
    grad_tokens = jnp.stack(input_list)[:, None]
    return (
        block_out,
        grad_tokens,
        dense_sums[0],
        dense_sums[1],
        dense_sums[2],
        dense_sums[3],
        dense_sums[4],
        expert_sums[0][None],
        expert_sums[1].T[None],
    )


BF = jnp.bfloat16
F32 = jnp.float32
QB = 256
AB = 512
GELU_K = 0.7978845608028654
VMEM_WHOLE = pl.BlockSpec(memory_space=pltpu.VMEM)
HBM_WHOLE = pl.BlockSpec(memory_space=pltpu.HBM)


def nn(left, right):
    return lax.dot_general(left, right, (((1,), (0,)), ((), ())), preferred_element_type=F32)


def nt(left, right):
    return lax.dot_general(left, right, (((1,), (1,)), ((), ())), preferred_element_type=F32)


def tn(left, right):
    return lax.dot_general(left, right, (((0,), (0,)), ((), ())), preferred_element_type=F32)


def lanes_of(shape, half):
    lane = lax.broadcasted_iota(jnp.int32, shape, 1)
    return (lane < HEAD_DIM) if half == 0 else (lane >= HEAD_DIM)


def masks_of(label_ref, micro):
    doc = label_ref[micro : micro + 1, :].astype(F32)
    real = label_ref[MICRO + micro : MICRO + micro + 1, :] == 1
    return doc, jnp.where(real, doc, -1.0)


def as_column(row):
    return jnp.transpose(jnp.broadcast_to(row, (128, row.shape[1])))[:, 0:1]


def attend_kernel(
    micro, h_ref, w_ref, label_ref, saved_ref, o_ref, lse_ref, col_ref, qkv_ref, sem
):
    seq, width = h_ref.shape[0], o_ref.shape[1]
    scale = HEAD_DIM ** (-0.5)
    doc_row, code_row = masks_of(label_ref, micro)
    col_ref[...] = as_column(doc_row)

    def project(block, carry):
        rows = pl.ds(block * AB, AB)
        qkv_ref[rows, :] = nn(h_ref[rows, :], w_ref[:, 0 : 3 * width]).astype(BF)
        return carry

    lax.fori_loop(0, seq // AB, project, 0)
    save = pltpu.make_async_copy(qkv_ref, saved_ref, sem)
    save.start()
    for block in range(seq // AB):
        low, kend = block * AB, (block + 1) * AB
        rows = slice(low, kend)
        qpos = lax.broadcasted_iota(jnp.int32, (AB, kend), 0) + low
        kpos = lax.broadcasted_iota(jnp.int32, (AB, kend), 1)
        same = col_ref[rows, :] == code_row[:, 0:kend]
        allowed = (same & (kpos < qpos)) | (kpos == qpos)
        bias = jnp.where(allowed, 0.0, NEGATIVE).astype(F32)
        lane = lax.broadcasted_iota(jnp.int32, (AB, 128), 1)

        def pair(index, stats):
            at = pl.multiple_of(index * 128, 128)
            q = qkv_ref[rows, pl.ds(at, 128)] * jnp.asarray(scale, BF)
            k = qkv_ref[0:kend, pl.ds(width + at, 128)]
            v = qkv_ref[0:kend, pl.ds(2 * width + at, 128)]
            outs = []
            for half in range(2):
                qm = jnp.where(lanes_of(q.shape, half), q, jnp.zeros_like(q))
                s = nt(qm, k) + bias
                top = jnp.max(s, axis=1, keepdims=True)
                e = jnp.exp(s - top)
                total = jnp.sum(e, axis=1, keepdims=True)
                outs.append(nn(e.astype(BF), v) * (1.0 / total))
                stats = jnp.where(lane == 2 * index + half, top + jnp.log(total), stats)
            o_ref[rows, pl.ds(at, 128)] = jnp.where(
                lanes_of(outs[0].shape, 0), outs[0], outs[1]
            ).astype(BF)
            return stats

        stats = lax.fori_loop(0, width // 128, pair, jnp.zeros((AB, 128), F32), unroll=True)
        lse_ref[:, rows] = jnp.transpose(stats)[0 : lse_ref.shape[0], :]
    save.wait()


def attend_back_kernel(
    micro, h_ref, w_ref, qkv_ref, do_ref, lse_ref, label_ref, dh_ref, dqkv_ref, dk_ref, dv_ref,
    kt_ref, col_ref,
):
    seq, width = do_ref.shape
    doc_row, code_row = masks_of(label_ref, micro)
    col_ref[...] = as_column(code_row)
    scale = HEAD_DIM ** (-0.5)
    dk_ref[...] = jnp.zeros_like(dk_ref)
    dv_ref[...] = jnp.zeros_like(dv_ref)
    kt_ref[...] = jnp.transpose(qkv_ref[:, width : 2 * width])
    for block in range(seq // AB):
        low, kend = block * AB, (block + 1) * AB
        rows = slice(low, kend)
        qpos = lax.broadcasted_iota(jnp.int32, (kend, AB), 1) + low
        kpos = lax.broadcasted_iota(jnp.int32, (kend, AB), 0)
        same = doc_row[:, rows] == col_ref[0:kend, :]
        allowed = (same & (kpos < qpos)) | (kpos == qpos)
        bias = jnp.where(allowed, 0.0, NEGATIVE).astype(F32)

        def pair(index, carry):
            at = pl.multiple_of(index * 128, 128)
            q = qkv_ref[rows, pl.ds(at, 128)] * jnp.asarray(scale, BF)
            k = qkv_ref[0:kend, pl.ds(width + at, 128)]
            v = qkv_ref[0:kend, pl.ds(2 * width + at, 128)]
            do = do_ref[rows, pl.ds(at, 128)]
            dqt = jnp.zeros((128, AB), F32)
            dv = dk = None
            for half in range(2):
                keep = lanes_of(q.shape, half)
                qm = jnp.where(keep, q, jnp.zeros_like(q))
                dom = jnp.where(keep, do, jnp.zeros_like(do))
                p = jnp.exp(nt(k, qm) + bias - lse_ref[pl.ds(2 * index + half, 1), rows])
                dp = nt(v, dom)
                delta = jnp.sum(p * dp, axis=0, keepdims=True)
                ds = (p * (dp - delta)).astype(BF)
                dv_half = nn(p.astype(BF), dom)
                dk_half = nn(ds, qm)
                dv = dv_half if dv is None else dv + dv_half
                dk = dk_half if dk is None else dk + dk_half
                kt = kt_ref[pl.ds(pl.multiple_of(at + half * HEAD_DIM, HEAD_DIM), HEAD_DIM), 0:kend]
                dqt = nn(kt, ds) if half == 0 else jnp.concatenate([dqt, nn(kt, ds)], axis=0)
            dv_ref[0:kend, pl.ds(at, 128)] += dv
            dk_ref[0:kend, pl.ds(at, 128)] += dk
            dqkv_ref[rows, pl.ds(at, 128)] = (jnp.transpose(dqt) * scale).astype(BF)
            return carry

        lax.fori_loop(0, width // 128, pair, 0, unroll=True)
    dqkv_ref[:, width : 2 * width] = dk_ref[...].astype(BF)
    dqkv_ref[:, 2 * width :] = dv_ref[...].astype(BF)

    def spread(block, carry):
        rows = pl.ds(block * AB, AB)
        dh_ref[rows, :] = nt(dqkv_ref[rows, :], w_ref[:, 0 : 3 * width])
        return carry

    lax.fori_loop(0, seq // AB, spread, 0)


def expert_kernel(has_prev, h_ref, g_ref, *refs):
    if has_prev:
        (c_ref, up_ref, down_ref, prev_up_ref, prev_down_ref, give_ref, extra_ref,
         y_out_ref, dh_out_ref, gc_ref, gup_ref, gdown_ref, got_ref, more_ref,
         dz_ref, gate_ref, z_ref, acc_ref, a_ref, du_ref, y_ref, dh_ref, sems,
         swap_send, swap_recv, more_send, more_recv) = refs
        exchanges = (
            (give_ref, got_ref, swap_send, swap_recv, sems.at[8], ROLES),
            (extra_ref, more_ref, more_send, more_recv, sems.at[9], EARLY_0),
        )
    else:
        (c_ref, up_ref, down_ref, give_ref, extra_ref, _,
         y_out_ref, dh_out_ref, gc_ref, gup_ref, gdown_ref, got_ref, more_ref,
         dz_ref, gate_ref, z_ref, acc_ref, a_ref, du_ref, y_ref, dh_ref, sems,
         swap_send, swap_recv, more_send, more_recv) = refs
        exchanges = (
            (give_ref, got_ref, swap_send, swap_recv, sems.at[8], ROLES),
            (extra_ref, more_ref, more_send, more_recv, sems.at[9], LATE_G),
        )
    step, steps = pl.program_id(0), pl.num_programs(0)
    capacity = h_ref.shape[1]
    rows_all = h_ref.shape[0] * capacity
    blocks = rows_all // QB
    each = QB // capacity

    def take(ref, block):
        return ref[pl.ds(pl.multiple_of(block * each, each), each)].reshape(QB, D)

    @pl.when(step == 0)
    def _():
        def start(block, carry):
            rows = pl.ds(pl.multiple_of(block * QB, QB), QB)
            logit = jnp.sum(take(h_ref, block).astype(F32) * c_ref[...], axis=1, keepdims=True)
            gate = 1.0 / (1.0 + jnp.exp(-logit))
            gate_ref[rows, :] = gate
            dz_ref[rows, :] = (gate * take(g_ref, block).astype(F32)).astype(BF)
            z_ref[rows, :] = jnp.zeros((QB, D), F32)
            acc_ref[rows, :] = jnp.zeros((QB, D), F32)
            return carry

        greet([{"shard": chip} for chip in all_chips()[1:]])
        trade_all(*exchanges)
        lax.fori_loop(0, blocks, start, 0)

    def forward(block, carry):
        rows = pl.ds(pl.multiple_of(block * QB, QB), QB)
        u = nn(take(h_ref, block), up_ref[...])
        square = u * u
        t = jnp.tanh(GELU_K * u * (1.0 + 0.044715 * square))
        a = (0.5 * u * (1.0 + t)).astype(BF)
        slope = 0.5 * (1.0 + t) + 0.5 * u * (1.0 - t * t) * (
            GELU_K * (1.0 + 3 * 0.044715 * square)
        )
        a_ref[rows, :] = a
        z_ref[rows, :] += nn(a, down_ref[...])
        du = (nt(dz_ref[rows, :], down_ref[...]) * slope).astype(BF)
        du_ref[rows, :] = du
        acc_ref[rows, :] += nt(du, up_ref[...])
        return carry

    lax.fori_loop(0, blocks, forward, 0, unroll=True)
    gup = tn(h_ref[...].reshape(rows_all, D), du_ref[...])
    gdown = tn(a_ref[...], dz_ref[...])
    if has_prev:
        gup = gup + prev_up_ref[...]
        gdown = gdown + prev_down_ref[...]
    gup_ref[...] = gup
    gdown_ref[...] = gdown

    @pl.when(step == steps - 1)
    def _():
        saves = []
        total = jnp.zeros((1, D), F32)
        for block in range(blocks):
            rows = slice(block * QB, (block + 1) * QB)
            group = slice(block * each, (block + 1) * each)
            z = z_ref[rows, :].astype(BF).astype(F32)
            gate = gate_ref[rows, :]
            dgate = jnp.sum(take(g_ref, block).astype(F32) * z, axis=1, keepdims=True)
            dlogit = dgate * gate * (1.0 - gate)
            y_ref[group] = (gate * z).astype(BF).reshape(each, capacity, D)
            dh = (acc_ref[rows, :] + dlogit * c_ref[...]).astype(BF)
            dh_ref[group] = dh.reshape(each, capacity, D)
            total = total + jnp.sum(dlogit * take(h_ref, block).astype(F32), axis=0, keepdims=True)
            saves += [
                pltpu.make_async_copy(
                    dh_ref.at[group], dh_out_ref.at[group], sems.at[2 * block]
                ),
                pltpu.make_async_copy(
                    y_ref.at[group], y_out_ref.at[group], sems.at[2 * block + 1]
                ),
            ]
            for save in saves[-2:]:
                save.start()
        gc_ref[...] = total
        for exchange in exchanges:
            saves += traded(*exchange)
        for save in saves:
            save.wait()


def expert(h_slots, g_slots, centre, up, down, give, prev):
    groups, capacity, _ = h_slots.shape
    rows = groups * capacity
    ff = up.shape[1]
    wide = ff // 3 if prev is None else ff // 4
    steps = ff // wide
    whole = lambda step: (0, 0)
    every = lambda step: (0, 0, 0)
    slot_block = (groups, capacity, D)
    up_block = pl.BlockSpec((D, wide), lambda step: (0, step))
    down_block = pl.BlockSpec((wide, D), lambda step: (step, 0))
    in_specs = [
        pl.BlockSpec(slot_block, every, pipeline_mode=pl.Buffered(1)),
        pl.BlockSpec(slot_block, every, pipeline_mode=pl.Buffered(1)),
        pl.BlockSpec((1, D), whole),
        up_block,
        down_block,
    ]
    args = [h_slots, g_slots, centre, up, down]
    out_shape = [
        pltpu.HBM((groups, capacity, D), BF),
        pltpu.HBM((groups, capacity, D), BF),
        jax.ShapeDtypeStruct((1, D), F32),
        pltpu.HBM((D, ff), F32),
        pltpu.HBM((ff, D), F32),
    ]
    out_specs = [HBM_WHOLE, HBM_WHOLE, pl.BlockSpec((1, D), whole), up_block, down_block]
    more = 2
    if prev is not None:
        in_specs += [up_block, down_block]
        args += list(prev)
    in_specs += [HBM_WHOLE] * len(give)
    args += list(give)
    out_shape += [pltpu.HBM((groups, capacity, D), BF)] * more
    out_specs += [HBM_WHOLE] * more
    return pl.pallas_call(
        functools.partial(expert_kernel, prev is not None),
        out_shape=tuple(out_shape),
        grid=(steps,),
        in_specs=in_specs,
        out_specs=tuple(out_specs),
        scratch_shapes=[
            pltpu.VMEM((rows, D), BF),
            pltpu.VMEM((rows, 1), F32),
            pltpu.VMEM((rows, D), F32),
            pltpu.VMEM((rows, D), F32),
            pltpu.VMEM((rows, wide), BF),
            pltpu.VMEM((rows, wide), BF),
            pltpu.VMEM((groups, capacity, D), BF),
            pltpu.VMEM((groups, capacity, D), BF),
            pltpu.SemaphoreType.DMA((10,)),
        ]
        + [pltpu.SemaphoreType.DMA((16,))] * (2 * more),
        input_output_aliases={7: 6} if prev is None else {},
        compiler_params=pltpu.CompilerParams(
            collective_id=2 if prev is None else 3, has_side_effects=True, vmem_limit_bytes=56 << 20
        ),
        cost_estimate=pl.CostEstimate(
            flops=12 * rows * D * ff, bytes_accessed=40 << 20, transcendentals=rows * ff
        ),
        name="expert",
    )(*args)


def emit_kernel(
    x0_ref, x1_ref, y0a_ref, y0b_ref, y1_ref, target_ref, in0_ref, in1_ref, out_ref, grad_ref,
    x_ref, y_ref, in_ref, sems,
):
    rows = x0_ref.shape[0]
    groups, capacity, _ = y0a_ref.shape
    slots = groups * capacity
    chips = all_chips()
    loads, moves, at = [], [], 0
    for micro, (x_in, grad_in, parts) in enumerate(
        (
            (x0_ref, in0_ref, ((y0a_ref, EARLY_0), (y0b_ref, LATE_0))),
            (x1_ref, in1_ref, ((y1_ref, ROLES),)),
        )
    ):
        mine = [pltpu.make_async_copy(x_in, x_ref.at[micro], sems.at[20 * micro])]
        for part_ref, roles in parts:
            mine += [
                pltpu.make_async_copy(
                    part_ref.at[chips[role]], y_ref.at[micro, chips[role]], sems.at[20 * micro + 1 + role]
                )
                for role in roles
            ]
        loads.append(mine)
        moves.append(
            (
                pltpu.make_async_copy(grad_in, in_ref.at[micro], sems.at[20 * micro + 17]),
                pltpu.make_async_copy(
                    in_ref.at[micro], grad_ref.at[micro * rows : (micro + 1) * rows, :],
                    sems.at[20 * micro + 18],
                ),
            )
        )
    for load in loads[0] + [moves[0][0]] + loads[1] + [moves[1][0]]:
        load.start()
    for micro in range(MICRO):
        for load in loads[micro]:
            load.wait()
        moves[micro][0].wait()
        moves[micro][1].start()
        slot = lax.broadcasted_iota(jnp.int32, (rows, slots), 1)
        pick = (slot == target_ref[:, micro : micro + 1]).astype(F32).astype(BF)
        value = x_ref[micro] + nn(pick, y_ref[micro].reshape(slots, D))
        out_ref[micro * rows : (micro + 1) * rows, :] = value.astype(BF)
    for move in moves:
        move[1].wait()


def emit(x0, x1, y0a, y0b, y1, target, in0, in1):
    rows = x0.shape[0]
    in_hbm = lambda array: pltpu.with_memory_space_constraint(array, pltpu.HBM)
    args = [in_hbm(array) for array in (x0, x1, y0a, y0b, y1)] + [target, in_hbm(in0), in_hbm(in1)]
    return pl.pallas_call(
        emit_kernel,
        out_shape=(
            jax.ShapeDtypeStruct((MICRO * rows, D), BF),
            pltpu.HBM((MICRO * rows, D), F32),
        ),
        in_specs=[HBM_WHOLE] * 5 + [VMEM_WHOLE] + [HBM_WHOLE] * 2,
        out_specs=(VMEM_WHOLE, HBM_WHOLE),
        scratch_shapes=[
            pltpu.VMEM((MICRO, rows, D), F32),
            pltpu.VMEM((MICRO,) + y0a.shape, BF),
            pltpu.VMEM((MICRO, rows, D), F32),
            pltpu.SemaphoreType.DMA((40,)),
        ],
        compiler_params=pltpu.CompilerParams(vmem_limit_bytes=32 << 20),
        cost_estimate=pl.CostEstimate(
            flops=4 * rows * D * y0a.shape[0] * y0a.shape[1], bytes_accessed=8 << 20, transcendentals=0
        ),
        name="emit",
    )(*args)


def greet(peers):
    barrier = pltpu.get_barrier_semaphore()
    for peer in peers:
        pl.semaphore_signal(
            barrier, inc=1, device_id=peer, device_id_type=pl.DeviceIdType.MESH
        )
    pl.semaphore_wait(barrier, len(peers))


def send(src, dst, send_sem, recv_sem, peer):
    return pltpu.make_async_remote_copy(
        src_ref=src,
        dst_ref=dst,
        send_sem=send_sem,
        recv_sem=recv_sem,
        device_id=peer,
        device_id_type=pl.DeviceIdType.MESH,
    )


def places():
    me, core = lax.axis_index("shard"), lax.axis_index("ctx")
    z, y, x = me // 4, (me // 2) % 2, me % 2
    along_y, along_x = me + 2 - 4 * y, me + 1 - 2 * x
    first = along_y * (1 - core) + along_x * core
    second = along_x * (1 - core) + along_y * core
    far = 4 * z + 3 - me % 4
    line = [z, z + 1 - 2 * (z % 2), (z + 2) % 4, 3 - z]
    return me, first, second, far, line


def all_chips():
    me, _, _, _, line = places()
    y, x = (me // 2) % 2, me % 2
    turns = [me % 4, me % 4 + 1 - 2 * x, me % 4 + 2 - 4 * y, 3 - me % 4]
    return [4 * line[j] + turns[i] for j in range(4) for i in range(4)]


ROLES = (8, 9, 10, 11, 12, 13, 14, 15, 4, 5, 6, 7, 1, 2, 3, 0)
EARLY_G, LATE_G = (8, 9, 10, 11, 12, 4, 5, 6, 1, 2, 0), (13, 14, 15, 7, 3)
EARLY_0, LATE_0 = (8, 9, 10, 4, 1), (11, 12, 13, 14, 15, 5, 6, 7, 2, 3, 0)
EARLY_1, LATE_1 = (8, 9, 10, 4, 1), (11, 12, 13, 14, 15, 5, 6, 7, 2, 3, 0)


def traded(src_ref, dst_ref, send_sem, recv_sem, keep_sem, roles=ROLES):
    chips = all_chips()
    me = chips[0]
    copies = []
    for role in roles:
        if role:
            copies.append(
                send(
                    src_ref.at[chips[role]], dst_ref.at[me], send_sem.at[role], recv_sem.at[role],
                    {"shard": chips[role]},
                )
            )
        else:
            copies.append(pltpu.make_async_copy(src_ref.at[me], dst_ref.at[me], keep_sem))
    return copies


def trade_all(*exchanges):
    copies = []
    for far in (True, False):
        for exchange in exchanges:
            roles = tuple(role for role in exchange[5] if (role >= 8) == far)
            copies += trade(*exchange[:5], roles)
    return copies


def trade(src_ref, dst_ref, send_sem, recv_sem, keep_sem, roles=ROLES):
    copies = traded(src_ref, dst_ref, send_sem, recv_sem, keep_sem, roles)
    for copy in copies:
        copy.start()
    return copies


def head_kernel(
    experts, capacity, qkv_ref, proj_ref, seg_ref, pad_ref, route_ref, tok_ref, cot_ref,
    centroid_ref, gains_ref,
    out_save_ref, full_save_ref, h0_save_ref, h1_save_ref, all_ref, target_ref, column_ref, centre_ref,
    in0_ref, in1_ref,
    take_ref, saved0_ref, lse0_ref, x10_ref, attended0_ref, saved1_ref, lse1_ref, x11_ref,
    attended1_ref, sent_ref, given_ref,
    hub_ref, w_ref, x_ref, g_ref, label_ref, slots_ref, out_ref, full_ref, h0_ref, h1_ref,
    col_ref, heads_ref, o_ref, first_ref, x1_ref, joined0_ref, joined1_ref, h2_ref,
    send_sem, recv_sem, swap_send, swap_recv, sems, post_sems,
):
    size = w_ref.shape[0]
    half = full_ref.shape[1] // 2
    wide = w_ref.shape[1] - half
    count = label_ref.shape[1]
    me, first, second, far, line = places()
    core = lax.axis_index("ctx")
    own = pl.multiple_of(core * half, 128)
    loads = [
        pltpu.make_async_copy(
            qkv_ref.at[:, pl.ds(2 * at * half + own, half)],
            w_ref.at[:, at * half : (at + 1) * half],
            sems.at[at],
        )
        for at in range(3)
    ]
    loads += [
        pltpu.make_async_copy(proj_ref.at[:, pl.ds(own, half)], w_ref.at[:, wide:], sems.at[3]),
        pltpu.make_async_copy(cot_ref, g_ref, sems.at[4]),
        pltpu.make_async_copy(tok_ref, x_ref, sems.at[5]),
    ]
    for load in loads:
        load.start()
    gain_ref, gain_two_ref = gains_ref.at[0:1, :], gains_ref.at[1:2, :]
    label_ref[...] = jnp.zeros_like(label_ref)
    names = [
        pltpu.make_async_copy(
            ref.at[micro], label_ref.at[MICRO * at + micro : MICRO * at + micro + 1, :],
            sems.at[16 + MICRO * at + micro],
        )
        for at, ref in enumerate((seg_ref, pad_ref, route_ref))
        for micro in range(MICRO)
    ]
    names.append(pltpu.make_async_copy(centroid_ref, hub_ref, sems.at[15]))
    for name in names:
        name.start()
    twin = {"ctx": 1 - core}
    lines = [4 * z for z in line]
    y, x = (me // 2) % 2, me % 2
    turns = [me % 4, me % 4 + 1 - 2 * x, me % 4 + 2 - 4 * y, 3 - me % 4]

    def rows(block):
        return out_ref.at[pl.ds(pl.multiple_of(block * size, 16), size), :]

    chips = [lines[j] + turns[i] for j in range(4) for i in range(4)]
    peers = [{"shard": chips[4 * j]} for j in (1, 2, 3)]
    one, two = {"shard": first}, {"shard": second}
    greet([{"shard": chip} for chip in chips[1:]] + [twin])
    copies, share = [], []

    def push(block, role, peer, src=None):
        copy = send(
            rows(block) if src is None else src, rows(block), send_sem.at[role], recv_sem.at[role], peer
        )
        copy.start()
        copies.append(copy)

    def arrive(block, role):
        send(rows(block), rows(block), send_sem.at[0], recv_sem.at[role], one).wait_recv()

    for load in loads[:4]:
        load.wait()
    push(me, 3, one, w_ref)
    push(me, 7, two, w_ref)
    for j in (1, 2, 3):
        push(me, j - 1, peers[j - 1], w_ref)
    out_ref[pl.ds(pl.multiple_of(me * size, 16), size), :] = w_ref[...]
    for name in names:
        name.wait()
    mine = pl.ds(pl.multiple_of(core * count, 128), count)
    share.append(send(label_ref, all_ref.at[:, mine], send_sem.at[15], recv_sem.at[15], twin))
    share[0].start()
    all_ref[:, mine] = label_ref[...]

    before = lax.broadcasted_iota(jnp.int32, (count, count), 0)
    after = lax.broadcasted_iota(jnp.int32, (count, count), 1)
    upto = (before <= after).astype(F32).astype(BF)
    ids = lax.broadcasted_iota(jnp.int32, (experts, count), 0)
    target_ref[...] = jnp.zeros_like(target_ref)
    for micro in range(MICRO):
        route = label_ref[2 * MICRO + micro : 2 * MICRO + micro + 1, :]
        chosen = (ids == route).astype(F32)
        rank = jnp.sum(nn(chosen.astype(BF), upto) * chosen, axis=0, keepdims=True)
        target_ref[micro : micro + 1, :] = route * capacity + rank.astype(jnp.int32) - 1
    wide_target = jnp.concatenate(
        [target_ref[...].astype(F32), jnp.zeros((120, count), F32)], axis=0
    )
    column_ref[...] = jnp.transpose(wide_target)[:, 0:8].astype(jnp.int32)
    row = lax.broadcasted_iota(jnp.int32, (experts, D), 0)
    centre_ref[...] = jnp.sum(
        jnp.where(row == me, hub_ref[...].astype(F32), 0.0), axis=0, keepdims=True
    )

    def place(micro, group):
        slot = lax.broadcasted_iota(jnp.int32, (4 * capacity, count), 0) + group * capacity
        pick = (slot == target_ref[micro : micro + 1, :]).astype(F32).astype(BF)
        value = nn(pick, g_ref[micro * count : (micro + 1) * count, :]).astype(BF)
        slots_ref[micro, pl.ds(pl.multiple_of(group, 4), 4)] = value.reshape(4, capacity, D)

    swaps = []

    def pass_one(micro, role):
        copy = send(
            slots_ref.at[micro, chips[role]],
            (in1_ref if micro else in0_ref).at[me],
            swap_send.at[16 * micro + role],
            swap_recv.at[16 * micro + role],
            {"shard": chips[role]},
        )
        copy.start()
        swaps.append(copy)

    def pass_on(micro, j):
        for i in range(4):
            if 4 * j + i:
                pass_one(micro, 4 * j + i)

    loads[4].wait()
    place(0, lines[2])
    pass_on(0, 2)

    def normed(micro, h_ref):
        def norm(block, carry):
            off = pl.multiple_of(block * RB, RB)
            unit = normal(x_ref[pl.ds(micro * count + off, RB), :].astype(F32))[0]
            at = pl.ds(pl.multiple_of(core * count + off, RB), RB)
            h_ref[at, :] = (unit * gain_ref[...]).astype(BF)
            return carry

        lax.fori_loop(0, count // RB, norm, 0)
        copy = send(
            h_ref.at[mine, :], h_ref.at[mine, :], send_sem.at[16 + micro], recv_sem.at[16 + micro], twin
        )
        copy.start()
        share.append(copy)

    arrive(lines[0] + first % 4, 3)
    push(lines[0] + first % 4, 11, two)
    block = lines[1] + me % 4
    arrive(block, 0)
    push(block, 4, one)
    push(block, 8, two)
    place(0, lines[3])
    pass_on(0, 3)
    loads[5].wait()
    normed(0, h0_ref)
    for j in (2, 3):
        block = lines[j] + me % 4
        arrive(block, j - 1)
        push(block, 3 + j, one)
        push(block, 7 + j, two)
        block = lines[j - 1] + first % 4
        arrive(block, 3 + j - 1)
        push(block, 11 + j - 1, two)
        if j == 2:
            place(0, lines[1])
            pass_on(0, 1)
    block = lines[3] + first % 4
    arrive(block, 6)
    push(block, 14, two)
    place(0, lines[0])
    pass_on(0, 0)
    normed(1, h1_ref)
    for group in range(0, experts, 4):
        place(1, group)
    saves = [
        pltpu.make_async_copy(slots_ref.at[0, me], in0_ref.at[me], sems.at[6]),
        pltpu.make_async_copy(slots_ref.at[1, me], in1_ref.at[me], sems.at[7]),
    ]
    for j in range(4):
        arrive(lines[j] + second % 4, 7 + j)
        arrive(lines[j] + far % 4, 11 + j)
    for role in EARLY_G:
        if role:
            pass_one(1, role)
    side = pl.ds(pl.multiple_of(core * half, 128), half)
    joint = send(
        out_ref.at[:, wide : wide + half], full_ref.at[:, side], send_sem.at[18], recv_sem.at[18], twin
    )
    joint.start()
    full_ref[:, side] = out_ref[:, wide : wide + half]
    for copy in share:
        copy.wait()
    saves += [
        pltpu.make_async_copy(out_ref, out_save_ref, sems.at[8]),
        pltpu.make_async_copy(h0_ref, h0_save_ref, sems.at[9]),
        pltpu.make_async_copy(h1_ref, h1_save_ref, sems.at[10]),
        pltpu.make_async_copy(slots_ref.at[1], given_ref, sems.at[22]),
        pltpu.make_async_copy(full_ref, full_save_ref, sems.at[11]),
    ]
    for save in saves[:-1]:
        save.start()
    attend_kernel(
        0, h0_ref, out_ref, all_ref, saved0_ref, o_ref, lse0_ref, col_ref, heads_ref, sems.at[12]
    )
    joint.wait()
    saves[-1].start()
    groups = [lines[j] for j in (2, 3, 1, 0)]
    steps = iter((2, 3, 1, 0))

    def hand_on(group):
        j = next(steps)
        for i in range(4):
            role = 4 * j + i
            if role:
                copy = send(
                    first_ref.at[0, chips[role]],
                    take_ref.at[me],
                    swap_send.at[32 + role],
                    swap_recv.at[32 + role],
                    {"shard": chips[role]},
                )
            else:
                copy = pltpu.make_async_copy(first_ref.at[0, me], take_ref.at[me], sems.at[13])
            copy.start()
            swaps.append(copy)

    post_stage(
        0, capacity, groups, x_ref, o_ref, full_ref, gain_two_ref, target_ref, hand_on, x10_ref,
        attended0_ref, first_ref.at[0], x1_ref, joined0_ref, h2_ref, post_sems,
        send_sem.at[19], recv_sem.at[19],
    )
    attend_kernel(
        1, h1_ref, out_ref, all_ref, saved1_ref, o_ref, lse1_ref, col_ref, heads_ref, sems.at[12]
    )
    post_stage(
        1, capacity, groups, x_ref, o_ref, full_ref, gain_two_ref, target_ref, lambda group: None,
        x11_ref, attended1_ref, first_ref.at[1], x1_ref, joined1_ref, h2_ref, post_sems,
        send_sem.at[20], recv_sem.at[20],
    )
    saves.append(pltpu.make_async_copy(first_ref.at[1], sent_ref, sems.at[14]))
    saves[-1].start()
    for copy in copies:
        copy.wait_send()
    for save in saves:
        save.wait()
    for copy in swaps:
        copy.wait()


def head(experts, capacity, qkv_weight, out_weight, seg, pad, route, x, g, centroids, gains):
    size, columns = qkv_weight.shape[0], 2 * D
    count = seg.shape[2]
    half = D // 2
    in_hbm = lambda array: pltpu.with_memory_space_constraint(array, pltpu.HBM)
    return pl.pallas_call(
        functools.partial(head_kernel, experts, capacity),
        out_shape=(
            pltpu.HBM((16 * size, columns), BF),
            pltpu.HBM((16 * size, D), BF),
            pltpu.HBM((2 * count, D), BF),
            pltpu.HBM((2 * count, D), BF),
            jax.ShapeDtypeStruct((8, 2 * count), jnp.int32),
            jax.ShapeDtypeStruct((8, count), jnp.int32),
            jax.ShapeDtypeStruct((count, 8), jnp.int32),
            jax.ShapeDtypeStruct((1, D), F32),
            pltpu.HBM((experts, capacity, D), BF),
            pltpu.HBM((experts, capacity, D), BF),
            pltpu.HBM((experts, capacity, D), BF),
        )
        + (
            pltpu.HBM((2 * count, 3 * half), BF),
            jax.ShapeDtypeStruct((8, 2 * count), F32),
            pltpu.HBM((count, D), F32),
            pltpu.HBM((count, D), BF),
        )
        * 2
        + (pltpu.HBM((experts, capacity, D), BF),) * 2,
        in_specs=[HBM_WHOLE] * 8 + [VMEM_WHOLE],
        out_specs=(HBM_WHOLE,) * 4
        + (VMEM_WHOLE,) * 4
        + (HBM_WHOLE,) * 3
        + (HBM_WHOLE, VMEM_WHOLE, HBM_WHOLE, HBM_WHOLE) * 2
        + (HBM_WHOLE,) * 2,
        scratch_shapes=[
            pltpu.VMEM((experts, D), BF),
            pltpu.VMEM((size, columns), BF),
            pltpu.VMEM((MICRO * count, D), BF),
            pltpu.VMEM((MICRO * count, D), BF),
            pltpu.VMEM((8, count), jnp.int32),
            pltpu.VMEM((MICRO, experts, capacity, D), BF),
            pltpu.VMEM((16 * size, columns), BF),
            pltpu.VMEM((16 * size, D), BF),
            pltpu.VMEM((2 * count, D), BF),
            pltpu.VMEM((2 * count, D), BF),
            pltpu.VMEM((2 * count, 1), F32),
            pltpu.VMEM((2 * count, 3 * half), BF),
            pltpu.VMEM((2 * count, half), BF),
            pltpu.VMEM((MICRO, experts, capacity, D), BF),
            pltpu.VMEM((count, D), F32),
            pltpu.VMEM((count, D), BF),
            pltpu.VMEM((count, D), BF),
            pltpu.VMEM((count, D), BF),
            pltpu.SemaphoreType.DMA((21,)),
            pltpu.SemaphoreType.DMA((21,)),
            pltpu.SemaphoreType.DMA((48,)),
            pltpu.SemaphoreType.DMA((48,)),
            pltpu.SemaphoreType.DMA((23,)),
            pltpu.SemaphoreType.DMA((2,)),
        ],
        compiler_params=pltpu.CompilerParams(
            collective_id=0, has_side_effects=True, vmem_limit_bytes=52 << 20
        ),
        cost_estimate=pl.CostEstimate(flops=0, bytes_accessed=100 << 20, transcendentals=0),
        name="head",
    )(
        in_hbm(qkv_weight), in_hbm(out_weight), in_hbm(seg), in_hbm(pad), in_hbm(route), in_hbm(x),
        in_hbm(g), in_hbm(centroids), gains,
    )


def scatter_stage(
    packed_ref, gqkv_ref, gout_ref, gsmall_ref,
    theirs_ref, rx1_ref, rx2_ref, rx3_ref, tx1_ref, tx2_ref, sum_ref, send_sem, recv_sem, between,
):
    me, first, second, far, line = places()
    core = lax.axis_index("ctx")
    lines = [4 * z for z in line]
    part = sum_ref.shape[0] // 2
    half = gout_ref.shape[1] // 2
    wide = 3 * half
    peers = [{"shard": lines[j] + me % 4} for j in (1, 2, 3)]
    one, two, twin = {"shard": first}, {"shard": second}, {"ctx": 1 - core}
    order = (3, 2, 1, 0)
    copies = []

    def push(src, dst, role, peer):
        copy = send(src, dst, send_sem.at[role], recv_sem.at[role], peer)
        copy.start()
        copies.append(copy)

    def arrive(dst, role):
        send(dst, dst, send_sem.at[role], recv_sem.at[role], one).wait_recv()

    for j in order:
        push(packed_ref.at[lines[j] + far % 4], rx1_ref.at[j], j, two)
    for j in order:
        push(packed_ref.at[lines[j] + second % 4], rx1_ref.at[4 + j], 4 + j, two)
    for j in order:
        arrive(rx1_ref.at[j], j)
        total = packed_ref[lines[j] + first % 4].astype(F32) + rx1_ref[j].astype(F32)
        tx1_ref[j] = total.astype(BF)
        push(tx1_ref.at[j], rx2_ref.at[j], 8 + j, one)
    between()
    own = None
    for j in order:
        arrive(rx1_ref.at[4 + j], 4 + j)
        total = packed_ref[lines[j] + me % 4].astype(F32) + rx1_ref[4 + j].astype(F32)
        arrive(rx2_ref.at[j], 8 + j)
        total = total + rx2_ref[j].astype(F32)
        if j:
            tx2_ref[j - 1] = total.astype(BF)
            push(tx2_ref.at[j - 1], rx3_ref.at[j - 1], 11 + j, peers[j - 1])
        else:
            own = total
    for j in (1, 2, 3):
        arrive(rx3_ref.at[j - 1], 11 + j)
        own = own + rx3_ref[j - 1].astype(F32)
    sum_ref[...] = own
    push(
        sum_ref.at[pl.ds(pl.multiple_of((1 - core) * part, 8), part), :], theirs_ref, 15, twin
    )
    arrive(theirs_ref, 15)
    mine, theirs = sum_ref[pl.ds(pl.multiple_of(core * part, 8), part), :], theirs_ref[...]
    low = jnp.where(core == 0, mine, theirs)
    high = jnp.where(core == 0, theirs, mine)
    for at in range(3):
        gqkv_ref[:, 2 * at * half : (2 * at + 1) * half] = low[:, at * half : (at + 1) * half]
        gqkv_ref[:, (2 * at + 1) * half : (2 * at + 2) * half] = high[:, at * half : (at + 1) * half]
    gout_ref[:, 0:half] = low[:, wide : wide + half]
    gout_ref[:, half:] = high[:, wide : wide + half]
    gsmall_ref[...] = mine[:, wide + half :] + theirs[:, wide + half :]
    for copy in copies:
        copy.wait_send()


def normal(values):
    centre = values - jnp.mean(values, axis=1, keepdims=True)
    spread = jnp.mean(centre * centre, axis=1, keepdims=True)
    scale = lax.rsqrt(spread + EPSILON)
    return centre * scale, scale


def normal_back(unit, scale, gain, grad):
    pull = grad * gain
    return scale * (
        pull
        - jnp.mean(pull, axis=1, keepdims=True)
        - unit * jnp.mean(pull * unit, axis=1, keepdims=True)
    )


RB = 256


def post_stage(
    micro, capacity, groups, x_ref, o_ref, wo_ref, gain_ref, target_ref, hand_on, x1_out_ref, full_out_ref,
    slots_ref, x1_ref, full_ref, h_ref, sems, send_sem, recv_sem,
):
    core = lax.axis_index("ctx")
    rows, width = x1_ref.shape[0], o_ref.shape[1]
    twin = {"ctx": 1 - core}
    mine = pl.ds(pl.multiple_of(core * width, 128), width)
    copy = send(
        o_ref.at[pl.ds(pl.multiple_of((1 - core) * rows, 128), rows), :],
        full_ref.at[:, mine],
        send_sem,
        recv_sem,
        twin,
    )
    copy.start()
    full_ref[:, mine] = o_ref[pl.ds(pl.multiple_of(core * rows, 128), rows), :]
    copy.wait()

    def norm(block, carry):
        at = pl.ds(pl.multiple_of(block * RB, RB), RB)
        value = x_ref[pl.ds(micro * rows + pl.multiple_of(block * RB, RB), RB), :].astype(F32)
        value = value + nn(full_ref[at, :], wo_ref[...])
        x1_ref[at, :] = value
        h_ref[at, :] = (normal(value)[0] * gain_ref[...]).astype(BF)
        return carry

    lax.fori_loop(0, rows // RB, norm, 0)
    saves = [
        pltpu.make_async_copy(full_ref, full_out_ref, sems.at[0]),
        pltpu.make_async_copy(x1_ref, x1_out_ref, sems.at[1]),
    ]
    for save in saves:
        save.start()
    for group in groups:
        slot = lax.broadcasted_iota(jnp.int32, (4 * capacity, rows), 0) + group * capacity
        pick = (slot == target_ref[micro : micro + 1, :]).astype(F32).astype(BF)
        value = nn(pick, h_ref[...]).astype(BF).reshape(4, capacity, D)
        slots_ref[pl.ds(pl.multiple_of(group, 4), 4)] = value
        hand_on(group)
    for save in saves:
        save.wait()


def fore_stage(
    has_prev, micro, dh_ref, target_ref, g_ref, x1_ref, gain_ref, wo_ref, full_ref, prev_two_ref,
    do_ref, dx_ref, gout_ref, gtwo_ref, dy_ref, all_ref, send_sem, recv_sem,
):
    core = lax.axis_index("ctx")
    rows, width = x1_ref.shape[0], do_ref.shape[1]
    slots = dh_ref.shape[0] * dh_ref.shape[1]
    twin = {"ctx": 1 - core}

    def norm(block, total):
        at = pl.ds(pl.multiple_of(block * RB, RB), RB)
        slot = lax.broadcasted_iota(jnp.int32, (RB, slots), 1)
        pick = (slot == target_ref[at, micro : micro + 1]).astype(F32).astype(BF)
        grad = nn(pick, dh_ref[...].reshape(slots, D))
        unit, scale = normal(x1_ref[at, :])
        dx = g_ref[at, :].astype(F32) + normal_back(unit, scale, gain_ref[...], grad)
        dx_ref[at, :] = dx
        dy = dx.astype(BF)
        dy_ref[at, :] = dy
        all_ref[at, :] = nt(dy, wo_ref[...]).astype(BF)
        return total + jnp.sum(grad * unit, axis=0, keepdims=True)

    total = lax.fori_loop(0, rows // RB, norm, jnp.zeros((1, D), F32))
    gtwo_ref[...] = prev_two_ref[...] + total if has_prev else total
    mine = pl.ds(pl.multiple_of(core * rows, 128), rows)
    copy = send(
        all_ref.at[:, pl.ds(pl.multiple_of((1 - core) * width, 128), width)],
        do_ref.at[mine, :],
        send_sem,
        recv_sem,
        twin,
    )
    copy.start()
    do_ref[mine, :] = all_ref[:, pl.ds(pl.multiple_of(core * width, 128), width)]
    grad = tn(full_ref[...], dy_ref[...])
    gout_ref[...] = gout_ref[...] + grad if has_prev else grad
    copy.wait()


def tail_stage(
    has_prev, dh_ref, x_ref, dx_ref, gain_ref, prev_ref, grad_out_ref, gone_ref, grad_ref, rx_ref, sems
):
    core = lax.axis_index("ctx")
    rows = dx_ref.shape[0]
    saves = []
    total = jnp.zeros((1, D), F32)
    for off in range(0, rows, RB):
        at = slice(off, off + RB)
        mine = pl.ds(pl.multiple_of(core * rows + off, RB), RB)
        grad = dh_ref[mine, :] + rx_ref[at, :].astype(F32)
        unit, scale = normal(x_ref[at, :].astype(F32))
        grad_ref[at, :] = dx_ref[at, :] + normal_back(unit, scale, gain_ref[...], grad)
        save = pltpu.make_async_copy(grad_ref.at[at, :], grad_out_ref.at[at, :], sems.at[off // RB])
        save.start()
        saves.append(save)
        total = total + jnp.sum(grad * unit, axis=0, keepdims=True)
    gone_ref[...] = prev_ref[...] + total if has_prev else total
    return saves


def back_kernel(
    slot_ref, target_ref, cot_ref, tok_ref, w_in_ref, wo_in_ref, label_ref, gains_ref, gc0_ref, gc1_ref,
    x10_ref, full0_ref, h0_ref, qkv0_ref, lse0_ref, x11_ref, full1_ref, h1_ref, qkv1_ref, lse1_ref,
    give_dh_ref, give_y0_ref, give_y1_ref,
    gqkv_ref, gproj_ref, gsmall_ref, in0_ref, in1_ref, take_dh_ref, take_y0_ref, take_y1_ref,
    dh_ref, g_ref, x_ref, x1_ref, full_ref, h_ref, w_ref, wo_ref, qkv_ref,
    do_ref, dx_ref, dy_ref, all_ref, part_ref, dqkv_ref, dk_ref, dv_ref, kt_ref, col_ref,
    tx_ref, rx_ref, go_ref, tgo_ref, rgo_ref, gw_ref, gout_ref, gtwo_ref, gone_ref, packed_ref, small_ref,
    theirs_ref, rx1_ref, rx2_ref, rx3_ref, tx1_ref, tx2_ref, sum_ref,
    sems, save_sems, dh_send, dh_recv, y0_send, y0_recv, y1_send, y1_recv, send_sem, recv_sem,
    ring_send, ring_recv,
):
    me, core = lax.axis_index("shard"), lax.axis_index("ctx")
    rows = x_ref.shape[0]
    half = gout_ref.shape[1]
    twin = {"ctx": 1 - core}
    gain_one_ref, gain_two_ref = gains_ref.at[0:1, :], gains_ref.at[1:2, :]
    sources = (
        (x10_ref, full0_ref, h0_ref, qkv0_ref, lse0_ref, in0_ref),
        (x11_ref, full1_ref, h1_ref, qkv1_ref, lse1_ref, in1_ref),
    )

    def loads_of(micro):
        x1_in_ref, full_in_ref, h_in_ref, qkv_in_ref = sources[micro][:4]
        mine = pl.ds(micro * rows, rows)
        pairs = dict(
            dh=((slot_ref, take_dh_ref)[micro], dh_ref),
            x1=(x1_in_ref, x1_ref),
            g=(cot_ref.at[mine, :], g_ref),
            full=(full_in_ref, full_ref),
            qkv=(qkv_in_ref, qkv_ref),
            h=(h_in_ref, h_ref),
            x=(tok_ref.at[mine, :], x_ref),
        )
        return {
            name: pltpu.make_async_copy(src, dst, sems.at[8 * micro + at])
            for at, (name, (src, dst)) in enumerate(pairs.items())
        }

    loads = [loads_of(0), loads_of(1)]
    shared = [
        pltpu.make_async_copy(wo_in_ref, wo_ref, sems.at[16]),
        pltpu.make_async_copy(w_in_ref, w_ref, sems.at[17]),
    ]
    for name in ("dh", "x1", "g", "full"):
        loads[0][name].start()
    shared[0].start()
    for name in ("qkv", "h", "x"):
        loads[0][name].start()
    shared[1].start()
    greet([{"shard": chip} for chip in all_chips()[1:]] + [twin])
    first_trade = trade(give_dh_ref, take_dh_ref, dh_send, dh_recv, sems.at[18])
    swaps = trade_all(
        (give_y0_ref, take_y0_ref, y0_send, y0_recv, sems.at[19], LATE_0),
        (give_y1_ref, take_y1_ref, y1_send, y1_recv, sems.at[20], EARLY_1),
    )
    for micro in range(MICRO):
        has_prev = micro > 0
        load, lse_ref, grad_out_ref = loads[micro], sources[micro][4], sources[micro][5]
        for name in ("dh", "x1", "g", "full"):
            load[name].wait()
        if not has_prev:
            shared[0].wait()
        fore_stage(
            has_prev, micro, dh_ref, target_ref, g_ref, x1_ref, gain_two_ref, wo_ref, full_ref, gtwo_ref,
            do_ref, dx_ref, go_ref, gtwo_ref, dy_ref, all_ref, send_sem.at[3 * micro],
            recv_sem.at[3 * micro],
        )
        if has_prev:
            tgo_ref[...] = go_ref[:, pl.ds(pl.multiple_of((1 - core) * half, 128), half)].astype(BF)
            cross = send(tgo_ref, rgo_ref, send_sem.at[6], recv_sem.at[6], twin)
            cross.start()
        else:
            loads[1]["g"].start()
            loads[1]["full"].start()
            shared[1].wait()
        load["qkv"].wait()
        load["h"].wait()
        attend_back_kernel(
            micro, h_ref, w_ref, qkv_ref, do_ref, lse_ref, label_ref, part_ref, dqkv_ref, dk_ref, dv_ref,
            kt_ref, col_ref,
        )
        tx_ref[...] = part_ref[pl.ds(pl.multiple_of((1 - core) * rows, 128), rows), :].astype(BF)
        joint = send(tx_ref, rx_ref, send_sem.at[3 * micro + 1], recv_sem.at[3 * micro + 1], twin)
        joint.start()
        if not has_prev:
            loads[1]["qkv"].start()
        for at in range(0, dqkv_ref.shape[1], 384):
            grad = tn(h_ref[...], dqkv_ref[:, at : at + 384])
            gw_ref[:, at : at + 384] = gw_ref[:, at : at + 384] + grad if has_prev else grad
        if not has_prev:
            loads[1]["h"].start()
        load["x"].wait()
        joint.wait()
        saves = tail_stage(
            has_prev, part_ref, x_ref, dx_ref, gain_one_ref, gone_ref, grad_out_ref, gone_ref,
            x1_ref, rx_ref, save_sems.at[pl.ds(micro * (rows // RB), rows // RB)],
        )
        if not has_prev:
            loads[1]["x"].start()
            for copy in saves:
                copy.wait()
            loads[1]["x1"].start()
            for copy in first_trade:
                copy.wait()
            loads[1]["dh"].start()
    cross.wait()
    own = go_ref[:, pl.ds(pl.multiple_of(core * half, 128), half)]
    gout_ref[...] = own + rgo_ref[...].astype(F32)
    row = lax.broadcasted_iota(jnp.int32, (128, D), 0)
    small = jnp.where(row == 0, gone_ref[...], 0.0) + jnp.where(row == 1, gtwo_ref[...], 0.0)
    small = small + jnp.where(row == 2 + me, gc0_ref[...] + gc1_ref[...], 0.0)
    small_ref[...] = jnp.transpose(small)
    part = packed_ref.shape[1] // 2

    def pack(chunk, carry):
        top = pl.ds(pl.multiple_of(chunk * part, 8), part)
        low = pl.ds(pl.multiple_of(D // 2 + chunk * part, 8), part)
        for ref, at, size in ((gw_ref, 0, 3 * half), (gout_ref, 3 * half, half), (small_ref, 4 * half, 128)):
            both = jnp.concatenate([ref[top, :], ref[low, :]], axis=0)
            packed_ref[chunk, :, at : at + size] = both.astype(BF)
        return carry

    lax.fori_loop(0, packed_ref.shape[0], pack, 0)

    def between():
        swaps.extend(trade(give_y1_ref, take_y1_ref, y1_send, y1_recv, sems.at[20], LATE_1))

    scatter_stage(
        packed_ref, gqkv_ref, gproj_ref, gsmall_ref, theirs_ref, rx1_ref, rx2_ref, rx3_ref, tx1_ref,
        tx2_ref, sum_ref, ring_send, ring_recv, between,
    )
    for copy in saves + swaps:
        copy.wait()


def back(dh, target, g, x, w_all, wo, labels, gains, gc0, gc1, kept0, kept1, dh1, y0, y1):
    x1, _, h_all, _, _ = kept0
    rows, seq, half = x1.shape[0], h_all.shape[0], D // 2
    groups = dh.shape[0]
    chunk = (2 * D // (2 * groups), 4 * half + 128)
    part = chunk[0] // 2
    in_hbm = lambda array: pltpu.with_memory_space_constraint(array, pltpu.HBM)
    kept = lambda arrays: [in_hbm(array) for array in arrays[:4]] + [arrays[4]]
    args = [in_hbm(dh), target, in_hbm(g), in_hbm(x), in_hbm(w_all), in_hbm(wo), labels, gains, gc0, gc1]
    args += kept(kept0) + kept(kept1) + [in_hbm(array) for array in (dh1, y0, y1)]
    kept_specs = [HBM_WHOLE] * 4 + [VMEM_WHOLE]
    return pl.pallas_call(
        back_kernel,
        out_shape=(
            jax.ShapeDtypeStruct((part, 3 * D), F32),
            jax.ShapeDtypeStruct((part, D), F32),
            jax.ShapeDtypeStruct((part, 128), F32),
            pltpu.HBM((rows, D), F32),
            pltpu.HBM((rows, D), F32),
            pltpu.HBM(dh.shape, BF),
            pltpu.HBM(dh.shape, BF),
            pltpu.HBM(dh.shape, BF),
        ),
        in_specs=[HBM_WHOLE, VMEM_WHOLE]
        + [HBM_WHOLE] * 4
        + [VMEM_WHOLE] * 4
        + kept_specs * 2
        + [HBM_WHOLE] * 3,
        out_specs=(VMEM_WHOLE,) * 3 + (HBM_WHOLE,) * 5,
        scratch_shapes=[
            pltpu.VMEM(dh.shape, BF),
            pltpu.VMEM((rows, D), BF),
            pltpu.VMEM((rows, D), BF),
            pltpu.VMEM((rows, D), F32),
            pltpu.VMEM((rows, D), BF),
            pltpu.VMEM((seq, D), BF),
            pltpu.VMEM((D, 2 * D), BF),
            pltpu.VMEM((D, D), BF),
            pltpu.VMEM((seq, 3 * half), BF),
            pltpu.VMEM((seq, half), BF),
            pltpu.VMEM((rows, D), F32),
            pltpu.VMEM((rows, D), BF),
            pltpu.VMEM((rows, D), BF),
            pltpu.VMEM((seq, D), F32),
            pltpu.VMEM((seq, 3 * half), BF),
            pltpu.VMEM((seq, half), F32),
            pltpu.VMEM((seq, half), F32),
            pltpu.VMEM((half, seq), BF),
            pltpu.VMEM((seq, 1), F32),
            pltpu.VMEM((rows, D), BF),
            pltpu.VMEM((rows, D), BF),
            pltpu.VMEM((D, D), F32),
            pltpu.VMEM((D, half), BF),
            pltpu.VMEM((D, half), BF),
            pltpu.VMEM((D, 3 * half), F32),
            pltpu.VMEM((D, half), F32),
            pltpu.VMEM((1, D), F32),
            pltpu.VMEM((1, D), F32),
            pltpu.VMEM((groups,) + chunk, BF),
            pltpu.VMEM((D, 128), F32),
            pltpu.VMEM((part, chunk[1]), F32),
            pltpu.VMEM((8,) + chunk, BF),
            pltpu.VMEM((4,) + chunk, BF),
            pltpu.VMEM((3,) + chunk, BF),
            pltpu.VMEM((4,) + chunk, BF),
            pltpu.VMEM((3,) + chunk, BF),
            pltpu.VMEM(chunk, F32),
            pltpu.SemaphoreType.DMA((21,)),
            pltpu.SemaphoreType.DMA((MICRO * (rows // RB),)),
        ]
        + [pltpu.SemaphoreType.DMA((16,))] * 6
        + [pltpu.SemaphoreType.DMA((7,))] * 2
        + [pltpu.SemaphoreType.DMA((16,))] * 2,
        compiler_params=pltpu.CompilerParams(
            collective_id=1, has_side_effects=True, vmem_limit_bytes=60 << 20
        ),
        cost_estimate=pl.CostEstimate(flops=4 << 33, bytes_accessed=60 << 20, transcendentals=0),
        name="back",
    )(*args)


def body_pair(
    tokens,
    cotangent,
    segment_ids,
    padding,
    routes,
    norm_one_gain,
    qkv_weight,
    out_weight,
    norm_two_gain,
    centroids,
    expert_in,
    expert_out,
):
    local_len = tokens.shape[2]
    experts = centroids.shape[1]
    capacity = max(2, 2 * local_len // experts)
    gains = jnp.stack([norm_one_gain, norm_two_gain]).astype(F32)
    x_all = tokens.reshape(MICRO * local_len, D)
    g_all = cotangent.reshape(MICRO * local_len, D)
    (w_all, out_full, h0, h1, labels, _, columns, centre, g0_in, g1_part, h0_in,
     qkv0, lse0, x10, full0, qkv1, lse1, x11, full1, sent1, g1_sent) = head(
        experts, capacity, qkv_weight, out_weight, segment_ids, padding,
        routes.reshape(MICRO, 1, local_len), x_all, g_all, centroids.T, gains
    )
    y0, dh0, gc0, gup, gdown, h1_in, g1_in = expert(
        h0_in, g0_in, centre, expert_in[0], expert_out[0], (sent1, g1_sent, g1_part), None
    )
    y1, dh1, gc1, gup, gdown, dh0_in, y0a = expert(
        h1_in, g1_in, centre, expert_in[0], expert_out[0], (dh0, y0), (gup, gdown)
    )
    grad_up = lax.psum_scatter(gup, "ctx", scatter_dimension=1, tiled=True)
    grad_down = lax.psum_scatter(gdown, "ctx", scatter_dimension=0, tiled=True)
    grad_qkv, grad_out, small, in0, in1, _, y0b, y1_in = back(
        dh0_in, columns, g_all, x_all, w_all, out_full, labels, gains, gc0, gc1,
        (x10, full0, h0, qkv0, lse0), (x11, full1, h1, qkv1, lse1), dh1, y0, y1,
    )
    block_out, grad_tokens = emit(x10, x11, y0a, y0b, y1_in, columns, in0, in1)

    return (
        block_out.reshape(MICRO, 1, local_len, D),
        grad_tokens.reshape(MICRO, 1, local_len, D),
        small[:, 0],
        grad_qkv,
        grad_out,
        small[:, 1],
        small[:, 2 : 2 + experts],
        grad_up[None],
        grad_down[None],
    )


def solution(mesh):
    plan = body_pair if (mesh.shape["ctx"], mesh.shape["shard"]) == (2, 16) else body
    in_specs = (
        P(None, "shard", "ctx", None),
        P(None, "shard", "ctx", None),
        P(None, "shard", "ctx"),
        P(None, "shard", "ctx"),
        P(None, "shard", "ctx", None),
        P(),
        P("shard", None),
        P("shard", None),
        P(),
        P(),
        P("shard", None, None),
        P("shard", None, None),
    )
    out_specs = (
        P(None, "shard", "ctx", None),
        P(None, "shard", "ctx", None),
        P(("ctx", "shard")),
        P(("ctx", "shard"), None),
        P(("ctx", "shard"), None),
        P(("ctx", "shard")),
        P(("ctx", "shard"), None),
        P("shard", None, "ctx"),
        P("shard", "ctx", None),
    )
    return jax.shard_map(plan, mesh=mesh, in_specs=in_specs, out_specs=out_specs, check_vma=False)
```

```python
import functools

import jax
import jax.numpy as jnp
from jax import lax
from jax.experimental import pallas as pl
from jax.experimental.pallas import tpu as pltpu
from jax.sharding import PartitionSpec as P

D = 768
HEADS = 12
HEAD_DIM = 64
FF = 3072
MICRO = 2


EPSILON = 1e-05
NEGATIVE = -1e30
HIGH = lax.Precision.HIGHEST


def layer_norm(values, gain_vec):
    centre = values - jnp.mean(values, axis=1, keepdims=True)
    spread = jnp.mean(centre * centre, axis=1, keepdims=True)
    return centre * lax.rsqrt(spread + EPSILON) * gain_vec


def gelu_tanh(values):
    return jax.nn.gelu(values, approximate=True)


def masked_scores(queries, key_heads, query_pos, key_pos, query_doc, key_doc, key_pad):
    scores = jnp.einsum(
        "qhd,khd->hqk", queries, key_heads, preferred_element_type=jnp.float32
    ) * HEAD_DIM ** (-0.5)
    allowed = (query_doc[:, None] == key_doc[None, :]) & (key_pos[None, :] <= query_pos[:, None])
    allowed = allowed & ((key_pad[None, :] == 1) | (key_pos[None, :] == query_pos[:, None]))
    return jnp.where(allowed[None], scores, NEGATIVE)


def rows_first(left, right):
    return lax.dot_general(
        left, right, (((0,), (0,)), ((), ())), preferred_element_type=jnp.float32
    )


def rows_last(left, right):
    return lax.dot_general(
        left, right, (((1,), (1,)), ((), ())), preferred_element_type=jnp.float32
    )


def body(
    tokens,
    cotangent,
    segment_ids,
    padding,
    routes,
    norm_one_gain,
    qkv_weight,
    out_weight,
    norm_two_gain,
    centroids,
    expert_in,
    expert_out,
):
    local_len = tokens.shape[2]
    experts = centroids.shape[1]
    capacity = max(2, 2 * local_len // experts)
    seq_len = local_len * lax.axis_size("ctx")
    qkv_full, out_full = (
        lax.all_gather(qkv_weight, "shard", axis=0, tiled=True),
        lax.all_gather(out_weight, "shard", axis=0, tiled=True),
    )
    gain_one = norm_one_gain.astype(jnp.float32)
    gain_two = norm_two_gain.astype(jnp.float32)
    centre_f = centroids.astype(jnp.float32)
    up_local = expert_in[0]
    down_local = expert_out[0]
    query_pos = lax.axis_index("ctx") * local_len + jnp.arange(local_len, dtype=jnp.int32)
    all_pos = jnp.arange(seq_len, dtype=jnp.int32)
    slot_ids = jnp.arange(experts * capacity, dtype=jnp.int32)
    expert_ids = jnp.arange(experts, dtype=jnp.int32)
    score_scale = HEAD_DIM ** (-0.5)
    grad_qkv_sum = jnp.zeros((D, 3 * D), jnp.float32)
    grad_out_sum = jnp.zeros((D, D), jnp.float32)
    grad_one_sum = jnp.zeros((D,), jnp.float32)
    grad_two_sum = jnp.zeros((D,), jnp.float32)
    grad_centre = jnp.zeros((D, experts), jnp.float32)
    grad_up_sum = jnp.zeros((D, FF), jnp.float32)
    grad_down_sum = jnp.zeros((D, FF), jnp.float32)
    block_list = []
    input_list = []
    for micro_index in range(MICRO):
        inputs = tokens[micro_index, 0].astype(jnp.float32)
        doc_ids = segment_ids[micro_index, 0]
        pad_mask = padding[micro_index, 0]
        route_ids = routes[micro_index, 0, :, 0]
        normed_one, norm_one_back = jax.vjp(layer_norm, inputs, gain_one)
        first_bf = normed_one.astype(jnp.bfloat16)
        qkv = jnp.dot(first_bf, qkv_full, preferred_element_type=jnp.float32)
        queries = qkv[:, :D].astype(jnp.bfloat16)
        key_rows = qkv[:, D : 2 * D].astype(jnp.bfloat16)
        value_rows = qkv[:, 2 * D :].astype(jnp.bfloat16)
        key_all, value_all, doc_all, pad_all = (
            lax.all_gather(key_rows, "ctx", axis=0, tiled=True),
            lax.all_gather(value_rows, "ctx", axis=0, tiled=True),
            lax.all_gather(doc_ids, "ctx", axis=0, tiled=True),
            lax.all_gather(pad_mask, "ctx", axis=0, tiled=True),
        )
        query_heads = queries.reshape(local_len, HEADS, HEAD_DIM)
        key_heads = key_all.reshape(seq_len, HEADS, HEAD_DIM)
        value_heads = value_all.reshape(seq_len, HEADS, HEAD_DIM)
        scores = masked_scores(
            query_heads, key_heads, query_pos, all_pos, doc_ids, doc_all, pad_all
        )
        row_max = jnp.max(scores, axis=2, keepdims=True)
        weights = jnp.exp(scores - row_max)
        row_total = jnp.sum(weights, axis=2, keepdims=True)
        probs_now = weights / row_total
        log_total = row_max + jnp.log(row_total)
        attended = jnp.einsum(
            "hqk,khd->qhd",
            probs_now.astype(jnp.bfloat16),
            value_heads,
            preferred_element_type=jnp.float32,
        )
        attended = attended.reshape(local_len, D).astype(jnp.bfloat16)
        residual = inputs + jnp.dot(attended, out_full, preferred_element_type=jnp.float32)
        normed_two, norm_two_back = jax.vjp(layer_norm, residual, gain_two)
        second_bf = normed_two.astype(jnp.bfloat16)
        choose_mask = route_ids[:, None] == expert_ids[None, :]
        choose_f = choose_mask.astype(jnp.float32)
        logit = jnp.sum(
            jnp.dot(second_bf, centroids, preferred_element_type=jnp.float32) * choose_f, axis=1
        )
        gate_value = jax.nn.sigmoid(logit)
        choose_int = choose_mask.astype(jnp.int32)
        counts = jnp.cumsum(choose_int, axis=0)
        slot_rank = jnp.sum(counts * choose_int, axis=1) - 1
        target = route_ids * capacity + slot_rank
        dispatch = (slot_ids[:, None] == target[None, :]).astype(jnp.bfloat16)
        outbound = jnp.dot(dispatch, second_bf, preferred_element_type=jnp.float32).astype(
            jnp.bfloat16
        )
        outbound = outbound.reshape(experts, capacity, D)
        received = lax.all_to_all(outbound, "shard", split_axis=0, concat_axis=0, tiled=True)
        slot_rows = received.reshape(-1, D)
        upward = jnp.dot(slot_rows, up_local, preferred_element_type=jnp.float32)
        hidden = gelu_tanh(upward).astype(jnp.bfloat16)
        result = jnp.dot(hidden, down_local, preferred_element_type=jnp.float32).astype(
            jnp.bfloat16
        )
        returned = lax.all_to_all(
            result.reshape(received.shape), "shard", split_axis=0, concat_axis=0, tiled=True
        )
        returned, received, upward = (
            returned,
            received,
            upward.reshape(received.shape[0], received.shape[1], FF),
        )
        expert_rows = rows_first(dispatch, returned.reshape(experts * capacity, D))
        block_list.append((residual + gate_value[:, None] * expert_rows).astype(jnp.bfloat16))
        grad_out = cotangent[micro_index, 0].astype(jnp.float32)
        grad_gate = jnp.sum(grad_out * expert_rows, axis=1)
        grad_logit = grad_gate * gate_value * (1.0 - gate_value)
        grad_rows = (gate_value[:, None] * grad_out).astype(jnp.bfloat16)
        grad_outbound = jnp.dot(dispatch, grad_rows, preferred_element_type=jnp.float32).astype(
            jnp.bfloat16
        )
        grad_received = lax.all_to_all(
            grad_outbound.reshape(experts, capacity, D),
            "shard",
            split_axis=0,
            concat_axis=0,
            tiled=True,
        )
        grad_result = grad_received.reshape(-1, D)
        hidden_again, gelu_back = jax.vjp(gelu_tanh, upward.reshape(-1, FF))
        grad_down_sum = grad_down_sum + rows_first(grad_result, hidden_again.astype(jnp.bfloat16))
        grad_hidden = rows_last(grad_result, down_local)
        grad_upward = gelu_back(grad_hidden)[0].astype(jnp.bfloat16)
        grad_up_sum = grad_up_sum + rows_first(received.reshape(-1, D), grad_upward)
        grad_send = (
            rows_last(grad_upward, up_local).astype(jnp.bfloat16).reshape(grad_received.shape)
        )
        grad_back = lax.all_to_all(grad_send, "shard", split_axis=0, concat_axis=0, tiled=True)
        grad_second = rows_first(dispatch, grad_back.reshape(experts * capacity, D))
        grad_second = grad_second + grad_logit[:, None] * jnp.dot(
            choose_f, centre_f.T, precision=HIGH
        )
        grad_centre = grad_centre + jnp.dot(
            second_bf.astype(jnp.float32).T, choose_f * grad_logit[:, None], precision=HIGH
        )
        grad_resid_norm, grad_two_term = norm_two_back(grad_second)
        grad_residual = grad_out + grad_resid_norm
        grad_two_sum = grad_two_sum + grad_two_term
        grad_branch = grad_residual.astype(jnp.bfloat16)
        grad_out_sum = grad_out_sum + rows_first(attended, grad_branch)
        grad_attend = (
            rows_last(grad_branch, out_full)
            .astype(jnp.bfloat16)
            .reshape(local_len, HEADS, HEAD_DIM)
        )
        probs_again = jnp.exp(
            masked_scores(query_heads, key_heads, query_pos, all_pos, doc_ids, doc_all, pad_all)
            - log_total
        )
        grad_probs = jnp.einsum(
            "qhd,khd->hqk", grad_attend, value_heads, preferred_element_type=jnp.float32
        )
        row_terms = jnp.sum(probs_again * grad_probs, axis=2, keepdims=True)
        grad_scores = (probs_again * (grad_probs - row_terms)).astype(jnp.bfloat16)
        grad_query = (
            jnp.einsum("hqk,khd->qhd", grad_scores, key_heads, preferred_element_type=jnp.float32)
            * score_scale
        )
        grad_key_all = (
            jnp.einsum("hqk,qhd->khd", grad_scores, query_heads, preferred_element_type=jnp.float32)
            * score_scale
        )
        grad_value_all = jnp.einsum(
            "hqk,qhd->khd",
            probs_again.astype(jnp.bfloat16),
            grad_attend,
            preferred_element_type=jnp.float32,
        )
        grad_key, grad_value = (
            lax.psum_scatter(
                grad_key_all.reshape(seq_len, D).astype(jnp.bfloat16),
                "ctx",
                scatter_dimension=0,
                tiled=True,
            ).astype(jnp.float32),
            lax.psum_scatter(
                grad_value_all.reshape(seq_len, D).astype(jnp.bfloat16),
                "ctx",
                scatter_dimension=0,
                tiled=True,
            ).astype(jnp.float32),
        )
        grad_qkv_rows = jnp.concatenate(
            [grad_query.reshape(local_len, D), grad_key, grad_value], axis=1
        ).astype(jnp.bfloat16)
        grad_qkv_sum = grad_qkv_sum + rows_first(first_bf, grad_qkv_rows)
        grad_first = rows_last(grad_qkv_rows, qkv_full)
        grad_in_norm, grad_one_term = norm_one_back(grad_first)
        grad_one_sum = grad_one_sum + grad_one_term
        input_list.append(grad_residual + grad_in_norm)
    dense_sums = (
        lax.psum_scatter(grad_one_sum, ("ctx", "shard"), scatter_dimension=0, tiled=True),
        lax.psum_scatter(grad_qkv_sum, ("ctx", "shard"), scatter_dimension=0, tiled=True),
        lax.psum_scatter(grad_out_sum, ("ctx", "shard"), scatter_dimension=0, tiled=True),
        lax.psum_scatter(grad_two_sum, ("ctx", "shard"), scatter_dimension=0, tiled=True),
        lax.psum_scatter(grad_centre, ("ctx", "shard"), scatter_dimension=0, tiled=True),
    )
    expert_sums = (
        lax.psum_scatter(
            grad_up_sum.astype(jnp.bfloat16), "ctx", scatter_dimension=1, tiled=True
        ).astype(jnp.float32),
        lax.psum_scatter(
            grad_down_sum.astype(jnp.bfloat16), "ctx", scatter_dimension=1, tiled=True
        ).astype(jnp.float32),
    )
    block_out = jnp.stack(block_list)[:, None]
    grad_tokens = jnp.stack(input_list)[:, None]
    return (
        block_out,
        grad_tokens,
        dense_sums[0],
        dense_sums[1],
        dense_sums[2],
        dense_sums[3],
        dense_sums[4],
        expert_sums[0][None],
        expert_sums[1].T[None],
    )


BF = jnp.bfloat16
F32 = jnp.float32
QB = 256
AB = 512
GELU_K = 0.7978845608028654
VMEM_WHOLE = pl.BlockSpec(memory_space=pltpu.VMEM)
HBM_WHOLE = pl.BlockSpec(memory_space=pltpu.HBM)


def nn(left, right):
    return lax.dot_general(left, right, (((1,), (0,)), ((), ())), preferred_element_type=F32)


def nt(left, right):
    return lax.dot_general(left, right, (((1,), (1,)), ((), ())), preferred_element_type=F32)


def tn(left, right):
    return lax.dot_general(left, right, (((0,), (0,)), ((), ())), preferred_element_type=F32)


def lanes_of(shape, half):
    lane = lax.broadcasted_iota(jnp.int32, shape, 1)
    return (lane < HEAD_DIM) if half == 0 else (lane >= HEAD_DIM)


def masks_of(label_ref, micro):
    doc = label_ref[micro : micro + 1, :].astype(F32)
    real = label_ref[MICRO + micro : MICRO + micro + 1, :] == 1
    return doc, jnp.where(real, doc, -1.0)


def as_column(row):
    return jnp.transpose(jnp.broadcast_to(row, (128, row.shape[1])))[:, 0:1]


def attend_kernel(
    micro, h_ref, w_ref, label_ref, saved_ref, o_ref, lse_ref, col_ref, qkv_ref, sem
):
    seq, width = h_ref.shape[0], o_ref.shape[1]
    scale = HEAD_DIM ** (-0.5)
    doc_row, code_row = masks_of(label_ref, micro)
    col_ref[...] = as_column(doc_row)

    def project(block, carry):
        rows = pl.ds(block * AB, AB)
        qkv_ref[rows, :] = nn(h_ref[rows, :], w_ref[:, 0 : 3 * width]).astype(BF)
        return carry

    lax.fori_loop(0, seq // AB, project, 0)
    save = pltpu.make_async_copy(qkv_ref, saved_ref, sem)
    save.start()
    for block in range(seq // AB):
        low, kend = block * AB, (block + 1) * AB
        rows = slice(low, kend)
        qpos = lax.broadcasted_iota(jnp.int32, (AB, kend), 0) + low
        kpos = lax.broadcasted_iota(jnp.int32, (AB, kend), 1)
        same = col_ref[rows, :] == code_row[:, 0:kend]
        allowed = (same & (kpos < qpos)) | (kpos == qpos)
        bias = jnp.where(allowed, 0.0, NEGATIVE).astype(F32)
        lane = lax.broadcasted_iota(jnp.int32, (AB, 128), 1)

        def pair(index, stats):
            at = pl.multiple_of(index * 128, 128)
            q = qkv_ref[rows, pl.ds(at, 128)] * jnp.asarray(scale, BF)
            k = qkv_ref[0:kend, pl.ds(width + at, 128)]
            v = qkv_ref[0:kend, pl.ds(2 * width + at, 128)]
            outs = []
            for half in range(2):
                qm = jnp.where(lanes_of(q.shape, half), q, jnp.zeros_like(q))
                s = nt(qm, k) + bias
                top = jnp.max(s, axis=1, keepdims=True)
                e = jnp.exp(s - top)
                total = jnp.sum(e, axis=1, keepdims=True)
                outs.append(nn(e.astype(BF), v) * (1.0 / total))
                stats = jnp.where(lane == 2 * index + half, top + jnp.log(total), stats)
            o_ref[rows, pl.ds(at, 128)] = jnp.where(
                lanes_of(outs[0].shape, 0), outs[0], outs[1]
            ).astype(BF)
            return stats

        stats = lax.fori_loop(0, width // 128, pair, jnp.zeros((AB, 128), F32), unroll=True)
        lse_ref[:, rows] = jnp.transpose(stats)[0 : lse_ref.shape[0], :]
    save.wait()


def attend_back_kernel(
    micro, h_ref, w_ref, qkv_ref, do_ref, lse_ref, label_ref, dh_ref, dqkv_ref, dk_ref, dv_ref,
    kt_ref, col_ref,
):
    seq, width = do_ref.shape
    doc_row, code_row = masks_of(label_ref, micro)
    col_ref[...] = as_column(code_row)
    scale = HEAD_DIM ** (-0.5)
    dk_ref[...] = jnp.zeros_like(dk_ref)
    dv_ref[...] = jnp.zeros_like(dv_ref)
    kt_ref[...] = jnp.transpose(qkv_ref[:, width : 2 * width])
    for block in range(seq // AB):
        low, kend = block * AB, (block + 1) * AB
        rows = slice(low, kend)
        qpos = lax.broadcasted_iota(jnp.int32, (kend, AB), 1) + low
        kpos = lax.broadcasted_iota(jnp.int32, (kend, AB), 0)
        same = doc_row[:, rows] == col_ref[0:kend, :]
        allowed = (same & (kpos < qpos)) | (kpos == qpos)
        bias = jnp.where(allowed, 0.0, NEGATIVE).astype(F32)

        def pair(index, carry):
            at = pl.multiple_of(index * 128, 128)
            q = qkv_ref[rows, pl.ds(at, 128)] * jnp.asarray(scale, BF)
            k = qkv_ref[0:kend, pl.ds(width + at, 128)]
            v = qkv_ref[0:kend, pl.ds(2 * width + at, 128)]
            do = do_ref[rows, pl.ds(at, 128)]
            dqt = jnp.zeros((128, AB), F32)
            dv = dk = None
            for half in range(2):
                keep = lanes_of(q.shape, half)
                qm = jnp.where(keep, q, jnp.zeros_like(q))
                dom = jnp.where(keep, do, jnp.zeros_like(do))
                p = jnp.exp(nt(k, qm) + bias - lse_ref[pl.ds(2 * index + half, 1), rows])
                dp = nt(v, dom)
                delta = jnp.sum(p * dp, axis=0, keepdims=True)
                ds = (p * (dp - delta)).astype(BF)
                dv_half = nn(p.astype(BF), dom)
                dk_half = nn(ds, qm)
                dv = dv_half if dv is None else dv + dv_half
                dk = dk_half if dk is None else dk + dk_half
                kt = kt_ref[pl.ds(pl.multiple_of(at + half * HEAD_DIM, HEAD_DIM), HEAD_DIM), 0:kend]
                dqt = nn(kt, ds) if half == 0 else jnp.concatenate([dqt, nn(kt, ds)], axis=0)
            dv_ref[0:kend, pl.ds(at, 128)] += dv
            dk_ref[0:kend, pl.ds(at, 128)] += dk
            dqkv_ref[rows, pl.ds(at, 128)] = (jnp.transpose(dqt) * scale).astype(BF)
            return carry

        lax.fori_loop(0, width // 128, pair, 0, unroll=True)
    dqkv_ref[:, width : 2 * width] = dk_ref[...].astype(BF)
    dqkv_ref[:, 2 * width :] = dv_ref[...].astype(BF)

    def spread(block, carry):
        rows = pl.ds(block * AB, AB)
        dh_ref[rows, :] = nt(dqkv_ref[rows, :], w_ref[:, 0 : 3 * width])
        return carry

    lax.fori_loop(0, seq // AB, spread, 0)


def expert_kernel(has_prev, h_ref, g_ref, *refs):
    if has_prev:
        (c_ref, up_ref, down_ref, prev_up_ref, prev_down_ref, give_ref, extra_ref,
         y_out_ref, dh_out_ref, gc_ref, gup_ref, gdown_ref, sup_ref, sdown_ref, got_ref, more_ref,
         dz_ref, gate_ref, z_ref, acc_ref, a_ref, du_ref, y_ref, dh_ref, sems,
         swap_send, swap_recv, more_send, more_recv) = refs
        exchanges = (
            (give_ref, got_ref, swap_send, swap_recv, sems.at[8], ROLES),
            (extra_ref, more_ref, more_send, more_recv, sems.at[9], EARLY_0),
        )
    else:
        (c_ref, up_ref, down_ref, give_ref, extra_ref, _,
         y_out_ref, dh_out_ref, gc_ref, gup_ref, gdown_ref, got_ref, more_ref,
         dz_ref, gate_ref, z_ref, acc_ref, a_ref, du_ref, y_ref, dh_ref, sems,
         swap_send, swap_recv, more_send, more_recv) = refs
        exchanges = (
            (give_ref, got_ref, swap_send, swap_recv, sems.at[8], ROLES),
            (extra_ref, more_ref, more_send, more_recv, sems.at[9], LATE_G),
        )
    step, steps = pl.program_id(0), pl.num_programs(0)
    capacity = h_ref.shape[1]
    rows_all = h_ref.shape[0] * capacity
    blocks = rows_all // QB
    each = QB // capacity

    def take(ref, block):
        return ref[pl.ds(pl.multiple_of(block * each, each), each)].reshape(QB, D)

    @pl.when(step == 0)
    def _():
        def start(block, carry):
            rows = pl.ds(pl.multiple_of(block * QB, QB), QB)
            logit = jnp.sum(take(h_ref, block).astype(F32) * c_ref[...], axis=1, keepdims=True)
            gate = 1.0 / (1.0 + jnp.exp(-logit))
            gate_ref[rows, :] = gate
            dz_ref[rows, :] = (gate * take(g_ref, block).astype(F32)).astype(BF)
            z_ref[rows, :] = jnp.zeros((QB, D), F32)
            acc_ref[rows, :] = jnp.zeros((QB, D), F32)
            return carry

        greet([{"shard": chip} for chip in all_chips()[1:]])
        trade_all(*exchanges)
        lax.fori_loop(0, blocks, start, 0)

    def forward(block, carry):
        rows = pl.ds(pl.multiple_of(block * QB, QB), QB)
        u = nn(take(h_ref, block), up_ref[...])
        square = u * u
        t = jnp.tanh(GELU_K * u * (1.0 + 0.044715 * square))
        a = (0.5 * u * (1.0 + t)).astype(BF)
        slope = 0.5 * (1.0 + t) + 0.5 * u * (1.0 - t * t) * (
            GELU_K * (1.0 + 3 * 0.044715 * square)
        )
        a_ref[rows, :] = a
        z_ref[rows, :] += nn(a, down_ref[...])
        du = (nt(dz_ref[rows, :], down_ref[...]) * slope).astype(BF)
        du_ref[rows, :] = du
        acc_ref[rows, :] += nt(du, up_ref[...])
        return carry

    lax.fori_loop(0, blocks, forward, 0, unroll=True)
    gup = tn(h_ref[...].reshape(rows_all, D), du_ref[...])
    gdown = tn(a_ref[...], dz_ref[...])
    if has_prev:
        gup = gup + prev_up_ref[...]
        gdown = gdown + prev_down_ref[...]

        @pl.when(step < 2)
        def _():
            sup_ref[...] = gup.astype(BF)
            sdown_ref[...] = gdown.astype(BF)

        @pl.when(step >= 2)
        def _():
            gup_ref[...] = gup.astype(BF)
            gdown_ref[...] = gdown.astype(BF)
    else:
        gup_ref[...] = gup
        gdown_ref[...] = gdown

    @pl.when(step == steps - 1)
    def _():
        saves = []
        total = jnp.zeros((1, D), F32)
        for block in range(blocks):
            rows = slice(block * QB, (block + 1) * QB)
            group = slice(block * each, (block + 1) * each)
            z = z_ref[rows, :].astype(BF).astype(F32)
            gate = gate_ref[rows, :]
            dgate = jnp.sum(take(g_ref, block).astype(F32) * z, axis=1, keepdims=True)
            dlogit = dgate * gate * (1.0 - gate)
            y_ref[group] = (gate * z).astype(BF).reshape(each, capacity, D)
            dh = (acc_ref[rows, :] + dlogit * c_ref[...]).astype(BF)
            dh_ref[group] = dh.reshape(each, capacity, D)
            total = total + jnp.sum(dlogit * take(h_ref, block).astype(F32), axis=0, keepdims=True)
            saves += [
                pltpu.make_async_copy(
                    dh_ref.at[group], dh_out_ref.at[group], sems.at[2 * block]
                ),
                pltpu.make_async_copy(
                    y_ref.at[group], y_out_ref.at[group], sems.at[2 * block + 1]
                ),
            ]
            for save in saves[-2:]:
                save.start()
        gc_ref[...] = total
        for exchange in exchanges:
            saves += traded(*exchange)
        for save in saves:
            save.wait()


def expert(h_slots, g_slots, centre, up, down, give, prev):
    groups, capacity, _ = h_slots.shape
    rows = groups * capacity
    ff = up.shape[1]
    wide = ff // 3 if prev is None else ff // 4
    steps = ff // wide
    turn = lambda step: step
    if prev is not None:
        turn = lambda step: (step + 2 * (1 - lax.axis_index("ctx"))) % 4
    early = lambda step: step // 2 + (1 - step // 2) * step
    late = lambda step: (step // 2) * (step - 2)
    whole = lambda step: (0, 0)
    every = lambda step: (0, 0, 0)
    slot_block = (groups, capacity, D)
    up_block = pl.BlockSpec((D, wide), lambda step: (0, turn(step)))
    down_block = pl.BlockSpec((wide, D), lambda step: (turn(step), 0))
    in_specs = [
        pl.BlockSpec(slot_block, every, pipeline_mode=pl.Buffered(1)),
        pl.BlockSpec(slot_block, every, pipeline_mode=pl.Buffered(1)),
        pl.BlockSpec((1, D), whole),
        up_block,
        down_block,
    ]
    args = [h_slots, g_slots, centre, up, down]
    out_shape = [
        pltpu.HBM((groups, capacity, D), BF),
        pltpu.HBM((groups, capacity, D), BF),
        jax.ShapeDtypeStruct((1, D), F32),
    ]
    out_specs = [HBM_WHOLE, HBM_WHOLE, pl.BlockSpec((1, D), whole)]
    more = 2
    if prev is None:
        out_shape += [pltpu.HBM((D, ff), F32), pltpu.HBM((ff, D), F32)]
        out_specs += [up_block, down_block]
    else:
        for at in (late, early):
            out_shape += [pltpu.HBM((D, ff // 2), BF), pltpu.HBM((ff // 2, D), BF)]
            out_specs += [
                pl.BlockSpec((D, wide), lambda step, at=at: (0, at(step))),
                pl.BlockSpec((wide, D), lambda step, at=at: (at(step), 0)),
            ]
        in_specs += [up_block, down_block]
        args += list(prev)
    in_specs += [HBM_WHOLE] * len(give)
    args += list(give)
    out_shape += [pltpu.HBM((groups, capacity, D), BF)] * more
    out_specs += [HBM_WHOLE] * more
    return pl.pallas_call(
        functools.partial(expert_kernel, prev is not None),
        out_shape=tuple(out_shape),
        grid=(steps,),
        in_specs=in_specs,
        out_specs=tuple(out_specs),
        scratch_shapes=[
            pltpu.VMEM((rows, D), BF),
            pltpu.VMEM((rows, 1), F32),
            pltpu.VMEM((rows, D), F32),
            pltpu.VMEM((rows, D), F32),
            pltpu.VMEM((rows, wide), BF),
            pltpu.VMEM((rows, wide), BF),
            pltpu.VMEM((groups, capacity, D), BF),
            pltpu.VMEM((groups, capacity, D), BF),
            pltpu.SemaphoreType.DMA((10,)),
        ]
        + [pltpu.SemaphoreType.DMA((16,))] * (2 * more),
        input_output_aliases={7: 6} if prev is None else {},
        compiler_params=pltpu.CompilerParams(
            collective_id=2 if prev is None else 3, has_side_effects=True, vmem_limit_bytes=56 << 20
        ),
        cost_estimate=pl.CostEstimate(
            flops=12 * rows * D * ff, bytes_accessed=40 << 20, transcendentals=rows * ff
        ),
        name="expert",
    )(*args)


PARTS = 4


def emit_kernel(
    x0_ref, x1_ref, y0a_ref, y0b_ref, y1_ref, target_in_ref, in0_ref, in1_ref,
    own_up_ref, got_up_ref, own_down_ref, got_down_ref, gqkv_in_ref, gproj_in_ref, small_in_ref,
    out_ref, grad_ref, up_ref, down_ref, gqkv_ref, gproj_ref, one_ref, two_ref, centre_ref,
    target_ref, small_ref, x_ref, y_ref, in_ref, up_parts_ref, down_parts_ref, up_sum_ref, down_sum_ref, sems, sum_sems,
):
    rows = x0_ref.shape[0]
    groups, capacity, _ = y0a_ref.shape
    slots = groups * capacity
    chips = all_chips()
    sums = []
    for pair, (own_ref, got_ref, parts_ref, sum_ref, result_ref) in enumerate(
        (
            (own_up_ref, got_up_ref, up_parts_ref, up_sum_ref, up_ref),
            (own_down_ref, got_down_ref, down_parts_ref, down_sum_ref, down_ref),
        )
    ):
        size = own_ref.shape[0] // PARTS
        for part in range(PARTS):
            at = slice(part * size, (part + 1) * size)
            sem = 3 * (PARTS * pair + part)
            sums.append(
                (
                    pltpu.make_async_copy(own_ref.at[at, :], parts_ref.at[0, at, :], sum_sems.at[sem]),
                    pltpu.make_async_copy(got_ref.at[at, :], parts_ref.at[1, at, :], sum_sems.at[sem + 1]),
                    pltpu.make_async_copy(sum_ref.at[at, :], result_ref.at[at, :], sum_sems.at[sem + 2]),
                    parts_ref, sum_ref, at,
                )
            )
    loads, moves = [], []
    for micro, (x_in, grad_in, parts) in enumerate(
        (
            (x0_ref, in0_ref, ((y0a_ref, EARLY_0), (y0b_ref, LATE_0))),
            (x1_ref, in1_ref, ((y1_ref, ROLES),)),
        )
    ):
        mine = [pltpu.make_async_copy(x_in, x_ref.at[micro], sems.at[20 * micro])]
        for part_ref, roles in parts:
            mine += [
                pltpu.make_async_copy(
                    part_ref.at[chips[role]], y_ref.at[micro, chips[role]], sems.at[20 * micro + 1 + role]
                )
                for role in roles
            ]
        loads.append(mine)
        moves.append(
            (
                pltpu.make_async_copy(grad_in, in_ref.at[micro], sems.at[20 * micro + 17]),
                pltpu.make_async_copy(
                    in_ref.at[micro], grad_ref.at[micro * rows : (micro + 1) * rows, :],
                    sems.at[20 * micro + 18],
                ),
            )
        )
    few = [
        pltpu.make_async_copy(src, dst, sems.at[40 + at])
        for at, (src, dst) in enumerate(
            (
                (gqkv_in_ref, gqkv_ref),
                (gproj_in_ref, gproj_ref),
                (small_in_ref, small_ref),
                (target_in_ref, target_ref),
            )
        )
    ]
    for part in sums:
        part[0].start()
        part[1].start()
    for load in few + loads[0] + [moves[0][0]] + loads[1] + [moves[1][0]]:
        load.start()
    for load in few:
        load.wait()
    size, experts = small_ref.shape[0], centre_ref.shape[0]
    small = jnp.concatenate([small_ref[...], jnp.zeros((128 - size, 128), F32)], axis=0)
    small = jnp.transpose(small)
    one_ref[...] = small[0:1, 0:size]
    two_ref[...] = small[1:2, 0:size]
    centre_ref[...] = small[2 : 2 + experts, 0:size]
    for own, got, store, parts_ref, sum_ref, at in sums:
        own.wait()
        got.wait()
        sum_ref[at, :] = parts_ref[0, at, :].astype(F32) + parts_ref[1, at, :].astype(F32)
        store.start()
    for micro in range(MICRO):
        for load in loads[micro]:
            load.wait()
        moves[micro][0].wait()
        moves[micro][1].start()
        slot = lax.broadcasted_iota(jnp.int32, (rows, slots), 1)
        pick = (slot == target_ref[:, micro : micro + 1]).astype(F32).astype(BF)
        value = x_ref[micro] + nn(pick, y_ref[micro].reshape(slots, D))
        out_ref[micro * rows : (micro + 1) * rows, :] = value.astype(BF)
    for part in sums:
        part[2].wait()
    for move in moves:
        move[1].wait()


def emit(x0, x1, y0a, y0b, y1, target, in0, in1, own_up, got_up, own_down, got_down, gqkv, gproj, small):
    rows, size = x0.shape[0], small.shape[0]
    groups = y0a.shape[0]
    in_hbm = lambda array: pltpu.with_memory_space_constraint(array, pltpu.HBM)
    args = [x0, x1, y0a, y0b, y1, target, in0, in1, own_up, got_up, own_down, got_down, gqkv, gproj, small]
    return pl.pallas_call(
        emit_kernel,
        out_shape=(
            jax.ShapeDtypeStruct((MICRO * rows, D), BF),
            pltpu.HBM((MICRO * rows, D), F32),
            pltpu.HBM(own_up.shape, F32),
            pltpu.HBM(own_down.shape, F32),
            jax.ShapeDtypeStruct(gqkv.shape, F32),
            jax.ShapeDtypeStruct(gproj.shape, F32),
            jax.ShapeDtypeStruct((1, size), F32),
            jax.ShapeDtypeStruct((1, size), F32),
            jax.ShapeDtypeStruct((groups, size), F32),
        ),
        in_specs=[HBM_WHOLE] * 15,
        out_specs=(VMEM_WHOLE,) + (HBM_WHOLE,) * 3 + (VMEM_WHOLE,) * 5,
        scratch_shapes=[
            pltpu.VMEM(target.shape, jnp.int32),
            pltpu.VMEM(small.shape, F32),
            pltpu.VMEM((MICRO, rows, D), F32),
            pltpu.VMEM((MICRO,) + y0a.shape, BF),
            pltpu.VMEM((MICRO, rows, D), F32),
            pltpu.VMEM((2,) + own_up.shape, BF),
            pltpu.VMEM((2,) + own_down.shape, BF),
            pltpu.VMEM(own_up.shape, F32),
            pltpu.VMEM(own_down.shape, F32),
            pltpu.SemaphoreType.DMA((44,)),
            pltpu.SemaphoreType.DMA((6 * PARTS,)),
        ],
        compiler_params=pltpu.CompilerParams(vmem_limit_bytes=50 << 20),
        cost_estimate=pl.CostEstimate(
            flops=4 * rows * D * groups * y0a.shape[1], bytes_accessed=30 << 20, transcendentals=0
        ),
        name="emit",
    )(*[in_hbm(array) for array in args])


def greet(peers):
    barrier = pltpu.get_barrier_semaphore()
    for peer in peers:
        pl.semaphore_signal(
            barrier, inc=1, device_id=peer, device_id_type=pl.DeviceIdType.MESH
        )
    pl.semaphore_wait(barrier, len(peers))


def send(src, dst, send_sem, recv_sem, peer):
    return pltpu.make_async_remote_copy(
        src_ref=src,
        dst_ref=dst,
        send_sem=send_sem,
        recv_sem=recv_sem,
        device_id=peer,
        device_id_type=pl.DeviceIdType.MESH,
    )


def places():
    me, core = lax.axis_index("shard"), lax.axis_index("ctx")
    z, y, x = me // 4, (me // 2) % 2, me % 2
    along_y, along_x = me + 2 - 4 * y, me + 1 - 2 * x
    first = along_y * (1 - core) + along_x * core
    second = along_x * (1 - core) + along_y * core
    far = 4 * z + 3 - me % 4
    line = [z, z + 1 - 2 * (z % 2), (z + 2) % 4, 3 - z]
    return me, first, second, far, line


def all_chips():
    me, _, _, _, line = places()
    y, x = (me // 2) % 2, me % 2
    turns = [me % 4, me % 4 + 1 - 2 * x, me % 4 + 2 - 4 * y, 3 - me % 4]
    return [4 * line[j] + turns[i] for j in range(4) for i in range(4)]


ROLES = (8, 9, 10, 11, 12, 13, 14, 15, 4, 5, 6, 7, 1, 2, 3, 0)
EARLY_G, LATE_G = (8, 9, 10, 11, 12, 4, 5, 6, 1, 2, 0), (13, 14, 15, 7, 3)
EARLY_0, LATE_0 = (8, 9, 10, 4, 1), (11, 12, 13, 14, 15, 5, 6, 7, 2, 3, 0)
EARLY_1, NEXT_1, LATE_1 = (8, 9, 10, 4, 1), (11, 12), (13, 14, 15, 5, 6, 7, 2, 3, 0)


def traded(src_ref, dst_ref, send_sem, recv_sem, keep_sem, roles=ROLES):
    chips = all_chips()
    me = chips[0]
    copies = []
    for role in roles:
        if role:
            copies.append(
                send(
                    src_ref.at[chips[role]], dst_ref.at[me], send_sem.at[role], recv_sem.at[role],
                    {"shard": chips[role]},
                )
            )
        else:
            copies.append(pltpu.make_async_copy(src_ref.at[me], dst_ref.at[me], keep_sem))
    return copies


def trade_all(*exchanges):
    copies = []
    for far in (True, False):
        for exchange in exchanges:
            roles = tuple(role for role in exchange[5] if (role >= 8) == far)
            copies += trade(*exchange[:5], roles)
    return copies


def trade(src_ref, dst_ref, send_sem, recv_sem, keep_sem, roles=ROLES):
    copies = traded(src_ref, dst_ref, send_sem, recv_sem, keep_sem, roles)
    for copy in copies:
        copy.start()
    return copies


def head_kernel(
    experts, capacity, qkv_ref, proj_ref, seg_ref, pad_ref, route_ref, tok_ref, cot_ref,
    centroid_ref, gains_ref,
    out_save_ref, full_save_ref, h0_save_ref, h1_save_ref, all_save_ref, column_save_ref, centre_ref,
    in0_ref, in1_ref,
    take_ref, saved0_ref, lse0_save_ref, x10_ref, attended0_ref, saved1_ref, lse1_save_ref, x11_ref,
    attended1_ref, sent_ref, given_ref,
    all_ref, target_ref, column_ref, lse0_ref, lse1_ref, hub_ref, w_ref, x_ref, g_ref, label_ref, slots_ref, out_ref, full_ref, h0_ref, h1_ref,
    col_ref, heads_ref, o_ref, first_ref, x1_ref, joined0_ref, joined1_ref, h2_ref,
    send_sem, recv_sem, swap_send, swap_recv, sems, post_sems,
):
    size = w_ref.shape[0]
    half = full_ref.shape[1] // 2
    wide = w_ref.shape[1] - half
    count = label_ref.shape[1]
    me, first, second, far, line = places()
    core = lax.axis_index("ctx")
    own = pl.multiple_of(core * half, 128)
    loads = [
        pltpu.make_async_copy(
            qkv_ref.at[:, pl.ds(2 * at * half + own, half)],
            w_ref.at[:, at * half : (at + 1) * half],
            sems.at[at],
        )
        for at in range(3)
    ]
    loads += [
        pltpu.make_async_copy(proj_ref.at[:, pl.ds(own, half)], w_ref.at[:, wide:], sems.at[3]),
        pltpu.make_async_copy(cot_ref, g_ref, sems.at[4]),
        pltpu.make_async_copy(tok_ref, x_ref, sems.at[5]),
    ]
    for load in loads:
        load.start()
    gain_ref, gain_two_ref = gains_ref.at[0:1, :], gains_ref.at[1:2, :]
    label_ref[...] = jnp.zeros_like(label_ref)
    names = [
        pltpu.make_async_copy(
            ref.at[micro], label_ref.at[MICRO * at + micro : MICRO * at + micro + 1, :],
            sems.at[16 + MICRO * at + micro],
        )
        for at, ref in enumerate((seg_ref, pad_ref, route_ref))
        for micro in range(MICRO)
    ]
    names.append(pltpu.make_async_copy(centroid_ref, hub_ref, sems.at[15]))
    for name in names:
        name.start()
    twin = {"ctx": 1 - core}
    lines = [4 * z for z in line]
    y, x = (me // 2) % 2, me % 2
    turns = [me % 4, me % 4 + 1 - 2 * x, me % 4 + 2 - 4 * y, 3 - me % 4]

    def rows(block):
        return out_ref.at[pl.ds(pl.multiple_of(block * size, 16), size), :]

    chips = [lines[j] + turns[i] for j in range(4) for i in range(4)]
    peers = [{"shard": chips[4 * j]} for j in (1, 2, 3)]
    one, two = {"shard": first}, {"shard": second}
    greet([{"shard": chip} for chip in chips[1:]] + [twin])
    copies, share = [], []

    def push(block, role, peer, src=None):
        copy = send(
            rows(block) if src is None else src, rows(block), send_sem.at[role], recv_sem.at[role], peer
        )
        copy.start()
        copies.append(copy)

    def arrive(block, role):
        send(rows(block), rows(block), send_sem.at[0], recv_sem.at[role], one).wait_recv()

    for load in loads[:4]:
        load.wait()
    push(me, 3, one, w_ref)
    push(me, 7, two, w_ref)
    for j in (1, 2, 3):
        push(me, j - 1, peers[j - 1], w_ref)
    out_ref[pl.ds(pl.multiple_of(me * size, 16), size), :] = w_ref[...]
    for name in names:
        name.wait()
    mine = pl.ds(pl.multiple_of(core * count, 128), count)
    share.append(send(label_ref, all_ref.at[:, mine], send_sem.at[15], recv_sem.at[15], twin))
    share[0].start()
    all_ref[:, mine] = label_ref[...]

    before = lax.broadcasted_iota(jnp.int32, (count, count), 0)
    after = lax.broadcasted_iota(jnp.int32, (count, count), 1)
    upto = (before <= after).astype(F32).astype(BF)
    ids = lax.broadcasted_iota(jnp.int32, (experts, count), 0)
    target_ref[...] = jnp.zeros_like(target_ref)
    for micro in range(MICRO):
        route = label_ref[2 * MICRO + micro : 2 * MICRO + micro + 1, :]
        chosen = (ids == route).astype(F32)
        rank = jnp.sum(nn(chosen.astype(BF), upto) * chosen, axis=0, keepdims=True)
        target_ref[micro : micro + 1, :] = route * capacity + rank.astype(jnp.int32) - 1
    wide_target = jnp.concatenate(
        [target_ref[...].astype(F32), jnp.zeros((120, count), F32)], axis=0
    )
    column_ref[...] = jnp.transpose(wide_target)[:, 0:8].astype(jnp.int32)
    row = lax.broadcasted_iota(jnp.int32, (experts, D), 0)
    centre_ref[...] = jnp.sum(
        jnp.where(row == me, hub_ref[...].astype(F32), 0.0), axis=0, keepdims=True
    )

    def place(micro, group):
        slot = lax.broadcasted_iota(jnp.int32, (4 * capacity, count), 0) + group * capacity
        pick = (slot == target_ref[micro : micro + 1, :]).astype(F32).astype(BF)
        value = nn(pick, g_ref[micro * count : (micro + 1) * count, :]).astype(BF)
        slots_ref[micro, pl.ds(pl.multiple_of(group, 4), 4)] = value.reshape(4, capacity, D)

    swaps = []

    def pass_one(micro, role):
        copy = send(
            slots_ref.at[micro, chips[role]],
            (in1_ref if micro else in0_ref).at[me],
            swap_send.at[16 * micro + role],
            swap_recv.at[16 * micro + role],
            {"shard": chips[role]},
        )
        copy.start()
        swaps.append(copy)

    def pass_on(micro, j):
        for i in range(4):
            if 4 * j + i:
                pass_one(micro, 4 * j + i)

    loads[4].wait()
    place(0, lines[2])
    pass_on(0, 2)

    def normed(micro, h_ref):
        def norm(block, carry):
            off = pl.multiple_of(block * RB, RB)
            unit = normal(x_ref[pl.ds(micro * count + off, RB), :].astype(F32))[0]
            at = pl.ds(pl.multiple_of(core * count + off, RB), RB)
            h_ref[at, :] = (unit * gain_ref[...]).astype(BF)
            return carry

        lax.fori_loop(0, count // RB, norm, 0)
        copy = send(
            h_ref.at[mine, :], h_ref.at[mine, :], send_sem.at[16 + micro], recv_sem.at[16 + micro], twin
        )
        copy.start()
        share.append(copy)

    arrive(lines[0] + first % 4, 3)
    push(lines[0] + first % 4, 11, two)
    block = lines[1] + me % 4
    arrive(block, 0)
    push(block, 4, one)
    push(block, 8, two)
    place(0, lines[3])
    pass_on(0, 3)
    loads[5].wait()
    normed(0, h0_ref)
    for j in (2, 3):
        block = lines[j] + me % 4
        arrive(block, j - 1)
        push(block, 3 + j, one)
        push(block, 7 + j, two)
        block = lines[j - 1] + first % 4
        arrive(block, 3 + j - 1)
        push(block, 11 + j - 1, two)
        if j == 2:
            place(0, lines[1])
            pass_on(0, 1)
    block = lines[3] + first % 4
    arrive(block, 6)
    push(block, 14, two)
    place(0, lines[0])
    pass_on(0, 0)
    normed(1, h1_ref)
    for group in range(0, experts, 4):
        place(1, group)
    saves = [
        pltpu.make_async_copy(slots_ref.at[0, me], in0_ref.at[me], sems.at[6]),
        pltpu.make_async_copy(slots_ref.at[1, me], in1_ref.at[me], sems.at[7]),
    ]
    for j in range(4):
        arrive(lines[j] + second % 4, 7 + j)
        arrive(lines[j] + far % 4, 11 + j)
    for role in EARLY_G:
        if role:
            pass_one(1, role)
    side = pl.ds(pl.multiple_of(core * half, 128), half)
    joint = send(
        out_ref.at[:, wide : wide + half], full_ref.at[:, side], send_sem.at[18], recv_sem.at[18], twin
    )
    joint.start()
    full_ref[:, side] = out_ref[:, wide : wide + half]
    for copy in share:
        copy.wait()
    saves += [
        pltpu.make_async_copy(out_ref, out_save_ref, sems.at[8]),
        pltpu.make_async_copy(h0_ref, h0_save_ref, sems.at[9]),
        pltpu.make_async_copy(h1_ref, h1_save_ref, sems.at[10]),
        pltpu.make_async_copy(slots_ref.at[1], given_ref, sems.at[22]),
        pltpu.make_async_copy(all_ref, all_save_ref, sems.at[23]),
        pltpu.make_async_copy(column_ref, column_save_ref, sems.at[24]),
        pltpu.make_async_copy(full_ref, full_save_ref, sems.at[11]),
    ]
    for save in saves[:-1]:
        save.start()
    attend_kernel(
        0, h0_ref, out_ref, all_ref, saved0_ref, o_ref, lse0_ref, col_ref, heads_ref, sems.at[12]
    )
    joint.wait()
    saves[-1].start()
    groups = [lines[j] for j in (2, 3, 1, 0)]
    steps = iter((2, 3, 1, 0))

    def hand_on(group):
        j = next(steps)
        for i in range(4):
            role = 4 * j + i
            if role:
                copy = send(
                    first_ref.at[0, chips[role]],
                    take_ref.at[me],
                    swap_send.at[32 + role],
                    swap_recv.at[32 + role],
                    {"shard": chips[role]},
                )
            else:
                copy = pltpu.make_async_copy(first_ref.at[0, me], take_ref.at[me], sems.at[13])
            copy.start()
            swaps.append(copy)

    post_stage(
        0, capacity, groups, x_ref, o_ref, full_ref, gain_two_ref, target_ref, hand_on, x10_ref,
        attended0_ref, first_ref.at[0], x1_ref, joined0_ref, h2_ref, post_sems,
        send_sem.at[19], recv_sem.at[19],
    )
    attend_kernel(
        1, h1_ref, out_ref, all_ref, saved1_ref, o_ref, lse1_ref, col_ref, heads_ref, sems.at[12]
    )
    post_stage(
        1, capacity, groups, x_ref, o_ref, full_ref, gain_two_ref, target_ref, lambda group: None,
        x11_ref, attended1_ref, first_ref.at[1], x1_ref, joined1_ref, h2_ref, post_sems,
        send_sem.at[20], recv_sem.at[20],
    )
    late = [
        pltpu.make_async_copy(first_ref.at[1], sent_ref, sems.at[14]),
        pltpu.make_async_copy(lse0_ref, lse0_save_ref, sems.at[25]),
        pltpu.make_async_copy(lse1_ref, lse1_save_ref, sems.at[26]),
    ]
    for save in late:
        save.start()
    saves += late
    for copy in copies:
        copy.wait_send()
    for save in saves:
        save.wait()
    for copy in swaps:
        copy.wait()


def head(experts, capacity, qkv_weight, out_weight, seg, pad, route, x, g, centroids, gains):
    size, columns = qkv_weight.shape[0], 2 * D
    count = seg.shape[2]
    half = D // 2
    in_hbm = lambda array: pltpu.with_memory_space_constraint(array, pltpu.HBM)
    return pl.pallas_call(
        functools.partial(head_kernel, experts, capacity),
        out_shape=(
            pltpu.HBM((16 * size, columns), BF),
            pltpu.HBM((16 * size, D), BF),
            pltpu.HBM((2 * count, D), BF),
            pltpu.HBM((2 * count, D), BF),
            pltpu.HBM((8, 2 * count), jnp.int32),
            pltpu.HBM((count, 8), jnp.int32),
            jax.ShapeDtypeStruct((1, D), F32),
            pltpu.HBM((experts, capacity, D), BF),
            pltpu.HBM((experts, capacity, D), BF),
            pltpu.HBM((experts, capacity, D), BF),
        )
        + (
            pltpu.HBM((2 * count, 3 * half), BF),
            pltpu.HBM((8, 2 * count), F32),
            pltpu.HBM((count, D), F32),
            pltpu.HBM((count, D), BF),
        )
        * 2
        + (pltpu.HBM((experts, capacity, D), BF),) * 2,
        in_specs=[HBM_WHOLE] * 8 + [VMEM_WHOLE],
        out_specs=(HBM_WHOLE,) * 6 + (VMEM_WHOLE,) + (HBM_WHOLE,) * 13,
        scratch_shapes=[
            pltpu.VMEM((8, 2 * count), jnp.int32),
            pltpu.VMEM((8, count), jnp.int32),
            pltpu.VMEM((count, 8), jnp.int32),
            pltpu.VMEM((8, 2 * count), F32),
            pltpu.VMEM((8, 2 * count), F32),
            pltpu.VMEM((experts, D), BF),
            pltpu.VMEM((size, columns), BF),
            pltpu.VMEM((MICRO * count, D), BF),
            pltpu.VMEM((MICRO * count, D), BF),
            pltpu.VMEM((8, count), jnp.int32),
            pltpu.VMEM((MICRO, experts, capacity, D), BF),
            pltpu.VMEM((16 * size, columns), BF),
            pltpu.VMEM((16 * size, D), BF),
            pltpu.VMEM((2 * count, D), BF),
            pltpu.VMEM((2 * count, D), BF),
            pltpu.VMEM((2 * count, 1), F32),
            pltpu.VMEM((2 * count, 3 * half), BF),
            pltpu.VMEM((2 * count, half), BF),
            pltpu.VMEM((MICRO, experts, capacity, D), BF),
            pltpu.VMEM((count, D), F32),
            pltpu.VMEM((count, D), BF),
            pltpu.VMEM((count, D), BF),
            pltpu.VMEM((count, D), BF),
            pltpu.SemaphoreType.DMA((21,)),
            pltpu.SemaphoreType.DMA((21,)),
            pltpu.SemaphoreType.DMA((48,)),
            pltpu.SemaphoreType.DMA((48,)),
            pltpu.SemaphoreType.DMA((27,)),
            pltpu.SemaphoreType.DMA((2,)),
        ],
        compiler_params=pltpu.CompilerParams(
            collective_id=0, has_side_effects=True, vmem_limit_bytes=52 << 20
        ),
        cost_estimate=pl.CostEstimate(flops=0, bytes_accessed=100 << 20, transcendentals=0),
        name="head",
    )(
        in_hbm(qkv_weight), in_hbm(out_weight), in_hbm(seg), in_hbm(pad), in_hbm(route), in_hbm(x),
        in_hbm(g), in_hbm(centroids), gains,
    )


def scatter_stage(
    packed_ref, gqkv_ref, gout_ref, gsmall_ref,
    theirs_ref, rx1_ref, rx2_ref, rx3_ref, tx1_ref, tx2_ref, sum_ref, send_sem, recv_sem, between,
):
    me, first, second, far, line = places()
    core = lax.axis_index("ctx")
    lines = [4 * z for z in line]
    part = sum_ref.shape[0] // 2
    half = gout_ref.shape[1] // 2
    wide = 3 * half
    peers = [{"shard": lines[j] + me % 4} for j in (1, 2, 3)]
    one, two, twin = {"shard": first}, {"shard": second}, {"ctx": 1 - core}
    order = (3, 2, 1, 0)
    copies = []

    def push(src, dst, role, peer):
        copy = send(src, dst, send_sem.at[role], recv_sem.at[role], peer)
        copy.start()
        copies.append(copy)

    def arrive(dst, role):
        send(dst, dst, send_sem.at[role], recv_sem.at[role], one).wait_recv()

    for j in order:
        push(packed_ref.at[lines[j] + far % 4], rx1_ref.at[j], j, two)
    for j in order:
        push(packed_ref.at[lines[j] + second % 4], rx1_ref.at[4 + j], 4 + j, two)
    between(NEXT_1)
    for j in order:
        arrive(rx1_ref.at[j], j)
        total = packed_ref[lines[j] + first % 4].astype(F32) + rx1_ref[j].astype(F32)
        tx1_ref[j] = total.astype(BF)
        push(tx1_ref.at[j], rx2_ref.at[j], 8 + j, one)
    own = None
    for j in order:
        arrive(rx1_ref.at[4 + j], 4 + j)
        total = packed_ref[lines[j] + me % 4].astype(F32) + rx1_ref[4 + j].astype(F32)
        arrive(rx2_ref.at[j], 8 + j)
        total = total + rx2_ref[j].astype(F32)
        if j:
            tx2_ref[j - 1] = total.astype(BF)
            push(tx2_ref.at[j - 1], rx3_ref.at[j - 1], 11 + j, peers[j - 1])
        else:
            own = total
    between(LATE_1)
    for j in (1, 2, 3):
        arrive(rx3_ref.at[j - 1], 11 + j)
        own = own + rx3_ref[j - 1].astype(F32)
    sum_ref[...] = own
    push(
        sum_ref.at[pl.ds(pl.multiple_of((1 - core) * part, 8), part), :], theirs_ref, 15, twin
    )
    arrive(theirs_ref, 15)
    mine, theirs = sum_ref[pl.ds(pl.multiple_of(core * part, 8), part), :], theirs_ref[...]
    low = jnp.where(core == 0, mine, theirs)
    high = jnp.where(core == 0, theirs, mine)
    for at in range(3):
        gqkv_ref[:, 2 * at * half : (2 * at + 1) * half] = low[:, at * half : (at + 1) * half]
        gqkv_ref[:, (2 * at + 1) * half : (2 * at + 2) * half] = high[:, at * half : (at + 1) * half]
    gout_ref[:, 0:half] = low[:, wide : wide + half]
    gout_ref[:, half:] = high[:, wide : wide + half]
    gsmall_ref[...] = mine[:, wide + half :] + theirs[:, wide + half :]
    for copy in copies:
        copy.wait_send()


def normal(values):
    centre = values - jnp.mean(values, axis=1, keepdims=True)
    spread = jnp.mean(centre * centre, axis=1, keepdims=True)
    scale = lax.rsqrt(spread + EPSILON)
    return centre * scale, scale


def normal_back(unit, scale, gain, grad):
    pull = grad * gain
    return scale * (
        pull
        - jnp.mean(pull, axis=1, keepdims=True)
        - unit * jnp.mean(pull * unit, axis=1, keepdims=True)
    )


RB = 256


def post_stage(
    micro, capacity, groups, x_ref, o_ref, wo_ref, gain_ref, target_ref, hand_on, x1_out_ref, full_out_ref,
    slots_ref, x1_ref, full_ref, h_ref, sems, send_sem, recv_sem,
):
    core = lax.axis_index("ctx")
    rows, width = x1_ref.shape[0], o_ref.shape[1]
    twin = {"ctx": 1 - core}
    mine = pl.ds(pl.multiple_of(core * width, 128), width)
    copy = send(
        o_ref.at[pl.ds(pl.multiple_of((1 - core) * rows, 128), rows), :],
        full_ref.at[:, mine],
        send_sem,
        recv_sem,
        twin,
    )
    copy.start()
    full_ref[:, mine] = o_ref[pl.ds(pl.multiple_of(core * rows, 128), rows), :]
    copy.wait()

    def norm(block, carry):
        at = pl.ds(pl.multiple_of(block * RB, RB), RB)
        value = x_ref[pl.ds(micro * rows + pl.multiple_of(block * RB, RB), RB), :].astype(F32)
        value = value + nn(full_ref[at, :], wo_ref[...])
        x1_ref[at, :] = value
        h_ref[at, :] = (normal(value)[0] * gain_ref[...]).astype(BF)
        return carry

    lax.fori_loop(0, rows // RB, norm, 0)
    saves = [
        pltpu.make_async_copy(full_ref, full_out_ref, sems.at[0]),
        pltpu.make_async_copy(x1_ref, x1_out_ref, sems.at[1]),
    ]
    for save in saves:
        save.start()
    for group in groups:
        slot = lax.broadcasted_iota(jnp.int32, (4 * capacity, rows), 0) + group * capacity
        pick = (slot == target_ref[micro : micro + 1, :]).astype(F32).astype(BF)
        value = nn(pick, h_ref[...]).astype(BF).reshape(4, capacity, D)
        slots_ref[pl.ds(pl.multiple_of(group, 4), 4)] = value
        hand_on(group)
    for save in saves:
        save.wait()


def fore_stage(
    has_prev, micro, dh_ref, target_ref, g_ref, x1_ref, gain_ref, wo_ref, full_ref, prev_two_ref,
    do_ref, dx_ref, gout_ref, gtwo_ref, dy_ref, all_ref, send_sem, recv_sem,
):
    core = lax.axis_index("ctx")
    rows, width = x1_ref.shape[0], do_ref.shape[1]
    slots = dh_ref.shape[0] * dh_ref.shape[1]
    twin = {"ctx": 1 - core}

    def norm(block, total):
        at = pl.ds(pl.multiple_of(block * RB, RB), RB)
        slot = lax.broadcasted_iota(jnp.int32, (RB, slots), 1)
        pick = (slot == target_ref[at, micro : micro + 1]).astype(F32).astype(BF)
        grad = nn(pick, dh_ref[...].reshape(slots, D))
        unit, scale = normal(x1_ref[at, :])
        dx = g_ref[at, :].astype(F32) + normal_back(unit, scale, gain_ref[...], grad)
        dx_ref[at, :] = dx
        dy = dx.astype(BF)
        dy_ref[at, :] = dy
        all_ref[at, :] = nt(dy, wo_ref[...]).astype(BF)
        return total + jnp.sum(grad * unit, axis=0, keepdims=True)

    total = lax.fori_loop(0, rows // RB, norm, jnp.zeros((1, D), F32))
    gtwo_ref[...] = prev_two_ref[...] + total if has_prev else total
    mine = pl.ds(pl.multiple_of(core * rows, 128), rows)
    copy = send(
        all_ref.at[:, pl.ds(pl.multiple_of((1 - core) * width, 128), width)],
        do_ref.at[mine, :],
        send_sem,
        recv_sem,
        twin,
    )
    copy.start()
    do_ref[mine, :] = all_ref[:, pl.ds(pl.multiple_of(core * width, 128), width)]
    grad = tn(full_ref[...], dy_ref[...])
    gout_ref[...] = gout_ref[...] + grad if has_prev else grad
    copy.wait()


def tail_stage(
    has_prev, dh_ref, x_ref, dx_ref, gain_ref, prev_ref, grad_out_ref, gone_ref, grad_ref, rx_ref, sems
):
    core = lax.axis_index("ctx")
    rows = dx_ref.shape[0]
    saves = []
    total = jnp.zeros((1, D), F32)
    for off in range(0, rows, RB):
        at = slice(off, off + RB)
        mine = pl.ds(pl.multiple_of(core * rows + off, RB), RB)
        grad = dh_ref[mine, :] + rx_ref[at, :].astype(F32)
        unit, scale = normal(x_ref[at, :].astype(F32))
        grad_ref[at, :] = dx_ref[at, :] + normal_back(unit, scale, gain_ref[...], grad)
        save = pltpu.make_async_copy(grad_ref.at[at, :], grad_out_ref.at[at, :], sems.at[off // RB])
        save.start()
        saves.append(save)
        total = total + jnp.sum(grad * unit, axis=0, keepdims=True)
    gone_ref[...] = prev_ref[...] + total if has_prev else total
    return saves


def back_kernel(
    slot_ref, target_ref, cot_ref, tok_ref, w_in_ref, wo_in_ref, label_ref, gains_ref, gc0_ref, gc1_ref,
    x10_ref, full0_ref, h0_ref, qkv0_ref, lse0_ref, x11_ref, full1_ref, h1_ref, qkv1_ref, lse1_ref,
    give_dh_ref, give_y0_ref, give_y1_ref, give_up_ref, give_down_ref,
    gqkv_ref, gproj_ref, gsmall_ref, in0_ref, in1_ref, take_dh_ref, take_y0_ref, take_y1_ref,
    take_up_ref, take_down_ref,
    dh_ref, g_ref, x_ref, x1_ref, full_ref, h_ref, w_ref, wo_ref, qkv_ref,
    do_ref, dx_ref, dy_ref, all_ref, part_ref, dqkv_ref, dk_ref, dv_ref, kt_ref, col_ref,
    tx_ref, rx_ref, go_ref, tgo_ref, rgo_ref, gw_ref, gout_ref, gtwo_ref, gone_ref, packed_ref, small_ref,
    theirs_ref, rx1_ref, rx2_ref, rx3_ref, tx1_ref, tx2_ref, sum_ref,
    sems, save_sems, dh_send, dh_recv, y0_send, y0_recv, y1_send, y1_recv, send_sem, recv_sem,
    ring_send, ring_recv,
):
    me, core = lax.axis_index("shard"), lax.axis_index("ctx")
    rows = x_ref.shape[0]
    half = gout_ref.shape[1]
    twin = {"ctx": 1 - core}
    gain_one_ref, gain_two_ref = gains_ref.at[0:1, :], gains_ref.at[1:2, :]
    sources = (
        (x10_ref, full0_ref, h0_ref, qkv0_ref, lse0_ref, in0_ref),
        (x11_ref, full1_ref, h1_ref, qkv1_ref, lse1_ref, in1_ref),
    )

    def loads_of(micro):
        x1_in_ref, full_in_ref, h_in_ref, qkv_in_ref = sources[micro][:4]
        mine = pl.ds(micro * rows, rows)
        pairs = dict(
            dh=((slot_ref, take_dh_ref)[micro], dh_ref),
            x1=(x1_in_ref, x1_ref),
            g=(cot_ref.at[mine, :], g_ref),
            full=(full_in_ref, full_ref),
            qkv=(qkv_in_ref, qkv_ref),
            h=(h_in_ref, h_ref),
            x=(tok_ref.at[mine, :], x_ref),
        )
        return {
            name: pltpu.make_async_copy(src, dst, sems.at[8 * micro + at])
            for at, (name, (src, dst)) in enumerate(pairs.items())
        }

    loads = [loads_of(0), loads_of(1)]
    shared = [
        pltpu.make_async_copy(wo_in_ref, wo_ref, sems.at[16]),
        pltpu.make_async_copy(w_in_ref, w_ref, sems.at[17]),
    ]
    for name in ("dh", "x1", "g", "full"):
        loads[0][name].start()
    shared[0].start()
    for name in ("qkv", "h", "x"):
        loads[0][name].start()
    shared[1].start()
    greet([{"shard": chip} for chip in all_chips()[1:]] + [twin])
    first_trade = trade(give_dh_ref, take_dh_ref, dh_send, dh_recv, sems.at[18])
    swaps = trade_all(
        (give_y0_ref, take_y0_ref, y0_send, y0_recv, sems.at[19], LATE_0),
        (give_y1_ref, take_y1_ref, y1_send, y1_recv, sems.at[20], EARLY_1),
    )
    for at, (give_ref, take_ref) in enumerate(((give_up_ref, take_up_ref), (give_down_ref, take_down_ref))):
        swaps.append(send(give_ref, take_ref, send_sem.at[7 + at], recv_sem.at[7 + at], twin))
        swaps[-1].start()
    for micro in range(MICRO):
        has_prev = micro > 0
        load, lse_ref, grad_out_ref = loads[micro], sources[micro][4], sources[micro][5]
        for name in ("dh", "x1", "g", "full"):
            load[name].wait()
        if not has_prev:
            shared[0].wait()
        fore_stage(
            has_prev, micro, dh_ref, target_ref, g_ref, x1_ref, gain_two_ref, wo_ref, full_ref, gtwo_ref,
            do_ref, dx_ref, go_ref, gtwo_ref, dy_ref, all_ref, send_sem.at[3 * micro],
            recv_sem.at[3 * micro],
        )
        if has_prev:
            tgo_ref[...] = go_ref[:, pl.ds(pl.multiple_of((1 - core) * half, 128), half)].astype(BF)
            cross = send(tgo_ref, rgo_ref, send_sem.at[6], recv_sem.at[6], twin)
            cross.start()
        else:
            loads[1]["g"].start()
            loads[1]["full"].start()
            shared[1].wait()
        load["qkv"].wait()
        load["h"].wait()
        attend_back_kernel(
            micro, h_ref, w_ref, qkv_ref, do_ref, lse_ref, label_ref, part_ref, dqkv_ref, dk_ref, dv_ref,
            kt_ref, col_ref,
        )
        tx_ref[...] = part_ref[pl.ds(pl.multiple_of((1 - core) * rows, 128), rows), :].astype(BF)
        joint = send(tx_ref, rx_ref, send_sem.at[3 * micro + 1], recv_sem.at[3 * micro + 1], twin)
        joint.start()
        if not has_prev:
            loads[1]["qkv"].start()
        for at in range(0, dqkv_ref.shape[1], 384):
            grad = tn(h_ref[...], dqkv_ref[:, at : at + 384])
            gw_ref[:, at : at + 384] = gw_ref[:, at : at + 384] + grad if has_prev else grad
        if not has_prev:
            loads[1]["h"].start()
        load["x"].wait()
        joint.wait()
        saves = tail_stage(
            has_prev, part_ref, x_ref, dx_ref, gain_one_ref, gone_ref, grad_out_ref, gone_ref,
            x1_ref, rx_ref, save_sems.at[pl.ds(micro * (rows // RB), rows // RB)],
        )
        if not has_prev:
            loads[1]["x"].start()
            for copy in saves:
                copy.wait()
            loads[1]["x1"].start()
            for copy in first_trade:
                copy.wait()
            loads[1]["dh"].start()
    cross.wait()
    own = go_ref[:, pl.ds(pl.multiple_of(core * half, 128), half)]
    gout_ref[...] = own + rgo_ref[...].astype(F32)
    row = lax.broadcasted_iota(jnp.int32, (128, D), 0)
    small = jnp.where(row == 0, gone_ref[...], 0.0) + jnp.where(row == 1, gtwo_ref[...], 0.0)
    small = small + jnp.where(row == 2 + me, gc0_ref[...] + gc1_ref[...], 0.0)
    small_ref[...] = jnp.transpose(small)
    part = packed_ref.shape[1] // 2

    def pack(chunk, carry):
        top = pl.ds(pl.multiple_of(chunk * part, 8), part)
        low = pl.ds(pl.multiple_of(D // 2 + chunk * part, 8), part)
        for ref, at, size in ((gw_ref, 0, 3 * half), (gout_ref, 3 * half, half), (small_ref, 4 * half, 128)):
            both = jnp.concatenate([ref[top, :], ref[low, :]], axis=0)
            packed_ref[chunk, :, at : at + size] = both.astype(BF)
        return carry

    lax.fori_loop(0, packed_ref.shape[0], pack, 0)

    def between(roles):
        swaps.extend(trade(give_y1_ref, take_y1_ref, y1_send, y1_recv, sems.at[20], roles))

    scatter_stage(
        packed_ref, gqkv_ref, gproj_ref, gsmall_ref, theirs_ref, rx1_ref, rx2_ref, rx3_ref, tx1_ref,
        tx2_ref, sum_ref, ring_send, ring_recv, between,
    )
    for copy in saves + swaps:
        copy.wait()


def back(dh, target, g, x, w_all, wo, labels, gains, gc0, gc1, kept0, kept1, *give):
    x1, _, h_all, _, _ = kept0
    rows, seq, half = x1.shape[0], h_all.shape[0], D // 2
    groups = dh.shape[0]
    chunk = (2 * D // (2 * groups), 4 * half + 128)
    part = chunk[0] // 2
    in_hbm = lambda array: pltpu.with_memory_space_constraint(array, pltpu.HBM)
    kept = lambda arrays: [in_hbm(array) for array in arrays[:4]] + [arrays[4]]
    args = [in_hbm(dh), target, in_hbm(g), in_hbm(x), in_hbm(w_all), in_hbm(wo), labels, gains, gc0, gc1]
    args += kept(kept0) + kept(kept1) + [in_hbm(array) for array in give]
    kept_specs = [HBM_WHOLE] * 4 + [VMEM_WHOLE]
    return pl.pallas_call(
        back_kernel,
        out_shape=(
            jax.ShapeDtypeStruct((part, 3 * D), F32),
            jax.ShapeDtypeStruct((part, D), F32),
            jax.ShapeDtypeStruct((part, 128), F32),
            pltpu.HBM((rows, D), F32),
            pltpu.HBM((rows, D), F32),
        )
        + tuple(pltpu.HBM(array.shape, BF) for array in give),
        in_specs=[HBM_WHOLE, VMEM_WHOLE]
        + [HBM_WHOLE] * 4
        + [VMEM_WHOLE] * 4
        + kept_specs * 2
        + [HBM_WHOLE] * 5,
        out_specs=(VMEM_WHOLE,) * 3 + (HBM_WHOLE,) * 7,
        scratch_shapes=[
            pltpu.VMEM(dh.shape, BF),
            pltpu.VMEM((rows, D), BF),
            pltpu.VMEM((rows, D), BF),
            pltpu.VMEM((rows, D), F32),
            pltpu.VMEM((rows, D), BF),
            pltpu.VMEM((seq, D), BF),
            pltpu.VMEM((D, 2 * D), BF),
            pltpu.VMEM((D, D), BF),
            pltpu.VMEM((seq, 3 * half), BF),
            pltpu.VMEM((seq, half), BF),
            pltpu.VMEM((rows, D), F32),
            pltpu.VMEM((rows, D), BF),
            pltpu.VMEM((rows, D), BF),
            pltpu.VMEM((seq, D), F32),
            pltpu.VMEM((seq, 3 * half), BF),
            pltpu.VMEM((seq, half), F32),
            pltpu.VMEM((seq, half), F32),
            pltpu.VMEM((half, seq), BF),
            pltpu.VMEM((seq, 1), F32),
            pltpu.VMEM((rows, D), BF),
            pltpu.VMEM((rows, D), BF),
            pltpu.VMEM((D, D), F32),
            pltpu.VMEM((D, half), BF),
            pltpu.VMEM((D, half), BF),
            pltpu.VMEM((D, 3 * half), F32),
            pltpu.VMEM((D, half), F32),
            pltpu.VMEM((1, D), F32),
            pltpu.VMEM((1, D), F32),
            pltpu.VMEM((groups,) + chunk, BF),
            pltpu.VMEM((D, 128), F32),
            pltpu.VMEM((part, chunk[1]), F32),
            pltpu.VMEM((8,) + chunk, BF),
            pltpu.VMEM((4,) + chunk, BF),
            pltpu.VMEM((3,) + chunk, BF),
            pltpu.VMEM((4,) + chunk, BF),
            pltpu.VMEM((3,) + chunk, BF),
            pltpu.VMEM(chunk, F32),
            pltpu.SemaphoreType.DMA((21,)),
            pltpu.SemaphoreType.DMA((MICRO * (rows // RB),)),
        ]
        + [pltpu.SemaphoreType.DMA((16,))] * 6
        + [pltpu.SemaphoreType.DMA((9,))] * 2
        + [pltpu.SemaphoreType.DMA((16,))] * 2,
        compiler_params=pltpu.CompilerParams(
            collective_id=1, has_side_effects=True, vmem_limit_bytes=60 << 20
        ),
        cost_estimate=pl.CostEstimate(flops=4 << 33, bytes_accessed=60 << 20, transcendentals=0),
        name="back",
    )(*args)


def body_pair(
    tokens,
    cotangent,
    segment_ids,
    padding,
    routes,
    norm_one_gain,
    qkv_weight,
    out_weight,
    norm_two_gain,
    centroids,
    expert_in,
    expert_out,
):
    local_len = tokens.shape[2]
    experts = centroids.shape[1]
    capacity = max(2, 2 * local_len // experts)
    gains = jnp.stack([norm_one_gain, norm_two_gain]).astype(F32)
    x_all = tokens.reshape(MICRO * local_len, D)
    g_all = cotangent.reshape(MICRO * local_len, D)
    (w_all, out_full, h0, h1, labels, columns, centre, g0_in, g1_part, h0_in,
     qkv0, lse0, x10, full0, qkv1, lse1, x11, full1, sent1, g1_sent) = head(
        experts, capacity, qkv_weight, out_weight, segment_ids, padding,
        routes.reshape(MICRO, 1, local_len), x_all, g_all, centroids.T, gains
    )
    y0, dh0, gc0, gup, gdown, h1_in, g1_in = expert(
        h0_in, g0_in, centre, expert_in[0], expert_out[0], (sent1, g1_sent, g1_part), None
    )
    y1, dh1, gc1, own_up, own_down, sent_up, sent_down, dh0_in, y0a = expert(
        h1_in, g1_in, centre, expert_in[0], expert_out[0], (dh0, y0), (gup, gdown)
    )
    grad_qkv, grad_out, small, in0, in1, _, y0b, y1_in, got_up, got_down = back(
        dh0_in, columns, g_all, x_all, w_all, out_full, labels, gains, gc0, gc1,
        (x10, full0, h0, qkv0, lse0), (x11, full1, h1, qkv1, lse1),
        dh1, y0, y1, sent_up, sent_down,
    )
    block_out, grad_tokens, grad_up, grad_down, grad_qkv, grad_out, grad_one, grad_two, grad_centre = emit(
        x10, x11, y0a, y0b, y1_in, columns, in0, in1, own_up, got_up, own_down, got_down,
        grad_qkv, grad_out, small,
    )
    return (
        block_out.reshape(MICRO, 1, local_len, D),
        grad_tokens.reshape(MICRO, 1, local_len, D),
        grad_one.reshape(-1),
        grad_qkv,
        grad_out,
        grad_two.reshape(-1),
        grad_centre.T,
        grad_up[None],
        grad_down[None],
    )


def solution(mesh):
    plan = body_pair if (mesh.shape["ctx"], mesh.shape["shard"]) == (2, 16) else body
    in_specs = (
        P(None, "shard", "ctx", None),
        P(None, "shard", "ctx", None),
        P(None, "shard", "ctx"),
        P(None, "shard", "ctx"),
        P(None, "shard", "ctx", None),
        P(),
        P("shard", None),
        P("shard", None),
        P(),
        P(),
        P("shard", None, None),
        P("shard", None, None),
    )
    out_specs = (
        P(None, "shard", "ctx", None),
        P(None, "shard", "ctx", None),
        P(("ctx", "shard")),
        P(("ctx", "shard"), None),
        P(("ctx", "shard"), None),
        P(("ctx", "shard")),
        P(("ctx", "shard"), None),
        P("shard", None, "ctx"),
        P("shard", "ctx", None),
    )
    return jax.shard_map(plan, mesh=mesh, in_specs=in_specs, out_specs=out_specs, check_vma=False)
```

```python
import functools

import jax
import jax.numpy as jnp
from jax import lax
from jax.experimental import pallas as pl
from jax.experimental.pallas import tpu as pltpu
from jax.sharding import PartitionSpec as P

D = 768
HEADS = 12
HEAD_DIM = 64
FF = 3072
MICRO = 2


EPSILON = 1e-05
NEGATIVE = -1e30
HIGH = lax.Precision.HIGHEST


def layer_norm(values, gain_vec):
    centre = values - jnp.mean(values, axis=1, keepdims=True)
    spread = jnp.mean(centre * centre, axis=1, keepdims=True)
    return centre * lax.rsqrt(spread + EPSILON) * gain_vec


def gelu_tanh(values):
    return jax.nn.gelu(values, approximate=True)


def masked_scores(queries, key_heads, query_pos, key_pos, query_doc, key_doc, key_pad):
    scores = jnp.einsum(
        "qhd,khd->hqk", queries, key_heads, preferred_element_type=jnp.float32
    ) * HEAD_DIM ** (-0.5)
    allowed = (query_doc[:, None] == key_doc[None, :]) & (key_pos[None, :] <= query_pos[:, None])
    allowed = allowed & ((key_pad[None, :] == 1) | (key_pos[None, :] == query_pos[:, None]))
    return jnp.where(allowed[None], scores, NEGATIVE)


def rows_first(left, right):
    return lax.dot_general(
        left, right, (((0,), (0,)), ((), ())), preferred_element_type=jnp.float32
    )


def rows_last(left, right):
    return lax.dot_general(
        left, right, (((1,), (1,)), ((), ())), preferred_element_type=jnp.float32
    )


def body(
    tokens,
    cotangent,
    segment_ids,
    padding,
    routes,
    norm_one_gain,
    qkv_weight,
    out_weight,
    norm_two_gain,
    centroids,
    expert_in,
    expert_out,
):
    local_len = tokens.shape[2]
    experts = centroids.shape[1]
    capacity = max(2, 2 * local_len // experts)
    seq_len = local_len * lax.axis_size("ctx")
    qkv_full, out_full = (
        lax.all_gather(qkv_weight, "shard", axis=0, tiled=True),
        lax.all_gather(out_weight, "shard", axis=0, tiled=True),
    )
    gain_one = norm_one_gain.astype(jnp.float32)
    gain_two = norm_two_gain.astype(jnp.float32)
    centre_f = centroids.astype(jnp.float32)
    up_local = expert_in[0]
    down_local = expert_out[0]
    query_pos = lax.axis_index("ctx") * local_len + jnp.arange(local_len, dtype=jnp.int32)
    all_pos = jnp.arange(seq_len, dtype=jnp.int32)
    slot_ids = jnp.arange(experts * capacity, dtype=jnp.int32)
    expert_ids = jnp.arange(experts, dtype=jnp.int32)
    score_scale = HEAD_DIM ** (-0.5)
    grad_qkv_sum = jnp.zeros((D, 3 * D), jnp.float32)
    grad_out_sum = jnp.zeros((D, D), jnp.float32)
    grad_one_sum = jnp.zeros((D,), jnp.float32)
    grad_two_sum = jnp.zeros((D,), jnp.float32)
    grad_centre = jnp.zeros((D, experts), jnp.float32)
    grad_up_sum = jnp.zeros((D, FF), jnp.float32)
    grad_down_sum = jnp.zeros((D, FF), jnp.float32)
    block_list = []
    input_list = []
    for micro_index in range(MICRO):
        inputs = tokens[micro_index, 0].astype(jnp.float32)
        doc_ids = segment_ids[micro_index, 0]
        pad_mask = padding[micro_index, 0]
        route_ids = routes[micro_index, 0, :, 0]
        normed_one, norm_one_back = jax.vjp(layer_norm, inputs, gain_one)
        first_bf = normed_one.astype(jnp.bfloat16)
        qkv = jnp.dot(first_bf, qkv_full, preferred_element_type=jnp.float32)
        queries = qkv[:, :D].astype(jnp.bfloat16)
        key_rows = qkv[:, D : 2 * D].astype(jnp.bfloat16)
        value_rows = qkv[:, 2 * D :].astype(jnp.bfloat16)
        key_all, value_all, doc_all, pad_all = (
            lax.all_gather(key_rows, "ctx", axis=0, tiled=True),
            lax.all_gather(value_rows, "ctx", axis=0, tiled=True),
            lax.all_gather(doc_ids, "ctx", axis=0, tiled=True),
            lax.all_gather(pad_mask, "ctx", axis=0, tiled=True),
        )
        query_heads = queries.reshape(local_len, HEADS, HEAD_DIM)
        key_heads = key_all.reshape(seq_len, HEADS, HEAD_DIM)
        value_heads = value_all.reshape(seq_len, HEADS, HEAD_DIM)
        scores = masked_scores(
            query_heads, key_heads, query_pos, all_pos, doc_ids, doc_all, pad_all
        )
        row_max = jnp.max(scores, axis=2, keepdims=True)
        weights = jnp.exp(scores - row_max)
        row_total = jnp.sum(weights, axis=2, keepdims=True)
        probs_now = weights / row_total
        log_total = row_max + jnp.log(row_total)
        attended = jnp.einsum(
            "hqk,khd->qhd",
            probs_now.astype(jnp.bfloat16),
            value_heads,
            preferred_element_type=jnp.float32,
        )
        attended = attended.reshape(local_len, D).astype(jnp.bfloat16)
        residual = inputs + jnp.dot(attended, out_full, preferred_element_type=jnp.float32)
        normed_two, norm_two_back = jax.vjp(layer_norm, residual, gain_two)
        second_bf = normed_two.astype(jnp.bfloat16)
        choose_mask = route_ids[:, None] == expert_ids[None, :]
        choose_f = choose_mask.astype(jnp.float32)
        logit = jnp.sum(
            jnp.dot(second_bf, centroids, preferred_element_type=jnp.float32) * choose_f, axis=1
        )
        gate_value = jax.nn.sigmoid(logit)
        choose_int = choose_mask.astype(jnp.int32)
        counts = jnp.cumsum(choose_int, axis=0)
        slot_rank = jnp.sum(counts * choose_int, axis=1) - 1
        target = route_ids * capacity + slot_rank
        dispatch = (slot_ids[:, None] == target[None, :]).astype(jnp.bfloat16)
        outbound = jnp.dot(dispatch, second_bf, preferred_element_type=jnp.float32).astype(
            jnp.bfloat16
        )
        outbound = outbound.reshape(experts, capacity, D)
        received = lax.all_to_all(outbound, "shard", split_axis=0, concat_axis=0, tiled=True)
        slot_rows = received.reshape(-1, D)
        upward = jnp.dot(slot_rows, up_local, preferred_element_type=jnp.float32)
        hidden = gelu_tanh(upward).astype(jnp.bfloat16)
        result = jnp.dot(hidden, down_local, preferred_element_type=jnp.float32).astype(
            jnp.bfloat16
        )
        returned = lax.all_to_all(
            result.reshape(received.shape), "shard", split_axis=0, concat_axis=0, tiled=True
        )
        returned, received, upward = (
            returned,
            received,
            upward.reshape(received.shape[0], received.shape[1], FF),
        )
        expert_rows = rows_first(dispatch, returned.reshape(experts * capacity, D))
        block_list.append((residual + gate_value[:, None] * expert_rows).astype(jnp.bfloat16))
        grad_out = cotangent[micro_index, 0].astype(jnp.float32)
        grad_gate = jnp.sum(grad_out * expert_rows, axis=1)
        grad_logit = grad_gate * gate_value * (1.0 - gate_value)
        grad_rows = (gate_value[:, None] * grad_out).astype(jnp.bfloat16)
        grad_outbound = jnp.dot(dispatch, grad_rows, preferred_element_type=jnp.float32).astype(
            jnp.bfloat16
        )
        grad_received = lax.all_to_all(
            grad_outbound.reshape(experts, capacity, D),
            "shard",
            split_axis=0,
            concat_axis=0,
            tiled=True,
        )
        grad_result = grad_received.reshape(-1, D)
        hidden_again, gelu_back = jax.vjp(gelu_tanh, upward.reshape(-1, FF))
        grad_down_sum = grad_down_sum + rows_first(grad_result, hidden_again.astype(jnp.bfloat16))
        grad_hidden = rows_last(grad_result, down_local)
        grad_upward = gelu_back(grad_hidden)[0].astype(jnp.bfloat16)
        grad_up_sum = grad_up_sum + rows_first(received.reshape(-1, D), grad_upward)
        grad_send = (
            rows_last(grad_upward, up_local).astype(jnp.bfloat16).reshape(grad_received.shape)
        )
        grad_back = lax.all_to_all(grad_send, "shard", split_axis=0, concat_axis=0, tiled=True)
        grad_second = rows_first(dispatch, grad_back.reshape(experts * capacity, D))
        grad_second = grad_second + grad_logit[:, None] * jnp.dot(
            choose_f, centre_f.T, precision=HIGH
        )
        grad_centre = grad_centre + jnp.dot(
            second_bf.astype(jnp.float32).T, choose_f * grad_logit[:, None], precision=HIGH
        )
        grad_resid_norm, grad_two_term = norm_two_back(grad_second)
        grad_residual = grad_out + grad_resid_norm
        grad_two_sum = grad_two_sum + grad_two_term
        grad_branch = grad_residual.astype(jnp.bfloat16)
        grad_out_sum = grad_out_sum + rows_first(attended, grad_branch)
        grad_attend = (
            rows_last(grad_branch, out_full)
            .astype(jnp.bfloat16)
            .reshape(local_len, HEADS, HEAD_DIM)
        )
        probs_again = jnp.exp(
            masked_scores(query_heads, key_heads, query_pos, all_pos, doc_ids, doc_all, pad_all)
            - log_total
        )
        grad_probs = jnp.einsum(
            "qhd,khd->hqk", grad_attend, value_heads, preferred_element_type=jnp.float32
        )
        row_terms = jnp.sum(probs_again * grad_probs, axis=2, keepdims=True)
        grad_scores = (probs_again * (grad_probs - row_terms)).astype(jnp.bfloat16)
        grad_query = (
            jnp.einsum("hqk,khd->qhd", grad_scores, key_heads, preferred_element_type=jnp.float32)
            * score_scale
        )
        grad_key_all = (
            jnp.einsum("hqk,qhd->khd", grad_scores, query_heads, preferred_element_type=jnp.float32)
            * score_scale
        )
        grad_value_all = jnp.einsum(
            "hqk,qhd->khd",
            probs_again.astype(jnp.bfloat16),
            grad_attend,
            preferred_element_type=jnp.float32,
        )
        grad_key, grad_value = (
            lax.psum_scatter(
                grad_key_all.reshape(seq_len, D).astype(jnp.bfloat16),
                "ctx",
                scatter_dimension=0,
                tiled=True,
            ).astype(jnp.float32),
            lax.psum_scatter(
                grad_value_all.reshape(seq_len, D).astype(jnp.bfloat16),
                "ctx",
                scatter_dimension=0,
                tiled=True,
            ).astype(jnp.float32),
        )
        grad_qkv_rows = jnp.concatenate(
            [grad_query.reshape(local_len, D), grad_key, grad_value], axis=1
        ).astype(jnp.bfloat16)
        grad_qkv_sum = grad_qkv_sum + rows_first(first_bf, grad_qkv_rows)
        grad_first = rows_last(grad_qkv_rows, qkv_full)
        grad_in_norm, grad_one_term = norm_one_back(grad_first)
        grad_one_sum = grad_one_sum + grad_one_term
        input_list.append(grad_residual + grad_in_norm)
    dense_sums = (
        lax.psum_scatter(grad_one_sum, ("ctx", "shard"), scatter_dimension=0, tiled=True),
        lax.psum_scatter(grad_qkv_sum, ("ctx", "shard"), scatter_dimension=0, tiled=True),
        lax.psum_scatter(grad_out_sum, ("ctx", "shard"), scatter_dimension=0, tiled=True),
        lax.psum_scatter(grad_two_sum, ("ctx", "shard"), scatter_dimension=0, tiled=True),
        lax.psum_scatter(grad_centre, ("ctx", "shard"), scatter_dimension=0, tiled=True),
    )
    expert_sums = (
        lax.psum_scatter(
            grad_up_sum.astype(jnp.bfloat16), "ctx", scatter_dimension=1, tiled=True
        ).astype(jnp.float32),
        lax.psum_scatter(
            grad_down_sum.astype(jnp.bfloat16), "ctx", scatter_dimension=1, tiled=True
        ).astype(jnp.float32),
    )
    block_out = jnp.stack(block_list)[:, None]
    grad_tokens = jnp.stack(input_list)[:, None]
    return (
        block_out,
        grad_tokens,
        dense_sums[0],
        dense_sums[1],
        dense_sums[2],
        dense_sums[3],
        dense_sums[4],
        expert_sums[0][None],
        expert_sums[1].T[None],
    )


BF = jnp.bfloat16
F32 = jnp.float32
QB = 256
AB = 512
GELU_K = 0.7978845608028654
VMEM_WHOLE = pl.BlockSpec(memory_space=pltpu.VMEM)
HBM_WHOLE = pl.BlockSpec(memory_space=pltpu.HBM)


def nn(left, right):
    return lax.dot_general(left, right, (((1,), (0,)), ((), ())), preferred_element_type=F32)


def nt(left, right):
    return lax.dot_general(left, right, (((1,), (1,)), ((), ())), preferred_element_type=F32)


def tn(left, right):
    return lax.dot_general(left, right, (((0,), (0,)), ((), ())), preferred_element_type=F32)


def lanes_of(shape, half):
    lane = lax.broadcasted_iota(jnp.int32, shape, 1)
    return (lane < HEAD_DIM) if half == 0 else (lane >= HEAD_DIM)


def masks_of(label_ref, micro):
    doc = label_ref[micro : micro + 1, :].astype(F32)
    real = label_ref[MICRO + micro : MICRO + micro + 1, :] == 1
    return doc, jnp.where(real, doc, -1.0)


def as_column(row):
    return jnp.transpose(jnp.broadcast_to(row, (128, row.shape[1])))[:, 0:1]


def attend_kernel(
    micro, h_ref, w_ref, label_ref, saved_ref, o_ref, lse_ref, col_ref, qkv_ref, sem
):
    seq, width = h_ref.shape[0], o_ref.shape[1]
    scale = HEAD_DIM ** (-0.5)
    doc_row, code_row = masks_of(label_ref, micro)
    col_ref[...] = as_column(doc_row)

    def project(block, carry):
        rows = pl.ds(block * AB, AB)
        qkv_ref[rows, :] = nn(h_ref[rows, :], w_ref[:, 0 : 3 * width]).astype(BF)
        return carry

    lax.fori_loop(0, seq // AB, project, 0)
    save = pltpu.make_async_copy(qkv_ref, saved_ref, sem)
    save.start()
    for block in range(seq // AB):
        low, kend = block * AB, (block + 1) * AB
        rows = slice(low, kend)
        qpos = lax.broadcasted_iota(jnp.int32, (AB, kend), 0) + low
        kpos = lax.broadcasted_iota(jnp.int32, (AB, kend), 1)
        same = col_ref[rows, :] == code_row[:, 0:kend]
        allowed = (same & (kpos < qpos)) | (kpos == qpos)
        bias = jnp.where(allowed, 0.0, NEGATIVE).astype(F32)
        lane = lax.broadcasted_iota(jnp.int32, (AB, 128), 1)

        def pair(index, stats):
            at = pl.multiple_of(index * 128, 128)
            q = qkv_ref[rows, pl.ds(at, 128)] * jnp.asarray(scale, BF)
            k = qkv_ref[0:kend, pl.ds(width + at, 128)]
            v = qkv_ref[0:kend, pl.ds(2 * width + at, 128)]
            outs = []
            for half in range(2):
                qm = jnp.where(lanes_of(q.shape, half), q, jnp.zeros_like(q))
                s = nt(qm, k) + bias
                top = jnp.max(s, axis=1, keepdims=True)
                e = jnp.exp(s - top)
                total = jnp.sum(e, axis=1, keepdims=True)
                outs.append(nn(e.astype(BF), v) * (1.0 / total))
                stats = jnp.where(lane == 2 * index + half, top + jnp.log(total), stats)
            o_ref[rows, pl.ds(at, 128)] = jnp.where(
                lanes_of(outs[0].shape, 0), outs[0], outs[1]
            ).astype(BF)
            return stats

        stats = lax.fori_loop(0, width // 128, pair, jnp.zeros((AB, 128), F32), unroll=True)
        lse_ref[:, rows] = jnp.transpose(stats)[0 : lse_ref.shape[0], :]
    save.wait()


def attend_back_kernel(
    micro, qkv_ref, do_ref, lse_ref, label_ref, dqkv_ref, dk_ref, dv_ref, kt_ref, col_ref
):
    seq, width = do_ref.shape
    doc_row, code_row = masks_of(label_ref, micro)
    col_ref[...] = as_column(code_row)
    scale = HEAD_DIM ** (-0.5)
    dk_ref[...] = jnp.zeros_like(dk_ref)
    dv_ref[...] = jnp.zeros_like(dv_ref)
    kt_ref[...] = jnp.transpose(qkv_ref[:, width : 2 * width])
    for block in range(seq // AB):
        low, kend = block * AB, (block + 1) * AB
        rows = slice(low, kend)
        qpos = lax.broadcasted_iota(jnp.int32, (kend, AB), 1) + low
        kpos = lax.broadcasted_iota(jnp.int32, (kend, AB), 0)
        same = doc_row[:, rows] == col_ref[0:kend, :]
        allowed = (same & (kpos < qpos)) | (kpos == qpos)
        bias = jnp.where(allowed, 0.0, NEGATIVE).astype(F32)

        def pair(index, carry):
            at = pl.multiple_of(index * 128, 128)
            q = qkv_ref[rows, pl.ds(at, 128)] * jnp.asarray(scale, BF)
            k = qkv_ref[0:kend, pl.ds(width + at, 128)]
            v = qkv_ref[0:kend, pl.ds(2 * width + at, 128)]
            do = do_ref[rows, pl.ds(at, 128)]
            dqt = jnp.zeros((128, AB), F32)
            dv = dk = None
            for half in range(2):
                keep = lanes_of(q.shape, half)
                qm = jnp.where(keep, q, jnp.zeros_like(q))
                dom = jnp.where(keep, do, jnp.zeros_like(do))
                p = jnp.exp(nt(k, qm) + bias - lse_ref[pl.ds(2 * index + half, 1), rows])
                dp = nt(v, dom)
                delta = jnp.sum(p * dp, axis=0, keepdims=True)
                ds = (p * (dp - delta)).astype(BF)
                dv_half = nn(p.astype(BF), dom)
                dk_half = nn(ds, qm)
                dv = dv_half if dv is None else dv + dv_half
                dk = dk_half if dk is None else dk + dk_half
                kt = kt_ref[pl.ds(pl.multiple_of(at + half * HEAD_DIM, HEAD_DIM), HEAD_DIM), 0:kend]
                dqt = nn(kt, ds) if half == 0 else jnp.concatenate([dqt, nn(kt, ds)], axis=0)
            dv_ref[0:kend, pl.ds(at, 128)] += dv
            dk_ref[0:kend, pl.ds(at, 128)] += dk
            dqkv_ref[rows, pl.ds(at, 128)] = (jnp.transpose(dqt) * scale).astype(BF)
            return carry

        lax.fori_loop(0, width // 128, pair, 0, unroll=True)
    dqkv_ref[:, width : 2 * width] = dk_ref[...].astype(BF)
    dqkv_ref[:, 2 * width :] = dv_ref[...].astype(BF)


def spread_stage(dqkv_ref, w_ref, dh_ref):
    seq, wide = dqkv_ref.shape

    def spread(block, carry):
        rows = pl.ds(pl.multiple_of(block * AB, AB), AB)
        dh_ref[rows, :] = nt(dqkv_ref[rows, :], w_ref[:, 0:wide])
        return carry

    lax.fori_loop(0, seq // AB, spread, 0)


def expert_kernel(has_prev, h_ref, g_ref, *refs):
    if has_prev:
        (c_ref, up_ref, down_ref, prev_up_ref, prev_down_ref, give_ref, extra_ref,
         y_out_ref, dh_out_ref, gc_ref, gup_ref, gdown_ref, sup_ref, sdown_ref, got_ref, more_ref,
         dz_ref, gate_ref, z_ref, acc_ref, a_ref, du_ref, y_ref, dh_ref, sems,
         swap_send, swap_recv, more_send, more_recv) = refs
        exchanges = (
            (give_ref, got_ref, swap_send, swap_recv, sems.at[8], ROLES),
            (extra_ref, more_ref, more_send, more_recv, sems.at[9], EARLY_0),
        )
    else:
        (c_ref, up_ref, down_ref, give_ref, extra_ref, _,
         y_out_ref, dh_out_ref, gc_ref, gup_ref, gdown_ref, got_ref, more_ref,
         dz_ref, gate_ref, z_ref, acc_ref, a_ref, du_ref, y_ref, dh_ref, sems,
         swap_send, swap_recv, more_send, more_recv) = refs
        exchanges = (
            (give_ref, got_ref, swap_send, swap_recv, sems.at[8], ROLES),
            (extra_ref, more_ref, more_send, more_recv, sems.at[9], LATE_G),
        )
    step, steps = pl.program_id(0), pl.num_programs(0)
    capacity = h_ref.shape[1]
    rows_all = h_ref.shape[0] * capacity
    blocks = rows_all // QB
    each = QB // capacity

    def take(ref, block):
        return ref[pl.ds(pl.multiple_of(block * each, each), each)].reshape(QB, D)

    @pl.when(step == 0)
    def _():
        def start(block, carry):
            rows = pl.ds(pl.multiple_of(block * QB, QB), QB)
            logit = jnp.sum(take(h_ref, block).astype(F32) * c_ref[...], axis=1, keepdims=True)
            gate = 1.0 / (1.0 + jnp.exp(-logit))
            gate_ref[rows, :] = gate
            dz_ref[rows, :] = (gate * take(g_ref, block).astype(F32)).astype(BF)
            z_ref[rows, :] = jnp.zeros((QB, D), F32)
            acc_ref[rows, :] = jnp.zeros((QB, D), F32)
            return carry

        greet([{"shard": chip} for chip in all_chips()[1:]])
        trade_all(*exchanges)
        lax.fori_loop(0, blocks, start, 0)

    def forward(block, carry):
        rows = pl.ds(pl.multiple_of(block * QB, QB), QB)
        u = nn(take(h_ref, block), up_ref[...])
        square = u * u
        t = jnp.tanh(GELU_K * u * (1.0 + 0.044715 * square))
        a = (0.5 * u * (1.0 + t)).astype(BF)
        slope = 0.5 * (1.0 + t) + 0.5 * u * (1.0 - t * t) * (
            GELU_K * (1.0 + 3 * 0.044715 * square)
        )
        a_ref[rows, :] = a
        z_ref[rows, :] += nn(a, down_ref[...])
        du = (nt(dz_ref[rows, :], down_ref[...]) * slope).astype(BF)
        du_ref[rows, :] = du
        acc_ref[rows, :] += nt(du, up_ref[...])
        return carry

    lax.fori_loop(0, blocks, forward, 0, unroll=True)
    gup = tn(h_ref[...].reshape(rows_all, D), du_ref[...])
    gdown = tn(a_ref[...], dz_ref[...])
    if has_prev:
        gup = gup + prev_up_ref[...]
        gdown = gdown + prev_down_ref[...]

        @pl.when(step < 2)
        def _():
            sup_ref[...] = gup.astype(BF)
            sdown_ref[...] = gdown.astype(BF)

        @pl.when(step >= 2)
        def _():
            gup_ref[...] = gup.astype(BF)
            gdown_ref[...] = gdown.astype(BF)
    else:
        gup_ref[...] = gup
        gdown_ref[...] = gdown

    @pl.when(step == steps - 1)
    def _():
        saves = []
        total = jnp.zeros((1, D), F32)
        for block in range(blocks):
            rows = slice(block * QB, (block + 1) * QB)
            group = slice(block * each, (block + 1) * each)
            z = z_ref[rows, :].astype(BF).astype(F32)
            gate = gate_ref[rows, :]
            dgate = jnp.sum(take(g_ref, block).astype(F32) * z, axis=1, keepdims=True)
            dlogit = dgate * gate * (1.0 - gate)
            y_ref[group] = (gate * z).astype(BF).reshape(each, capacity, D)
            dh = (acc_ref[rows, :] + dlogit * c_ref[...]).astype(BF)
            dh_ref[group] = dh.reshape(each, capacity, D)
            total = total + jnp.sum(dlogit * take(h_ref, block).astype(F32), axis=0, keepdims=True)
            saves += [
                pltpu.make_async_copy(
                    dh_ref.at[group], dh_out_ref.at[group], sems.at[2 * block]
                ),
                pltpu.make_async_copy(
                    y_ref.at[group], y_out_ref.at[group], sems.at[2 * block + 1]
                ),
            ]
            for save in saves[-2:]:
                save.start()
        gc_ref[...] = total
        for exchange in exchanges:
            saves += traded(*exchange)
        for save in saves:
            save.wait()


def expert(h_slots, g_slots, centre, up, down, give, prev):
    groups, capacity, _ = h_slots.shape
    rows = groups * capacity
    ff = up.shape[1]
    wide = ff // 3 if prev is None else ff // 4
    steps = ff // wide
    turn = lambda step: step
    if prev is not None:
        turn = lambda step: (step + 2 * (1 - lax.axis_index("ctx"))) % 4
    early = lambda step: step // 2 + (1 - step // 2) * step
    late = lambda step: (step // 2) * (step - 2)
    whole = lambda step: (0, 0)
    every = lambda step: (0, 0, 0)
    slot_block = (groups, capacity, D)
    up_block = pl.BlockSpec((D, wide), lambda step: (0, turn(step)))
    down_block = pl.BlockSpec((wide, D), lambda step: (turn(step), 0))
    in_specs = [
        pl.BlockSpec(slot_block, every, pipeline_mode=pl.Buffered(1)),
        pl.BlockSpec(slot_block, every, pipeline_mode=pl.Buffered(1)),
        pl.BlockSpec((1, D), whole),
        up_block,
        down_block,
    ]
    args = [h_slots, g_slots, centre, up, down]
    out_shape = [
        pltpu.HBM((groups, capacity, D), BF),
        pltpu.HBM((groups, capacity, D), BF),
        jax.ShapeDtypeStruct((1, D), F32),
    ]
    out_specs = [HBM_WHOLE, HBM_WHOLE, pl.BlockSpec((1, D), whole)]
    more = 2
    if prev is None:
        out_shape += [pltpu.HBM((D, ff), F32), pltpu.HBM((ff, D), F32)]
        out_specs += [up_block, down_block]
    else:
        for at in (late, early):
            out_shape += [pltpu.HBM((D, ff // 2), BF), pltpu.HBM((ff // 2, D), BF)]
            out_specs += [
                pl.BlockSpec((D, wide), lambda step, at=at: (0, at(step))),
                pl.BlockSpec((wide, D), lambda step, at=at: (at(step), 0)),
            ]
        in_specs += [up_block, down_block]
        args += list(prev)
    in_specs += [HBM_WHOLE] * len(give)
    args += list(give)
    out_shape += [pltpu.HBM((groups, capacity, D), BF)] * more
    out_specs += [HBM_WHOLE] * more
    return pl.pallas_call(
        functools.partial(expert_kernel, prev is not None),
        out_shape=tuple(out_shape),
        grid=(steps,),
        in_specs=in_specs,
        out_specs=tuple(out_specs),
        scratch_shapes=[
            pltpu.VMEM((rows, D), BF),
            pltpu.VMEM((rows, 1), F32),
            pltpu.VMEM((rows, D), F32),
            pltpu.VMEM((rows, D), F32),
            pltpu.VMEM((rows, wide), BF),
            pltpu.VMEM((rows, wide), BF),
            pltpu.VMEM((groups, capacity, D), BF),
            pltpu.VMEM((groups, capacity, D), BF),
            pltpu.SemaphoreType.DMA((10,)),
        ]
        + [pltpu.SemaphoreType.DMA((16,))] * (2 * more),
        input_output_aliases={7: 6} if prev is None else {},
        compiler_params=pltpu.CompilerParams(
            collective_id=2 if prev is None else 3, has_side_effects=True, vmem_limit_bytes=56 << 20
        ),
        cost_estimate=pl.CostEstimate(
            flops=12 * rows * D * ff, bytes_accessed=40 << 20, transcendentals=rows * ff
        ),
        name="expert",
    )(*args)


PARTS = 4


def emit_kernel(
    x0_ref, x1_ref, y0a_ref, y0b_ref, y1_ref, target_in_ref, in0_ref, in1_ref,
    own_up_ref, got_up_ref, own_down_ref, got_down_ref, gqkv_in_ref, gproj_in_ref, small_in_ref,
    out_ref, grad_ref, up_ref, down_ref, gqkv_ref, gproj_ref, one_ref, two_ref, centre_ref,
    target_ref, small_ref, x_ref, y_ref, in_ref, up_parts_ref, down_parts_ref, up_sum_ref, down_sum_ref, sems, sum_sems,
):
    rows = x0_ref.shape[0]
    groups, capacity, _ = y0a_ref.shape
    slots = groups * capacity
    chips = all_chips()
    sums = []
    for pair, (own_ref, got_ref, parts_ref, sum_ref, result_ref) in enumerate(
        (
            (own_up_ref, got_up_ref, up_parts_ref, up_sum_ref, up_ref),
            (own_down_ref, got_down_ref, down_parts_ref, down_sum_ref, down_ref),
        )
    ):
        size = own_ref.shape[0] // PARTS
        for part in range(PARTS):
            at = slice(part * size, (part + 1) * size)
            sem = 3 * (PARTS * pair + part)
            sums.append(
                (
                    pltpu.make_async_copy(own_ref.at[at, :], parts_ref.at[0, at, :], sum_sems.at[sem]),
                    pltpu.make_async_copy(got_ref.at[at, :], parts_ref.at[1, at, :], sum_sems.at[sem + 1]),
                    pltpu.make_async_copy(sum_ref.at[at, :], result_ref.at[at, :], sum_sems.at[sem + 2]),
                    parts_ref, sum_ref, at,
                )
            )
    loads, moves = [], []
    for micro, (x_in, grad_in, parts) in enumerate(
        (
            (x0_ref, in0_ref, ((y0a_ref, EARLY_0), (y0b_ref, LATE_0))),
            (x1_ref, in1_ref, ((y1_ref, ROLES),)),
        )
    ):
        mine = [pltpu.make_async_copy(x_in, x_ref.at[micro], sems.at[20 * micro])]
        for part_ref, roles in parts:
            mine += [
                pltpu.make_async_copy(
                    part_ref.at[chips[role]], y_ref.at[micro, chips[role]], sems.at[20 * micro + 1 + role]
                )
                for role in roles
            ]
        loads.append(mine)
        moves.append(
            (
                pltpu.make_async_copy(grad_in, in_ref.at[micro], sems.at[20 * micro + 17]),
                pltpu.make_async_copy(
                    in_ref.at[micro], grad_ref.at[micro * rows : (micro + 1) * rows, :],
                    sems.at[20 * micro + 18],
                ),
            )
        )
    few = [
        pltpu.make_async_copy(src, dst, sems.at[40 + at])
        for at, (src, dst) in enumerate(
            (
                (gqkv_in_ref, gqkv_ref),
                (gproj_in_ref, gproj_ref),
                (small_in_ref, small_ref),
                (target_in_ref, target_ref),
            )
        )
    ]
    for part in sums:
        part[0].start()
        part[1].start()
    for load in few + loads[0] + [moves[0][0]] + loads[1] + [moves[1][0]]:
        load.start()
    for load in few:
        load.wait()
    size, experts = small_ref.shape[0], centre_ref.shape[0]
    small = jnp.concatenate([small_ref[...], jnp.zeros((128 - size, 128), F32)], axis=0)
    small = jnp.transpose(small)
    one_ref[...] = small[0:1, 0:size]
    two_ref[...] = small[1:2, 0:size]
    centre_ref[...] = small[2 : 2 + experts, 0:size]
    for own, got, store, parts_ref, sum_ref, at in sums:
        own.wait()
        got.wait()
        sum_ref[at, :] = parts_ref[0, at, :].astype(F32) + parts_ref[1, at, :].astype(F32)
        store.start()
    for micro in range(MICRO):
        for load in loads[micro]:
            load.wait()
        moves[micro][0].wait()
        moves[micro][1].start()
        slot = lax.broadcasted_iota(jnp.int32, (rows, slots), 1)
        pick = (slot == target_ref[:, micro : micro + 1]).astype(F32).astype(BF)
        value = x_ref[micro] + nn(pick, y_ref[micro].reshape(slots, D))
        out_ref[micro * rows : (micro + 1) * rows, :] = value.astype(BF)
    for part in sums:
        part[2].wait()
    for move in moves:
        move[1].wait()


def emit(x0, x1, y0a, y0b, y1, target, in0, in1, own_up, got_up, own_down, got_down, gqkv, gproj, small):
    rows, size = x0.shape[0], small.shape[0]
    groups = y0a.shape[0]
    in_hbm = lambda array: pltpu.with_memory_space_constraint(array, pltpu.HBM)
    args = [x0, x1, y0a, y0b, y1, target, in0, in1, own_up, got_up, own_down, got_down, gqkv, gproj, small]
    return pl.pallas_call(
        emit_kernel,
        out_shape=(
            jax.ShapeDtypeStruct((MICRO * rows, D), BF),
            pltpu.HBM((MICRO * rows, D), F32),
            pltpu.HBM(own_up.shape, F32),
            pltpu.HBM(own_down.shape, F32),
            jax.ShapeDtypeStruct(gqkv.shape, F32),
            jax.ShapeDtypeStruct(gproj.shape, F32),
            jax.ShapeDtypeStruct((1, size), F32),
            jax.ShapeDtypeStruct((1, size), F32),
            jax.ShapeDtypeStruct((groups, size), F32),
        ),
        in_specs=[HBM_WHOLE] * 15,
        out_specs=(VMEM_WHOLE,) + (HBM_WHOLE,) * 3 + (VMEM_WHOLE,) * 5,
        scratch_shapes=[
            pltpu.VMEM(target.shape, jnp.int32),
            pltpu.VMEM(small.shape, F32),
            pltpu.VMEM((MICRO, rows, D), F32),
            pltpu.VMEM((MICRO,) + y0a.shape, BF),
            pltpu.VMEM((MICRO, rows, D), F32),
            pltpu.VMEM((2,) + own_up.shape, BF),
            pltpu.VMEM((2,) + own_down.shape, BF),
            pltpu.VMEM(own_up.shape, F32),
            pltpu.VMEM(own_down.shape, F32),
            pltpu.SemaphoreType.DMA((44,)),
            pltpu.SemaphoreType.DMA((6 * PARTS,)),
        ],
        compiler_params=pltpu.CompilerParams(vmem_limit_bytes=50 << 20),
        cost_estimate=pl.CostEstimate(
            flops=4 * rows * D * groups * y0a.shape[1], bytes_accessed=30 << 20, transcendentals=0
        ),
        name="emit",
    )(*[in_hbm(array) for array in args])


def greet(peers):
    barrier = pltpu.get_barrier_semaphore()
    for peer in peers:
        pl.semaphore_signal(
            barrier, inc=1, device_id=peer, device_id_type=pl.DeviceIdType.MESH
        )
    pl.semaphore_wait(barrier, len(peers))


def send(src, dst, send_sem, recv_sem, peer):
    return pltpu.make_async_remote_copy(
        src_ref=src,
        dst_ref=dst,
        send_sem=send_sem,
        recv_sem=recv_sem,
        device_id=peer,
        device_id_type=pl.DeviceIdType.MESH,
    )


def places():
    me, core = lax.axis_index("shard"), lax.axis_index("ctx")
    z, y, x = me // 4, (me // 2) % 2, me % 2
    along_y, along_x = me + 2 - 4 * y, me + 1 - 2 * x
    first = along_y * (1 - core) + along_x * core
    second = along_x * (1 - core) + along_y * core
    far = 4 * z + 3 - me % 4
    line = [z, z + 1 - 2 * (z % 2), (z + 2) % 4, 3 - z]
    return me, first, second, far, line


def all_chips():
    me, _, _, _, line = places()
    y, x = (me // 2) % 2, me % 2
    turns = [me % 4, me % 4 + 1 - 2 * x, me % 4 + 2 - 4 * y, 3 - me % 4]
    return [4 * line[j] + turns[i] for j in range(4) for i in range(4)]


ROLES = (8, 9, 10, 11, 12, 13, 14, 15, 4, 5, 6, 7, 1, 2, 3, 0)
EARLY_G, LATE_G = (8, 9, 10, 11, 12, 4, 5, 6, 1, 2, 0), (13, 14, 15, 7, 3)
EARLY_0, LATE_0 = (8, 4, 1), (9, 10, 11, 12, 13, 14, 15, 5, 6, 7, 2, 3, 0)
EARLY_1, NEXT_1, LATE_1 = (8, 4, 1), (9, 10, 11), (12, 13, 14, 15, 5, 6, 7, 2, 3, 0)


def traded(src_ref, dst_ref, send_sem, recv_sem, keep_sem, roles=ROLES):
    chips = all_chips()
    me = chips[0]
    copies = []
    for role in roles:
        if role:
            copies.append(
                send(
                    src_ref.at[chips[role]], dst_ref.at[me], send_sem.at[role], recv_sem.at[role],
                    {"shard": chips[role]},
                )
            )
        else:
            copies.append(pltpu.make_async_copy(src_ref.at[me], dst_ref.at[me], keep_sem))
    return copies


def trade_all(*exchanges):
    copies = []
    for far in (True, False):
        for exchange in exchanges:
            roles = tuple(role for role in exchange[5] if (role >= 8) == far)
            copies += trade(*exchange[:5], roles)
    return copies


def trade(src_ref, dst_ref, send_sem, recv_sem, keep_sem, roles=ROLES):
    copies = traded(src_ref, dst_ref, send_sem, recv_sem, keep_sem, roles)
    for copy in copies:
        copy.start()
    return copies


def head_kernel(
    experts, capacity, qkv_ref, proj_ref, seg_ref, pad_ref, route_ref, tok_ref, cot_ref,
    centroid_ref, gain_in_ref, gain_two_in_ref,
    out_save_ref, full_save_ref, h0_save_ref, h1_save_ref, all_save_ref, column_save_ref, centre_ref,
    in0_ref, in1_ref,
    take_ref, saved0_ref, lse0_save_ref, x10_ref, attended0_ref, saved1_ref, lse1_save_ref, x11_ref,
    attended1_ref, sent_ref, given_ref, gains_save_ref,
    gains_ref, raw_one_ref, raw_two_ref, all_ref, target_ref, column_ref, lse0_ref, lse1_ref, hub_ref, w_ref, x_ref, g_ref, label_ref, slots_ref, out_ref, full_ref, h0_ref, h1_ref,
    col_ref, heads_ref, o_ref, first_ref, x1_ref, joined0_ref, joined1_ref, h2_ref,
    send_sem, recv_sem, swap_send, swap_recv, sems, post_sems,
):
    size = w_ref.shape[0]
    half = full_ref.shape[1] // 2
    wide = w_ref.shape[1] - half
    count = label_ref.shape[1]
    me, first, second, far, line = places()
    core = lax.axis_index("ctx")
    own = pl.multiple_of(core * half, 128)
    loads = [
        pltpu.make_async_copy(
            qkv_ref.at[:, pl.ds(2 * at * half + own, half)],
            w_ref.at[:, at * half : (at + 1) * half],
            sems.at[at],
        )
        for at in range(3)
    ]
    loads += [
        pltpu.make_async_copy(proj_ref.at[:, pl.ds(own, half)], w_ref.at[:, wide:], sems.at[3]),
        pltpu.make_async_copy(cot_ref, g_ref, sems.at[4]),
        pltpu.make_async_copy(tok_ref, x_ref, sems.at[5]),
    ]
    for load in loads:
        load.start()
    gain_ref, gain_two_ref = gains_ref.at[0:1, :], gains_ref.at[1:2, :]
    label_ref[...] = jnp.zeros_like(label_ref)
    names = [
        pltpu.make_async_copy(
            ref.at[micro], label_ref.at[MICRO * at + micro : MICRO * at + micro + 1, :],
            sems.at[16 + MICRO * at + micro],
        )
        for at, ref in enumerate((seg_ref, pad_ref, route_ref))
        for micro in range(MICRO)
    ]
    names += [
        pltpu.make_async_copy(centroid_ref, hub_ref, sems.at[15]),
        pltpu.make_async_copy(gain_in_ref, raw_one_ref, sems.at[27]),
        pltpu.make_async_copy(gain_two_in_ref, raw_two_ref, sems.at[28]),
    ]
    for name in names:
        name.start()
    twin = {"ctx": 1 - core}
    lines = [4 * z for z in line]
    y, x = (me // 2) % 2, me % 2
    turns = [me % 4, me % 4 + 1 - 2 * x, me % 4 + 2 - 4 * y, 3 - me % 4]

    def rows(block):
        return out_ref.at[pl.ds(pl.multiple_of(block * size, 16), size), :]

    chips = [lines[j] + turns[i] for j in range(4) for i in range(4)]
    peers = [{"shard": chips[4 * j]} for j in (1, 2, 3)]
    one, two = {"shard": first}, {"shard": second}
    greet([{"shard": chip} for chip in chips[1:]] + [twin])
    copies, share = [], []

    def push(block, role, peer, src=None):
        copy = send(
            rows(block) if src is None else src, rows(block), send_sem.at[role], recv_sem.at[role], peer
        )
        copy.start()
        copies.append(copy)

    def arrive(block, role):
        send(rows(block), rows(block), send_sem.at[0], recv_sem.at[role], one).wait_recv()

    for load in loads[:4]:
        load.wait()
    push(me, 3, one, w_ref)
    push(me, 7, two, w_ref)
    for j in (1, 2, 3):
        push(me, j - 1, peers[j - 1], w_ref)
    out_ref[pl.ds(pl.multiple_of(me * size, 16), size), :] = w_ref[...]
    for name in names:
        name.wait()
    gains_ref[0:1, :] = raw_one_ref[...].astype(F32).reshape(1, D)
    gains_ref[1:2, :] = raw_two_ref[...].astype(F32).reshape(1, D)
    mine = pl.ds(pl.multiple_of(core * count, 128), count)
    share.append(send(label_ref, all_ref.at[:, mine], send_sem.at[15], recv_sem.at[15], twin))
    share[0].start()
    all_ref[:, mine] = label_ref[...]

    before = lax.broadcasted_iota(jnp.int32, (count, count), 0)
    after = lax.broadcasted_iota(jnp.int32, (count, count), 1)
    upto = (before <= after).astype(F32).astype(BF)
    ids = lax.broadcasted_iota(jnp.int32, (experts, count), 0)
    target_ref[...] = jnp.zeros_like(target_ref)
    for micro in range(MICRO):
        route = label_ref[2 * MICRO + micro : 2 * MICRO + micro + 1, :]
        chosen = (ids == route).astype(F32)
        rank = jnp.sum(nn(chosen.astype(BF), upto) * chosen, axis=0, keepdims=True)
        target_ref[micro : micro + 1, :] = route * capacity + rank.astype(jnp.int32) - 1
    wide_target = jnp.concatenate(
        [target_ref[...].astype(F32), jnp.zeros((120, count), F32)], axis=0
    )
    column_ref[...] = jnp.transpose(wide_target)[:, 0:8].astype(jnp.int32)
    row = lax.broadcasted_iota(jnp.int32, (experts, D), 0)
    centre_ref[...] = jnp.sum(
        jnp.where(row == me, hub_ref[...].astype(F32), 0.0), axis=0, keepdims=True
    )

    def place(micro, group):
        slot = lax.broadcasted_iota(jnp.int32, (4 * capacity, count), 0) + group * capacity
        pick = (slot == target_ref[micro : micro + 1, :]).astype(F32).astype(BF)
        value = nn(pick, g_ref[micro * count : (micro + 1) * count, :]).astype(BF)
        slots_ref[micro, pl.ds(pl.multiple_of(group, 4), 4)] = value.reshape(4, capacity, D)

    swaps = []

    def pass_one(micro, role):
        copy = send(
            slots_ref.at[micro, chips[role]],
            (in1_ref if micro else in0_ref).at[me],
            swap_send.at[16 * micro + role],
            swap_recv.at[16 * micro + role],
            {"shard": chips[role]},
        )
        copy.start()
        swaps.append(copy)

    def pass_on(micro, j):
        for i in range(4):
            if 4 * j + i:
                pass_one(micro, 4 * j + i)

    loads[4].wait()
    place(0, lines[2])
    pass_on(0, 2)

    def normed(micro, h_ref):
        def norm(block, carry):
            off = pl.multiple_of(block * RB, RB)
            unit = normal(x_ref[pl.ds(micro * count + off, RB), :].astype(F32))[0]
            at = pl.ds(pl.multiple_of(core * count + off, RB), RB)
            h_ref[at, :] = (unit * gain_ref[...]).astype(BF)
            return carry

        lax.fori_loop(0, count // RB, norm, 0)
        copy = send(
            h_ref.at[mine, :], h_ref.at[mine, :], send_sem.at[16 + micro], recv_sem.at[16 + micro], twin
        )
        copy.start()
        share.append(copy)

    arrive(lines[0] + first % 4, 3)
    push(lines[0] + first % 4, 11, two)
    block = lines[1] + me % 4
    arrive(block, 0)
    push(block, 4, one)
    push(block, 8, two)
    place(0, lines[3])
    pass_on(0, 3)
    loads[5].wait()
    normed(0, h0_ref)
    for j in (2, 3):
        block = lines[j] + me % 4
        arrive(block, j - 1)
        push(block, 3 + j, one)
        push(block, 7 + j, two)
        block = lines[j - 1] + first % 4
        arrive(block, 3 + j - 1)
        push(block, 11 + j - 1, two)
        if j == 2:
            place(0, lines[1])
            pass_on(0, 1)
    block = lines[3] + first % 4
    arrive(block, 6)
    push(block, 14, two)
    place(0, lines[0])
    pass_on(0, 0)
    normed(1, h1_ref)
    for group in range(0, experts, 4):
        place(1, group)
    saves = [
        pltpu.make_async_copy(slots_ref.at[0, me], in0_ref.at[me], sems.at[6]),
        pltpu.make_async_copy(slots_ref.at[1, me], in1_ref.at[me], sems.at[7]),
    ]
    for j in range(4):
        arrive(lines[j] + second % 4, 7 + j)
        arrive(lines[j] + far % 4, 11 + j)
    for role in EARLY_G:
        if role:
            pass_one(1, role)
    side = pl.ds(pl.multiple_of(core * half, 128), half)
    joint = send(
        out_ref.at[:, wide : wide + half], full_ref.at[:, side], send_sem.at[18], recv_sem.at[18], twin
    )
    joint.start()
    full_ref[:, side] = out_ref[:, wide : wide + half]
    for copy in share:
        copy.wait()
    saves += [
        pltpu.make_async_copy(out_ref, out_save_ref, sems.at[8]),
        pltpu.make_async_copy(h0_ref, h0_save_ref, sems.at[9]),
        pltpu.make_async_copy(h1_ref, h1_save_ref, sems.at[10]),
        pltpu.make_async_copy(slots_ref.at[1], given_ref, sems.at[22]),
        pltpu.make_async_copy(all_ref, all_save_ref, sems.at[23]),
        pltpu.make_async_copy(column_ref, column_save_ref, sems.at[24]),
        pltpu.make_async_copy(gains_ref, gains_save_ref, sems.at[29]),
        pltpu.make_async_copy(full_ref, full_save_ref, sems.at[11]),
    ]
    for save in saves[:-1]:
        save.start()
    attend_kernel(
        0, h0_ref, out_ref, all_ref, saved0_ref, o_ref, lse0_ref, col_ref, heads_ref, sems.at[12]
    )
    joint.wait()
    saves[-1].start()
    groups = [lines[j] for j in (2, 3, 1, 0)]
    steps = iter((2, 3, 1, 0))

    def hand_on(group):
        j = next(steps)
        for i in range(4):
            role = 4 * j + i
            if role:
                copy = send(
                    first_ref.at[0, chips[role]],
                    take_ref.at[me],
                    swap_send.at[32 + role],
                    swap_recv.at[32 + role],
                    {"shard": chips[role]},
                )
            else:
                copy = pltpu.make_async_copy(first_ref.at[0, me], take_ref.at[me], sems.at[13])
            copy.start()
            swaps.append(copy)

    post_stage(
        0, capacity, groups, x_ref, o_ref, full_ref, gain_two_ref, target_ref, hand_on, x10_ref,
        attended0_ref, first_ref.at[0], x1_ref, joined0_ref, h2_ref, post_sems,
        send_sem.at[19], recv_sem.at[19],
    )
    attend_kernel(
        1, h1_ref, out_ref, all_ref, saved1_ref, o_ref, lse1_ref, col_ref, heads_ref, sems.at[12]
    )
    post_stage(
        1, capacity, groups, x_ref, o_ref, full_ref, gain_two_ref, target_ref, lambda group: None,
        x11_ref, attended1_ref, first_ref.at[1], x1_ref, joined1_ref, h2_ref, post_sems,
        send_sem.at[20], recv_sem.at[20],
    )
    late = [
        pltpu.make_async_copy(first_ref.at[1], sent_ref, sems.at[14]),
        pltpu.make_async_copy(lse0_ref, lse0_save_ref, sems.at[25]),
        pltpu.make_async_copy(lse1_ref, lse1_save_ref, sems.at[26]),
    ]
    for save in late:
        save.start()
    saves += late
    for copy in copies:
        copy.wait_send()
    for save in saves:
        save.wait()
    for copy in swaps:
        copy.wait()


def head(experts, capacity, qkv_weight, out_weight, seg, pad, route, x, g, centroids, gain, gain_two):
    size, columns = qkv_weight.shape[0], 2 * D
    count = seg.shape[2]
    half = D // 2
    in_hbm = lambda array: pltpu.with_memory_space_constraint(array, pltpu.HBM)
    return pl.pallas_call(
        functools.partial(head_kernel, experts, capacity),
        out_shape=(
            pltpu.HBM((16 * size, columns), BF),
            pltpu.HBM((16 * size, D), BF),
            pltpu.HBM((2 * count, D), BF),
            pltpu.HBM((2 * count, D), BF),
            pltpu.HBM((8, 2 * count), jnp.int32),
            pltpu.HBM((count, 8), jnp.int32),
            jax.ShapeDtypeStruct((1, D), F32),
            pltpu.HBM((experts, capacity, D), BF),
            pltpu.HBM((experts, capacity, D), BF),
            pltpu.HBM((experts, capacity, D), BF),
        )
        + (
            pltpu.HBM((2 * count, 3 * half), BF),
            pltpu.HBM((8, 2 * count), F32),
            pltpu.HBM((count, D), F32),
            pltpu.HBM((count, D), BF),
        )
        * 2
        + (pltpu.HBM((experts, capacity, D), BF),) * 2
        + (pltpu.HBM((MICRO, D), F32),),
        in_specs=[HBM_WHOLE] * 10,
        out_specs=(HBM_WHOLE,) * 6 + (VMEM_WHOLE,) + (HBM_WHOLE,) * 14,
        scratch_shapes=[
            pltpu.VMEM((MICRO, D), F32),
            pltpu.VMEM((D,), BF),
            pltpu.VMEM((D,), BF),
            pltpu.VMEM((8, 2 * count), jnp.int32),
            pltpu.VMEM((8, count), jnp.int32),
            pltpu.VMEM((count, 8), jnp.int32),
            pltpu.VMEM((8, 2 * count), F32),
            pltpu.VMEM((8, 2 * count), F32),
            pltpu.VMEM((experts, D), BF),
            pltpu.VMEM((size, columns), BF),
            pltpu.VMEM((MICRO * count, D), BF),
            pltpu.VMEM((MICRO * count, D), BF),
            pltpu.VMEM((8, count), jnp.int32),
            pltpu.VMEM((MICRO, experts, capacity, D), BF),
            pltpu.VMEM((16 * size, columns), BF),
            pltpu.VMEM((16 * size, D), BF),
            pltpu.VMEM((2 * count, D), BF),
            pltpu.VMEM((2 * count, D), BF),
            pltpu.VMEM((2 * count, 1), F32),
            pltpu.VMEM((2 * count, 3 * half), BF),
            pltpu.VMEM((2 * count, half), BF),
            pltpu.VMEM((MICRO, experts, capacity, D), BF),
            pltpu.VMEM((count, D), F32),
            pltpu.VMEM((count, D), BF),
            pltpu.VMEM((count, D), BF),
            pltpu.VMEM((count, D), BF),
            pltpu.SemaphoreType.DMA((21,)),
            pltpu.SemaphoreType.DMA((21,)),
            pltpu.SemaphoreType.DMA((48,)),
            pltpu.SemaphoreType.DMA((48,)),
            pltpu.SemaphoreType.DMA((30,)),
            pltpu.SemaphoreType.DMA((2,)),
        ],
        compiler_params=pltpu.CompilerParams(
            collective_id=0, has_side_effects=True, vmem_limit_bytes=52 << 20
        ),
        cost_estimate=pl.CostEstimate(flops=0, bytes_accessed=100 << 20, transcendentals=0),
        name="head",
    )(
        in_hbm(qkv_weight), in_hbm(out_weight), in_hbm(seg), in_hbm(pad), in_hbm(route), in_hbm(x),
        in_hbm(g), in_hbm(centroids), in_hbm(gain), in_hbm(gain_two),
    )


def scatter_stage(
    packed_ref, few, gqkv_ref, gout_ref, gsmall_ref,
    theirs_ref, rx1_ref, rx2_ref, rx3_ref, tx1_ref, tx2_ref, sum_ref, send_sem, recv_sem, between,
):
    me, first, second, far, line = places()
    core = lax.axis_index("ctx")
    lines = [4 * z for z in line]
    part = sum_ref.shape[0] // 2
    half = gout_ref.shape[1] // 2
    wide = 3 * half
    peers = [{"shard": lines[j] + me % 4} for j in (1, 2, 3)]
    one, two, twin = {"shard": first}, {"shard": second}, {"ctx": 1 - core}
    order = (3, 2, 1, 0)
    copies = []

    def push(src, dst, role, peer):
        copy = send(src, dst, send_sem.at[role], recv_sem.at[role], peer)
        copy.start()
        copies.append(copy)

    def arrive(dst, role):
        send(dst, dst, send_sem.at[role], recv_sem.at[role], one).wait_recv()

    for j in order:
        push(packed_ref.at[lines[j] + far % 4], rx1_ref.at[j], j, two)
    for j in order:
        push(packed_ref.at[lines[j] + second % 4], rx1_ref.at[4 + j], 4 + j, two)
    between(0)
    for j in order:
        arrive(rx1_ref.at[j], j)
        total = packed_ref[lines[j] + first % 4].astype(F32) + rx1_ref[j].astype(F32)
        tx1_ref[j] = total.astype(BF)
        push(tx1_ref.at[j], rx2_ref.at[j], 8 + j, one)
    own = None
    for j in order:
        arrive(rx1_ref.at[4 + j], 4 + j)
        total = packed_ref[lines[j] + me % 4].astype(F32) + rx1_ref[4 + j].astype(F32)
        arrive(rx2_ref.at[j], 8 + j)
        total = total + rx2_ref[j].astype(F32)
        if j:
            tx2_ref[j - 1] = total.astype(BF)
            push(tx2_ref.at[j - 1], rx3_ref.at[j - 1], 11 + j, peers[j - 1])
        else:
            own = total
    between(1)
    for j in (1, 2, 3):
        arrive(rx3_ref.at[j - 1], 11 + j)
        own = own + rx3_ref[j - 1].astype(F32)
    for copy in traded(*few):
        copy.wait()
    sum_ref[:, 0 : wide + half] = own
    sum_ref[:, wide + half :] = jnp.sum(few[1][...], axis=0)
    push(
        sum_ref.at[pl.ds(pl.multiple_of((1 - core) * part, 8), part), :], theirs_ref, 15, twin
    )
    arrive(theirs_ref, 15)
    mine, theirs = sum_ref[pl.ds(pl.multiple_of(core * part, 8), part), :], theirs_ref[...]
    low = jnp.where(core == 0, mine, theirs)
    high = jnp.where(core == 0, theirs, mine)
    for at in range(3):
        gqkv_ref[:, 2 * at * half : (2 * at + 1) * half] = low[:, at * half : (at + 1) * half]
        gqkv_ref[:, (2 * at + 1) * half : (2 * at + 2) * half] = high[:, at * half : (at + 1) * half]
    gout_ref[:, 0:half] = low[:, wide : wide + half]
    gout_ref[:, half:] = high[:, wide : wide + half]
    gsmall_ref[...] = mine[:, wide + half :] + theirs[:, wide + half :]
    for copy in copies:
        copy.wait_send()


def normal(values):
    centre = values - jnp.mean(values, axis=1, keepdims=True)
    spread = jnp.mean(centre * centre, axis=1, keepdims=True)
    scale = lax.rsqrt(spread + EPSILON)
    return centre * scale, scale


def normal_back(unit, scale, gain, grad):
    pull = grad * gain
    return scale * (
        pull
        - jnp.mean(pull, axis=1, keepdims=True)
        - unit * jnp.mean(pull * unit, axis=1, keepdims=True)
    )


RB = 256


def post_stage(
    micro, capacity, groups, x_ref, o_ref, wo_ref, gain_ref, target_ref, hand_on, x1_out_ref, full_out_ref,
    slots_ref, x1_ref, full_ref, h_ref, sems, send_sem, recv_sem,
):
    core = lax.axis_index("ctx")
    rows, width = x1_ref.shape[0], o_ref.shape[1]
    twin = {"ctx": 1 - core}
    mine = pl.ds(pl.multiple_of(core * width, 128), width)
    copy = send(
        o_ref.at[pl.ds(pl.multiple_of((1 - core) * rows, 128), rows), :],
        full_ref.at[:, mine],
        send_sem,
        recv_sem,
        twin,
    )
    copy.start()
    full_ref[:, mine] = o_ref[pl.ds(pl.multiple_of(core * rows, 128), rows), :]
    copy.wait()

    def norm(block, carry):
        at = pl.ds(pl.multiple_of(block * RB, RB), RB)
        value = x_ref[pl.ds(micro * rows + pl.multiple_of(block * RB, RB), RB), :].astype(F32)
        value = value + nn(full_ref[at, :], wo_ref[...])
        x1_ref[at, :] = value
        h_ref[at, :] = (normal(value)[0] * gain_ref[...]).astype(BF)
        return carry

    lax.fori_loop(0, rows // RB, norm, 0)
    saves = [
        pltpu.make_async_copy(full_ref, full_out_ref, sems.at[0]),
        pltpu.make_async_copy(x1_ref, x1_out_ref, sems.at[1]),
    ]
    for save in saves:
        save.start()
    for group in groups:
        slot = lax.broadcasted_iota(jnp.int32, (4 * capacity, rows), 0) + group * capacity
        pick = (slot == target_ref[micro : micro + 1, :]).astype(F32).astype(BF)
        value = nn(pick, h_ref[...]).astype(BF).reshape(4, capacity, D)
        slots_ref[pl.ds(pl.multiple_of(group, 4), 4)] = value
        hand_on(group)
    for save in saves:
        save.wait()


def fore_stage(
    has_prev, micro, dh_ref, target_ref, g_ref, x1_ref, gain_ref, wo_ref, full_ref, prev_two_ref,
    do_ref, dx_ref, gout_ref, gtwo_ref, dy_ref, all_ref, send_sem, recv_sem,
):
    core = lax.axis_index("ctx")
    rows, width = x1_ref.shape[0], do_ref.shape[1]
    slots = dh_ref.shape[0] * dh_ref.shape[1]
    twin = {"ctx": 1 - core}

    def norm(block, total):
        at = pl.ds(pl.multiple_of(block * RB, RB), RB)
        slot = lax.broadcasted_iota(jnp.int32, (RB, slots), 1)
        pick = (slot == target_ref[at, micro : micro + 1]).astype(F32).astype(BF)
        grad = nn(pick, dh_ref[...].reshape(slots, D))
        unit, scale = normal(x1_ref[at, :])
        dx = g_ref[at, :].astype(F32) + normal_back(unit, scale, gain_ref[...], grad)
        dx_ref[at, :] = dx
        dy = dx.astype(BF)
        dy_ref[at, :] = dy
        all_ref[at, :] = nt(dy, wo_ref[...]).astype(BF)
        return total + jnp.sum(grad * unit, axis=0, keepdims=True)

    total = lax.fori_loop(0, rows // RB, norm, jnp.zeros((1, D), F32))
    gtwo_ref[...] = prev_two_ref[...] + total if has_prev else total
    mine = pl.ds(pl.multiple_of(core * rows, 128), rows)
    copy = send(
        all_ref.at[:, pl.ds(pl.multiple_of((1 - core) * width, 128), width)],
        do_ref.at[mine, :],
        send_sem,
        recv_sem,
        twin,
    )
    copy.start()
    do_ref[mine, :] = all_ref[:, pl.ds(pl.multiple_of(core * width, 128), width)]
    grad = tn(full_ref[...], dy_ref[...])
    gout_ref[...] = gout_ref[...] + grad if has_prev else grad
    copy.wait()


def tail_stage(
    has_prev, dh_ref, x_ref, dx_ref, gain_ref, prev_ref, grad_out_ref, gone_ref, grad_ref, rx_ref, sems
):
    core = lax.axis_index("ctx")
    rows = dx_ref.shape[0]
    saves = []
    total = jnp.zeros((1, D), F32)
    for off in range(0, rows, RB):
        at = slice(off, off + RB)
        mine = pl.ds(pl.multiple_of(core * rows + off, RB), RB)
        grad = dh_ref[mine, :] + rx_ref[at, :].astype(F32)
        unit, scale = normal(x_ref[at, :].astype(F32))
        grad_ref[at, :] = dx_ref[at, :] + normal_back(unit, scale, gain_ref[...], grad)
        save = pltpu.make_async_copy(grad_ref.at[at, :], grad_out_ref.at[at, :], sems.at[off // RB])
        save.start()
        saves.append(save)
        total = total + jnp.sum(grad * unit, axis=0, keepdims=True)
    gone_ref[...] = prev_ref[...] + total if has_prev else total
    return saves


def back_kernel(
    slot_ref, target_ref, cot_ref, tok_ref, w_in_ref, wo_in_ref, label_ref, gains_ref, gc0_ref, gc1_ref,
    x10_ref, full0_ref, h0_ref, qkv0_ref, lse0_ref, x11_ref, full1_ref, h1_ref, qkv1_ref, lse1_ref,
    give_dh_ref, give_y0_ref, give_y1_ref, give_up_ref, give_down_ref,
    gqkv_ref, gproj_ref, gsmall_ref, in0_ref, in1_ref, take_dh_ref, take_y0_ref, take_y1_ref,
    take_up_ref, take_down_ref,
    dh_ref, g_ref, x_ref, x1_ref, full_ref, h_ref, w_ref, wo_ref, qkv_ref,
    do_ref, dx_ref, dy_ref, all_ref, part_ref, dqkv_ref, dk_ref, dv_ref, kt_ref, col_ref,
    tx_ref, rx_ref, go_ref, tgo_ref, rgo_ref, gw_ref, gout_ref, gtwo_ref, gone_ref, packed_ref, small_ref,
    theirs_ref, rx1_ref, rx2_ref, rx3_ref, tx1_ref, tx2_ref, sum_ref, few_ref, few_rx_ref,
    sems, save_sems, dh_send, dh_recv, y0_send, y0_recv, y1_send, y1_recv, send_sem, recv_sem,
    ring_send, ring_recv, few_send, few_recv,
):
    me, core = lax.axis_index("shard"), lax.axis_index("ctx")
    rows = x_ref.shape[0]
    half = gout_ref.shape[1]
    twin = {"ctx": 1 - core}
    gain_one_ref, gain_two_ref = gains_ref.at[0:1, :], gains_ref.at[1:2, :]
    sources = (
        (x10_ref, full0_ref, h0_ref, qkv0_ref, lse0_ref, in0_ref),
        (x11_ref, full1_ref, h1_ref, qkv1_ref, lse1_ref, in1_ref),
    )

    def loads_of(micro):
        x1_in_ref, full_in_ref, h_in_ref, qkv_in_ref = sources[micro][:4]
        mine = pl.ds(micro * rows, rows)
        pairs = dict(
            dh=((slot_ref, take_dh_ref)[micro], dh_ref),
            x1=(x1_in_ref, x1_ref),
            g=(cot_ref.at[mine, :], g_ref),
            full=(full_in_ref, full_ref),
            qkv=(qkv_in_ref, qkv_ref),
            h=(h_in_ref, h_ref),
            x=(tok_ref.at[mine, :], x_ref),
        )
        return {
            name: pltpu.make_async_copy(src, dst, sems.at[8 * micro + at])
            for at, (name, (src, dst)) in enumerate(pairs.items())
        }

    loads = [loads_of(0), loads_of(1)]
    shared = [
        pltpu.make_async_copy(wo_in_ref, wo_ref, sems.at[16]),
        pltpu.make_async_copy(w_in_ref, w_ref, sems.at[17]),
    ]
    for name in ("dh", "x1", "g", "full"):
        loads[0][name].start()
    shared[0].start()
    for name in ("qkv", "h", "x"):
        loads[0][name].start()
    shared[1].start()
    greet([{"shard": chip} for chip in all_chips()[1:]] + [twin])
    first_trade = trade(give_dh_ref, take_dh_ref, dh_send, dh_recv, sems.at[18])
    swaps = trade_all(
        (give_y0_ref, take_y0_ref, y0_send, y0_recv, sems.at[19], LATE_0),
        (give_y1_ref, take_y1_ref, y1_send, y1_recv, sems.at[20], EARLY_1),
    )
    for micro in range(MICRO):
        has_prev = micro > 0
        load, lse_ref, grad_out_ref = loads[micro], sources[micro][4], sources[micro][5]
        for name in ("dh", "x1", "g", "full"):
            load[name].wait()
        if not has_prev:
            shared[0].wait()
        fore_stage(
            has_prev, micro, dh_ref, target_ref, g_ref, x1_ref, gain_two_ref, wo_ref, full_ref, gtwo_ref,
            do_ref, dx_ref, go_ref, gtwo_ref, dy_ref, all_ref, send_sem.at[3 * micro],
            recv_sem.at[3 * micro],
        )
        if has_prev:
            tgo_ref[...] = go_ref[:, pl.ds(pl.multiple_of((1 - core) * half, 128), half)].astype(BF)
            cross = send(tgo_ref, rgo_ref, send_sem.at[6], recv_sem.at[6], twin)
            cross.start()
        else:
            loads[1]["g"].start()
            loads[1]["full"].start()
            shared[1].wait()
        load["qkv"].wait()
        load["h"].wait()
        attend_back_kernel(
            micro, qkv_ref, do_ref, lse_ref, label_ref, dqkv_ref, dk_ref, dv_ref, kt_ref, col_ref
        )

        def weigh():
            for at in range(0, dqkv_ref.shape[1], 384):
                grad = tn(h_ref[...], dqkv_ref[:, at : at + 384])
                gw_ref[:, at : at + 384] = gw_ref[:, at : at + 384] + grad if has_prev else grad

        def hand_over():
            spread_stage(dqkv_ref, w_ref, part_ref)
            tx_ref[...] = part_ref[pl.ds(pl.multiple_of((1 - core) * rows, 128), rows), :].astype(BF)
            joint = send(tx_ref, rx_ref, send_sem.at[3 * micro + 1], recv_sem.at[3 * micro + 1], twin)
            joint.start()
            return joint

        def finish(joint):
            load["x"].wait()
            joint.wait()
            return tail_stage(
                has_prev, part_ref, x_ref, dx_ref, gain_one_ref, gone_ref, grad_out_ref, gone_ref,
                x1_ref, rx_ref, save_sems.at[pl.ds(micro * (rows // RB), rows // RB)],
            )

        if not has_prev:
            joint = hand_over()
            loads[1]["qkv"].start()
            weigh()
            loads[1]["h"].start()
            saves = finish(joint)
            loads[1]["x"].start()
            for copy in saves:
                copy.wait()
            loads[1]["x1"].start()
            for copy in first_trade:
                copy.wait()
            loads[1]["dh"].start()
    weigh()
    cross.wait()
    own = go_ref[:, pl.ds(pl.multiple_of(core * half, 128), half)]
    gout_ref[...] = own + rgo_ref[...].astype(F32)
    part = packed_ref.shape[1] // 2

    def cut(chunk):
        top = pl.ds(pl.multiple_of(chunk * part, 8), part)
        low = pl.ds(pl.multiple_of(D // 2 + chunk * part, 8), part)
        return lambda ref: jnp.concatenate([ref[top, :], ref[low, :]], axis=0)

    def pack(chunk, carry):
        both = cut(chunk)
        packed_ref[chunk, :, 0 : 3 * half] = both(gw_ref).astype(BF)
        packed_ref[chunk, :, 3 * half :] = both(gout_ref).astype(BF)
        return carry

    lax.fori_loop(0, packed_ref.shape[0], pack, 0)
    few = (few_ref, few_rx_ref, few_send, few_recv, sems.at[21])

    def between(step):
        roles = (NEXT_1, LATE_1)[step]
        swaps.extend(trade(give_y1_ref, take_y1_ref, y1_send, y1_recv, sems.at[20], roles))
        if step == 0:
            swaps.extend(finish(hand_over()))
            row = lax.broadcasted_iota(jnp.int32, (128, D), 0)
            small = jnp.where(row == 0, gone_ref[...], 0.0) + jnp.where(row == 1, gtwo_ref[...], 0.0)
            small = small + jnp.where(row == 2 + me, gc0_ref[...] + gc1_ref[...], 0.0)
            small_ref[...] = jnp.transpose(small)

            def pack_few(chunk, carry):
                few_ref[chunk] = cut(chunk)(small_ref)
                return carry

            lax.fori_loop(0, few_ref.shape[0], pack_few, 0)
            trade(*few)
            for at, (give_ref, take_ref) in enumerate(((give_up_ref, take_up_ref), (give_down_ref, take_down_ref))):
                swaps.append(send(give_ref, take_ref, send_sem.at[7 + at], recv_sem.at[7 + at], twin))
                swaps[-1].start()

    scatter_stage(
        packed_ref, few, gqkv_ref, gproj_ref, gsmall_ref, theirs_ref, rx1_ref, rx2_ref, rx3_ref, tx1_ref,
        tx2_ref, sum_ref, ring_send, ring_recv, between,
    )
    for copy in swaps:
        copy.wait()


def back(dh, target, g, x, w_all, wo, labels, gains, gc0, gc1, kept0, kept1, *give):
    x1, _, h_all, _, _ = kept0
    rows, seq, half = x1.shape[0], h_all.shape[0], D // 2
    groups = dh.shape[0]
    chunk = (D // groups, 4 * half)
    part = chunk[0] // 2
    in_hbm = lambda array: pltpu.with_memory_space_constraint(array, pltpu.HBM)
    kept = lambda arrays: [in_hbm(array) for array in arrays[:4]] + [arrays[4]]
    args = [in_hbm(dh), target, in_hbm(g), in_hbm(x), in_hbm(w_all), in_hbm(wo), labels, gains, gc0, gc1]
    args += kept(kept0) + kept(kept1) + [in_hbm(array) for array in give]
    kept_specs = [HBM_WHOLE] * 4 + [VMEM_WHOLE]
    return pl.pallas_call(
        back_kernel,
        out_shape=(
            jax.ShapeDtypeStruct((part, 3 * D), F32),
            jax.ShapeDtypeStruct((part, D), F32),
            jax.ShapeDtypeStruct((part, 128), F32),
            pltpu.HBM((rows, D), F32),
            pltpu.HBM((rows, D), F32),
        )
        + tuple(pltpu.HBM(array.shape, BF) for array in give),
        in_specs=[HBM_WHOLE, VMEM_WHOLE]
        + [HBM_WHOLE] * 4
        + [VMEM_WHOLE] * 4
        + kept_specs * 2
        + [HBM_WHOLE] * 5,
        out_specs=(VMEM_WHOLE,) * 3 + (HBM_WHOLE,) * 7,
        scratch_shapes=[
            pltpu.VMEM(dh.shape, BF),
            pltpu.VMEM((rows, D), BF),
            pltpu.VMEM((rows, D), BF),
            pltpu.VMEM((rows, D), F32),
            pltpu.VMEM((rows, D), BF),
            pltpu.VMEM((seq, D), BF),
            pltpu.VMEM((D, 2 * D), BF),
            pltpu.VMEM((D, D), BF),
            pltpu.VMEM((seq, 3 * half), BF),
            pltpu.VMEM((seq, half), BF),
            pltpu.VMEM((rows, D), F32),
            pltpu.VMEM((rows, D), BF),
            pltpu.VMEM((rows, D), BF),
            pltpu.VMEM((seq, D), F32),
            pltpu.VMEM((seq, 3 * half), BF),
            pltpu.VMEM((seq, half), F32),
            pltpu.VMEM((seq, half), F32),
            pltpu.VMEM((half, seq), BF),
            pltpu.VMEM((seq, 1), F32),
            pltpu.VMEM((rows, D), BF),
            pltpu.VMEM((rows, D), BF),
            pltpu.VMEM((D, D), F32),
            pltpu.VMEM((D, half), BF),
            pltpu.VMEM((D, half), BF),
            pltpu.VMEM((D, 3 * half), F32),
            pltpu.VMEM((D, half), F32),
            pltpu.VMEM((1, D), F32),
            pltpu.VMEM((1, D), F32),
            pltpu.VMEM((groups,) + chunk, BF),
            pltpu.VMEM((D, 128), F32),
            pltpu.VMEM((part, chunk[1] + 128), F32),
            pltpu.VMEM((8,) + chunk, BF),
            pltpu.VMEM((4,) + chunk, BF),
            pltpu.VMEM((3,) + chunk, BF),
            pltpu.VMEM((4,) + chunk, BF),
            pltpu.VMEM((3,) + chunk, BF),
            pltpu.VMEM((chunk[0], chunk[1] + 128), F32),
            pltpu.VMEM((groups, chunk[0], 128), F32),
            pltpu.VMEM((groups, chunk[0], 128), F32),
            pltpu.SemaphoreType.DMA((22,)),
            pltpu.SemaphoreType.DMA((MICRO * (rows // RB),)),
        ]
        + [pltpu.SemaphoreType.DMA((16,))] * 6
        + [pltpu.SemaphoreType.DMA((9,))] * 2
        + [pltpu.SemaphoreType.DMA((16,))] * 4,
        compiler_params=pltpu.CompilerParams(
            collective_id=1, has_side_effects=True, vmem_limit_bytes=60 << 20
        ),
        cost_estimate=pl.CostEstimate(flops=4 << 33, bytes_accessed=60 << 20, transcendentals=0),
        name="back",
    )(*args)


def body_pair(
    tokens,
    cotangent,
    segment_ids,
    padding,
    routes,
    norm_one_gain,
    qkv_weight,
    out_weight,
    norm_two_gain,
    centroids,
    expert_in,
    expert_out,
):
    local_len = tokens.shape[2]
    experts = centroids.shape[1]
    capacity = max(2, 2 * local_len // experts)
    x_all = tokens.reshape(MICRO * local_len, D)
    g_all = cotangent.reshape(MICRO * local_len, D)
    (w_all, out_full, h0, h1, labels, columns, centre, g0_in, g1_part, h0_in,
     qkv0, lse0, x10, full0, qkv1, lse1, x11, full1, sent1, g1_sent, gains) = head(
        experts, capacity, qkv_weight, out_weight, segment_ids, padding,
        routes.reshape(MICRO, 1, local_len), x_all, g_all, centroids.T,
        norm_one_gain, norm_two_gain,
    )
    y0, dh0, gc0, gup, gdown, h1_in, g1_in = expert(
        h0_in, g0_in, centre, expert_in[0], expert_out[0], (sent1, g1_sent, g1_part), None
    )
    y1, dh1, gc1, own_up, own_down, sent_up, sent_down, dh0_in, y0a = expert(
        h1_in, g1_in, centre, expert_in[0], expert_out[0], (dh0, y0), (gup, gdown)
    )
    grad_qkv, grad_out, small, in0, in1, _, y0b, y1_in, got_up, got_down = back(
        dh0_in, columns, g_all, x_all, w_all, out_full, labels, gains, gc0, gc1,
        (x10, full0, h0, qkv0, lse0), (x11, full1, h1, qkv1, lse1),
        dh1, y0, y1, sent_up, sent_down,
    )
    block_out, grad_tokens, grad_up, grad_down, grad_qkv, grad_out, grad_one, grad_two, grad_centre = emit(
        x10, x11, y0a, y0b, y1_in, columns, in0, in1, own_up, got_up, own_down, got_down,
        grad_qkv, grad_out, small,
    )
    return (
        block_out.reshape(MICRO, 1, local_len, D),
        grad_tokens.reshape(MICRO, 1, local_len, D),
        grad_one.reshape(-1),
        grad_qkv,
        grad_out,
        grad_two.reshape(-1),
        grad_centre.T,
        grad_up[None],
        grad_down[None],
    )


def solution(mesh):
    plan = body_pair if (mesh.shape["ctx"], mesh.shape["shard"]) == (2, 16) else body
    in_specs = (
        P(None, "shard", "ctx", None),
        P(None, "shard", "ctx", None),
        P(None, "shard", "ctx"),
        P(None, "shard", "ctx"),
        P(None, "shard", "ctx", None),
        P(),
        P("shard", None),
        P("shard", None),
        P(),
        P(),
        P("shard", None, None),
        P("shard", None, None),
    )
    out_specs = (
        P(None, "shard", "ctx", None),
        P(None, "shard", "ctx", None),
        P(("ctx", "shard")),
        P(("ctx", "shard"), None),
        P(("ctx", "shard"), None),
        P(("ctx", "shard")),
        P(("ctx", "shard"), None),
        P("shard", None, "ctx"),
        P("shard", "ctx", None),
    )
    return jax.shard_map(plan, mesh=mesh, in_specs=in_specs, out_specs=out_specs, check_vma=False)
```

```python
import functools

import jax
import jax.numpy as jnp
from jax import lax
from jax.experimental import pallas as pl
from jax.experimental.pallas import tpu as pltpu
from jax.sharding import PartitionSpec as P

D = 768
HEADS = 12
HEAD_DIM = 64
FF = 3072
MICRO = 2


EPSILON = 1e-05
NEGATIVE = -1e30
HIGH = lax.Precision.HIGHEST


def layer_norm(values, gain_vec):
    centre = values - jnp.mean(values, axis=1, keepdims=True)
    spread = jnp.mean(centre * centre, axis=1, keepdims=True)
    return centre * lax.rsqrt(spread + EPSILON) * gain_vec


def gelu_tanh(values):
    return jax.nn.gelu(values, approximate=True)


def masked_scores(queries, key_heads, query_pos, key_pos, query_doc, key_doc, key_pad):
    scores = jnp.einsum(
        "qhd,khd->hqk", queries, key_heads, preferred_element_type=jnp.float32
    ) * HEAD_DIM ** (-0.5)
    allowed = (query_doc[:, None] == key_doc[None, :]) & (key_pos[None, :] <= query_pos[:, None])
    allowed = allowed & ((key_pad[None, :] == 1) | (key_pos[None, :] == query_pos[:, None]))
    return jnp.where(allowed[None], scores, NEGATIVE)


def rows_first(left, right):
    return lax.dot_general(
        left, right, (((0,), (0,)), ((), ())), preferred_element_type=jnp.float32
    )


def rows_last(left, right):
    return lax.dot_general(
        left, right, (((1,), (1,)), ((), ())), preferred_element_type=jnp.float32
    )


def body(
    tokens,
    cotangent,
    segment_ids,
    padding,
    routes,
    norm_one_gain,
    qkv_weight,
    out_weight,
    norm_two_gain,
    centroids,
    expert_in,
    expert_out,
):
    local_len = tokens.shape[2]
    experts = centroids.shape[1]
    capacity = max(2, 2 * local_len // experts)
    seq_len = local_len * lax.axis_size("ctx")
    qkv_full, out_full = (
        lax.all_gather(qkv_weight, "shard", axis=0, tiled=True),
        lax.all_gather(out_weight, "shard", axis=0, tiled=True),
    )
    gain_one = norm_one_gain.astype(jnp.float32)
    gain_two = norm_two_gain.astype(jnp.float32)
    centre_f = centroids.astype(jnp.float32)
    up_local = expert_in[0]
    down_local = expert_out[0]
    query_pos = lax.axis_index("ctx") * local_len + jnp.arange(local_len, dtype=jnp.int32)
    all_pos = jnp.arange(seq_len, dtype=jnp.int32)
    slot_ids = jnp.arange(experts * capacity, dtype=jnp.int32)
    expert_ids = jnp.arange(experts, dtype=jnp.int32)
    score_scale = HEAD_DIM ** (-0.5)
    grad_qkv_sum = jnp.zeros((D, 3 * D), jnp.float32)
    grad_out_sum = jnp.zeros((D, D), jnp.float32)
    grad_one_sum = jnp.zeros((D,), jnp.float32)
    grad_two_sum = jnp.zeros((D,), jnp.float32)
    grad_centre = jnp.zeros((D, experts), jnp.float32)
    grad_up_sum = jnp.zeros((D, FF), jnp.float32)
    grad_down_sum = jnp.zeros((D, FF), jnp.float32)
    block_list = []
    input_list = []
    for micro_index in range(MICRO):
        inputs = tokens[micro_index, 0].astype(jnp.float32)
        doc_ids = segment_ids[micro_index, 0]
        pad_mask = padding[micro_index, 0]
        route_ids = routes[micro_index, 0, :, 0]
        normed_one, norm_one_back = jax.vjp(layer_norm, inputs, gain_one)
        first_bf = normed_one.astype(jnp.bfloat16)
        qkv = jnp.dot(first_bf, qkv_full, preferred_element_type=jnp.float32)
        queries = qkv[:, :D].astype(jnp.bfloat16)
        key_rows = qkv[:, D : 2 * D].astype(jnp.bfloat16)
        value_rows = qkv[:, 2 * D :].astype(jnp.bfloat16)
        key_all, value_all, doc_all, pad_all = (
            lax.all_gather(key_rows, "ctx", axis=0, tiled=True),
            lax.all_gather(value_rows, "ctx", axis=0, tiled=True),
            lax.all_gather(doc_ids, "ctx", axis=0, tiled=True),
            lax.all_gather(pad_mask, "ctx", axis=0, tiled=True),
        )
        query_heads = queries.reshape(local_len, HEADS, HEAD_DIM)
        key_heads = key_all.reshape(seq_len, HEADS, HEAD_DIM)
        value_heads = value_all.reshape(seq_len, HEADS, HEAD_DIM)
        scores = masked_scores(
            query_heads, key_heads, query_pos, all_pos, doc_ids, doc_all, pad_all
        )
        row_max = jnp.max(scores, axis=2, keepdims=True)
        weights = jnp.exp(scores - row_max)
        row_total = jnp.sum(weights, axis=2, keepdims=True)
        probs_now = weights / row_total
        log_total = row_max + jnp.log(row_total)
        attended = jnp.einsum(
            "hqk,khd->qhd",
            probs_now.astype(jnp.bfloat16),
            value_heads,
            preferred_element_type=jnp.float32,
        )
        attended = attended.reshape(local_len, D).astype(jnp.bfloat16)
        residual = inputs + jnp.dot(attended, out_full, preferred_element_type=jnp.float32)
        normed_two, norm_two_back = jax.vjp(layer_norm, residual, gain_two)
        second_bf = normed_two.astype(jnp.bfloat16)
        choose_mask = route_ids[:, None] == expert_ids[None, :]
        choose_f = choose_mask.astype(jnp.float32)
        logit = jnp.sum(
            jnp.dot(second_bf, centroids, preferred_element_type=jnp.float32) * choose_f, axis=1
        )
        gate_value = jax.nn.sigmoid(logit)
        choose_int = choose_mask.astype(jnp.int32)
        counts = jnp.cumsum(choose_int, axis=0)
        slot_rank = jnp.sum(counts * choose_int, axis=1) - 1
        target = route_ids * capacity + slot_rank
        dispatch = (slot_ids[:, None] == target[None, :]).astype(jnp.bfloat16)
        outbound = jnp.dot(dispatch, second_bf, preferred_element_type=jnp.float32).astype(
            jnp.bfloat16
        )
        outbound = outbound.reshape(experts, capacity, D)
        received = lax.all_to_all(outbound, "shard", split_axis=0, concat_axis=0, tiled=True)
        slot_rows = received.reshape(-1, D)
        upward = jnp.dot(slot_rows, up_local, preferred_element_type=jnp.float32)
        hidden = gelu_tanh(upward).astype(jnp.bfloat16)
        result = jnp.dot(hidden, down_local, preferred_element_type=jnp.float32).astype(
            jnp.bfloat16
        )
        returned = lax.all_to_all(
            result.reshape(received.shape), "shard", split_axis=0, concat_axis=0, tiled=True
        )
        returned, received, upward = (
            returned,
            received,
            upward.reshape(received.shape[0], received.shape[1], FF),
        )
        expert_rows = rows_first(dispatch, returned.reshape(experts * capacity, D))
        block_list.append((residual + gate_value[:, None] * expert_rows).astype(jnp.bfloat16))
        grad_out = cotangent[micro_index, 0].astype(jnp.float32)
        grad_gate = jnp.sum(grad_out * expert_rows, axis=1)
        grad_logit = grad_gate * gate_value * (1.0 - gate_value)
        grad_rows = (gate_value[:, None] * grad_out).astype(jnp.bfloat16)
        grad_outbound = jnp.dot(dispatch, grad_rows, preferred_element_type=jnp.float32).astype(
            jnp.bfloat16
        )
        grad_received = lax.all_to_all(
            grad_outbound.reshape(experts, capacity, D),
            "shard",
            split_axis=0,
            concat_axis=0,
            tiled=True,
        )
        grad_result = grad_received.reshape(-1, D)
        hidden_again, gelu_back = jax.vjp(gelu_tanh, upward.reshape(-1, FF))
        grad_down_sum = grad_down_sum + rows_first(grad_result, hidden_again.astype(jnp.bfloat16))
        grad_hidden = rows_last(grad_result, down_local)
        grad_upward = gelu_back(grad_hidden)[0].astype(jnp.bfloat16)
        grad_up_sum = grad_up_sum + rows_first(received.reshape(-1, D), grad_upward)
        grad_send = (
            rows_last(grad_upward, up_local).astype(jnp.bfloat16).reshape(grad_received.shape)
        )
        grad_back = lax.all_to_all(grad_send, "shard", split_axis=0, concat_axis=0, tiled=True)
        grad_second = rows_first(dispatch, grad_back.reshape(experts * capacity, D))
        grad_second = grad_second + grad_logit[:, None] * jnp.dot(
            choose_f, centre_f.T, precision=HIGH
        )
        grad_centre = grad_centre + jnp.dot(
            second_bf.astype(jnp.float32).T, choose_f * grad_logit[:, None], precision=HIGH
        )
        grad_resid_norm, grad_two_term = norm_two_back(grad_second)
        grad_residual = grad_out + grad_resid_norm
        grad_two_sum = grad_two_sum + grad_two_term
        grad_branch = grad_residual.astype(jnp.bfloat16)
        grad_out_sum = grad_out_sum + rows_first(attended, grad_branch)
        grad_attend = (
            rows_last(grad_branch, out_full)
            .astype(jnp.bfloat16)
            .reshape(local_len, HEADS, HEAD_DIM)
        )
        probs_again = jnp.exp(
            masked_scores(query_heads, key_heads, query_pos, all_pos, doc_ids, doc_all, pad_all)
            - log_total
        )
        grad_probs = jnp.einsum(
            "qhd,khd->hqk", grad_attend, value_heads, preferred_element_type=jnp.float32
        )
        row_terms = jnp.sum(probs_again * grad_probs, axis=2, keepdims=True)
        grad_scores = (probs_again * (grad_probs - row_terms)).astype(jnp.bfloat16)
        grad_query = (
            jnp.einsum("hqk,khd->qhd", grad_scores, key_heads, preferred_element_type=jnp.float32)
            * score_scale
        )
        grad_key_all = (
            jnp.einsum("hqk,qhd->khd", grad_scores, query_heads, preferred_element_type=jnp.float32)
            * score_scale
        )
        grad_value_all = jnp.einsum(
            "hqk,qhd->khd",
            probs_again.astype(jnp.bfloat16),
            grad_attend,
            preferred_element_type=jnp.float32,
        )
        grad_key, grad_value = (
            lax.psum_scatter(
                grad_key_all.reshape(seq_len, D).astype(jnp.bfloat16),
                "ctx",
                scatter_dimension=0,
                tiled=True,
            ).astype(jnp.float32),
            lax.psum_scatter(
                grad_value_all.reshape(seq_len, D).astype(jnp.bfloat16),
                "ctx",
                scatter_dimension=0,
                tiled=True,
            ).astype(jnp.float32),
        )
        grad_qkv_rows = jnp.concatenate(
            [grad_query.reshape(local_len, D), grad_key, grad_value], axis=1
        ).astype(jnp.bfloat16)
        grad_qkv_sum = grad_qkv_sum + rows_first(first_bf, grad_qkv_rows)
        grad_first = rows_last(grad_qkv_rows, qkv_full)
        grad_in_norm, grad_one_term = norm_one_back(grad_first)
        grad_one_sum = grad_one_sum + grad_one_term
        input_list.append(grad_residual + grad_in_norm)
    dense_sums = (
        lax.psum_scatter(grad_one_sum, ("ctx", "shard"), scatter_dimension=0, tiled=True),
        lax.psum_scatter(grad_qkv_sum, ("ctx", "shard"), scatter_dimension=0, tiled=True),
        lax.psum_scatter(grad_out_sum, ("ctx", "shard"), scatter_dimension=0, tiled=True),
        lax.psum_scatter(grad_two_sum, ("ctx", "shard"), scatter_dimension=0, tiled=True),
        lax.psum_scatter(grad_centre, ("ctx", "shard"), scatter_dimension=0, tiled=True),
    )
    expert_sums = (
        lax.psum_scatter(
            grad_up_sum.astype(jnp.bfloat16), "ctx", scatter_dimension=1, tiled=True
        ).astype(jnp.float32),
        lax.psum_scatter(
            grad_down_sum.astype(jnp.bfloat16), "ctx", scatter_dimension=1, tiled=True
        ).astype(jnp.float32),
    )
    block_out = jnp.stack(block_list)[:, None]
    grad_tokens = jnp.stack(input_list)[:, None]
    return (
        block_out,
        grad_tokens,
        dense_sums[0],
        dense_sums[1],
        dense_sums[2],
        dense_sums[3],
        dense_sums[4],
        expert_sums[0][None],
        expert_sums[1].T[None],
    )


BF = jnp.bfloat16
F32 = jnp.float32
QB = 256
AB = 512
GELU_K = 0.7978845608028654
VMEM_WHOLE = pl.BlockSpec(memory_space=pltpu.VMEM)
HBM_WHOLE = pl.BlockSpec(memory_space=pltpu.HBM)


def nn(left, right):
    return lax.dot_general(left, right, (((1,), (0,)), ((), ())), preferred_element_type=F32)


def nt(left, right):
    return lax.dot_general(left, right, (((1,), (1,)), ((), ())), preferred_element_type=F32)


def tn(left, right):
    return lax.dot_general(left, right, (((0,), (0,)), ((), ())), preferred_element_type=F32)


def lanes_of(shape, half):
    lane = lax.broadcasted_iota(jnp.int32, shape, 1)
    return (lane < HEAD_DIM) if half == 0 else (lane >= HEAD_DIM)


def masks_of(label_ref, micro):
    doc = label_ref[micro : micro + 1, :].astype(F32)
    real = label_ref[MICRO + micro : MICRO + micro + 1, :] == 1
    return doc, jnp.where(real, doc, -1.0)


def as_column(row):
    return jnp.transpose(jnp.broadcast_to(row, (128, row.shape[1])))[:, 0:1]


def attend_kernel(
    micro, h_ref, w_ref, label_ref, saved_ref, o_ref, lse_ref, col_ref, qkv_ref, sem
):
    seq, width = h_ref.shape[0], o_ref.shape[1]
    scale = HEAD_DIM ** (-0.5)
    doc_row, code_row = masks_of(label_ref, micro)
    col_ref[...] = as_column(doc_row)

    def project(block, carry):
        rows = pl.ds(block * AB, AB)
        qkv_ref[rows, :] = nn(h_ref[rows, :], w_ref[:, 0 : 3 * width]).astype(BF)
        return carry

    lax.fori_loop(0, seq // AB, project, 0)
    save = pltpu.make_async_copy(qkv_ref, saved_ref, sem)
    save.start()
    for block in range(seq // AB):
        low, kend = block * AB, (block + 1) * AB
        rows = slice(low, kend)
        qpos = lax.broadcasted_iota(jnp.int32, (AB, kend), 0) + low
        kpos = lax.broadcasted_iota(jnp.int32, (AB, kend), 1)
        same = col_ref[rows, :] == code_row[:, 0:kend]
        allowed = (same & (kpos < qpos)) | (kpos == qpos)
        bias = jnp.where(allowed, 0.0, NEGATIVE).astype(F32)
        lane = lax.broadcasted_iota(jnp.int32, (AB, 128), 1)

        def pair(index, stats):
            at = pl.multiple_of(index * 128, 128)
            q = qkv_ref[rows, pl.ds(at, 128)] * jnp.asarray(scale, BF)
            k = qkv_ref[0:kend, pl.ds(width + at, 128)]
            v = qkv_ref[0:kend, pl.ds(2 * width + at, 128)]
            outs = []
            for half in range(2):
                qm = jnp.where(lanes_of(q.shape, half), q, jnp.zeros_like(q))
                s = nt(qm, k) + bias
                top = jnp.max(s, axis=1, keepdims=True)
                e = jnp.exp(s - top)
                total = jnp.sum(e, axis=1, keepdims=True)
                outs.append(nn(e.astype(BF), v) * (1.0 / total))
                stats = jnp.where(lane == 2 * index + half, top + jnp.log(total), stats)
            o_ref[rows, pl.ds(at, 128)] = jnp.where(
                lanes_of(outs[0].shape, 0), outs[0], outs[1]
            ).astype(BF)
            return stats

        stats = lax.fori_loop(0, width // 128, pair, jnp.zeros((AB, 128), F32), unroll=True)
        lse_ref[:, rows] = jnp.transpose(stats)[0 : lse_ref.shape[0], :]
    save.wait()


def attend_back_kernel(
    micro, qkv_ref, do_ref, lse_ref, label_ref, dqkv_ref, dk_ref, dv_ref, kt_ref, col_ref
):
    seq, width = do_ref.shape
    doc_row, code_row = masks_of(label_ref, micro)
    col_ref[...] = as_column(code_row)
    scale = HEAD_DIM ** (-0.5)
    dk_ref[...] = jnp.zeros_like(dk_ref)
    dv_ref[...] = jnp.zeros_like(dv_ref)
    kt_ref[...] = jnp.transpose(qkv_ref[:, width : 2 * width])
    for block in range(seq // AB):
        low, kend = block * AB, (block + 1) * AB
        rows = slice(low, kend)
        qpos = lax.broadcasted_iota(jnp.int32, (kend, AB), 1) + low
        kpos = lax.broadcasted_iota(jnp.int32, (kend, AB), 0)
        same = doc_row[:, rows] == col_ref[0:kend, :]
        allowed = (same & (kpos < qpos)) | (kpos == qpos)
        bias = jnp.where(allowed, 0.0, NEGATIVE).astype(F32)

        def pair(index, carry):
            at = pl.multiple_of(index * 128, 128)
            q = qkv_ref[rows, pl.ds(at, 128)] * jnp.asarray(scale, BF)
            k = qkv_ref[0:kend, pl.ds(width + at, 128)]
            v = qkv_ref[0:kend, pl.ds(2 * width + at, 128)]
            do = do_ref[rows, pl.ds(at, 128)]
            dqt = jnp.zeros((128, AB), F32)
            dv = dk = None
            for half in range(2):
                keep = lanes_of(q.shape, half)
                qm = jnp.where(keep, q, jnp.zeros_like(q))
                dom = jnp.where(keep, do, jnp.zeros_like(do))
                p = jnp.exp(nt(k, qm) + bias - lse_ref[pl.ds(2 * index + half, 1), rows])
                dp = nt(v, dom)
                delta = jnp.sum(p * dp, axis=0, keepdims=True)
                ds = (p * (dp - delta)).astype(BF)
                dv_half = nn(p.astype(BF), dom)
                dk_half = nn(ds, qm)
                dv = dv_half if dv is None else dv + dv_half
                dk = dk_half if dk is None else dk + dk_half
                kt = kt_ref[pl.ds(pl.multiple_of(at + half * HEAD_DIM, HEAD_DIM), HEAD_DIM), 0:kend]
                dqt = nn(kt, ds) if half == 0 else jnp.concatenate([dqt, nn(kt, ds)], axis=0)
            dv_ref[0:kend, pl.ds(at, 128)] += dv
            dk_ref[0:kend, pl.ds(at, 128)] += dk
            dqkv_ref[rows, pl.ds(at, 128)] = (jnp.transpose(dqt) * scale).astype(BF)
            return carry

        lax.fori_loop(0, width // 128, pair, 0, unroll=True)
    dqkv_ref[:, width : 2 * width] = dk_ref[...].astype(BF)
    dqkv_ref[:, 2 * width :] = dv_ref[...].astype(BF)


def spread_stage(dqkv_ref, w_ref, dh_ref):
    seq, wide = dqkv_ref.shape

    def spread(block, carry):
        rows = pl.ds(pl.multiple_of(block * AB, AB), AB)
        dh_ref[rows, :] = nt(dqkv_ref[rows, :], w_ref[:, 0:wide])
        return carry

    lax.fori_loop(0, seq // AB, spread, 0)


def expert_kernel(has_prev, h_ref, g_ref, *refs):
    if has_prev:
        (c_ref, up_ref, down_ref, prev_up_ref, prev_down_ref, give_ref, extra_ref,
         y_out_ref, dh_out_ref, gc_ref, gup_ref, gdown_ref, sup_ref, sdown_ref, got_ref, more_ref,
         dz_ref, gate_ref, z_ref, acc_ref, a_ref, du_ref, y_ref, dh_ref, sems,
         swap_send, swap_recv, more_send, more_recv) = refs
        exchanges = (
            (give_ref, got_ref, swap_send, swap_recv, sems.at[8], ROLES),
            (extra_ref, more_ref, more_send, more_recv, sems.at[9], EARLY_0),
        )
    else:
        (c_ref, up_ref, down_ref, give_ref, extra_ref, _,
         y_out_ref, dh_out_ref, gc_ref, gup_ref, gdown_ref, got_ref, more_ref,
         dz_ref, gate_ref, z_ref, acc_ref, a_ref, du_ref, y_ref, dh_ref, sems,
         swap_send, swap_recv, more_send, more_recv) = refs
        exchanges = (
            (give_ref, got_ref, swap_send, swap_recv, sems.at[8], ROLES),
            (extra_ref, more_ref, more_send, more_recv, sems.at[9], LATE_G),
        )
    step, steps = pl.program_id(0), pl.num_programs(0)
    capacity = h_ref.shape[1]
    rows_all = h_ref.shape[0] * capacity
    blocks = rows_all // QB
    each = QB // capacity

    def take(ref, block):
        return ref[pl.ds(pl.multiple_of(block * each, each), each)].reshape(QB, D)

    @pl.when(step == 0)
    def _():
        def start(block, carry):
            rows = pl.ds(pl.multiple_of(block * QB, QB), QB)
            logit = jnp.sum(take(h_ref, block).astype(F32) * c_ref[...], axis=1, keepdims=True)
            gate = 1.0 / (1.0 + jnp.exp(-logit))
            gate_ref[rows, :] = gate
            dz_ref[rows, :] = (gate * take(g_ref, block).astype(F32)).astype(BF)
            z_ref[rows, :] = jnp.zeros((QB, D), F32)
            acc_ref[rows, :] = jnp.zeros((QB, D), F32)
            return carry

        greet([{"shard": chip} for chip in all_chips()[1:]])
        trade_all(*exchanges, order=(False, True))
        lax.fori_loop(0, blocks, start, 0)

    def forward(block, carry):
        rows = pl.ds(pl.multiple_of(block * QB, QB), QB)
        u = nn(take(h_ref, block), up_ref[...])
        square = u * u
        t = jnp.tanh(GELU_K * u * (1.0 + 0.044715 * square))
        a = (0.5 * u * (1.0 + t)).astype(BF)
        slope = 0.5 * (1.0 + t) + 0.5 * u * (1.0 - t * t) * (
            GELU_K * (1.0 + 3 * 0.044715 * square)
        )
        a_ref[rows, :] = a
        z_ref[rows, :] += nn(a, down_ref[...])
        du = (nt(dz_ref[rows, :], down_ref[...]) * slope).astype(BF)
        du_ref[rows, :] = du
        acc_ref[rows, :] += nt(du, up_ref[...])
        return carry

    lax.fori_loop(0, blocks, forward, 0, unroll=True)
    gup = tn(h_ref[...].reshape(rows_all, D), du_ref[...])
    gdown = tn(a_ref[...], dz_ref[...])
    if has_prev:
        gup = gup + prev_up_ref[...]
        gdown = gdown + prev_down_ref[...]

        @pl.when(step < 2)
        def _():
            sup_ref[...] = gup.astype(BF)
            sdown_ref[...] = gdown.astype(BF)

        @pl.when(step >= 2)
        def _():
            gup_ref[...] = gup.astype(BF)
            gdown_ref[...] = gdown.astype(BF)
    else:
        gup_ref[...] = gup
        gdown_ref[...] = gdown

    @pl.when(step == steps - 1)
    def _():
        saves = []
        total = jnp.zeros((1, D), F32)
        for block in range(blocks):
            rows = slice(block * QB, (block + 1) * QB)
            group = slice(block * each, (block + 1) * each)
            z = z_ref[rows, :].astype(BF).astype(F32)
            gate = gate_ref[rows, :]
            dgate = jnp.sum(take(g_ref, block).astype(F32) * z, axis=1, keepdims=True)
            dlogit = dgate * gate * (1.0 - gate)
            y_ref[group] = (gate * z).astype(BF).reshape(each, capacity, D)
            dh = (acc_ref[rows, :] + dlogit * c_ref[...]).astype(BF)
            dh_ref[group] = dh.reshape(each, capacity, D)
            total = total + jnp.sum(dlogit * take(h_ref, block).astype(F32), axis=0, keepdims=True)
            saves += [
                pltpu.make_async_copy(
                    dh_ref.at[group], dh_out_ref.at[group], sems.at[2 * block]
                ),
                pltpu.make_async_copy(
                    y_ref.at[group], y_out_ref.at[group], sems.at[2 * block + 1]
                ),
            ]
            for save in saves[-2:]:
                save.start()
        gc_ref[...] = total
        for exchange in exchanges:
            saves += traded(*exchange)
        for save in saves:
            save.wait()


def expert(h_slots, g_slots, centre, up, down, give, prev):
    groups, capacity, _ = h_slots.shape
    rows = groups * capacity
    ff = up.shape[1]
    wide = ff // 3 if prev is None else ff // 4
    steps = ff // wide
    turn = lambda step: step
    if prev is not None:
        turn = lambda step: (step + 2 * (1 - lax.axis_index("ctx"))) % 4
    early = lambda step: step // 2 + (1 - step // 2) * step
    late = lambda step: (step // 2) * (step - 2)
    whole = lambda step: (0, 0)
    every = lambda step: (0, 0, 0)
    slot_block = (groups, capacity, D)
    up_block = pl.BlockSpec((D, wide), lambda step: (0, turn(step)))
    down_block = pl.BlockSpec((wide, D), lambda step: (turn(step), 0))
    in_specs = [
        pl.BlockSpec(slot_block, every, pipeline_mode=pl.Buffered(1)),
        pl.BlockSpec(slot_block, every, pipeline_mode=pl.Buffered(1)),
        pl.BlockSpec((1, D), whole),
        up_block,
        down_block,
    ]
    args = [h_slots, g_slots, centre, up, down]
    out_shape = [
        pltpu.HBM((groups, capacity, D), BF),
        pltpu.HBM((groups, capacity, D), BF),
        jax.ShapeDtypeStruct((1, D), F32),
    ]
    out_specs = [HBM_WHOLE, HBM_WHOLE, pl.BlockSpec((1, D), whole)]
    more = 2
    if prev is None:
        out_shape += [pltpu.HBM((D, ff), F32), pltpu.HBM((ff, D), F32)]
        out_specs += [up_block, down_block]
    else:
        for at in (late, early):
            out_shape += [pltpu.HBM((D, ff // 2), BF), pltpu.HBM((ff // 2, D), BF)]
            out_specs += [
                pl.BlockSpec((D, wide), lambda step, at=at: (0, at(step))),
                pl.BlockSpec((wide, D), lambda step, at=at: (at(step), 0)),
            ]
        in_specs += [up_block, down_block]
        args += list(prev)
    in_specs += [HBM_WHOLE] * len(give)
    args += list(give)
    out_shape += [pltpu.HBM((groups, capacity, D), BF)] * more
    out_specs += [HBM_WHOLE] * more
    return pl.pallas_call(
        functools.partial(expert_kernel, prev is not None),
        out_shape=tuple(out_shape),
        grid=(steps,),
        in_specs=in_specs,
        out_specs=tuple(out_specs),
        scratch_shapes=[
            pltpu.VMEM((rows, D), BF),
            pltpu.VMEM((rows, 1), F32),
            pltpu.VMEM((rows, D), F32),
            pltpu.VMEM((rows, D), F32),
            pltpu.VMEM((rows, wide), BF),
            pltpu.VMEM((rows, wide), BF),
            pltpu.VMEM((groups, capacity, D), BF),
            pltpu.VMEM((groups, capacity, D), BF),
            pltpu.SemaphoreType.DMA((10,)),
        ]
        + [pltpu.SemaphoreType.DMA((16,))] * (2 * more),
        input_output_aliases={7: 6} if prev is None else {},
        compiler_params=pltpu.CompilerParams(
            collective_id=2 if prev is None else 3, has_side_effects=True, vmem_limit_bytes=56 << 20
        ),
        cost_estimate=pl.CostEstimate(
            flops=12 * rows * D * ff, bytes_accessed=40 << 20, transcendentals=rows * ff
        ),
        name="expert",
    )(*args)


PARTS = 4


def emit_kernel(
    x0_ref, x1_ref, y0a_ref, y0b_ref, y1_ref, target_in_ref, in0_ref, in1_ref,
    own_up_ref, got_up_ref, own_down_ref, got_down_ref, gqkv_in_ref, gproj_in_ref, small_in_ref,
    out_ref, grad_ref, up_ref, down_ref, gqkv_ref, gproj_ref, one_ref, two_ref, centre_ref,
    target_ref, small_ref, x_ref, y_ref, in_ref, up_parts_ref, down_parts_ref, up_sum_ref, down_sum_ref, sems, sum_sems,
):
    rows = x0_ref.shape[0]
    groups, capacity, _ = y0a_ref.shape
    slots = groups * capacity
    chips = all_chips()
    sums = []
    for pair, (own_ref, got_ref, parts_ref, sum_ref, result_ref) in enumerate(
        (
            (own_up_ref, got_up_ref, up_parts_ref, up_sum_ref, up_ref),
            (own_down_ref, got_down_ref, down_parts_ref, down_sum_ref, down_ref),
        )
    ):
        size = own_ref.shape[0] // PARTS
        for part in range(PARTS):
            at = slice(part * size, (part + 1) * size)
            sem = 3 * (PARTS * pair + part)
            sums.append(
                (
                    pltpu.make_async_copy(own_ref.at[at, :], parts_ref.at[0, at, :], sum_sems.at[sem]),
                    pltpu.make_async_copy(got_ref.at[at, :], parts_ref.at[1, at, :], sum_sems.at[sem + 1]),
                    pltpu.make_async_copy(sum_ref.at[at, :], result_ref.at[at, :], sum_sems.at[sem + 2]),
                    parts_ref, sum_ref, at,
                )
            )
    loads, moves = [], []
    for micro, (x_in, grad_in, parts) in enumerate(
        (
            (x0_ref, in0_ref, ((y0a_ref, EARLY_0), (y0b_ref, LATE_0))),
            (x1_ref, in1_ref, ((y1_ref, ROLES),)),
        )
    ):
        mine = [pltpu.make_async_copy(x_in, x_ref.at[micro], sems.at[20 * micro])]
        for part_ref, roles in parts:
            mine += [
                pltpu.make_async_copy(
                    part_ref.at[chips[role]], y_ref.at[micro, chips[role]], sems.at[20 * micro + 1 + role]
                )
                for role in roles
            ]
        loads.append(mine)
        moves.append(
            (
                pltpu.make_async_copy(grad_in, in_ref.at[micro], sems.at[20 * micro + 17]),
                pltpu.make_async_copy(
                    in_ref.at[micro], grad_ref.at[micro * rows : (micro + 1) * rows, :],
                    sems.at[20 * micro + 18],
                ),
            )
        )
    few = [
        pltpu.make_async_copy(src, dst, sems.at[40 + at])
        for at, (src, dst) in enumerate(
            (
                (gqkv_in_ref, gqkv_ref),
                (gproj_in_ref, gproj_ref),
                (small_in_ref, small_ref),
                (target_in_ref, target_ref),
            )
        )
    ]
    for part in sums:
        part[0].start()
        part[1].start()
    for load in few + loads[0] + [moves[0][0]] + loads[1] + [moves[1][0]]:
        load.start()
    for load in few:
        load.wait()
    size, experts = small_ref.shape[0], centre_ref.shape[0]
    small = jnp.concatenate([small_ref[...], jnp.zeros((128 - size, 128), F32)], axis=0)
    small = jnp.transpose(small)
    one_ref[...] = small[0:1, 0:size]
    two_ref[...] = small[1:2, 0:size]
    centre_ref[...] = small[2 : 2 + experts, 0:size]
    for own, got, store, parts_ref, sum_ref, at in sums:
        own.wait()
        got.wait()
        sum_ref[at, :] = parts_ref[0, at, :].astype(F32) + parts_ref[1, at, :].astype(F32)
        store.start()
    for micro in range(MICRO):
        for load in loads[micro]:
            load.wait()
        moves[micro][0].wait()
        moves[micro][1].start()
        slot = lax.broadcasted_iota(jnp.int32, (rows, slots), 1)
        pick = (slot == target_ref[:, micro : micro + 1]).astype(F32).astype(BF)
        value = x_ref[micro] + nn(pick, y_ref[micro].reshape(slots, D))
        out_ref[micro * rows : (micro + 1) * rows, :] = value.astype(BF)
    for part in sums:
        part[2].wait()
    for move in moves:
        move[1].wait()


def emit(x0, x1, y0a, y0b, y1, target, in0, in1, own_up, got_up, own_down, got_down, gqkv, gproj, small):
    rows, size = x0.shape[0], small.shape[0]
    groups = y0a.shape[0]
    in_hbm = lambda array: pltpu.with_memory_space_constraint(array, pltpu.HBM)
    args = [x0, x1, y0a, y0b, y1, target, in0, in1, own_up, got_up, own_down, got_down, gqkv, gproj, small]
    return pl.pallas_call(
        emit_kernel,
        out_shape=(
            jax.ShapeDtypeStruct((MICRO * rows, D), BF),
            pltpu.HBM((MICRO * rows, D), F32),
            pltpu.HBM(own_up.shape, F32),
            pltpu.HBM(own_down.shape, F32),
            jax.ShapeDtypeStruct(gqkv.shape, F32),
            jax.ShapeDtypeStruct(gproj.shape, F32),
            jax.ShapeDtypeStruct((1, size), F32),
            jax.ShapeDtypeStruct((1, size), F32),
            jax.ShapeDtypeStruct((groups, size), F32),
        ),
        in_specs=[HBM_WHOLE] * 15,
        out_specs=(VMEM_WHOLE,) + (HBM_WHOLE,) * 3 + (VMEM_WHOLE,) * 5,
        scratch_shapes=[
            pltpu.VMEM(target.shape, jnp.int32),
            pltpu.VMEM(small.shape, F32),
            pltpu.VMEM((MICRO, rows, D), F32),
            pltpu.VMEM((MICRO,) + y0a.shape, BF),
            pltpu.VMEM((MICRO, rows, D), F32),
            pltpu.VMEM((2,) + own_up.shape, BF),
            pltpu.VMEM((2,) + own_down.shape, BF),
            pltpu.VMEM(own_up.shape, F32),
            pltpu.VMEM(own_down.shape, F32),
            pltpu.SemaphoreType.DMA((44,)),
            pltpu.SemaphoreType.DMA((6 * PARTS,)),
        ],
        compiler_params=pltpu.CompilerParams(vmem_limit_bytes=50 << 20),
        cost_estimate=pl.CostEstimate(
            flops=4 * rows * D * groups * y0a.shape[1], bytes_accessed=30 << 20, transcendentals=0
        ),
        name="emit",
    )(*[in_hbm(array) for array in args])


def greet(peers):
    barrier = pltpu.get_barrier_semaphore()
    for peer in peers:
        pl.semaphore_signal(
            barrier, inc=1, device_id=peer, device_id_type=pl.DeviceIdType.MESH
        )
    pl.semaphore_wait(barrier, len(peers))


def send(src, dst, send_sem, recv_sem, peer):
    return pltpu.make_async_remote_copy(
        src_ref=src,
        dst_ref=dst,
        send_sem=send_sem,
        recv_sem=recv_sem,
        device_id=peer,
        device_id_type=pl.DeviceIdType.MESH,
    )


def places():
    me, core = lax.axis_index("shard"), lax.axis_index("ctx")
    z, y, x = me // 4, (me // 2) % 2, me % 2
    along_y, along_x = me + 2 - 4 * y, me + 1 - 2 * x
    first = along_y * (1 - core) + along_x * core
    second = along_x * (1 - core) + along_y * core
    far = 4 * z + 3 - me % 4
    line = [z, z + 1 - 2 * (z % 2), (z + 2) % 4, 3 - z]
    return me, first, second, far, line


def all_chips():
    me, _, _, _, line = places()
    y, x = (me // 2) % 2, me % 2
    turns = [me % 4, me % 4 + 1 - 2 * x, me % 4 + 2 - 4 * y, 3 - me % 4]
    return [4 * line[j] + turns[i] for j in range(4) for i in range(4)]


ROLES = (8, 9, 10, 11, 12, 13, 14, 15, 4, 5, 6, 7, 1, 2, 3, 0)
EARLY_G, LATE_G = (8, 9, 10, 11, 12, 4, 5, 6, 1, 2, 0), (13, 14, 15, 7, 3)
EARLY_0, LATE_0 = (8, 4, 1), (9, 10, 11, 12, 13, 14, 15, 5, 6, 7, 2, 3, 0)
EARLY_1, NEXT_1, LATE_1 = (8, 4, 1), (9, 10, 11), (12, 13, 14, 15, 5, 6, 7, 2, 3, 0)


def traded(src_ref, dst_ref, send_sem, recv_sem, keep_sem, roles=ROLES):
    chips = all_chips()
    me = chips[0]
    copies = []
    for role in roles:
        if role:
            copies.append(
                send(
                    src_ref.at[chips[role]], dst_ref.at[me], send_sem.at[role], recv_sem.at[role],
                    {"shard": chips[role]},
                )
            )
        else:
            copies.append(pltpu.make_async_copy(src_ref.at[me], dst_ref.at[me], keep_sem))
    return copies


def trade_all(*exchanges, order=(True, False)):
    copies = []
    for far in order:
        for exchange in exchanges:
            roles = tuple(role for role in exchange[5] if (role >= 8) == far)
            copies += trade(*exchange[:5], roles)
    return copies


def trade(src_ref, dst_ref, send_sem, recv_sem, keep_sem, roles=ROLES):
    copies = traded(src_ref, dst_ref, send_sem, recv_sem, keep_sem, roles)
    for copy in copies:
        copy.start()
    return copies


def head_kernel(
    experts, capacity, qkv_ref, proj_ref, seg_ref, pad_ref, route_ref, tok_ref, cot_ref,
    centroid_ref, gain_in_ref, gain_two_in_ref,
    out_save_ref, full_save_ref, h0_save_ref, h1_save_ref, all_save_ref, column_save_ref, centre_ref,
    in0_ref, in1_ref,
    take_ref, saved0_ref, lse0_save_ref, x10_ref, attended0_ref, saved1_ref, lse1_save_ref, x11_ref,
    attended1_ref, sent_ref, given_ref, gains_save_ref,
    gains_ref, raw_one_ref, raw_two_ref, all_ref, target_ref, column_ref, lse0_ref, lse1_ref, hub_ref, w_ref, x_ref, g_ref, label_ref, slots_ref, out_ref, full_ref, h0_ref, h1_ref,
    col_ref, heads_ref, o_ref, first_ref, x1_ref, joined0_ref, joined1_ref, h2_ref,
    send_sem, recv_sem, swap_send, swap_recv, sems, post_sems,
):
    size = w_ref.shape[0]
    half = full_ref.shape[1] // 2
    wide = w_ref.shape[1] - half
    count = label_ref.shape[1]
    me, first, second, far, line = places()
    core = lax.axis_index("ctx")
    own = pl.multiple_of(core * half, 128)
    loads = [
        pltpu.make_async_copy(
            qkv_ref.at[:, pl.ds(2 * at * half + own, half)],
            w_ref.at[:, at * half : (at + 1) * half],
            sems.at[at],
        )
        for at in range(3)
    ]
    loads += [
        pltpu.make_async_copy(proj_ref.at[:, pl.ds(own, half)], w_ref.at[:, wide:], sems.at[3]),
        pltpu.make_async_copy(cot_ref, g_ref, sems.at[4]),
        pltpu.make_async_copy(tok_ref, x_ref, sems.at[5]),
    ]
    for load in loads:
        load.start()
    gain_ref, gain_two_ref = gains_ref.at[0:1, :], gains_ref.at[1:2, :]
    label_ref[...] = jnp.zeros_like(label_ref)
    names = [
        pltpu.make_async_copy(
            ref.at[micro], label_ref.at[MICRO * at + micro : MICRO * at + micro + 1, :],
            sems.at[16 + MICRO * at + micro],
        )
        for at, ref in enumerate((seg_ref, pad_ref, route_ref))
        for micro in range(MICRO)
    ]
    names += [
        pltpu.make_async_copy(centroid_ref, hub_ref, sems.at[15]),
        pltpu.make_async_copy(gain_in_ref, raw_one_ref, sems.at[27]),
        pltpu.make_async_copy(gain_two_in_ref, raw_two_ref, sems.at[28]),
    ]
    for name in names:
        name.start()
    twin = {"ctx": 1 - core}
    lines = [4 * z for z in line]
    y, x = (me // 2) % 2, me % 2
    turns = [me % 4, me % 4 + 1 - 2 * x, me % 4 + 2 - 4 * y, 3 - me % 4]

    def rows(block):
        return out_ref.at[pl.ds(pl.multiple_of(block * size, 16), size), :]

    chips = [lines[j] + turns[i] for j in range(4) for i in range(4)]
    peers = [{"shard": chips[4 * j]} for j in (1, 2, 3)]
    one, two = {"shard": first}, {"shard": second}
    greet([{"shard": chip} for chip in chips[1:]] + [twin])
    copies, share = [], []

    def push(block, role, peer, src=None):
        copy = send(
            rows(block) if src is None else src, rows(block), send_sem.at[role], recv_sem.at[role], peer
        )
        copy.start()
        copies.append(copy)

    def arrive(block, role):
        send(rows(block), rows(block), send_sem.at[0], recv_sem.at[role], one).wait_recv()

    for load in loads[:4]:
        load.wait()
    push(me, 3, one, w_ref)
    push(me, 7, two, w_ref)
    for j in (1, 2, 3):
        push(me, j - 1, peers[j - 1], w_ref)
    out_ref[pl.ds(pl.multiple_of(me * size, 16), size), :] = w_ref[...]
    for name in names:
        name.wait()
    gains_ref[0:1, :] = raw_one_ref[...].astype(F32).reshape(1, D)
    gains_ref[1:2, :] = raw_two_ref[...].astype(F32).reshape(1, D)
    mine = pl.ds(pl.multiple_of(core * count, 128), count)
    share.append(send(label_ref, all_ref.at[:, mine], send_sem.at[15], recv_sem.at[15], twin))
    share[0].start()
    all_ref[:, mine] = label_ref[...]

    before = lax.broadcasted_iota(jnp.int32, (count, count), 0)
    after = lax.broadcasted_iota(jnp.int32, (count, count), 1)
    upto = (before <= after).astype(F32).astype(BF)
    ids = lax.broadcasted_iota(jnp.int32, (experts, count), 0)
    target_ref[...] = jnp.zeros_like(target_ref)
    for micro in range(MICRO):
        route = label_ref[2 * MICRO + micro : 2 * MICRO + micro + 1, :]
        chosen = (ids == route).astype(F32)
        rank = jnp.sum(nn(chosen.astype(BF), upto) * chosen, axis=0, keepdims=True)
        target_ref[micro : micro + 1, :] = route * capacity + rank.astype(jnp.int32) - 1
    wide_target = jnp.concatenate(
        [target_ref[...].astype(F32), jnp.zeros((120, count), F32)], axis=0
    )
    column_ref[...] = jnp.transpose(wide_target)[:, 0:8].astype(jnp.int32)
    row = lax.broadcasted_iota(jnp.int32, (experts, D), 0)
    centre_ref[...] = jnp.sum(
        jnp.where(row == me, hub_ref[...].astype(F32), 0.0), axis=0, keepdims=True
    )

    def place(micro, group):
        slot = lax.broadcasted_iota(jnp.int32, (4 * capacity, count), 0) + group * capacity
        pick = (slot == target_ref[micro : micro + 1, :]).astype(F32).astype(BF)
        value = nn(pick, g_ref[micro * count : (micro + 1) * count, :]).astype(BF)
        slots_ref[micro, pl.ds(pl.multiple_of(group, 4), 4)] = value.reshape(4, capacity, D)

    swaps = []

    def pass_one(micro, role):
        copy = send(
            slots_ref.at[micro, chips[role]],
            (in1_ref if micro else in0_ref).at[me],
            swap_send.at[16 * micro + role],
            swap_recv.at[16 * micro + role],
            {"shard": chips[role]},
        )
        copy.start()
        swaps.append(copy)

    def pass_on(micro, j):
        for i in range(4):
            if 4 * j + i:
                pass_one(micro, 4 * j + i)

    loads[4].wait()
    place(0, lines[2])
    pass_on(0, 2)

    def normed(micro, h_ref):
        def norm(block, carry):
            off = pl.multiple_of(block * RB, RB)
            unit = normal(x_ref[pl.ds(micro * count + off, RB), :].astype(F32))[0]
            at = pl.ds(pl.multiple_of(core * count + off, RB), RB)
            h_ref[at, :] = (unit * gain_ref[...]).astype(BF)
            return carry

        lax.fori_loop(0, count // RB, norm, 0)
        copy = send(
            h_ref.at[mine, :], h_ref.at[mine, :], send_sem.at[16 + micro], recv_sem.at[16 + micro], twin
        )
        copy.start()
        share.append(copy)

    arrive(lines[0] + first % 4, 3)
    push(lines[0] + first % 4, 11, two)
    block = lines[1] + me % 4
    arrive(block, 0)
    push(block, 4, one)
    push(block, 8, two)
    place(0, lines[3])
    pass_on(0, 3)
    loads[5].wait()
    normed(0, h0_ref)
    for j in (2, 3):
        block = lines[j] + me % 4
        arrive(block, j - 1)
        push(block, 3 + j, one)
        push(block, 7 + j, two)
        block = lines[j - 1] + first % 4
        arrive(block, 3 + j - 1)
        push(block, 11 + j - 1, two)
        if j == 2:
            place(0, lines[1])
            pass_on(0, 1)
    block = lines[3] + first % 4
    arrive(block, 6)
    push(block, 14, two)
    place(0, lines[0])
    pass_on(0, 0)
    normed(1, h1_ref)
    for group in range(0, experts, 4):
        place(1, group)
    saves = [
        pltpu.make_async_copy(slots_ref.at[0, me], in0_ref.at[me], sems.at[6]),
        pltpu.make_async_copy(slots_ref.at[1, me], in1_ref.at[me], sems.at[7]),
    ]
    for j in range(4):
        arrive(lines[j] + second % 4, 7 + j)
        arrive(lines[j] + far % 4, 11 + j)
    for role in EARLY_G:
        if role:
            pass_one(1, role)
    side = pl.ds(pl.multiple_of(core * half, 128), half)
    joint = send(
        out_ref.at[:, wide : wide + half], full_ref.at[:, side], send_sem.at[18], recv_sem.at[18], twin
    )
    joint.start()
    full_ref[:, side] = out_ref[:, wide : wide + half]
    for copy in share:
        copy.wait()
    saves += [
        pltpu.make_async_copy(out_ref, out_save_ref, sems.at[8]),
        pltpu.make_async_copy(h0_ref, h0_save_ref, sems.at[9]),
        pltpu.make_async_copy(h1_ref, h1_save_ref, sems.at[10]),
        pltpu.make_async_copy(slots_ref.at[1], given_ref, sems.at[22]),
        pltpu.make_async_copy(all_ref, all_save_ref, sems.at[23]),
        pltpu.make_async_copy(column_ref, column_save_ref, sems.at[24]),
        pltpu.make_async_copy(gains_ref, gains_save_ref, sems.at[29]),
        pltpu.make_async_copy(full_ref, full_save_ref, sems.at[11]),
    ]
    for save in saves[:-1]:
        save.start()
    attend_kernel(
        0, h0_ref, out_ref, all_ref, saved0_ref, o_ref, lse0_ref, col_ref, heads_ref, sems.at[12]
    )
    joint.wait()
    saves[-1].start()
    groups = [lines[j] for j in (2, 3, 1, 0)]
    steps = iter((2, 3, 1, 0))

    def hand_on(group):
        j = next(steps)
        for i in range(4):
            role = 4 * j + i
            if role:
                copy = send(
                    first_ref.at[0, chips[role]],
                    take_ref.at[me],
                    swap_send.at[32 + role],
                    swap_recv.at[32 + role],
                    {"shard": chips[role]},
                )
            else:
                copy = pltpu.make_async_copy(first_ref.at[0, me], take_ref.at[me], sems.at[13])
            copy.start()
            swaps.append(copy)

    post_stage(
        0, capacity, groups, x_ref, o_ref, full_ref, gain_two_ref, target_ref, hand_on, x10_ref,
        attended0_ref, first_ref.at[0], x1_ref, joined0_ref, h2_ref, post_sems,
        send_sem.at[19], recv_sem.at[19],
    )
    attend_kernel(
        1, h1_ref, out_ref, all_ref, saved1_ref, o_ref, lse1_ref, col_ref, heads_ref, sems.at[12]
    )
    post_stage(
        1, capacity, groups, x_ref, o_ref, full_ref, gain_two_ref, target_ref, lambda group: None,
        x11_ref, attended1_ref, first_ref.at[1], x1_ref, joined1_ref, h2_ref, post_sems,
        send_sem.at[20], recv_sem.at[20],
    )
    late = [
        pltpu.make_async_copy(first_ref.at[1], sent_ref, sems.at[14]),
        pltpu.make_async_copy(lse0_ref, lse0_save_ref, sems.at[25]),
        pltpu.make_async_copy(lse1_ref, lse1_save_ref, sems.at[26]),
    ]
    for save in late:
        save.start()
    saves += late
    for copy in copies:
        copy.wait_send()
    for save in saves:
        save.wait()
    for copy in swaps:
        copy.wait()


def head(experts, capacity, qkv_weight, out_weight, seg, pad, route, x, g, centroids, gain, gain_two):
    size, columns = qkv_weight.shape[0], 2 * D
    count = seg.shape[2]
    half = D // 2
    in_hbm = lambda array: pltpu.with_memory_space_constraint(array, pltpu.HBM)
    return pl.pallas_call(
        functools.partial(head_kernel, experts, capacity),
        out_shape=(
            pltpu.HBM((16 * size, columns), BF),
            pltpu.HBM((16 * size, D), BF),
            pltpu.HBM((2 * count, D), BF),
            pltpu.HBM((2 * count, D), BF),
            pltpu.HBM((8, 2 * count), jnp.int32),
            pltpu.HBM((count, 8), jnp.int32),
            jax.ShapeDtypeStruct((1, D), F32),
            pltpu.HBM((experts, capacity, D), BF),
            pltpu.HBM((experts, capacity, D), BF),
            pltpu.HBM((experts, capacity, D), BF),
        )
        + (
            pltpu.HBM((2 * count, 3 * half), BF),
            pltpu.HBM((8, 2 * count), F32),
            pltpu.HBM((count, D), F32),
            pltpu.HBM((count, D), BF),
        )
        * 2
        + (pltpu.HBM((experts, capacity, D), BF),) * 2
        + (pltpu.HBM((MICRO, D), F32),),
        in_specs=[HBM_WHOLE] * 10,
        out_specs=(HBM_WHOLE,) * 6 + (VMEM_WHOLE,) + (HBM_WHOLE,) * 14,
        scratch_shapes=[
            pltpu.VMEM((MICRO, D), F32),
            pltpu.VMEM((D,), BF),
            pltpu.VMEM((D,), BF),
            pltpu.VMEM((8, 2 * count), jnp.int32),
            pltpu.VMEM((8, count), jnp.int32),
            pltpu.VMEM((count, 8), jnp.int32),
            pltpu.VMEM((8, 2 * count), F32),
            pltpu.VMEM((8, 2 * count), F32),
            pltpu.VMEM((experts, D), BF),
            pltpu.VMEM((size, columns), BF),
            pltpu.VMEM((MICRO * count, D), BF),
            pltpu.VMEM((MICRO * count, D), BF),
            pltpu.VMEM((8, count), jnp.int32),
            pltpu.VMEM((MICRO, experts, capacity, D), BF),
            pltpu.VMEM((16 * size, columns), BF),
            pltpu.VMEM((16 * size, D), BF),
            pltpu.VMEM((2 * count, D), BF),
            pltpu.VMEM((2 * count, D), BF),
            pltpu.VMEM((2 * count, 1), F32),
            pltpu.VMEM((2 * count, 3 * half), BF),
            pltpu.VMEM((2 * count, half), BF),
            pltpu.VMEM((MICRO, experts, capacity, D), BF),
            pltpu.VMEM((count, D), F32),
            pltpu.VMEM((count, D), BF),
            pltpu.VMEM((count, D), BF),
            pltpu.VMEM((count, D), BF),
            pltpu.SemaphoreType.DMA((21,)),
            pltpu.SemaphoreType.DMA((21,)),
            pltpu.SemaphoreType.DMA((48,)),
            pltpu.SemaphoreType.DMA((48,)),
            pltpu.SemaphoreType.DMA((30,)),
            pltpu.SemaphoreType.DMA((2,)),
        ],
        compiler_params=pltpu.CompilerParams(
            collective_id=0, has_side_effects=True, vmem_limit_bytes=52 << 20
        ),
        cost_estimate=pl.CostEstimate(flops=0, bytes_accessed=100 << 20, transcendentals=0),
        name="head",
    )(
        in_hbm(qkv_weight), in_hbm(out_weight), in_hbm(seg), in_hbm(pad), in_hbm(route), in_hbm(x),
        in_hbm(g), in_hbm(centroids), in_hbm(gain), in_hbm(gain_two),
    )


def scatter_stage(
    packed_ref, few, gqkv_ref, gout_ref, gsmall_ref,
    theirs_ref, rx1_ref, rx2_ref, rx3_ref, tx1_ref, tx2_ref, sum_ref, send_sem, recv_sem, between,
):
    me, first, second, far, line = places()
    core = lax.axis_index("ctx")
    lines = [4 * z for z in line]
    part = sum_ref.shape[0] // 2
    half = gout_ref.shape[1] // 2
    wide = 3 * half
    peers = [{"shard": lines[j] + me % 4} for j in (1, 2, 3)]
    one, two, twin = {"shard": first}, {"shard": second}, {"ctx": 1 - core}
    order = (3, 2, 1, 0)
    copies = []

    def push(src, dst, role, peer):
        copy = send(src, dst, send_sem.at[role], recv_sem.at[role], peer)
        copy.start()
        copies.append(copy)

    def arrive(dst, role):
        send(dst, dst, send_sem.at[role], recv_sem.at[role], one).wait_recv()

    for j in order:
        push(packed_ref.at[lines[j] + far % 4], rx1_ref.at[j], j, two)
    for j in order:
        push(packed_ref.at[lines[j] + second % 4], rx1_ref.at[4 + j], 4 + j, two)
    between(0)
    for j in order:
        arrive(rx1_ref.at[j], j)
        total = packed_ref[lines[j] + first % 4].astype(F32) + rx1_ref[j].astype(F32)
        tx1_ref[j] = total.astype(BF)
        push(tx1_ref.at[j], rx2_ref.at[j], 8 + j, one)
    own = None
    for j in order:
        arrive(rx1_ref.at[4 + j], 4 + j)
        total = packed_ref[lines[j] + me % 4].astype(F32) + rx1_ref[4 + j].astype(F32)
        arrive(rx2_ref.at[j], 8 + j)
        total = total + rx2_ref[j].astype(F32)
        if j:
            tx2_ref[j - 1] = total.astype(BF)
            push(tx2_ref.at[j - 1], rx3_ref.at[j - 1], 11 + j, peers[j - 1])
        else:
            own = total
    between(1)
    for j in (1, 2, 3):
        arrive(rx3_ref.at[j - 1], 11 + j)
        own = own + rx3_ref[j - 1].astype(F32)
    for copy in traded(*few):
        copy.wait()
    sum_ref[:, 0 : wide + half] = own
    sum_ref[:, wide + half :] = jnp.sum(few[1][...], axis=0)
    push(
        sum_ref.at[pl.ds(pl.multiple_of((1 - core) * part, 8), part), :], theirs_ref, 15, twin
    )
    arrive(theirs_ref, 15)
    mine, theirs = sum_ref[pl.ds(pl.multiple_of(core * part, 8), part), :], theirs_ref[...]
    low = jnp.where(core == 0, mine, theirs)
    high = jnp.where(core == 0, theirs, mine)
    for at in range(3):
        gqkv_ref[:, 2 * at * half : (2 * at + 1) * half] = low[:, at * half : (at + 1) * half]
        gqkv_ref[:, (2 * at + 1) * half : (2 * at + 2) * half] = high[:, at * half : (at + 1) * half]
    gout_ref[:, 0:half] = low[:, wide : wide + half]
    gout_ref[:, half:] = high[:, wide : wide + half]
    gsmall_ref[...] = mine[:, wide + half :] + theirs[:, wide + half :]
    for copy in copies:
        copy.wait_send()


def normal(values):
    centre = values - jnp.mean(values, axis=1, keepdims=True)
    spread = jnp.mean(centre * centre, axis=1, keepdims=True)
    scale = lax.rsqrt(spread + EPSILON)
    return centre * scale, scale


def normal_back(unit, scale, gain, grad):
    pull = grad * gain
    return scale * (
        pull
        - jnp.mean(pull, axis=1, keepdims=True)
        - unit * jnp.mean(pull * unit, axis=1, keepdims=True)
    )


RB = 256


def post_stage(
    micro, capacity, groups, x_ref, o_ref, wo_ref, gain_ref, target_ref, hand_on, x1_out_ref, full_out_ref,
    slots_ref, x1_ref, full_ref, h_ref, sems, send_sem, recv_sem,
):
    core = lax.axis_index("ctx")
    rows, width = x1_ref.shape[0], o_ref.shape[1]
    twin = {"ctx": 1 - core}
    mine = pl.ds(pl.multiple_of(core * width, 128), width)
    copy = send(
        o_ref.at[pl.ds(pl.multiple_of((1 - core) * rows, 128), rows), :],
        full_ref.at[:, mine],
        send_sem,
        recv_sem,
        twin,
    )
    copy.start()
    full_ref[:, mine] = o_ref[pl.ds(pl.multiple_of(core * rows, 128), rows), :]
    copy.wait()

    def norm(block, carry):
        at = pl.ds(pl.multiple_of(block * RB, RB), RB)
        value = x_ref[pl.ds(micro * rows + pl.multiple_of(block * RB, RB), RB), :].astype(F32)
        value = value + nn(full_ref[at, :], wo_ref[...])
        x1_ref[at, :] = value
        h_ref[at, :] = (normal(value)[0] * gain_ref[...]).astype(BF)
        return carry

    lax.fori_loop(0, rows // RB, norm, 0)
    saves = [
        pltpu.make_async_copy(full_ref, full_out_ref, sems.at[0]),
        pltpu.make_async_copy(x1_ref, x1_out_ref, sems.at[1]),
    ]
    for save in saves:
        save.start()
    for group in groups:
        slot = lax.broadcasted_iota(jnp.int32, (4 * capacity, rows), 0) + group * capacity
        pick = (slot == target_ref[micro : micro + 1, :]).astype(F32).astype(BF)
        value = nn(pick, h_ref[...]).astype(BF).reshape(4, capacity, D)
        slots_ref[pl.ds(pl.multiple_of(group, 4), 4)] = value
        hand_on(group)
    for save in saves:
        save.wait()


def fore_stage(
    has_prev, micro, dh_ref, target_ref, g_ref, x1_ref, gain_ref, wo_ref, full_ref, prev_two_ref,
    do_ref, dx_ref, gout_ref, gtwo_ref, dy_ref, all_ref, send_sem, recv_sem,
):
    core = lax.axis_index("ctx")
    rows, width = x1_ref.shape[0], do_ref.shape[1]
    slots = dh_ref.shape[0] * dh_ref.shape[1]
    twin = {"ctx": 1 - core}

    def norm(block, total):
        at = pl.ds(pl.multiple_of(block * RB, RB), RB)
        slot = lax.broadcasted_iota(jnp.int32, (RB, slots), 1)
        pick = (slot == target_ref[at, micro : micro + 1]).astype(F32).astype(BF)
        grad = nn(pick, dh_ref[...].reshape(slots, D))
        unit, scale = normal(x1_ref[at, :])
        dx = g_ref[at, :].astype(F32) + normal_back(unit, scale, gain_ref[...], grad)
        dx_ref[at, :] = dx
        dy = dx.astype(BF)
        dy_ref[at, :] = dy
        all_ref[at, :] = nt(dy, wo_ref[...]).astype(BF)
        return total + jnp.sum(grad * unit, axis=0, keepdims=True)

    total = lax.fori_loop(0, rows // RB, norm, jnp.zeros((1, D), F32))
    gtwo_ref[...] = prev_two_ref[...] + total if has_prev else total
    mine = pl.ds(pl.multiple_of(core * rows, 128), rows)
    copy = send(
        all_ref.at[:, pl.ds(pl.multiple_of((1 - core) * width, 128), width)],
        do_ref.at[mine, :],
        send_sem,
        recv_sem,
        twin,
    )
    copy.start()
    do_ref[mine, :] = all_ref[:, pl.ds(pl.multiple_of(core * width, 128), width)]
    grad = tn(full_ref[...], dy_ref[...])
    gout_ref[...] = gout_ref[...] + grad if has_prev else grad
    copy.wait()


def tail_stage(
    has_prev, dh_ref, x_ref, dx_ref, gain_ref, prev_ref, grad_out_ref, gone_ref, grad_ref, rx_ref, sems
):
    core = lax.axis_index("ctx")
    rows = dx_ref.shape[0]
    saves = []
    total = jnp.zeros((1, D), F32)
    for off in range(0, rows, RB):
        at = slice(off, off + RB)
        mine = pl.ds(pl.multiple_of(core * rows + off, RB), RB)
        grad = dh_ref[mine, :] + rx_ref[at, :].astype(F32)
        unit, scale = normal(x_ref[at, :].astype(F32))
        grad_ref[at, :] = dx_ref[at, :] + normal_back(unit, scale, gain_ref[...], grad)
        save = pltpu.make_async_copy(grad_ref.at[at, :], grad_out_ref.at[at, :], sems.at[off // RB])
        save.start()
        saves.append(save)
        total = total + jnp.sum(grad * unit, axis=0, keepdims=True)
    gone_ref[...] = prev_ref[...] + total if has_prev else total
    return saves


def back_kernel(
    slot_ref, target_ref, cot_ref, tok_ref, w_in_ref, wo_in_ref, label_ref, gains_ref, gc0_ref, gc1_ref,
    x10_ref, full0_ref, h0_ref, qkv0_ref, lse0_ref, x11_ref, full1_ref, h1_ref, qkv1_ref, lse1_ref,
    give_dh_ref, give_y0_ref, give_y1_ref, give_up_ref, give_down_ref,
    gqkv_ref, gproj_ref, gsmall_ref, in0_ref, in1_ref, take_dh_ref, take_y0_ref, take_y1_ref,
    take_up_ref, take_down_ref,
    dh_ref, g_ref, x_ref, x1_ref, full_ref, h_ref, w_ref, wo_ref, qkv_ref,
    do_ref, dx_ref, dy_ref, all_ref, part_ref, dqkv_ref, dk_ref, dv_ref, kt_ref, col_ref,
    tx_ref, rx_ref, go_ref, tgo_ref, rgo_ref, gw_ref, gout_ref, gtwo_ref, gone_ref, packed_ref, small_ref,
    theirs_ref, rx1_ref, rx2_ref, rx3_ref, tx1_ref, tx2_ref, sum_ref, few_ref, few_rx_ref,
    sems, save_sems, dh_send, dh_recv, y0_send, y0_recv, y1_send, y1_recv, send_sem, recv_sem,
    ring_send, ring_recv, few_send, few_recv,
):
    me, core = lax.axis_index("shard"), lax.axis_index("ctx")
    rows = x_ref.shape[0]
    half = gout_ref.shape[1]
    twin = {"ctx": 1 - core}
    gain_one_ref, gain_two_ref = gains_ref.at[0:1, :], gains_ref.at[1:2, :]
    sources = (
        (x10_ref, full0_ref, h0_ref, qkv0_ref, lse0_ref, in0_ref),
        (x11_ref, full1_ref, h1_ref, qkv1_ref, lse1_ref, in1_ref),
    )

    def loads_of(micro):
        x1_in_ref, full_in_ref, h_in_ref, qkv_in_ref = sources[micro][:4]
        mine = pl.ds(micro * rows, rows)
        pairs = dict(
            dh=((slot_ref, take_dh_ref)[micro], dh_ref),
            x1=(x1_in_ref, x1_ref),
            g=(cot_ref.at[mine, :], g_ref),
            full=(full_in_ref, full_ref),
            qkv=(qkv_in_ref, qkv_ref),
            h=(h_in_ref, h_ref),
            x=(tok_ref.at[mine, :], x_ref),
        )
        return {
            name: pltpu.make_async_copy(src, dst, sems.at[8 * micro + at])
            for at, (name, (src, dst)) in enumerate(pairs.items())
        }

    loads = [loads_of(0), loads_of(1)]
    shared = [
        pltpu.make_async_copy(wo_in_ref, wo_ref, sems.at[16]),
        pltpu.make_async_copy(w_in_ref, w_ref, sems.at[17]),
    ]
    for name in ("dh", "x1", "g", "full"):
        loads[0][name].start()
    shared[0].start()
    for name in ("qkv", "h", "x"):
        loads[0][name].start()
    shared[1].start()
    greet([{"shard": chip} for chip in all_chips()[1:]] + [twin])
    first_trade = trade(give_dh_ref, take_dh_ref, dh_send, dh_recv, sems.at[18])
    swaps = trade_all(
        (give_y0_ref, take_y0_ref, y0_send, y0_recv, sems.at[19], LATE_0),
        (give_y1_ref, take_y1_ref, y1_send, y1_recv, sems.at[20], EARLY_1),
    )
    for micro in range(MICRO):
        has_prev = micro > 0
        load, lse_ref, grad_out_ref = loads[micro], sources[micro][4], sources[micro][5]
        for name in ("dh", "x1", "g", "full"):
            load[name].wait()
        if not has_prev:
            shared[0].wait()
        fore_stage(
            has_prev, micro, dh_ref, target_ref, g_ref, x1_ref, gain_two_ref, wo_ref, full_ref, gtwo_ref,
            do_ref, dx_ref, go_ref, gtwo_ref, dy_ref, all_ref, send_sem.at[3 * micro],
            recv_sem.at[3 * micro],
        )
        if has_prev:
            tgo_ref[...] = go_ref[:, pl.ds(pl.multiple_of((1 - core) * half, 128), half)].astype(BF)
            cross = send(tgo_ref, rgo_ref, send_sem.at[6], recv_sem.at[6], twin)
            cross.start()
        else:
            loads[1]["g"].start()
            loads[1]["full"].start()
            shared[1].wait()
        load["qkv"].wait()
        load["h"].wait()
        attend_back_kernel(
            micro, qkv_ref, do_ref, lse_ref, label_ref, dqkv_ref, dk_ref, dv_ref, kt_ref, col_ref
        )

        def weigh():
            for at in range(0, dqkv_ref.shape[1], 384):
                grad = tn(h_ref[...], dqkv_ref[:, at : at + 384])
                gw_ref[:, at : at + 384] = gw_ref[:, at : at + 384] + grad if has_prev else grad

        def hand_over():
            spread_stage(dqkv_ref, w_ref, part_ref)
            tx_ref[...] = part_ref[pl.ds(pl.multiple_of((1 - core) * rows, 128), rows), :].astype(BF)
            joint = send(tx_ref, rx_ref, send_sem.at[3 * micro + 1], recv_sem.at[3 * micro + 1], twin)
            joint.start()
            return joint

        def finish(joint):
            load["x"].wait()
            joint.wait()
            return tail_stage(
                has_prev, part_ref, x_ref, dx_ref, gain_one_ref, gone_ref, grad_out_ref, gone_ref,
                x1_ref, rx_ref, save_sems.at[pl.ds(micro * (rows // RB), rows // RB)],
            )

        if not has_prev:
            joint = hand_over()
            loads[1]["qkv"].start()
            weigh()
            loads[1]["h"].start()
            saves = finish(joint)
            loads[1]["x"].start()
            for copy in saves:
                copy.wait()
            loads[1]["x1"].start()
            for copy in first_trade:
                copy.wait()
            loads[1]["dh"].start()
    weigh()
    cross.wait()
    own = go_ref[:, pl.ds(pl.multiple_of(core * half, 128), half)]
    gout_ref[...] = own + rgo_ref[...].astype(F32)
    part = packed_ref.shape[1] // 2

    def cut(chunk):
        top = pl.ds(pl.multiple_of(chunk * part, 8), part)
        low = pl.ds(pl.multiple_of(D // 2 + chunk * part, 8), part)
        return lambda ref: jnp.concatenate([ref[top, :], ref[low, :]], axis=0)

    def pack(chunk, carry):
        both = cut(chunk)
        packed_ref[chunk, :, 0 : 3 * half] = both(gw_ref).astype(BF)
        packed_ref[chunk, :, 3 * half :] = both(gout_ref).astype(BF)
        return carry

    lax.fori_loop(0, packed_ref.shape[0], pack, 0)
    few = (few_ref, few_rx_ref, few_send, few_recv, sems.at[21])

    def between(step):
        roles = (NEXT_1, LATE_1)[step]
        swaps.extend(trade(give_y1_ref, take_y1_ref, y1_send, y1_recv, sems.at[20], roles))
        if step == 0:
            swaps.extend(finish(hand_over()))
            row = lax.broadcasted_iota(jnp.int32, (128, D), 0)
            small = jnp.where(row == 0, gone_ref[...], 0.0) + jnp.where(row == 1, gtwo_ref[...], 0.0)
            small = small + jnp.where(row == 2 + me, gc0_ref[...] + gc1_ref[...], 0.0)
            small_ref[...] = jnp.transpose(small)

            def pack_few(chunk, carry):
                few_ref[chunk] = cut(chunk)(small_ref)
                return carry

            lax.fori_loop(0, few_ref.shape[0], pack_few, 0)
            trade(*few)
            for at, (give_ref, take_ref) in enumerate(((give_up_ref, take_up_ref), (give_down_ref, take_down_ref))):
                swaps.append(send(give_ref, take_ref, send_sem.at[7 + at], recv_sem.at[7 + at], twin))
                swaps[-1].start()

    scatter_stage(
        packed_ref, few, gqkv_ref, gproj_ref, gsmall_ref, theirs_ref, rx1_ref, rx2_ref, rx3_ref, tx1_ref,
        tx2_ref, sum_ref, ring_send, ring_recv, between,
    )
    for copy in swaps:
        copy.wait()


def back(dh, target, g, x, w_all, wo, labels, gains, gc0, gc1, kept0, kept1, *give):
    x1, _, h_all, _, _ = kept0
    rows, seq, half = x1.shape[0], h_all.shape[0], D // 2
    groups = dh.shape[0]
    chunk = (D // groups, 4 * half)
    part = chunk[0] // 2
    in_hbm = lambda array: pltpu.with_memory_space_constraint(array, pltpu.HBM)
    kept = lambda arrays: [in_hbm(array) for array in arrays[:4]] + [arrays[4]]
    args = [in_hbm(dh), target, in_hbm(g), in_hbm(x), in_hbm(w_all), in_hbm(wo), labels, gains, gc0, gc1]
    args += kept(kept0) + kept(kept1) + [in_hbm(array) for array in give]
    kept_specs = [HBM_WHOLE] * 4 + [VMEM_WHOLE]
    return pl.pallas_call(
        back_kernel,
        out_shape=(
            jax.ShapeDtypeStruct((part, 3 * D), F32),
            jax.ShapeDtypeStruct((part, D), F32),
            jax.ShapeDtypeStruct((part, 128), F32),
            pltpu.HBM((rows, D), F32),
            pltpu.HBM((rows, D), F32),
        )
        + tuple(pltpu.HBM(array.shape, BF) for array in give),
        in_specs=[HBM_WHOLE, VMEM_WHOLE]
        + [HBM_WHOLE] * 4
        + [VMEM_WHOLE] * 4
        + kept_specs * 2
        + [HBM_WHOLE] * 5,
        out_specs=(VMEM_WHOLE,) * 3 + (HBM_WHOLE,) * 7,
        scratch_shapes=[
            pltpu.VMEM(dh.shape, BF),
            pltpu.VMEM((rows, D), BF),
            pltpu.VMEM((rows, D), BF),
            pltpu.VMEM((rows, D), F32),
            pltpu.VMEM((rows, D), BF),
            pltpu.VMEM((seq, D), BF),
            pltpu.VMEM((D, 2 * D), BF),
            pltpu.VMEM((D, D), BF),
            pltpu.VMEM((seq, 3 * half), BF),
            pltpu.VMEM((seq, half), BF),
            pltpu.VMEM((rows, D), F32),
            pltpu.VMEM((rows, D), BF),
            pltpu.VMEM((rows, D), BF),
            pltpu.VMEM((seq, D), F32),
            pltpu.VMEM((seq, 3 * half), BF),
            pltpu.VMEM((seq, half), F32),
            pltpu.VMEM((seq, half), F32),
            pltpu.VMEM((half, seq), BF),
            pltpu.VMEM((seq, 1), F32),
            pltpu.VMEM((rows, D), BF),
            pltpu.VMEM((rows, D), BF),
            pltpu.VMEM((D, D), F32),
            pltpu.VMEM((D, half), BF),
            pltpu.VMEM((D, half), BF),
            pltpu.VMEM((D, 3 * half), F32),
            pltpu.VMEM((D, half), F32),
            pltpu.VMEM((1, D), F32),
            pltpu.VMEM((1, D), F32),
            pltpu.VMEM((groups,) + chunk, BF),
            pltpu.VMEM((D, 128), F32),
            pltpu.VMEM((part, chunk[1] + 128), F32),
            pltpu.VMEM((8,) + chunk, BF),
            pltpu.VMEM((4,) + chunk, BF),
            pltpu.VMEM((3,) + chunk, BF),
            pltpu.VMEM((4,) + chunk, BF),
            pltpu.VMEM((3,) + chunk, BF),
            pltpu.VMEM((chunk[0], chunk[1] + 128), F32),
            pltpu.VMEM((groups, chunk[0], 128), F32),
            pltpu.VMEM((groups, chunk[0], 128), F32),
            pltpu.SemaphoreType.DMA((22,)),
            pltpu.SemaphoreType.DMA((MICRO * (rows // RB),)),
        ]
        + [pltpu.SemaphoreType.DMA((16,))] * 6
        + [pltpu.SemaphoreType.DMA((9,))] * 2
        + [pltpu.SemaphoreType.DMA((16,))] * 4,
        compiler_params=pltpu.CompilerParams(
            collective_id=1, has_side_effects=True, vmem_limit_bytes=60 << 20
        ),
        cost_estimate=pl.CostEstimate(flops=4 << 33, bytes_accessed=60 << 20, transcendentals=0),
        name="back",
    )(*args)


def body_pair(
    tokens,
    cotangent,
    segment_ids,
    padding,
    routes,
    norm_one_gain,
    qkv_weight,
    out_weight,
    norm_two_gain,
    centroids,
    expert_in,
    expert_out,
):
    local_len = tokens.shape[2]
    experts = centroids.shape[1]
    capacity = max(2, 2 * local_len // experts)
    x_all = tokens.reshape(MICRO * local_len, D)
    g_all = cotangent.reshape(MICRO * local_len, D)
    (w_all, out_full, h0, h1, labels, columns, centre, g0_in, g1_part, h0_in,
     qkv0, lse0, x10, full0, qkv1, lse1, x11, full1, sent1, g1_sent, gains) = head(
        experts, capacity, qkv_weight, out_weight, segment_ids, padding,
        routes.reshape(MICRO, 1, local_len), x_all, g_all, centroids.T,
        norm_one_gain, norm_two_gain,
    )
    y0, dh0, gc0, gup, gdown, h1_in, g1_in = expert(
        h0_in, g0_in, centre, expert_in[0], expert_out[0], (sent1, g1_sent, g1_part), None
    )
    y1, dh1, gc1, own_up, own_down, sent_up, sent_down, dh0_in, y0a = expert(
        h1_in, g1_in, centre, expert_in[0], expert_out[0], (dh0, y0), (gup, gdown)
    )
    grad_qkv, grad_out, small, in0, in1, _, y0b, y1_in, got_up, got_down = back(
        dh0_in, columns, g_all, x_all, w_all, out_full, labels, gains, gc0, gc1,
        (x10, full0, h0, qkv0, lse0), (x11, full1, h1, qkv1, lse1),
        dh1, y0, y1, sent_up, sent_down,
    )
    block_out, grad_tokens, grad_up, grad_down, grad_qkv, grad_out, grad_one, grad_two, grad_centre = emit(
        x10, x11, y0a, y0b, y1_in, columns, in0, in1, own_up, got_up, own_down, got_down,
        grad_qkv, grad_out, small,
    )
    return (
        block_out.reshape(MICRO, 1, local_len, D),
        grad_tokens.reshape(MICRO, 1, local_len, D),
        grad_one.reshape(-1),
        grad_qkv,
        grad_out,
        grad_two.reshape(-1),
        grad_centre.T,
        grad_up[None],
        grad_down[None],
    )


def solution(mesh):
    plan = body_pair if (mesh.shape["ctx"], mesh.shape["shard"]) == (2, 16) else body
    in_specs = (
        P(None, "shard", "ctx", None),
        P(None, "shard", "ctx", None),
        P(None, "shard", "ctx"),
        P(None, "shard", "ctx"),
        P(None, "shard", "ctx", None),
        P(),
        P("shard", None),
        P("shard", None),
        P(),
        P(),
        P("shard", None, None),
        P("shard", None, None),
    )
    out_specs = (
        P(None, "shard", "ctx", None),
        P(None, "shard", "ctx", None),
        P(("ctx", "shard")),
        P(("ctx", "shard"), None),
        P(("ctx", "shard"), None),
        P(("ctx", "shard")),
        P(("ctx", "shard"), None),
        P("shard", None, "ctx"),
        P("shard", "ctx", None),
    )
    return jax.shard_map(plan, mesh=mesh, in_specs=in_specs, out_specs=out_specs, check_vma=False)
```
